32 devices in a mesh: dp: 16 (over z, x, core), ctx: 2 (over y).
Axes of the slice: x: 2, y: 2, z: 4, core: 2. Of those that a mesh axis runs over, the one named last changes fastest.
Arguments:
- inputs: bfloat16 [16, 1024, 768], P('dp', 'ctx'), may hold values from -6 to 6
- cotangent: bfloat16 [16, 1024, 768], P('dp', 'ctx'), may hold values from -6 to 6
- query_weight: bfloat16 [768, 768], P(('dp', 'ctx')), may hold values from -0.649519 to 0.649519
- query_bias: bfloat16 [768], P(('dp', 'ctx')), may hold values from -3 to 3
- key_weight: bfloat16 [768, 768], P(('dp', 'ctx')), may hold values from -0.21875 to 0.21875
- value_weight: bfloat16 [768, 768], P(('dp', 'ctx')), may hold values from -0.21875 to 0.21875
- value_bias: bfloat16 [768], P(('dp', 'ctx')), may hold values from -2 to 2
- output_weight: bfloat16 [768, 768], P(('dp', 'ctx')), may hold values from -0.875 to 0.875
- output_bias: bfloat16 [768], P(('dp', 'ctx')), may hold values from -2 to 2
- first_gain: bfloat16 [768], P(('dp', 'ctx')), may hold values from 0.5 to 1.5
- first_shift: bfloat16 [768], P(('dp', 'ctx')), may hold values from -2 to 2
- inner_weight: bfloat16 [768, 3072], P(('dp', 'ctx')), may hold values from -0.21875 to 0.21875
- inner_bias: bfloat16 [3072], P(('dp', 'ctx')), may hold values from -2 to 2
- outer_weight: bfloat16 [3072, 768], P(('dp', 'ctx')), may hold values from -0.15625 to 0.15625
- outer_bias: bfloat16 [768], P(('dp', 'ctx')), may hold values from -2 to 2
- second_gain: bfloat16 [768], P(('dp', 'ctx')), may hold values from 0.5 to 1.5
- second_shift: bfloat16 [768], P(('dp', 'ctx')), may hold values from -2 to 2
- lengths: int32 [16], P('dp'), may hold values from 256 to 1024, as said below
- random_blocks: int32 [16, 16, 12, 3], P('dp'), may hold values from 0 to 15
- threshold: int32 [1], replicated, may hold values from 100 to 399
Outputs:
- output: bfloat16 [16, 1024, 768], P('dp', 'ctx')
- input_grad: float32 [16, 1024, 768], P('dp', 'ctx')
- query_weight_grad: float32 [768, 768], P(('dp', 'ctx'))
- query_bias_grad: float32 [768], P(('dp', 'ctx'))
- key_weight_grad: float32 [768, 768], P(('dp', 'ctx'))
- value_weight_grad: float32 [768, 768], P(('dp', 'ctx'))
- value_bias_grad: float32 [768], P(('dp', 'ctx'))
- output_weight_grad: float32 [768, 768], P(('dp', 'ctx'))
- output_bias_grad: float32 [768], P(('dp', 'ctx'))
- first_gain_grad: float32 [768], P(('dp', 'ctx'))
- first_shift_grad: float32 [768], P(('dp', 'ctx'))
- inner_weight_grad: float32 [768, 3072], P(('dp', 'ctx'))
- inner_bias_grad: float32 [3072], P(('dp', 'ctx'))
- outer_weight_grad: float32 [3072, 768], P(('dp', 'ctx'))
- outer_bias_grad: float32 [768], P(('dp', 'ctx'))
- second_gain_grad: float32 [768], P(('dp', 'ctx'))
- second_shift_grad: float32 [768], P(('dp', 'ctx'))
- query_weight_clipped: bfloat16 [768, 768], P(('dp', 'ctx'))
- query_bias_clipped: bfloat16 [768], P(('dp', 'ctx'))
- key_weight_clipped: bfloat16 [768, 768], P(('dp', 'ctx'))
- logit_maxima: float32 [12], replicated
The draws below stay inside these ranges and needn't reach their ends.
Inputs may be any that keep to these rules, and one draw needn't show every extreme that they name: `lengths`: each sequence's valid tokens are its first ones; at least one sequence has all 1024 valid.
All inputs are finite; a program needn't handle non-finite values.
Results may differ from the reference program's by a relative error of at most 0.015.
The reference program's roundings to bfloat16 on the way count: a program that leaves them out, or rounds other values in their place, can miss the bound.
Values may be sent and summed in bfloat16 or wider, within the bound.
A program may use at most 256 MiB of HBM per device.

```python
import math
import jax
import jax.numpy as jnp
from jax import lax

D = 768
H = 12
HD = 64
FF = 3072
BLK = 64
RB = 3
LEN = 1024
NB = 16
SEQS = 16


def draw_lengths(key, part):
    first_key, second_key = jax.random.split(jax.random.fold_in(key, 11))
    drawn = jax.random.randint(first_key, (SEQS,), LEN // 4, LEN + 1)
    full_spot = jax.random.randint(second_key, (), 0, SEQS)
    return jnp.where(jnp.arange(SEQS) == full_spot, LEN, drawn).astype(jnp.int32)


def draw_query_weight(key, part):
    order_key, spread_key, entry_key = jax.random.split(jax.random.fold_in(key, 23), 3)
    ranks = jax.random.permutation(order_key, H)
    spread = jax.random.uniform(spread_key, (H,), jnp.float32, 0.0, 1.0)
    head_scale = jnp.where(ranks < H // 2, 0.8 + 0.2 * spread, 2.6 + 0.4 * spread)
    column_scale = jnp.repeat(head_scale, HD)
    entries = jax.random.truncated_normal(entry_key, -6.0, 6.0, (D, D), jnp.float32)
    return (entries * column_scale[None, :] * D ** (-0.5)).astype(jnp.bfloat16)


def set_ends(values, stream_key, least, largest):
    extent = values.shape
    place = [jax.random.randint(jax.random.fold_in(stream_key, axis), (), 0, extent[axis]) for axis in range(len(extent))]
    values = values.at[tuple(place)].set(least)
    longest = extent.index(max(extent))
    place[longest] = (place[longest] + 1) % extent[longest]
    return values.at[tuple(place)].set(largest)


def steps_of(stream_key, dims, pieces, smallest, top_value):
    gain, own = 1.0, jax.random.fold_in(stream_key, 6)
    for position, blocks in pieces:
        steps = jnp.exp(jax.random.uniform(jax.random.fold_in(own, position), (blocks,), jnp.float32, smallest / len(pieces), top_value / len(pieces)))
        gain = gain * jnp.repeat(steps, dims[position] // blocks).reshape([-1 if axis == position else 1 for axis in range(len(dims))])
    return gain


def noise(own_key, dims, scale, most, cuts=(), held_as=jnp.bfloat16):
    values = jax.random.normal(own_key, dims, jnp.float32) * scale
    if len(cuts) > 0:
        values = steps_of(own_key, dims, cuts, -0.22, 0.18) * values
    return jnp.clip(values, min=-most, max=most).astype(held_as)


def setup_inputs(seed: int = 0) -> dict:
    key_list = jax.random.split(jax.random.key(seed), 21)
    inputs = noise(key_list[0], (SEQS, LEN, D), 1.0, 6.0, ((0, 16), (1, 2)))
    cotangent = noise(key_list[1], (SEQS, LEN, D), 1.0, 6.0, ((0, 16), (1, 2)))
    query_weight = draw_query_weight(jax.random.fold_in(key_list[20], 71), 0)
    query_bias = noise(key_list[3], (D,), 0.5, 3.0, ((0, 32),))
    key_weight = noise(key_list[4], (D, D), D ** -0.5, 0.21875, ((0, 32),))
    value_weight = noise(key_list[5], (D, D), D ** -0.5, 0.21875, ((0, 32),))
    value_bias = noise(key_list[6], (D,), 0.3, 2.0, ((0, 32),))
    output_weight = noise(key_list[7], (D, D), (D // 16) ** -0.5, 0.875, ((0, 32),))
    output_bias = noise(key_list[8], (D,), 0.3, 2.0, ((0, 32),))
    first_gain = jnp.clip(1.0 + 0.1 * jax.random.normal(key_list[9], (D,), jnp.float32), 0.5, 1.5).astype(jnp.bfloat16)
    first_shift = noise(key_list[10], (D,), 0.3, 2.0, ((0, 32),))
    inner_weight = noise(key_list[11], (D, FF), D ** -0.5, 0.21875, ((0, 32),))
    inner_bias = noise(key_list[12], (FF,), 0.3, 2.0, ((0, 32),))
    outer_weight = noise(key_list[13], (FF, D), (FF // 2) ** -0.5, 0.15625, ((0, 32),))
    outer_bias = noise(key_list[14], (D,), 0.3, 2.0, ((0, 32),))
    second_gain = jnp.clip(1.0 + 0.1 * jax.random.normal(key_list[15], (D,), jnp.float32), 0.5, 1.5).astype(jnp.bfloat16)
    second_shift = noise(key_list[16], (D,), 0.3, 2.0, ((0, 32),))
    lengths = draw_lengths(jax.random.fold_in(key_list[20], 71), 0)
    random_blocks = set_ends(jax.random.randint(key_list[18], (SEQS, NB, H, RB), 0, NB), jax.random.fold_in(key_list[18], 1), 0, NB - 1).astype(jnp.int32)
    threshold = jax.random.randint(key_list[19], (1,), 100, 400).astype(jnp.int32)
    return {"inputs": inputs, "cotangent": cotangent, "query_weight": query_weight, "query_bias": query_bias, "key_weight": key_weight, "value_weight": value_weight, "value_bias": value_bias, "output_weight": output_weight, "output_bias": output_bias, "first_gain": first_gain, "first_shift": first_shift, "inner_weight": inner_weight, "inner_bias": inner_bias, "outer_weight": outer_weight, "outer_bias": outer_bias, "second_gain": second_gain, "second_shift": second_shift, "lengths": lengths, "random_blocks": random_blocks, "threshold": threshold}


@jax.custom_vjp
def low(v):
    return lax.optimization_barrier(v.astype(jnp.bfloat16)).astype(jnp.float32)

@jax.custom_vjp
def low_back(v):
    return v

def low_keep(v):
    return (low(v), None)

def low_pass(kept, grad):
    return (grad,)

def back_keep(v):
    return (v, None)

def back_low(kept, grad):
    return (low(grad),)
low.defvjp(low_keep, low_pass)
low_back.defvjp(back_keep, back_low)
norm_eps = 1e-12
neg_large = -1e+30

def highest(former, latter):
    return jnp.dot(former, latter, precision=lax.Precision.HIGHEST)

def layer_norm(row_values, gain_vector, shift_vector):
    centre = row_values - lax.optimization_barrier(jnp.mean(row_values, axis=-1, keepdims=True))
    spread = lax.optimization_barrier(jnp.mean(centre * centre, axis=-1, keepdims=True))
    return centre * lax.rsqrt(spread + norm_eps) * gain_vector + shift_vector

def block_pattern(length, random_here, first_block):
    query_index = first_block + jnp.arange(random_here.shape[0]).astype(jnp.int32)[:, None]
    key_index = jnp.arange(NB).astype(jnp.int32)[None, :]
    last_block = (length - 1) // BLK
    fixed_part = (jnp.abs(query_index - key_index) <= 1) | (key_index == 0) | (key_index == last_block)
    fixed_part = fixed_part | (query_index == 0) | (query_index == last_block)
    chosen = jnp.any(random_here[:, :, :, None] == jnp.arange(NB).astype(jnp.int32)[None, None, None, :], axis=2)
    return fixed_part[None, :, :] | jnp.transpose(chosen, (1, 0, 2))

def token_pattern(pattern, length):
    heads_count, blocks_query, blocks_key = pattern.shape
    expanded = jnp.broadcast_to(pattern[:, :, None, :, None], (heads_count, blocks_query, BLK, blocks_key, BLK))
    expanded = expanded.reshape(heads_count, blocks_query * BLK, blocks_key * BLK)
    return expanded & (jnp.arange(blocks_key * BLK) < length)[None, None, :]

def attend(inputs):
    queries, keys, values, length, random_here = inputs
    slice_rows = math.gcd(LEN, 512)
    slice_count = LEN // slice_rows
    key_heads = keys.reshape(LEN, H, HD)
    value_heads = values.reshape(LEN, H, HD)

    def one_slice(piece):
        query_piece, random_piece, start_block = piece
        allowed = token_pattern(block_pattern(length, random_piece, start_block), length)
        query_heads = query_piece.reshape(slice_rows, H, HD)
        raw_scores = jnp.einsum('qhd,khd->hqk', query_heads, key_heads, precision=lax.Precision.HIGHEST) * HD ** (-0.5)
        scores = low_back(raw_scores)
        masked = jnp.where(allowed, scores, neg_large)
        positions = start_block * BLK + jnp.arange(slice_rows).astype(jnp.int32)
        counted = allowed & (positions < length)[None, :, None]
        top_logit = lax.optimization_barrier(jnp.max(jnp.where(counted, scores, neg_large), axis=(1, 2)))
        shifted = masked - lax.optimization_barrier(jnp.max(masked, axis=-1, keepdims=True))
        exponent = jnp.exp(shifted)
        softmax_rows = low(exponent / lax.optimization_barrier(jnp.sum(exponent, axis=-1, keepdims=True)))
        mixture = jnp.einsum('hqk,khd->qhd', softmax_rows, value_heads, precision=lax.Precision.HIGHEST)
        return (mixture.reshape(slice_rows, D), top_logit)
    starts = (jnp.arange(slice_count) * (slice_rows // BLK)).astype(jnp.int32)
    mixtures, tops = lax.map(jax.checkpoint(one_slice), (queries.reshape(slice_count, slice_rows, D), random_here.reshape(slice_count, slice_rows // BLK, H, RB), starts))
    return (mixtures.reshape(LEN, D), lax.optimization_barrier(jnp.max(tops, axis=0)))

def layer(inputs, params, lengths, random_blocks):
    query_weight, query_bias, key_weight, value_weight, value_bias, output_weight, output_bias, first_gain, first_shift, inner_weight, inner_bias, outer_weight, outer_bias, second_gain, second_shift = params
    group_size = inputs.shape[0]
    token_rows = inputs.reshape(group_size * LEN, D)
    queries = low(low_back(highest(token_rows, query_weight) + query_bias))
    keys = low(low_back(highest(token_rows, key_weight)))
    values = low(low_back(highest(token_rows, value_weight) + value_bias))
    attended, top_logits = lax.map(attend, (queries.reshape(group_size, LEN, D), keys.reshape(group_size, LEN, D), values.reshape(group_size, LEN, D), lengths, random_blocks))
    attended = low(low_back(attended.reshape(group_size * LEN, D)))
    projected = low_back(highest(attended, output_weight) + output_bias)
    normed = layer_norm(token_rows + projected, first_gain, first_shift)
    pre_act = low_back(highest(low(normed), inner_weight) + inner_bias)
    activated = low(jax.nn.gelu(pre_act, approximate=False))
    outer_rows = low_back(highest(activated, outer_weight) + outer_bias)
    result = layer_norm(normed + outer_rows, second_gain, second_shift)
    return (result.reshape(group_size, LEN, D), lax.optimization_barrier(jnp.max(top_logits, axis=0)))

def reference(inputs, cotangent, query_weight, query_bias, key_weight, value_weight, value_bias, output_weight, output_bias, first_gain, first_shift, inner_weight, inner_bias, outer_weight, outer_bias, second_gain, second_shift, lengths, random_blocks, threshold):
    params = tuple((tensor.astype(jnp.float32) for tensor in (query_weight, query_bias, key_weight, value_weight, value_bias, output_weight, output_bias, first_gain, first_shift, inner_weight, inner_bias, outer_weight, outer_bias, second_gain, second_shift)))
    per_group = math.gcd(SEQS, max(1, 4096 // LEN))
    group_count = SEQS // per_group

    def regroup(array):
        return array.reshape((group_count, per_group) + array.shape[1:])

    def one_group(state_pair, group_item):
        grad_sums, top_sofar = state_pair
        group_inputs, group_cot, group_lengths, group_random = group_item
        valid_rows = (jnp.arange(LEN)[None, :] < group_lengths[:, None]).astype(jnp.float32)

        def forward(inputs_float, params_float):
            return layer(inputs_float, params_float, group_lengths, group_random)
        result, pullback, group_top = jax.vjp(forward, group_inputs.astype(jnp.float32), params, has_aux=True)
        input_part, param_grads = pullback(group_cot.astype(jnp.float32) * valid_rows[:, :, None])
        grad_sums = jax.tree.map(jnp.add, grad_sums, param_grads)
        return ((grad_sums, jnp.maximum(top_sofar, group_top)), (result.astype(jnp.bfloat16), input_part))
    zero_grads = jax.tree.map(jnp.zeros_like, params)
    start_top = jnp.full((H,), neg_large, jnp.float32)
    (grad_sums, logit_maxima), (outputs, input_parts) = lax.scan(one_group, (zero_grads, start_top), (regroup(inputs), regroup(cotangent), regroup(lengths), regroup(random_blocks)))
    output = outputs.reshape(SEQS, LEN, D)
    input_grad = input_parts.reshape(SEQS, LEN, D)
    query_weight_grad, query_bias_grad, key_weight_grad, value_weight_grad, value_bias_grad, output_weight_grad, output_bias_grad, first_gain_grad, first_shift_grad, inner_weight_grad, inner_bias_grad, outer_weight_grad, outer_bias_grad, second_gain_grad, second_shift_grad = grad_sums
    clip_limit = threshold.astype(jnp.float32)[0] * 0.01
    factors = jnp.sqrt(clip_limit / jnp.maximum(logit_maxima, clip_limit))
    column = jnp.repeat(factors, HD)
    query_weight_clipped = (params[0] * column[None, :]).astype(jnp.bfloat16)
    query_bias_clipped = (params[1] * column).astype(jnp.bfloat16)
    key_weight_clipped = (params[2] * column[None, :]).astype(jnp.bfloat16)
    return (output, input_grad, query_weight_grad, query_bias_grad, key_weight_grad, value_weight_grad, value_bias_grad, output_weight_grad, output_bias_grad, first_gain_grad, first_shift_grad, inner_weight_grad, inner_bias_grad, outer_weight_grad, outer_bias_grad, second_gain_grad, second_shift_grad, query_weight_clipped, query_bias_clipped, key_weight_clipped, logit_maxima)
```

```python
import functools

import jax
import jax.numpy as jnp
import numpy as np
from jax import lax
from jax.experimental import pallas as pl
from jax.experimental.pallas import tpu as pltpu
from jax.sharding import PartitionSpec as P

H = 12
HD = 64
BLK = 64
LEN = 1024
NB = 16
D = 768
FF = 3072

norm_eps = 1e-12
neg_large = -1e30
bf16 = jnp.bfloat16
f32 = jnp.float32
ANY = pl.BlockSpec(memory_space=pl.ANY)
INVMEM = pl.BlockSpec(memory_space=pltpu.VMEM)
INSMEM = pl.BlockSpec(memory_space=pltpu.SMEM)
MESH = pl.DeviceIdType.MESH


def dot_nn(a, b):
    return jnp.dot(a, b, preferred_element_type=f32)


def dot_nt(a, b):
    return lax.dot_general(a, b, (((1,), (1,)), ((), ())), preferred_element_type=f32)


def dot_tn(a, b):
    return lax.dot_general(a, b, (((0,), (0,)), ((), ())), preferred_element_type=f32)


def ds128(index, width):
    return pl.ds(pl.multiple_of(index * width, width), width)


class Place:
    def __init__(self, nz):
        self.nz = nz
        dp = lax.axis_index("dp")
        self.y = lax.axis_index("ctx")
        self.c = lax.rem(dp, 2)
        self.x = lax.rem(lax.div(dp, 2), 2)
        self.z = lax.div(dp, 4)

    def at(self, z=None, x=None, c=None, y=None):
        z = self.z if z is None else z
        x = self.x if x is None else x
        c = self.c if c is None else c
        y = self.y if y is None else y
        return ((z * 2 + x) * 2 + c, y)

    def z_off(self, k):
        return lax.rem(self.z + k, self.nz)

    def peers(self):
        return (
            [self.at(z=self.z_off(k)) for k in range(1, self.nz)]
            + [self.at(x=1 - self.x), self.at(y=1 - self.y), self.at(c=1 - self.c)]
        )


def entry_barrier(place):
    barrier = pltpu.get_barrier_semaphore()
    peers = place.peers()
    for peer in peers:
        pl.semaphore_signal(barrier, inc=1, device_id=peer, device_id_type=MESH)
    pl.semaphore_wait(barrier, len(peers))


class Remote:
    def __init__(self, send_sems, recv_sems):
        self.send_sems, self.recv_sems, self.used, self.copies = send_sems, recv_sems, 0, []

    def make(self, src, dst, peer):
        k = self.used
        self.used += 1
        copy = pltpu.make_async_remote_copy(
            src_ref=src, dst_ref=dst, send_sem=self.send_sems.at[k], recv_sem=self.recv_sems.at[k],
            device_id=peer, device_id_type=MESH,
        )
        self.copies.append(copy)
        return copy

    def finish(self):
        for copy in self.copies:
            copy.wait_send()


class Gather:
    def __init__(self, remote, place, buf, width):
        z, x, c, y = place.z, place.x, place.c, place.y
        half = width // 2
        a, b = slice(0, half), slice(half, width)
        zs = range(1, place.nz)

        def make(ref, peer):
            return remote.make(ref, ref, peer)

        self.az = [make(buf.at[z, x, c, y, :, a], place.at(z=place.z_off(k))) for k in zs]
        self.ax = make(buf.at[:, x, c, y, :, a], place.at(x=1 - x))
        self.ay = make(buf.at[:, :, c, y, :, a], place.at(y=1 - y))
        self.by = make(buf.at[z, x, c, y, :, b], place.at(y=1 - y))
        self.bz = [make(buf.at[z, x, c, :, :, b], place.at(z=place.z_off(k))) for k in zs]
        self.bx = make(buf.at[:, x, c, :, :, b], place.at(x=1 - x))
        self.ca = make(buf.at[:, :, c, :, :, a], place.at(c=1 - c))
        self.cb = make(buf.at[:, :, c, :, :, b], place.at(c=1 - c))

    def step(self, n):
        if n == 0:
            self.by.start()
            for copy in self.az:
                copy.start()
        elif n == 1:
            self.by.wait_recv()
            for copy in self.bz:
                copy.start()
        elif n == 2:
            for copy in self.az:
                copy.wait_recv()
            self.ax.start()
        elif n == 3:
            for copy in self.bz:
                copy.wait_recv()
            self.bx.start()
        elif n == 4:
            self.ax.wait_recv()
            self.ay.start()
        elif n == 5:
            self.bx.wait_recv()
            self.cb.start()
        elif n == 6:
            self.ay.wait_recv()
            self.ca.start()
        elif n == 7:
            self.ca.wait_recv()
            self.cb.wait_recv()


def layer_norm_parts(rows):
    centre = rows - jnp.mean(rows, axis=-1, keepdims=True)
    spread = jnp.mean(centre * centre, axis=-1, keepdims=True)
    inverse = lax.rsqrt(spread + norm_eps)
    return centre * inverse, inverse


def head_lanes(rows, half):
    lane = lax.broadcasted_iota(jnp.int32, rows.shape, 1)
    return jnp.where((lane >= HD) == (half == 1), rows, jnp.zeros_like(rows))


def key_structure(seq_len, length):
    lane = lax.broadcasted_iota(jnp.int32, (seq_len, 128), 1)
    row = lax.broadcasted_iota(jnp.int32, (seq_len, 128), 0)
    own = lane == lax.shift_right_logical(row, 6)
    beyond = (lane == NB) & (row >= length)
    return jnp.where(own | beyond, 1.0, 0.0).astype(bf16)


def query_structure(compact):
    blocks = compact.shape[0]
    return jnp.broadcast_to(compact[:, None, :], (blocks, BLK, 128)).reshape(blocks * BLK, 128).astype(bf16)


def spread_vectors(tiles, width, pieces):
    rows = tiles.shape[1]
    total = pieces * width
    lane = lax.broadcasted_iota(jnp.int32, (128, total), 1).astype(f32)
    row = lax.broadcasted_iota(jnp.int32, (128, total), 0).astype(f32)
    owner = jnp.floor((lane + 0.5) * (1.0 / width))
    chooser = jnp.where(lane - owner * width == row, 1.0, 0.0).astype(bf16)
    wide = dot_nn(tiles.reshape(pieces * rows, 128), chooser).reshape(pieces, rows, total)
    lane3 = lax.broadcasted_iota(jnp.int32, (pieces, rows, total), 2).astype(f32)
    piece3 = lax.broadcasted_iota(jnp.int32, (pieces, rows, total), 0).astype(f32)
    mine = jnp.floor((lane3 + 0.5) * (1.0 / width)) == piece3
    return jnp.sum(jnp.where(mine, wide, 0.0), axis=0)


def forward_kernel(
    nz, local, length_ref, compact_ref, x_hbm, wq, wk, wv, wo, wi, wu, small,
    out_hbm, r1_hbm, u_hbm, r2_hbm, a_hbm, q_hbm, k_hbm, v_hbm, xf_hbm, lse_hbm, top_hbm, wa_hbm, wi_hbm, wu_hbm, vec_hbm,
    WA, WI, WU, SM, XF, Q, K, V, VT, AT, A, R1, R2, N1L, U, G, PB, S, E, VEC, IB, LSE, TOP, OUT,
    send_sems, recv_sems, local_sems, out_sems,
):
    place = Place(nz)
    z, x, c, y = place.z, place.x, place.c, place.y
    remote = Remote(send_sems, recv_sems)
    mine = (z, x, c, y)
    locals_ = [
        pltpu.make_async_copy(x_hbm, XF.at[y], local_sems.at[0]),
        pltpu.make_async_copy(wq, WA.at[(*mine, slice(None), slice(0, D))], local_sems.at[1]),
        pltpu.make_async_copy(wk, WA.at[(*mine, slice(None), slice(D, 2 * D))], local_sems.at[2]),
        pltpu.make_async_copy(wv, WA.at[(*mine, slice(None), slice(2 * D, 3 * D))], local_sems.at[3]),
        pltpu.make_async_copy(wo, WA.at[(*mine, slice(None), slice(3 * D, 4 * D))], local_sems.at[4]),
        pltpu.make_async_copy(wi, WI.at[mine], local_sems.at[5]),
        pltpu.make_async_copy(wu, WU.at[mine], local_sems.at[6]),
        pltpu.make_async_copy(small, SM.at[mine], local_sems.at[7]),
    ]
    for copy in locals_:
        copy.start()
    entry_barrier(place)
    for copy in locals_:
        copy.wait()

    outs = []

    def put(src, dst):
        copy = pltpu.make_async_copy(src, dst, out_sems.at[len(outs)])
        copy.start()
        outs.append(copy)

    xs = remote.make(XF.at[y], XF.at[y], place.at(y=1 - y))
    ga = Gather(remote, place, WA, 4 * D)
    gi = Gather(remote, place, WI, FF)
    gu = Gather(remote, place, WU, D)
    sz = [remote.make(SM.at[mine], SM.at[mine], place.at(z=place.z_off(k))) for k in range(1, nz)]
    sx = remote.make(SM.at[:, x, c, y], SM.at[:, x, c, y], place.at(x=1 - x))
    sy = remote.make(SM.at[:, :, c, y], SM.at[:, :, c, y], place.at(y=1 - y))
    sc = remote.make(SM.at[:, :, c], SM.at[:, :, c], place.at(c=1 - c))

    ga.step(0)
    for copy in sz:
        copy.start()
    xs.start()
    length = length_ref[0]
    seq_len = XF.shape[0] * local
    E[...] = key_structure(seq_len, length)
    ga.step(1)
    ga.step(2)
    for copy in sz:
        copy.wait_recv()
    sx.start()
    ga.step(3)
    ga.step(4)
    sx.wait_recv()
    sy.start()
    gi.step(0)
    gu.step(0)
    ga.step(5)
    ga.step(6)
    sy.wait_recv()
    sc.start()
    sc.wait_recv()
    ga.step(7)
    gi.step(1)
    gu.step(1)
    gi.step(2)
    put(WA, wa_hbm)

    tiles = SM[...].reshape(-1, 16, 128)
    pieces = tiles.shape[0]
    VEC[...] = spread_vectors(tiles, D // pieces, pieces)
    IB[...] = spread_vectors(tiles[:, 8:16, :], FF // pieces, pieces)
    put(VEC, vec_hbm)

    def wa(which):
        return WA[:, :, :, :, :, which * D : (which + 1) * D].reshape(D, D)

    Q[...] = ((dot_nn(XF[y], wa(0)) + VEC[0:1, :]).astype(bf16).astype(f32) * (HD**-0.5)).astype(bf16)
    put(Q, q_hbm)
    gu.step(2)
    gi.step(3)
    xs.wait_recv()
    put(XF, xf_hbm)
    for part in range(XF.shape[0]):
        rows = slice(part * local, (part + 1) * local)
        K[rows, :] = dot_nn(XF[part], wa(1)).astype(bf16)
    gu.step(3)
    gi.step(4)
    for part in range(XF.shape[0]):
        rows = slice(part * local, (part + 1) * local)
        values = (dot_nn(XF[part], wa(2)) + VEC[1:2, :]).astype(bf16)
        V[rows, :] = values
        VT[:, rows] = values.T
    put(K, k_hbm)
    put(V, v_hbm)

    position = y * local + lax.broadcasted_iota(jnp.int32, (1, local), 1)
    live = position < length

    def head_step(h, carry):
        pair = lax.div(h, 2)
        half = lax.rem(h, 2)
        lanes = ds128(pair, 128)
        own = pl.ds(pl.multiple_of(h * HD, HD), HD)
        left = jnp.concatenate([K[:, lanes], E[...]], axis=1)
        right = jnp.concatenate([head_lanes(Q[:, lanes], half), query_structure(compact_ref[h])], axis=1)
        for part in range(local // 256):
            cols = slice(part * 256, (part + 1) * 256)
            scores = dot_nt(left, right[cols, :])
            top = jnp.max(scores, axis=0, keepdims=True)
            exponent = jnp.exp(scores - top)
            total = jnp.sum(exponent, axis=0, keepdims=True)
            low = (exponent * (1.0 / total)).astype(bf16)
            AT[own, cols] = dot_nn(VT[own, :], low).astype(bf16)
            LSE[h, :, cols] = top + jnp.log(total)
            TOP[h, :, cols] = jnp.where(live[:, cols], top, neg_large)

        @pl.when(h == 0)
        def _():
            gu.step(4)

        @pl.when(h == 1)
        def _():
            gi.step(5)

        @pl.when(h == 2)
        def _():
            gu.step(5)

        @pl.when(h == 4)
        def _():
            gi.step(6)

        @pl.when(h == 6)
        def _():
            gu.step(6)

        return carry

    lax.fori_loop(0, H, head_step, 0)
    put(LSE, lse_hbm)
    put(TOP, top_hbm)
    A[...] = AT[...].T
    put(A, a_hbm)
    R1[...] = dot_nn(A[...], wa(3))

    def first_norm(k, carry):
        rows = ds128(k, 64)
        summed = XF[y, rows, :].astype(f32) + R1[rows, :] + VEC[2:3, :]
        R1[rows, :] = summed
        normal, _ = layer_norm_parts(summed)
        value = normal * VEC[3:4, :] + VEC[4:5, :]
        N1L[rows, :] = value.astype(bf16)
        R2[rows, :] = value + VEC[5:6, :]
        return carry

    lax.fori_loop(0, local // 64, first_norm, 0)
    put(R1, r1_hbm)
    gi.step(7)
    put(WI, wi_hbm)
    for part in range(3):
        cols = slice(part * 1024, (part + 1) * 1024)
        U[:, cols] = dot_nn(N1L[...], WI[:, :, :, :, :, cols].reshape(D, 1024)) + IB[0:1, cols]

    def activate(k, carry):
        rows = ds128(k, 16)
        u = U[rows, :]
        G[rows, :] = (u * (0.5 * (1.0 + lax.erf(u * np.float32(0.5**0.5))))).astype(bf16)
        return carry

    lax.fori_loop(0, local // 16, activate, 0)
    put(U, u_hbm)
    gu.step(7)
    put(WU, wu_hbm)
    R2[...] += dot_nn(G[...], WU[...].reshape(FF, D))

    def second_norm(k, carry):
        rows = ds128(k, 64)
        normal, _ = layer_norm_parts(R2[rows, :])
        OUT[rows, :] = (normal * VEC[6:7, :] + VEC[7:8, :]).astype(bf16)
        return carry

    lax.fori_loop(0, local // 64, second_norm, 0)
    put(R2, r2_hbm)
    put(OUT, out_hbm)
    remote.finish()
    for copy in outs:
        copy.wait()


def run_forward(nz, x, weights, small, compact, length):
    local = x.shape[0]
    wq, wk, wv, wo, wi, wu = weights
    grid = (nz, 2, 2, 2)
    rows, rows_u = wq.shape[0], wu.shape[0]
    seq = 2 * local
    outs = [
        ((local, D), bf16), ((local, D), f32), ((local, FF), f32), ((local, D), f32), ((local, D), bf16),
        ((local, D), bf16), ((seq, D), bf16), ((seq, D), bf16), ((2, local, D), bf16),
        ((H, 1, local), f32), ((H, 1, local), f32),
        ((*grid, rows, 4 * D), bf16), ((*grid, rows, FF), bf16), ((*grid, rows_u, D), bf16), ((16, D), f32),
    ]
    scratch = [
        ((*grid, rows, 4 * D), bf16), ((*grid, rows, FF), bf16), ((*grid, rows_u, D), bf16), ((*grid, 16, 128), bf16),
        ((2, local, D), bf16), ((local, D), bf16), ((seq, D), bf16), ((seq, D), bf16), ((D, seq), bf16),
        ((D, local), bf16), ((local, D), bf16), ((local, D), f32), ((local, D), f32), ((local, D), bf16),
        ((local, FF), f32), ((local, FF), bf16), ((8, 128), bf16), ((8, 128), f32), ((seq, 128), bf16),
        ((16, D), f32), ((8, FF), f32), ((H, 1, local), f32), ((H, 1, local), f32), ((local, D), bf16),
    ]
    copies = 1 + 3 * (2 * (nz - 1) + 6) + (nz - 1) + 3
    return pl.pallas_call(
        functools.partial(forward_kernel, nz, local),
        out_shape=[jax.ShapeDtypeStruct(*o) for o in outs],
        in_specs=[INSMEM, INVMEM] + [ANY] * 8,
        out_specs=[ANY] * len(outs),
        scratch_shapes=[pltpu.VMEM(*s) for s in scratch]
        + [
            pltpu.SemaphoreType.DMA((copies,)),
            pltpu.SemaphoreType.DMA((copies,)),
            pltpu.SemaphoreType.DMA((8,)),
            pltpu.SemaphoreType.DMA((len(outs),)),
        ],
        compiler_params=pltpu.CompilerParams(collective_id=1, has_side_effects=True, vmem_limit_bytes=60 << 20),
        name="gather_forward",
    )(length, compact, x, wq, wk, wv, wo, wi, wu, small)


def compact_mask(random_here, length, first_block):
    blocks = random_here.shape[0]
    query = (first_block + jnp.arange(blocks, dtype=jnp.int32))[None, :, None]
    lane = jnp.arange(128, dtype=jnp.int32)[None, None, :]
    last = (length - 1) // BLK
    ok = (jnp.abs(query - lane) <= 1) | (lane == 0) | (lane == last) | (query == 0) | (query == last)
    heads = jnp.transpose(random_here, (1, 0, 2))
    for k in range(heads.shape[2]):
        ok = ok | (heads[:, :, k : k + 1] == lane)
    shown = jnp.where(lane < NB, jnp.where(ok, 0.0, neg_large), jnp.where(lane == NB, neg_large, 0.0))
    return shown.astype(f32)


def pack_small(vectors, wide):
    rows = [jnp.pad(v, (0, 128 - v.shape[0])) for v in vectors] + [jnp.pad(wide, (0, 128 - wide.shape[0]))]
    rows += [jnp.zeros((128,), bf16)] * (16 - len(rows))
    return jnp.stack(rows)


def back_pair(pair, local, compact_ref, Q, K, V, KT, DA, LSE, E, PB, DS, DQT, DK, DV):
    lanes = ds128(pair, 128)
    q_pair, a_pair, k_pair, v_pair = Q[:, lanes], DA[:, lanes], K[:, lanes], V[:, lanes]
    left = jnp.concatenate([k_pair, E[...]], axis=1)
    q_heads = [head_lanes(q_pair, half) for half in (0, 1)]
    a_heads = [head_lanes(a_pair, half) for half in (0, 1)]
    for half in (0, 1):
        h = pair * 2 + half
        own = pl.ds(pl.multiple_of(h * HD, HD), HD)
        right = jnp.concatenate([q_heads[half], query_structure(compact_ref[h])], axis=1)
        for part in range(local // 256):
            cols = slice(part * 256, (part + 1) * 256)
            place = slice(half * local + part * 256, half * local + (part + 1) * 256)
            prob = jnp.exp(dot_nt(left, right[cols, :]) - LSE[h, :, cols])
            PB[:, place] = prob.astype(bf16)
            dprob = dot_nt(v_pair, a_heads[half][cols, :])
            inner = jnp.sum(prob * dprob, axis=0, keepdims=True)
            low = (prob * (dprob - inner)).astype(bf16)
            DS[:, place] = low
            DQT[own, cols] = (dot_nn(KT[own, :], low) * (HD**-0.5)).astype(bf16)
    DK[:, lanes] = dot_nn(DS[...], jnp.concatenate(q_heads, axis=0)).astype(bf16)
    DV[:, lanes] = dot_nn(PB[...], jnp.concatenate(a_heads, axis=0)).astype(bf16)


def attend_back_kernel(local, length_ref, compact_ref, Q, K, V, DA, LSE, DQ, DK, DV, E, KT, PB, DS, DQT):
    E[...] = key_structure(K.shape[0], length_ref[0])
    KT[...] = K[...].T

    def step(pair, carry):
        back_pair(pair, local, compact_ref, Q, K, V, KT, DA, LSE, E, PB, DS, DQT, DK, DV)
        return carry

    lax.fori_loop(0, H // 2, step, 0)
    DQ[...] = DQT[...].T


def run_attend_back(q, k, v, da, lse, compact, length):
    local, seq = q.shape[0], k.shape[0]
    outs = [((local, D), bf16), ((seq, D), bf16), ((seq, D), bf16)]
    scratch = [((seq, 128), bf16), ((D, seq), bf16), ((seq, 2 * local), bf16), ((seq, 2 * local), bf16), ((D, local), bf16)]
    return pl.pallas_call(
        functools.partial(attend_back_kernel, local),
        out_shape=[jax.ShapeDtypeStruct(*o) for o in outs],
        in_specs=[INSMEM] + [INVMEM] * 6,
        out_specs=[INVMEM] * 3,
        scratch_shapes=[pltpu.VMEM(*s) for s in scratch],
        compiler_params=pltpu.CompilerParams(vmem_limit_bytes=60 << 20),
        name="attend_back",
    )(length, compact, q, k, v, da, lse)


class Scatter:
    def __init__(self, remote, place, g, bufs, out, width):
        rc, ra1, ra2, raz, rb1, rbz, rb2 = bufs
        z, x, c, y = place.z, place.x, place.c, place.y
        half = width // 2
        a, b = slice(0, half), slice(half, width)
        self.place, self.g, self.bufs, self.out, self.a, self.b = place, g, bufs, out, a, b
        self.core = remote.make(g.at[:, :, 1 - c], rc, place.at(c=1 - c))
        self.a1 = remote.make(g.at[:, :, c, 1 - y, :, a], ra1, place.at(y=1 - y))
        self.b1 = remote.make(g.at[:, 1 - x, c, :, :, b], rb1, place.at(x=1 - x))
        self.a2 = remote.make(g.at[:, 1 - x, c, y, :, a], ra2, place.at(x=1 - x))
        self.bz, self.az = [], []
        for k in range(1, place.nz):
            zk = place.z_off(k)
            self.bz.append(remote.make(g.at[zk, x, c, :, :, b], rbz.at[k - 1], place.at(z=zk)))
            self.az.append(remote.make(g.at[zk, x, c, y, :, a], raz.at[k - 1], place.at(z=zk)))
        self.b2 = remote.make(g.at[z, x, c, 1 - y, :, b], rb2, place.at(y=1 - y))

    def step(self, n):
        rc, ra1, ra2, raz, rb1, rbz, rb2 = self.bufs
        place, g, a, b = self.place, self.g, self.a, self.b
        z, x, c, y = place.z, place.x, place.c, place.y
        if n == 0:
            self.core.start()
        elif n == 1:
            self.core.wait_recv()

            def add_core(k, carry):
                zz, xx = lax.div(k, 2), lax.rem(k, 2)
                for yy in range(2):
                    g[zz, xx, c, yy] = (g[zz, xx, c, yy].astype(f32) + rc[zz, xx, yy].astype(f32)).astype(bf16)
                return carry

            lax.fori_loop(0, place.nz * 2, add_core, 0)
            self.a1.start()
            self.b1.start()
        elif n == 2:
            self.a1.wait_recv()

            def add_a1(k, carry):
                zz, xx = lax.div(k, 2), lax.rem(k, 2)
                g[zz, xx, c, y, :, a] = (g[zz, xx, c, y, :, a].astype(f32) + ra1[zz, xx].astype(f32)).astype(bf16)
                return carry

            lax.fori_loop(0, place.nz * 2, add_a1, 0)
            self.a2.start()
        elif n == 3:
            self.b1.wait_recv()

            def add_b1(k, carry):
                zz, yy = lax.div(k, 2), lax.rem(k, 2)
                g[zz, x, c, yy, :, b] = (g[zz, x, c, yy, :, b].astype(f32) + rb1[zz, yy].astype(f32)).astype(bf16)
                return carry

            lax.fori_loop(0, place.nz * 2, add_b1, 0)
            for copy in self.bz:
                copy.start()
        elif n == 4:
            self.a2.wait_recv()
            for zz in range(place.nz):
                g[zz, x, c, y, :, a] = (g[zz, x, c, y, :, a].astype(f32) + ra2[zz].astype(f32)).astype(bf16)
            for copy in self.az:
                copy.start()
        elif n == 5:
            for copy in self.bz:
                copy.wait_recv()
            for yy in range(2):
                total = g[z, x, c, yy, :, b].astype(f32)
                for k in range(place.nz - 1):
                    total = total + rbz[k, yy].astype(f32)
                g[z, x, c, yy, :, b] = total.astype(bf16)
            self.b2.start()
        elif n == 6:
            for copy in self.az:
                copy.wait_recv()
            total = g[z, x, c, y, :, a].astype(f32)
            for k in range(place.nz - 1):
                total = total + raz[k].astype(f32)
            self.out[:, a] = total
        elif n == 7:
            self.b2.wait_recv()
            self.out[:, b] = g[z, x, c, y, :, b].astype(f32) + rb2[...].astype(f32)


def scatter_buffers(nz, rows, width):
    half = width // 2
    return [
        ((nz, 2, 2, rows, width), bf16), ((nz, 2, rows, half), bf16), ((nz, rows, half), bf16), ((nz - 1, rows, half), bf16),
        ((nz, 2, rows, half), bf16), ((nz - 1, 2, rows, half), bf16), ((rows, half), bf16),
    ]


class SmallSums:
    def __init__(self, remote, place, t, bufs, top, tops):
        rc, ry, rx, rz = bufs
        z, x, c, y = place.z, place.x, place.c, place.y
        self.place, self.t, self.bufs, self.top, self.tops = place, t, bufs, top, tops
        self.stages = [
            [remote.make(t.at[:, :, 1 - c], rc, place.at(c=1 - c))],
            [remote.make(t.at[:, :, c, 1 - y], ry, place.at(y=1 - y))],
            [remote.make(t.at[:, 1 - x, c, y], rx, place.at(x=1 - x))],
            [
                remote.make(t.at[place.z_off(k), x, c, y], rz.at[k - 1], place.at(z=place.z_off(k)))
                for k in range(1, place.nz)
            ],
        ]
        to = [[place.at(c=1 - c)], [place.at(y=1 - y)], [place.at(x=1 - x)]]
        to.append([place.at(z=place.z_off(k)) for k in range(1, place.nz)])
        self.top_stages, slot = [], 0
        for n, peers in enumerate(to):
            made = []
            for peer in peers:
                made.append((remote.make(top.at[n], tops.at[slot], peer), slot))
                slot += 1
            self.top_stages.append(made)

    def start(self, n):
        for copy in self.stages[n]:
            copy.start()
        for copy, _ in self.top_stages[n]:
            copy.start()

    def take(self, n):
        place, t = self.place, self.t
        rc, ry, rx, rz = self.bufs
        z, x, c, y = place.z, place.x, place.c, place.y
        for copy in self.stages[n]:
            copy.wait_recv()
        best = self.top[n]
        for copy, slot in self.top_stages[n]:
            copy.wait_recv()
            best = jnp.maximum(best, self.tops[slot])
        self.top[n + 1] = best
        if n == 0:
            t[:, :, c] = t[:, :, c] + rc[...]
        elif n == 1:
            t[:, :, c, y] = t[:, :, c, y] + ry[...]
        elif n == 2:
            t[:, x, c, y] = t[:, x, c, y] + rx[...]
        else:
            total = t[z, x, c, y]
            for k in range(place.nz - 1):
                total = total + rz[k]
            t[z, x, c, y] = total


def small_buffers(nz):
    return [((nz, 2, 2, 16, 128), f32), ((nz, 2, 16, 128), f32), ((nz, 16, 128), f32), ((nz - 1, 16, 128), f32)]


def scatter_kernel(nz, widths, da_hbm, di_hbm, du_hbm, sm_hbm, top_hbm, oa, oi, ou, osm, otop, *rest):
    place = Place(nz)
    ga, gi, gu, t, top, tops = rest[:6]
    bufs = [rest[6 + 7 * k : 13 + 7 * k] for k in range(3)]
    sbufs = rest[27:31]
    send_sems, recv_sems, local_sems = rest[31:]
    loads = [
        pltpu.make_async_copy(src, dst, local_sems.at[k])
        for k, (src, dst) in enumerate([(sm_hbm, t), (top_hbm, top.at[0]), (du_hbm, gu), (di_hbm, gi), (da_hbm, ga)])
    ]
    for copy in loads:
        copy.start()
    entry_barrier(place)
    remote = Remote(send_sems, recv_sems)
    small = SmallSums(remote, place, t, sbufs, top, tops)
    parts = [
        Scatter(remote, place, g, bufs[k], out, width)
        for k, (g, out, width) in enumerate([(gu, ou, widths[2]), (gi, oi, widths[1]), (ga, oa, widths[0])])
    ]
    loads[0].wait()
    loads[1].wait()
    small.start(0)
    for n, part in enumerate(parts):
        loads[2 + n].wait()
        part.step(0)
    small.take(0)
    small.start(1)
    for n in range(1, 8):
        for part in parts:
            part.step(n)
        if n < 4:
            small.take(n)
            if n < 3:
                small.start(n + 1)
    osm[...] = t[place.z, place.x, place.c, place.y]
    otop[...] = top[4]
    remote.finish()


def run_scatter(nz, da, di, du, sm, top):
    grid = (nz, 2, 2, 2)
    shapes = [a.shape[-2:] for a in (da, di, du)]
    outs = [(s, f32) for s in shapes] + [((16, 128), f32), ((16, 128), f32)]
    scratch = [(a.shape, bf16) for a in (da, di, du)] + [(sm.shape, f32), ((5, 16, 128), f32), ((3 + nz - 1, 16, 128), f32)]
    for s in (shapes[2], shapes[1], shapes[0]):
        scratch += scatter_buffers(nz, *s)
    scratch += small_buffers(nz)
    copies = 3 * (2 * (nz - 1) + 5) + 2 * (3 + nz - 1)
    return pl.pallas_call(
        functools.partial(scatter_kernel, nz, [s[1] for s in shapes]),
        out_shape=[jax.ShapeDtypeStruct(*o) for o in outs],
        in_specs=[ANY] * 5,
        out_specs=[INVMEM] * 5,
        scratch_shapes=[pltpu.VMEM(*s) for s in scratch]
        + [pltpu.SemaphoreType.DMA((copies,)), pltpu.SemaphoreType.DMA((copies,)), pltpu.SemaphoreType.DMA((5,))],
        compiler_params=pltpu.CompilerParams(collective_id=2, has_side_effects=True, vmem_limit_bytes=60 << 20),
        name="scatter_gradients",
    )(da, di, du, sm, top)


def layer_norm(row_values, gain_vector, shift_vector):
    centre = row_values - jnp.mean(row_values, axis=-1, keepdims=True)
    spread = jnp.mean(centre * centre, axis=-1, keepdims=True)
    return centre * lax.rsqrt(spread + norm_eps) * gain_vector + shift_vector


def gelu_exact(values):
    return jax.nn.gelu(values, approximate=False)


def column_sums(values):
    return jnp.sum(values.astype(f32), axis=0)


def clip_outputs(logit_maxima, threshold, query_weight, query_bias, key_weight, device_rank):
    clip_limit = threshold.astype(f32)[0] * 0.01
    factors = jnp.sqrt(clip_limit / jnp.maximum(logit_maxima, clip_limit))
    column_scale = jnp.repeat(factors, HD)
    query_clipped = (query_weight.astype(f32) * column_scale[None, :]).astype(bf16)
    key_clipped = (key_weight.astype(f32) * column_scale[None, :]).astype(bf16)
    bias_count = query_bias.shape[0]
    bias_heads = (device_rank * bias_count + jnp.arange(bias_count)) // HD
    bias_scale = jnp.sum(jnp.where(bias_heads[:, None] == jnp.arange(H)[None, :], factors[None, :], 0.0), axis=1)
    return query_clipped, (query_bias.astype(f32) * bias_scale).astype(bf16), key_clipped


def tiles_of(vectors, wide, pieces, grid):
    rows = [jnp.pad(v.reshape(pieces, -1), ((0, 0), (0, 128 - v.shape[0] // pieces))) for v in vectors]
    rows.append(jnp.pad(wide.reshape(pieces, -1), ((0, 0), (0, 128 - wide.shape[0] // pieces))))
    rows += [jnp.zeros((pieces, 128), f32)] * (16 - len(rows))
    return jnp.stack(rows, axis=1).reshape(*grid, 16, 128)


def fast_shards(
    nz,
    inputs, cotangent, query_weight, query_bias, key_weight, value_weight, value_bias, output_weight, output_bias,
    first_gain, first_shift, inner_weight, inner_bias, outer_weight, outer_bias, second_gain, second_shift,
    lengths, random_blocks, threshold,
):
    local = inputs.shape[1]
    grid = (nz, 2, 2, 2)
    pieces = nz * 8
    rows, rows_u = query_weight.shape[0], outer_weight.shape[0]
    y = lax.axis_index("ctx")
    blocks = local // BLK
    first_block = y * blocks
    random_here = lax.dynamic_slice_in_dim(random_blocks[0], first_block, blocks, 0)
    compact = compact_mask(random_here, lengths[0], first_block)
    small = pack_small(
        [query_bias, value_bias, output_bias, first_gain, first_shift, outer_bias, second_gain, second_shift], inner_bias
    )
    x = inputs[0]
    weights = (query_weight, key_weight, value_weight, output_weight, inner_weight, outer_weight)
    (
        output, first_sum, pre_act, second_sum, attended, q, k, v, x_both, lse, tops, wa, wi, wu, vectors
    ) = run_forward(nz, x, weights, small, compact, lengths)
    wa, wi, wu = wa.reshape(D, 4 * D), wi.reshape(D, FF), wu.reshape(FF, D)
    full_query, full_key, full_value, full_out = (wa[:, n * D : (n + 1) * D] for n in range(4))
    gain_one, shift_one, gain_two, shift_two = vectors[3], vectors[4], vectors[6], vectors[7]
    normed_low = layer_norm(first_sum, gain_one, shift_one).astype(bf16)
    activated = gelu_exact(pre_act).astype(bf16)
    live = (y * local + jnp.arange(local)) < lengths[0]
    cot_rows = jnp.where(live[:, None], cotangent[0].astype(f32), 0.0)
    second_pull = jax.vjp(layer_norm, second_sum, gain_two, shift_two)[1]
    grad_second, second_gain_grad, second_shift_grad = second_pull(cot_rows)
    grad_outer_low = grad_second.astype(bf16)
    outer_bias_grad = column_sums(grad_outer_low)
    outer_weight_grad = dot_tn(activated, grad_outer_low)
    grad_activated = dot_nt(grad_outer_low, wu)
    grad_pre_low = jax.vjp(gelu_exact, pre_act)[1](grad_activated)[0].astype(bf16)
    inner_bias_grad = column_sums(grad_pre_low)
    inner_weight_grad = dot_tn(normed_low, grad_pre_low)
    grad_normed = grad_second + dot_nt(grad_pre_low, wi)
    first_pull = jax.vjp(layer_norm, first_sum, gain_one, shift_one)[1]
    grad_first, first_gain_grad, first_shift_grad = first_pull(grad_normed)
    grad_proj_low = grad_first.astype(bf16)
    output_bias_grad = column_sums(grad_proj_low)
    output_weight_grad = dot_tn(attended, grad_proj_low)
    grad_attended = dot_nt(grad_proj_low, full_out).astype(bf16)
    dq, dk, dv = run_attend_back(q, k, v, grad_attended, lse, compact, lengths)
    x_rows = x_both.reshape(2 * local, D)
    query_weight_grad = dot_tn(x, dq)
    query_bias_grad = column_sums(dq)
    key_weight_grad = dot_tn(x_rows, dk)
    value_weight_grad = dot_tn(x_rows, dv)
    value_bias_grad = column_sums(dv)
    through = dot_nt(dk, full_key) + dot_nt(dv, full_value)
    own = lax.dynamic_slice_in_dim(through, y * local, local, 0)
    other = lax.dynamic_slice_in_dim(through, (1 - y) * local, local, 0).astype(bf16)
    received = lax.ppermute(other, "ctx", [(0, 1), (1, 0)]).astype(f32)
    input_grad = grad_first + dot_nt(dq, full_query) + own + received
    da = jnp.concatenate(
        [query_weight_grad, key_weight_grad, value_weight_grad, output_weight_grad], axis=1
    ).astype(bf16).reshape(*grid, rows, 4 * D)
    di = inner_weight_grad.astype(bf16).reshape(*grid, rows, FF)
    du = outer_weight_grad.astype(bf16).reshape(*grid, rows_u, D)
    sm = tiles_of(
        [query_bias_grad, value_bias_grad, output_bias_grad, first_gain_grad, first_shift_grad, outer_bias_grad,
         second_gain_grad, second_shift_grad], inner_bias_grad, pieces, grid,
    )
    top_here = jnp.broadcast_to(jnp.pad(jnp.max(tops[:, 0, :], axis=1), (0, 4))[:, None], (16, 128))
    ga, gi, gu, gs, top = run_scatter(nz, da, di, du, sm, top_here)
    logit_maxima = top[:H, 0]
    rank = lax.axis_index("dp") * 2 + y
    query_clipped, bias_clipped, key_clipped = clip_outputs(
        logit_maxima, threshold, query_weight, query_bias, key_weight, rank
    )
    vec = [gs[n, :rows] for n in range(8)]
    return (
        output[None], input_grad[None],
        ga[:, :D], vec[0], ga[:, D : 2 * D], ga[:, 2 * D : 3 * D], vec[1], ga[:, 3 * D :], vec[2], vec[3], vec[4],
        gi, gs[8, : FF // pieces], gu, vec[5], vec[6], vec[7],
        query_clipped, bias_clipped, key_clipped, logit_maxima,
    )


def general_shards(
    inputs, cotangent, query_weight, query_bias, key_weight, value_weight, value_bias, output_weight, output_bias,
    first_gain, first_shift, inner_weight, inner_bias, outer_weight, outer_bias, second_gain, second_shift,
    lengths, random_blocks, threshold,
):
    both = ("dp", "ctx")
    shards = (
        query_weight, query_bias, key_weight, value_weight, value_bias, output_weight, output_bias, first_gain, first_shift,
        inner_weight, inner_bias, outer_weight, outer_bias, second_gain, second_shift,
    )
    wq, bq, wk, wv, bv, wo, bo, g1, s1, wi, bi, wu, bu, g2, s2 = (lax.all_gather(w, both, axis=0, tiled=True) for w in shards)
    bq, bv, bo, g1, s1, bi, bu, g2, s2 = (v.astype(f32) for v in (bq, bv, bo, g1, s1, bi, bu, g2, s2))
    seqs, local, _ = inputs.shape
    blocks = local // BLK
    y = lax.axis_index("ctx")
    first_block = y * blocks
    scale = HD**-0.5
    outs = []
    sums = None
    top = jnp.full((H,), neg_large, f32)
    for s in range(seqs):
        x, length = inputs[s], lengths[s]
        random_here = lax.dynamic_slice_in_dim(random_blocks[s], first_block, blocks, 0)
        mask = compact_mask(random_here, length, first_block)[:, :, :NB]
        mask = jnp.repeat(jnp.repeat(mask, BLK, axis=1), BLK, axis=2)
        seen = jnp.arange(NB * BLK) < length
        mask = jnp.where(seen[None, None, :], mask, neg_large)
        live = (y * local + jnp.arange(local)) < length
        q = (dot_nn(x, wq) + bq).astype(bf16)
        k = lax.all_gather(dot_nn(x, wk).astype(bf16), "ctx", axis=0, tiled=True)
        v = lax.all_gather((dot_nn(x, wv) + bv).astype(bf16), "ctx", axis=0, tiled=True)
        qh, kh, vh = (a.reshape(-1, H, HD) for a in (q, k, v))
        raw = jnp.einsum("qhd,khd->hqk", qh, kh, preferred_element_type=f32) * scale + mask
        row_top = jnp.max(raw, axis=-1, keepdims=True)
        top = jnp.maximum(top, jnp.max(jnp.where(live[None, :, None], row_top, neg_large), axis=(1, 2)))
        exponent = jnp.exp(raw - row_top)
        prob = exponent / jnp.sum(exponent, axis=-1, keepdims=True)
        low = prob.astype(bf16)
        attended = jnp.einsum("hqk,khd->qhd", low, vh, preferred_element_type=f32).reshape(local, D).astype(bf16)
        first_sum = x.astype(f32) + dot_nn(attended, wo) + bo
        normed = layer_norm(first_sum, g1, s1)
        normed_low = normed.astype(bf16)
        pre_act = dot_nn(normed_low, wi) + bi
        activated = gelu_exact(pre_act).astype(bf16)
        second_sum = normed + dot_nn(activated, wu) + bu
        output = layer_norm(second_sum, g2, s2).astype(bf16)
        cot = jnp.where(live[:, None], cotangent[s].astype(f32), 0.0)
        grad_second, g2_grad, s2_grad = jax.vjp(layer_norm, second_sum, g2, s2)[1](cot)
        dm = grad_second.astype(bf16)
        du = jax.vjp(gelu_exact, pre_act)[1](dot_nt(dm, wu))[0].astype(bf16)
        grad_normed = grad_second + dot_nt(du, wi)
        grad_first, g1_grad, s1_grad = jax.vjp(layer_norm, first_sum, g1, s1)[1](grad_normed)
        dp = grad_first.astype(bf16)
        da = dot_nt(dp, wo).astype(bf16).reshape(local, H, HD)
        dprob = jnp.einsum("qhd,khd->hqk", da, vh, preferred_element_type=f32)
        ds = (prob * (dprob - jnp.sum(prob * dprob, axis=-1, keepdims=True))).astype(bf16)
        dq = (jnp.einsum("hqk,khd->qhd", ds, kh, preferred_element_type=f32) * scale).reshape(local, D).astype(bf16)
        dk = (jnp.einsum("hqk,qhd->khd", ds, qh, preferred_element_type=f32) * scale).reshape(-1, D)
        dv = jnp.einsum("hqk,qhd->khd", low, da, preferred_element_type=f32).reshape(-1, D)
        dk, dv = (lax.psum_scatter(a.astype(bf16), "ctx", scatter_dimension=0, tiled=True).astype(bf16) for a in (dk, dv))
        input_grad = grad_first + dot_nt(dq, wq) + dot_nt(dk, wk) + dot_nt(dv, wv)
        outs.append((output, input_grad))
        here = (
            dot_tn(x, dq), column_sums(dq), dot_tn(x, dk), dot_tn(x, dv), column_sums(dv), dot_tn(attended, dp),
            column_sums(dp), g1_grad, s1_grad, dot_tn(normed_low, du), column_sums(du), dot_tn(activated, dm),
            column_sums(dm), g2_grad, s2_grad,
        )
        sums = here if sums is None else tuple(a + b for a, b in zip(sums, here))
    grads = tuple(lax.psum_scatter(g, both, scatter_dimension=0, tiled=True) for g in sums)
    logit_maxima = lax.pmax(top, both)
    rank = lax.axis_index(both)
    clipped = clip_outputs(logit_maxima, threshold, query_weight, query_bias, key_weight, rank)
    return (jnp.stack([o for o, _ in outs]), jnp.stack([g for _, g in outs]), *grads, *clipped, logit_maxima)


def solution(mesh):
    both = P(("dp", "ctx"))
    rows = P(("dp", "ctx"), None)
    tokens = P("dp", "ctx", None)
    in_specs = (
        tokens, tokens, rows, both, rows, rows, both, rows, both, both, both, rows, both, rows, both, both, both,
        P("dp"), P("dp", None, None, None), P(),
    )
    out_specs = (
        tokens, tokens, rows, both, rows, rows, both, rows, both, both, both, rows, both, rows, both, both, both,
        rows, both, rows, P(),
    )
    dp, ctx = mesh.shape["dp"], mesh.shape["ctx"]
    pieces = dp * ctx
    fits = ctx == 2 and dp % 4 == 0 and D % (8 * pieces) == 0 and FF // pieces <= 128

    def step(*args):
        if fits and args[0].shape[0] == 1:
            return fast_shards(dp // 4, *args)
        return general_shards(*args)

    return jax.shard_map(step, mesh=mesh, in_specs=in_specs, out_specs=out_specs, check_vma=False)
```

```python
import functools

import jax
import jax.numpy as jnp
import numpy as np
from jax import lax
from jax.experimental import pallas as pl
from jax.experimental.pallas import tpu as pltpu
from jax.sharding import PartitionSpec as P

H = 12
HD = 64
BLK = 64
LEN = 1024
NB = 16
D = 768
FF = 3072

norm_eps = 1e-12
neg_large = -1e30
bf16 = jnp.bfloat16
f32 = jnp.float32
ANY = pl.BlockSpec(memory_space=pl.ANY)
INVMEM = pl.BlockSpec(memory_space=pltpu.VMEM)
INSMEM = pl.BlockSpec(memory_space=pltpu.SMEM)
MESH = pl.DeviceIdType.MESH


def dot_nn(a, b):
    return jnp.dot(a, b, preferred_element_type=f32)


def dot_nt(a, b):
    return lax.dot_general(a, b, (((1,), (1,)), ((), ())), preferred_element_type=f32)


def dot_tn(a, b):
    return lax.dot_general(a, b, (((0,), (0,)), ((), ())), preferred_element_type=f32)


def ds128(index, width):
    return pl.ds(pl.multiple_of(index * width, width), width)


class Place:
    def __init__(self, nz):
        self.nz = nz
        dp = lax.axis_index("dp")
        self.y = lax.axis_index("ctx")
        self.c = lax.rem(dp, 2)
        self.x = lax.rem(lax.div(dp, 2), 2)
        self.z = lax.div(dp, 4)

    def at(self, z=None, x=None, c=None, y=None):
        z = self.z if z is None else z
        x = self.x if x is None else x
        c = self.c if c is None else c
        y = self.y if y is None else y
        return ((z * 2 + x) * 2 + c, y)

    def z_off(self, k):
        return lax.rem(self.z + k, self.nz)

    def peers(self):
        return (
            [self.at(z=self.z_off(k)) for k in range(1, self.nz)]
            + [self.at(x=1 - self.x), self.at(y=1 - self.y), self.at(c=1 - self.c)]
        )


def entry_barrier(place):
    barrier = pltpu.get_barrier_semaphore()
    peers = place.peers()
    for peer in peers:
        pl.semaphore_signal(barrier, inc=1, device_id=peer, device_id_type=MESH)
    pl.semaphore_wait(barrier, len(peers))


class Remote:
    def __init__(self, send_sems, recv_sems):
        self.send_sems, self.recv_sems, self.used, self.copies = send_sems, recv_sems, 0, []

    def make(self, src, dst, peer):
        k = self.used
        self.used += 1
        copy = pltpu.make_async_remote_copy(
            src_ref=src, dst_ref=dst, send_sem=self.send_sems.at[k], recv_sem=self.recv_sems.at[k],
            device_id=peer, device_id_type=MESH,
        )
        self.copies.append(copy)
        return copy

    def finish(self):
        for copy in self.copies:
            copy.wait_send()


class Gather:
    def __init__(self, remote, place, buf, lo, width):
        z, x, c, y = place.z, place.x, place.c, place.y
        a, b, both = slice(lo, lo + width // 2), slice(lo + width // 2, lo + width), slice(lo, lo + width)
        zs = range(1, place.nz)

        def make(ref, peer):
            return remote.make(ref, ref, peer)

        self.az = [make(buf.at[z, x, c, y, :, a], place.at(z=place.z_off(k))) for k in zs]
        self.ax = make(buf.at[:, x, c, y, :, a], place.at(x=1 - x))
        self.ay = make(buf.at[:, :, c, y, :, a], place.at(y=1 - y))
        self.by = make(buf.at[z, x, c, y, :, b], place.at(y=1 - y))
        self.bz = [make(buf.at[z, x, c, :, :, b], place.at(z=place.z_off(k))) for k in zs]
        self.bx = make(buf.at[:, x, c, :, :, b], place.at(x=1 - x))
        self.core = make(buf.at[:, :, c, :, :, both], place.at(c=1 - c))
        self.steps = 5

    def step(self, n):
        if n == 0:
            self.by.start()
            for copy in self.az:
                copy.start()
        elif n == 1:
            self.by.wait_recv()
            for copy in self.bz:
                copy.start()
            for copy in self.az:
                copy.wait_recv()
            self.ax.start()
        elif n == 2:
            self.ax.wait_recv()
            self.ay.start()
            for copy in self.bz:
                copy.wait_recv()
            self.bx.start()
        elif n == 3:
            self.ay.wait_recv()
            self.bx.wait_recv()
            self.core.start()
        elif n == 4:
            self.core.wait_recv()


class SmallGather:
    def __init__(self, remote, place, buf):
        z, x, c, y = place.z, place.x, place.c, place.y
        self.stages = [
            [remote.make(buf.at[z, x, c, y], buf.at[z, x, c, y], place.at(z=place.z_off(k))) for k in range(1, place.nz)],
            [remote.make(buf.at[:, x, c, y], buf.at[:, x, c, y], place.at(x=1 - x))],
            [remote.make(buf.at[:, :, c, y], buf.at[:, :, c, y], place.at(y=1 - y))],
            [remote.make(buf.at[:, :, c], buf.at[:, :, c], place.at(c=1 - c))],
        ]
        self.steps = 5

    def step(self, n):
        if n > 0:
            for copy in self.stages[n - 1]:
                copy.wait_recv()
        if n < 4:
            for copy in self.stages[n]:
                copy.start()


class Rounds:
    def __init__(self):
        self.active = []

    def add(self, *items):
        for item in items:
            item.step(0)
            self.active.append([item, 1])

    def round(self):
        for entry in self.active:
            entry[0].step(entry[1])
            entry[1] += 1
        self.active = [e for e in self.active if e[1] < e[0].steps]


def layer_norm_parts(rows):
    centre = rows - jnp.mean(rows, axis=-1, keepdims=True)
    spread = jnp.mean(centre * centre, axis=-1, keepdims=True)
    inverse = lax.rsqrt(spread + norm_eps)
    return centre * inverse, inverse


def head_lanes(rows, half):
    lane = lax.broadcasted_iota(jnp.int32, rows.shape, 1)
    return jnp.where((lane >= HD) == (half == 1), rows, jnp.zeros_like(rows))


def key_structure(seq_len, length):
    lane = lax.broadcasted_iota(jnp.int32, (seq_len, 128), 1)
    row = lax.broadcasted_iota(jnp.int32, (seq_len, 128), 0)
    own = lane == lax.shift_right_logical(row, 6)
    beyond = (lane == NB) & (row >= length)
    return jnp.where(own | beyond, 1.0, 0.0).astype(bf16)


def query_structure(compact):
    blocks = compact.shape[0]
    return jnp.broadcast_to(compact[:, None, :], (blocks, BLK, 128)).reshape(blocks * BLK, 128).astype(bf16)


def spread_vectors(tiles, width, pieces):
    rows = tiles.shape[1]
    total = pieces * width
    lane = lax.broadcasted_iota(jnp.int32, (128, total), 1).astype(f32)
    row = lax.broadcasted_iota(jnp.int32, (128, total), 0).astype(f32)
    owner = jnp.floor((lane + 0.5) * (1.0 / width))
    chooser = jnp.where(lane - owner * width == row, 1.0, 0.0).astype(bf16)
    wide = dot_nn(tiles.reshape(pieces * rows, 128), chooser).reshape(pieces, rows, total)
    lane3 = lax.broadcasted_iota(jnp.int32, (pieces, rows, total), 2).astype(f32)
    piece3 = lax.broadcasted_iota(jnp.int32, (pieces, rows, total), 0).astype(f32)
    mine = jnp.floor((lane3 + 0.5) * (1.0 / width)) == piece3
    return jnp.sum(jnp.where(mine, wide, 0.0), axis=0)


def forward_kernel(
    nz, local, length_ref, compact_ref, x_hbm, wq, wk, wv, wo, wi, wu, small,
    out_hbm, r1_hbm, r2_hbm, gp_hbm, gt_hbm, n1t_hbm, at_hbm, q_hbm, k_hbm, kt_hbm, v_hbm, xt_hbm, lse_hbm, top_hbm,
    wa_hbm, wi_hbm, wu_hbm, vec_hbm,
    WA, WI, WU, SM, XF, XT, Q, K, KT, V, VT, AT, R1, R2, N1L, N1T, U, GP, G, GT, E, VEC, IB, LSE, TOP, OUT,
    send_sems, recv_sems, local_sems, out_sems,
):
    place = Place(nz)
    z, x, c, y = place.z, place.x, place.c, place.y
    remote = Remote(send_sems, recv_sems)
    mine = (z, x, c, y)
    seq_len = 2 * local
    locals_ = [(x_hbm, XF.at[y]), (small, SM.at[mine])]
    for g in range(3):
        for n, w in enumerate((wq, wk, wv)):
            lo = g * D + n * 256
            locals_.append((w.at[:, g * 256 : (g + 1) * 256], WA.at[(*mine, slice(None), slice(lo, lo + 256))]))
    locals_ += [(wo, WA.at[(*mine, slice(None), slice(3 * D, 4 * D))]), (wi, WI.at[mine]), (wu, WU.at[mine])]
    locals_ = [pltpu.make_async_copy(src, dst, local_sems.at[k]) for k, (src, dst) in enumerate(locals_)]
    for copy in locals_:
        copy.start()
    entry_barrier(place)
    for copy in locals_:
        copy.wait()

    outs = []

    def put(src, dst):
        copy = pltpu.make_async_copy(src, dst, out_sems.at[len(outs)])
        copy.start()
        outs.append(copy)

    other = 1 - y
    xs = remote.make(XF.at[y], XF.at[y], place.at(y=other))
    chunks = [Gather(remote, place, WA, g * D, D) for g in range(4)]
    chunks += [Gather(remote, place, WI, n * D, D) for n in range(FF // D)]
    chunks += [Gather(remote, place, WU, n * 256, 256) for n in range(3)]
    rounds = Rounds()
    rounds.add(chunks[0], SmallGather(remote, place, SM))
    xs.start()
    length = length_ref[0]
    E[...] = key_structure(seq_len, length)
    for n in range(1, 4):
        rounds.round()
        rounds.add(chunks[n])
    own_rows = pl.ds(pl.multiple_of(y * local, local), local)
    other_rows = pl.ds(pl.multiple_of(other * local, local), local)
    XT[:, own_rows] = XF[y].T
    rounds.round()
    rounds.add(chunks[4])
    xs.wait_recv()

    tiles = SM[...].reshape(-1, 16, 128)
    pieces = tiles.shape[0]
    VEC[...] = spread_vectors(tiles, D // pieces, pieces)
    IB[...] = spread_vectors(tiles[:, 8:16, :], FF // pieces, pieces)
    put(VEC, vec_hbm)
    position = y * local + lax.broadcasted_iota(jnp.int32, (1, local), 1)
    live = position < length

    def head_step(h, carry):
        pair = lax.div(h, 2)
        half = lax.rem(h, 2)
        lanes = ds128(pair, 128)
        own = pl.ds(pl.multiple_of(h * HD, HD), HD)
        left = jnp.concatenate([K[:, lanes], E[...]], axis=1)
        right = jnp.concatenate([head_lanes(Q[:, lanes], half), query_structure(compact_ref[h])], axis=1)
        for part in range(local // 256):
            cols = slice(part * 256, (part + 1) * 256)
            scores = dot_nt(left, right[cols, :])
            top = jnp.max(scores, axis=0, keepdims=True)
            exponent = jnp.exp(scores - top)
            total = jnp.sum(exponent, axis=0, keepdims=True)
            low = (exponent * (1.0 / total)).astype(bf16)
            AT[own, cols] = dot_nn(VT[own, :], low).astype(bf16)
            LSE[h, :, cols] = top + jnp.log(total)
            TOP[h, :, cols] = jnp.where(live[:, cols], top, neg_large)
        return carry

    def wide(buf, lo, width):
        return buf[:, :, :, :, :, lo : lo + width].reshape(-1, width)

    for g in range(3):
        cols = slice(g * 256, (g + 1) * 256)
        lo = g * D
        own = dot_nn(XF[y], wide(WA, lo, D))
        Q[:, cols] = ((own[:, :256] + VEC[0:1, cols]).astype(bf16).astype(f32) * (HD**-0.5)).astype(bf16)
        K[own_rows, cols] = own[:, 256:512].astype(bf16)
        values = (own[:, 512:] + VEC[1:2, cols]).astype(bf16)
        V[own_rows, cols] = values
        VT[cols, own_rows] = values.T
        theirs = dot_nn(XF[other], wide(WA, lo + 256, 512))
        K[other_rows, cols] = theirs[:, :256].astype(bf16)
        values = (theirs[:, 256:] + VEC[1:2, cols]).astype(bf16)
        V[other_rows, cols] = values
        VT[cols, other_rows] = values.T
        lax.fori_loop(4 * g, 4 * g + 2, head_step, 0)
        rounds.round()
        rounds.add(chunks[5 + 2 * g])
        lax.fori_loop(4 * g + 2, 4 * g + 4, head_step, 0)
        if g < 2:
            rounds.round()
            rounds.add(chunks[6 + 2 * g])
    put(WA, wa_hbm)
    put(Q, q_hbm)
    put(K, k_hbm)
    put(V, v_hbm)
    put(LSE, lse_hbm)
    put(TOP, top_hbm)
    put(AT, at_hbm)
    R1[...] = dot_nn(AT[...].T, wide(WA, 3 * D, D))

    def first_norm(k, carry):
        rows = ds128(k, 64)
        summed = XF[y, rows, :].astype(f32) + R1[rows, :] + VEC[2:3, :]
        R1[rows, :] = summed
        normal, _ = layer_norm_parts(summed)
        value = normal * VEC[3:4, :] + VEC[4:5, :]
        N1L[rows, :] = value.astype(bf16)
        R2[rows, :] = value + VEC[5:6, :]
        return carry

    lax.fori_loop(0, local // 64, first_norm, 0)
    put(R1, r1_hbm)
    rounds.round()
    rounds.add(chunks[10])
    N1T[...] = N1L[...].T
    put(N1T, n1t_hbm)
    KT[...] = K[...].T
    put(KT, kt_hbm)
    XT[:, other_rows] = XF[other].T
    put(XT, xt_hbm)
    for n in range(FF // D):
        cols = slice(n * D, (n + 1) * D)
        U[...] = dot_nn(N1L[...], wide(WI, n * D, D)) + IB[0:1, cols]

        def activate(k, carry):
            rows = ds128(k, 16)
            u = U[rows, :]
            below = 0.5 * (1.0 + lax.erf(u * np.float32(0.5**0.5)))
            G[rows, cols] = (u * below).astype(bf16)
            GP[n, rows, :] = below + u * jnp.exp(-0.5 * u * u) * np.float32((2.0 * np.pi) ** -0.5)
            return carry

        lax.fori_loop(0, local // 16, activate, 0)
        GT[cols, :] = G[:, cols].T
        rounds.round()
    put(WI, wi_hbm)
    put(GP, gp_hbm)
    put(GT, gt_hbm)
    while rounds.active:
        rounds.round()
    put(WU, wu_hbm)
    R2[...] += dot_nn(G[...], WU[...].reshape(FF, D))

    def second_norm(k, carry):
        rows = ds128(k, 64)
        normal, _ = layer_norm_parts(R2[rows, :])
        OUT[rows, :] = (normal * VEC[6:7, :] + VEC[7:8, :]).astype(bf16)
        return carry

    lax.fori_loop(0, local // 64, second_norm, 0)
    put(R2, r2_hbm)
    put(OUT, out_hbm)
    remote.finish()
    for copy in outs:
        copy.wait()


def run_forward(nz, x, weights, small, compact, length):
    local = x.shape[0]
    wq, wk, wv, wo, wi, wu = weights
    grid = (nz, 2, 2, 2)
    rows, rows_u = wq.shape[0], wu.shape[0]
    seq = 2 * local
    blocks = FF // D
    outs = [
        ((local, D), bf16), ((local, D), f32), ((local, D), f32), ((blocks, local, D), f32), ((FF, local), bf16),
        ((D, local), bf16), ((D, local), bf16), ((local, D), bf16), ((seq, D), bf16), ((D, seq), bf16), ((seq, D), bf16),
        ((D, seq), bf16), ((H, 1, local), f32), ((H, 1, local), f32),
        ((*grid, rows, 4 * D), bf16), ((*grid, rows, FF), bf16), ((*grid, rows_u, D), bf16), ((16, D), f32),
    ]
    scratch = [
        ((*grid, rows, 4 * D), bf16), ((*grid, rows, FF), bf16), ((*grid, rows_u, D), bf16), ((*grid, 16, 128), bf16),
        ((2, local, D), bf16), ((D, seq), bf16), ((local, D), bf16), ((seq, D), bf16), ((D, seq), bf16), ((seq, D), bf16),
        ((D, seq), bf16), ((D, local), bf16), ((local, D), f32), ((local, D), f32), ((local, D), bf16), ((D, local), bf16),
        ((local, D), f32), ((blocks, local, D), f32), ((local, FF), bf16), ((FF, local), bf16), ((seq, 128), bf16),
        ((16, D), f32), ((8, FF), f32), ((H, 1, local), f32), ((H, 1, local), f32), ((local, D), bf16),
    ]
    copies = 1 + 11 * (2 * (nz - 1) + 5) + (nz - 1) + 3
    return pl.pallas_call(
        functools.partial(forward_kernel, nz, local),
        out_shape=[jax.ShapeDtypeStruct(*o) for o in outs],
        in_specs=[INSMEM, INVMEM] + [ANY] * 8,
        out_specs=[ANY] * len(outs),
        scratch_shapes=[pltpu.VMEM(*s) for s in scratch]
        + [
            pltpu.SemaphoreType.DMA((copies,)),
            pltpu.SemaphoreType.DMA((copies,)),
            pltpu.SemaphoreType.DMA((14,)),
            pltpu.SemaphoreType.DMA((len(outs),)),
        ],
        compiler_params=pltpu.CompilerParams(collective_id=1, has_side_effects=True, vmem_limit_bytes=60 << 20),
        name="gather_forward",
    )(length, compact, x, wq, wk, wv, wo, wi, wu, small)


def compact_mask(random_here, length, first_block):
    blocks = random_here.shape[0]
    query = (first_block + jnp.arange(blocks, dtype=jnp.int32))[None, :, None]
    lane = jnp.arange(128, dtype=jnp.int32)[None, None, :]
    last = (length - 1) // BLK
    ok = (jnp.abs(query - lane) <= 1) | (lane == 0) | (lane == last) | (query == 0) | (query == last)
    heads = jnp.transpose(random_here, (1, 0, 2))
    for k in range(heads.shape[2]):
        ok = ok | (heads[:, :, k : k + 1] == lane)
    shown = jnp.where(lane < NB, jnp.where(ok, 0.0, neg_large), jnp.where(lane == NB, neg_large, 0.0))
    return shown.astype(f32)


def pack_small(vectors, wide):
    rows = [jnp.pad(v, (0, 128 - v.shape[0])) for v in vectors] + [jnp.pad(wide, (0, 128 - wide.shape[0]))]
    rows += [jnp.zeros((128,), bf16)] * (16 - len(rows))
    return jnp.stack(rows)


def back_pair(pair, local, compact_ref, Q, K, V, KT, DA, LSE, E, PB, DS, DQT, DKG, DVG):
    lanes = ds128(pair, 128)
    q_pair, a_pair, k_pair, v_pair = Q[:, lanes], DA[:, lanes], K[:, lanes], V[:, lanes]
    left = jnp.concatenate([k_pair, E[...]], axis=1)
    q_heads = [head_lanes(q_pair, half) for half in (0, 1)]
    a_heads = [head_lanes(a_pair, half) for half in (0, 1)]
    for half in (0, 1):
        h = pair * 2 + half
        own = pl.ds(pl.multiple_of(h * HD, HD), HD)
        right = jnp.concatenate([q_heads[half], query_structure(compact_ref[h])], axis=1)
        for part in range(local // 256):
            cols = slice(part * 256, (part + 1) * 256)
            place = slice(half * local + part * 256, half * local + (part + 1) * 256)
            prob = jnp.exp(dot_nt(left, right[cols, :]) - LSE[h, :, cols])
            PB[:, place] = prob.astype(bf16)
            dprob = dot_nt(v_pair, a_heads[half][cols, :])
            inner = jnp.sum(prob * dprob, axis=0, keepdims=True)
            low = (prob * (dprob - inner)).astype(bf16)
            DS[:, place] = low
            DQT[own, cols] = (dot_nn(KT[own, :], low) * (HD**-0.5)).astype(bf16)
    spot = ds128(lax.rem(pair, 2), 128)
    DKG[:, spot] = dot_nn(DS[...], jnp.concatenate(q_heads, axis=0)).astype(bf16)
    DVG[:, spot] = dot_nn(PB[...], jnp.concatenate(a_heads, axis=0)).astype(bf16)


class Scatter:
    def __init__(self, remote, place, g, bufs, out, lo, width):
        rc, ra1, ra2, raz, rb1, rbz, rb2 = bufs
        z, x, c, y = place.z, place.x, place.c, place.y
        half = width // 2
        a, b, both = slice(lo, lo + half), slice(lo + half, lo + width), slice(lo, lo + width)
        self.place, self.g, self.bufs, self.out, self.a, self.b, self.both = place, g, bufs, out, a, b, both
        self.core = remote.make(g.at[:, :, 1 - c, :, :, both], rc, place.at(c=1 - c))
        self.a1 = remote.make(g.at[:, :, c, 1 - y, :, a], ra1, place.at(y=1 - y))
        self.b1 = remote.make(g.at[:, 1 - x, c, :, :, b], rb1, place.at(x=1 - x))
        self.a2 = remote.make(g.at[:, 1 - x, c, y, :, a], ra2, place.at(x=1 - x))
        self.bz, self.az = [], []
        for k in range(1, place.nz):
            zk = place.z_off(k)
            self.bz.append(remote.make(g.at[zk, x, c, :, :, b], rbz.at[k - 1], place.at(z=zk)))
            self.az.append(remote.make(g.at[zk, x, c, y, :, a], raz.at[k - 1], place.at(z=zk)))
        self.b2 = remote.make(g.at[z, x, c, 1 - y, :, b], rb2, place.at(y=1 - y))
        self.steps = 5

    def step(self, n):
        rc, ra1, ra2, raz, rb1, rbz, rb2 = self.bufs
        place, g, a, b, both = self.place, self.g, self.a, self.b, self.both
        z, x, c, y = place.z, place.x, place.c, place.y
        if n == 0:
            self.core.start()
        elif n == 1:
            self.core.wait_recv()

            def add_core(k, carry):
                zz, xx = lax.div(k, 2), lax.rem(k, 2)
                for yy in range(2):
                    total = g[zz, xx, c, yy, :, both].astype(f32) + rc[zz, xx, yy].astype(f32)
                    g[zz, xx, c, yy, :, both] = total.astype(bf16)
                return carry

            lax.fori_loop(0, place.nz * 2, add_core, 0)
            self.a1.start()
            self.b1.start()
        elif n == 2:
            self.b1.wait_recv()

            def add_b1(k, carry):
                zz, yy = lax.div(k, 2), lax.rem(k, 2)
                g[zz, x, c, yy, :, b] = (g[zz, x, c, yy, :, b].astype(f32) + rb1[zz, yy].astype(f32)).astype(bf16)
                return carry

            lax.fori_loop(0, place.nz * 2, add_b1, 0)
            for copy in self.bz:
                copy.start()
            self.a1.wait_recv()

            def add_a1(k, carry):
                zz, xx = lax.div(k, 2), lax.rem(k, 2)
                g[zz, xx, c, y, :, a] = (g[zz, xx, c, y, :, a].astype(f32) + ra1[zz, xx].astype(f32)).astype(bf16)
                return carry

            lax.fori_loop(0, place.nz * 2, add_a1, 0)
            self.a2.start()
        elif n == 3:
            self.a2.wait_recv()

            def add_a2(zz, carry):
                g[zz, x, c, y, :, a] = (g[zz, x, c, y, :, a].astype(f32) + ra2[zz].astype(f32)).astype(bf16)
                return carry

            lax.fori_loop(0, place.nz, add_a2, 0)
            for copy in self.az:
                copy.start()
            for copy in self.bz:
                copy.wait_recv()

            def add_bz(yy, carry):
                total = g[z, x, c, yy, :, b].astype(f32)
                for k in range(place.nz - 1):
                    total = total + rbz[k, yy].astype(f32)
                g[z, x, c, yy, :, b] = total.astype(bf16)
                return carry

            lax.fori_loop(0, 2, add_bz, 0)
            self.b2.start()
        elif n == 4:
            for copy in self.az:
                copy.wait_recv()
            total = g[z, x, c, y, :, a].astype(f32)
            for k in range(place.nz - 1):
                total = total + raz[k].astype(f32)
            self.out[:, a] = total
            self.b2.wait_recv()
            self.out[:, b] = g[z, x, c, y, :, b].astype(f32) + rb2[...].astype(f32)


def scatter_buffers(nz, rows, width):
    half = width // 2
    return [
        ((nz, 2, 2, rows, width), bf16), ((nz, 2, rows, half), bf16), ((nz, rows, half), bf16), ((nz - 1, rows, half), bf16),
        ((nz, 2, rows, half), bf16), ((nz - 1, 2, rows, half), bf16), ((rows, half), bf16),
    ]


class SmallSums:
    def __init__(self, remote, place, t, bufs):
        rc, ry, rx, rz = bufs
        z, x, c, y = place.z, place.x, place.c, place.y
        self.place, self.t, self.bufs = place, t, bufs
        self.stages = [
            [remote.make(t.at[:, :, 1 - c], rc, place.at(c=1 - c))],
            [remote.make(t.at[:, :, c, 1 - y], ry, place.at(y=1 - y))],
            [remote.make(t.at[:, 1 - x, c, y], rx, place.at(x=1 - x))],
            [
                remote.make(t.at[place.z_off(k), x, c, y], rz.at[k - 1], place.at(z=place.z_off(k)))
                for k in range(1, place.nz)
            ],
        ]
        self.steps = 5

    def step(self, n):
        place, t = self.place, self.t
        rc, ry, rx, rz = self.bufs
        z, x, c, y = place.z, place.x, place.c, place.y
        if n > 0:
            for copy in self.stages[n - 1]:
                copy.wait_recv()
        if n == 1:
            t[:, :, c] = t[:, :, c] + rc[...]
        elif n == 2:
            t[:, :, c, y] = t[:, :, c, y] + ry[...]
        elif n == 3:
            t[:, x, c, y] = t[:, x, c, y] + rx[...]
        elif n == 4:
            total = t[z, x, c, y]
            for k in range(place.nz - 1):
                total = total + rz[k]
            t[z, x, c, y] = total
        if n < 4:
            for copy in self.stages[n]:
                copy.start()


def small_buffers(nz):
    return [((nz, 2, 2, 16, 128), f32), ((nz, 2, 16, 128), f32), ((nz, 16, 128), f32), ((nz - 1, 16, 128), f32)]


class TopOfAll:
    def __init__(self, remote, place, top, tops):
        x, c, y = place.x, place.c, place.y
        to = [[place.at(c=1 - c)], [place.at(y=1 - y)], [place.at(x=1 - x)]]
        to.append([place.at(z=place.z_off(k)) for k in range(1, place.nz)])
        self.top, self.tops, self.stages, slot = top, tops, [], 0
        for n, peers in enumerate(to):
            made = []
            for peer in peers:
                made.append((remote.make(top.at[n], tops.at[slot], peer), slot))
                slot += 1
            self.stages.append(made)
        self.steps = 5

    def step(self, n):
        if n > 0:
            best = self.top[n - 1]
            for copy, slot in self.stages[n - 1]:
                copy.wait_recv()
                best = jnp.maximum(best, self.tops[slot])
            self.top[n] = best
        if n < 4:
            for copy, _ in self.stages[n]:
                copy.start()


def gather_vectors(rows, width, pieces):
    n, total = rows.shape
    lane3 = lax.broadcasted_iota(jnp.int32, (pieces, n, total), 2).astype(f32)
    piece3 = lax.broadcasted_iota(jnp.int32, (pieces, n, total), 0).astype(f32)
    mine = jnp.floor((lane3 + 0.5) * (1.0 / width)) == piece3
    spread = jnp.where(mine, rows[None], 0.0).reshape(pieces * n, total)
    lane = lax.broadcasted_iota(jnp.int32, (128, total), 1).astype(f32)
    row = lax.broadcasted_iota(jnp.int32, (128, total), 0).astype(f32)
    owner = jnp.floor((lane + 0.5) * (1.0 / width))
    chooser = jnp.where(lane - owner * width == row, 1.0, 0.0).astype(bf16)
    high = spread.astype(bf16)
    rest = spread - high.astype(f32)
    middle = rest.astype(bf16)
    lowest = (rest - middle.astype(f32)).astype(bf16)
    tiles = dot_nt(high, chooser) + (dot_nt(middle, chooser) + dot_nt(lowest, chooser))
    return tiles.reshape(pieces, n, 128)


def norm_back(normal, inverse, grads, gain):
    scaled = grads * gain
    first = jnp.mean(scaled, axis=-1, keepdims=True)
    second = jnp.mean(scaled * normal, axis=-1, keepdims=True)
    return inverse * (scaled - first - normal * second)


def row_sum(values):
    return jnp.sum(values, axis=0, keepdims=True)


def backward_kernel(
    nz, local, length_ref, compact_ref, VEC, cot_hbm, r1_hbm, r2_hbm, gp_hbm, gt_hbm, n1t_hbm, at_hbm, q_hbm, k_hbm, kt_hbm,
    v_hbm, xt_hbm, lse_hbm, top_hbm, wa_hbm, wi_hbm, wu_hbm,
    dx_hbm, OA, OI, OU, OS, OT, *rest,
):
    place = Place(nz)
    z, x, c, y = place.z, place.x, place.c, place.y
    GA, GI, GU, WA, T, TOP, TOPS, TOPV, DP, DA, AT, DR1, E, SUMS, ISUM, SEND, RECV = rest[:17]
    bufs = [rest[17 + 7 * k : 24 + 7 * k] for k in range(11)]
    sbufs = rest[94:98]
    send_sems, recv_sems, load_sems = rest[98:]
    blocks = FF // D
    pieces = nz * 8
    seq_len = 2 * local
    length = length_ref[0]
    loads = [0]

    def load(src, dst):
        copy = pltpu.make_async_copy(src, dst, load_sems.at[loads[0]])
        loads[0] += 1
        copy.start()
        return copy

    remote = Remote(send_sems, recv_sems)
    ups = [Scatter(remote, place, GU, bufs[n], OU, n * 256, 256) for n in range(3)]
    ins = [Scatter(remote, place, GI, bufs[3 + n], OI, n * D, D) for n in range(blocks)]
    att = [Scatter(remote, place, GA, bufs[7 + n], OA, n * D, D) for n in range(4)]
    small = SmallSums(remote, place, T, sbufs)
    best = TopOfAll(remote, place, TOP, TOPS)
    swap = remote.make(SEND, RECV, place.at(y=1 - y))
    rounds = Rounds()
    grid = (nz, 2, 2, 2)
    SUMS[...] = jnp.zeros_like(SUMS)
    ISUM[...] = jnp.zeros_like(ISUM)

    def first_stage(COT, R2, R1, DM, GT, DU, GP, N1T, WUS, WIS):
        l_r2, l_cot = load(r2_hbm, R2), load(cot_hbm, COT)
        l_wu = [load(wu_hbm.at[0], WUS.at[0]), load(wu_hbm.at[1], WUS.at[1])]
        l_gp = [load(gp_hbm.at[0], GP.at[0]), load(gp_hbm.at[1], GP.at[1])]
        l_gt = load(gt_hbm, GT)
        l_n1t, l_r1 = load(n1t_hbm, N1T), load(r1_hbm, R1)

        def wi_of(n):
            return wi_hbm.at[:, :, :, :, :, n * D : (n + 1) * D]

        l_wi = [load(wi_of(0), WIS.at[0]), load(wi_of(1), WIS.at[1])]
        l_top, l_at, l_wa = load(top_hbm, TOPV), load(at_hbm, AT), load(wa_hbm, WA)
        entry_barrier(place)
        E[...] = key_structure(seq_len, length)
        l_r2.wait()
        l_cot.wait()

        def second_norm(k, carry):
            rows = ds128(k, 64)
            normal, inverse = layer_norm_parts(R2[rows, :])
            position = y * local + k * 64 + lax.broadcasted_iota(jnp.int32, (64, D), 0)
            grads = jnp.where(position < length, COT[rows, :].astype(f32), 0.0)
            through = norm_back(normal, inverse, grads, VEC[6:7, :])
            R2[rows, :] = through
            low = through.astype(bf16)
            DM[rows, :] = low
            SUMS[5:6, :] += row_sum(low.astype(f32))
            SUMS[6:7, :] += row_sum(grads * normal)
            SUMS[7:8, :] += row_sum(grads)
            return carry

        lax.fori_loop(0, local // 64, second_norm, 0)
        for n in range(blocks):
            l_wu[n].wait()
            l_gp[n].wait()
            grads = dot_nt(DM[...], WUS[n % 2].reshape(D, D)) * GP[n % 2]
            low = grads.astype(bf16)
            DU[n] = low
            ISUM[0:1, n * D : (n + 1) * D] = row_sum(low.astype(f32))
            if n + 2 < blocks:
                l_wu.append(load(wu_hbm.at[n + 2], WUS.at[n % 2]))
                l_gp.append(load(gp_hbm.at[n + 2], GP.at[n % 2]))
        l_gt.wait()
        for n in range(3):
            cols = slice(n * 256, (n + 1) * 256)

            def outer_grad(zz, carry):
                rows = ds128(zz, FF // nz)
                made = dot_nn(GT[rows, :], DM[:, cols]).astype(bf16)
                GU[zz, :, :, :, :, cols] = made.reshape(2, 2, 2, -1, 256)
                return carry

            lax.fori_loop(0, nz, outer_grad, 0)
            rounds.round()
            rounds.add(ups[n])
        l_top.wait()
        TOP[0] = jnp.zeros((16, 128), f32) + neg_large
        TOP[0, 0:H, :] = jnp.broadcast_to(jnp.max(TOPV[:, 0, :], axis=1, keepdims=True), (H, 128))
        l_n1t.wait()
        for n in range(blocks):
            made = dot_nn(N1T[...], DU[n]).astype(bf16)
            GI[:, :, :, :, :, n * D : (n + 1) * D] = made.reshape(*grid, -1, D)
            rounds.round()
            rounds.add(ins[n])
            if n == 0:
                rounds.add(best)
        for n in range(blocks):
            l_wi[n].wait()
            R2[...] += dot_nt(DU[n], WIS[n % 2].reshape(D, D))
            if n + 2 < blocks:
                l_wi.append(load(wi_of(n + 2), WIS.at[n % 2]))
        rounds.round()
        l_r1.wait()

        def first_norm(k, carry):
            rows = ds128(k, 64)
            normal, inverse = layer_norm_parts(R1[rows, :])
            grads = R2[rows, :]
            through = norm_back(normal, inverse, grads, VEC[3:4, :])
            DR1[rows, :] = through
            low = through.astype(bf16)
            DP[rows, :] = low
            SUMS[2:3, :] += row_sum(low.astype(f32))
            SUMS[3:4, :] += row_sum(grads * normal)
            SUMS[4:5, :] += row_sum(grads)
            return carry

        lax.fori_loop(0, local // 64, first_norm, 0)
        l_at.wait()
        l_wa.wait()

    pl.run_scoped(
        first_stage,
        pltpu.VMEM((local, D), bf16), pltpu.VMEM((local, D), f32), pltpu.VMEM((local, D), f32), pltpu.VMEM((local, D), bf16),
        pltpu.VMEM((FF, local), bf16), pltpu.VMEM((blocks, local, D), bf16), pltpu.VMEM((2, local, D), f32),
        pltpu.VMEM((D, local), bf16), pltpu.VMEM((2, 2, 2, 2, FF // (nz * 8), D), bf16),
        pltpu.VMEM((2, *grid, D // (nz * 8), D), bf16),
    )

    def second_stage(Q, K, KT, V, XT, LSE, PB, DS, DQT, DKG, DVG, DX, DXO):
        waits = [load(s, d) for s, d in ((q_hbm, Q), (k_hbm, K), (kt_hbm, KT), (v_hbm, V), (lse_hbm, LSE), (xt_hbm, XT))]
        made = dot_nn(AT[...], DP[...]).astype(bf16)
        GA[:, :, :, :, :, 3 * D : 4 * D] = made.reshape(*grid, -1, D)
        rounds.round()
        rounds.add(att[3])
        DA[...] = dot_nt(DP[...], WA[:, :, :, :, :, 3 * D : 4 * D].reshape(D, D)).astype(bf16)
        for wait in waits:
            wait.wait()
        DX[...] = jnp.zeros_like(DX)
        DXO[...] = jnp.zeros_like(DXO)
        own_rows = pl.ds(pl.multiple_of(y * local, local), local)
        other_rows = pl.ds(pl.multiple_of((1 - y) * local, local), local)

        def pair_step(pair, carry):
            back_pair(pair, local, compact_ref, Q, K, V, KT, DA, LSE, E, PB, DS, DQT, DKG, DVG)
            return carry

        for g in range(3):
            lo = g * D
            cols = slice(g * 256, (g + 1) * 256)
            lax.fori_loop(2 * g, 2 * g + 1, pair_step, 0)
            rounds.round()
            lax.fori_loop(2 * g + 1, 2 * g + 2, pair_step, 0)
            dq = DQT[cols, :].T
            SUMS[0:1, cols] = row_sum(dq.astype(f32))
            SUMS[1:2, cols] = row_sum(DVG[...].astype(f32))
            for n, made in enumerate((dot_nn(XT[:, own_rows], dq), dot_nn(XT[...], DKG[...]), dot_nn(XT[...], DVG[...]))):
                GA[:, :, :, :, :, lo + n * 256 : lo + (n + 1) * 256] = made.astype(bf16).reshape(*grid, -1, 256)
            rounds.round()
            rounds.add(att[g])
            theirs = jnp.concatenate([DKG[other_rows, :], DVG[other_rows, :]], axis=1)
            DXO[...] += dot_nt(theirs, WA[:, :, :, :, :, lo + 256 : lo + D].reshape(D, 512))
            if g == 2:
                SEND[...] = DXO[...].astype(bf16)
                swap.start()
            ours = jnp.concatenate([dq, DKG[own_rows, :], DVG[own_rows, :]], axis=1)
            DX[...] += dot_nt(ours, WA[:, :, :, :, :, lo : lo + D].reshape(D, D))
        rounds.round()
        T[:, :, :, :, 0:8, :] = gather_vectors(SUMS[0:8, :], D // pieces, pieces).reshape(*grid, 8, 128)
        wide = gather_vectors(ISUM[...], FF // pieces, pieces)
        T[:, :, :, :, 8:16, :] = wide.reshape(*grid, 8, 128)
        rounds.add(small)
        while rounds.active:
            rounds.round()
        swap.wait_recv()

        def last(k, carry):
            rows = ds128(k, 64)
            DX[rows, :] = DX[rows, :] + DR1[rows, :] + RECV[rows, :].astype(f32)
            return carry

        lax.fori_loop(0, local // 64, last, 0)
        out = pltpu.make_async_copy(DX, dx_hbm, load_sems.at[loads[0]])
        out.start()
        OS[...] = T[z, x, c, y]
        OT[...] = TOP[4]
        out.wait()

    pl.run_scoped(
        second_stage,
        pltpu.VMEM((local, D), bf16), pltpu.VMEM((seq_len, D), bf16), pltpu.VMEM((D, seq_len), bf16),
        pltpu.VMEM((seq_len, D), bf16), pltpu.VMEM((D, seq_len), bf16), pltpu.VMEM((H, 1, local), f32),
        pltpu.VMEM((seq_len, 2 * local), bf16), pltpu.VMEM((seq_len, 2 * local), bf16), pltpu.VMEM((D, local), bf16),
        pltpu.VMEM((seq_len, 256), bf16), pltpu.VMEM((seq_len, 256), bf16), pltpu.VMEM((local, D), f32),
        pltpu.VMEM((local, D), f32),
    )
    remote.finish()


def run_backward(nz, local, rows, rows_u, length, compact, vec, *arrays):
    grid = (nz, 2, 2, 2)
    seq = 2 * local
    outs = [((local, D), f32), ((rows, 4 * D), f32), ((rows, FF), f32), ((rows_u, D), f32), ((16, 128), f32), ((16, 128), f32)]
    scratch = [
        ((*grid, rows, 4 * D), bf16), ((*grid, rows, FF), bf16), ((*grid, rows_u, D), bf16), ((*grid, rows, 4 * D), bf16),
        ((*grid, 16, 128), f32), ((5, 16, 128), f32), ((3 + nz - 1, 16, 128), f32), ((H, 1, local), f32),
        ((local, D), bf16), ((local, D), bf16), ((D, local), bf16), ((local, D), f32), ((seq, 128), bf16),
        ((8, D), f32), ((8, FF), f32), ((local, D), bf16), ((local, D), bf16),
    ]
    for n in range(3):
        scratch += scatter_buffers(nz, rows_u, 256)
    for n in range(8):
        scratch += scatter_buffers(nz, rows, D)
    scratch += small_buffers(nz)
    copies = 11 * (2 * (nz - 1) + 5) + 2 * (3 + nz - 1) + 1
    return pl.pallas_call(
        functools.partial(backward_kernel, nz, local),
        out_shape=[jax.ShapeDtypeStruct(*o) for o in outs],
        in_specs=[INSMEM, INVMEM, INVMEM] + [ANY] * len(arrays),
        out_specs=[ANY] + [INVMEM] * 5,
        scratch_shapes=[pltpu.VMEM(*s) for s in scratch]
        + [pltpu.SemaphoreType.DMA((copies,)), pltpu.SemaphoreType.DMA((copies,)), pltpu.SemaphoreType.DMA((32,))],
        compiler_params=pltpu.CompilerParams(collective_id=2, has_side_effects=True, vmem_limit_bytes=60 << 20),
        name="backward_scatter",
    )(length, compact, vec, *arrays)


def layer_norm(row_values, gain_vector, shift_vector):
    centre = row_values - jnp.mean(row_values, axis=-1, keepdims=True)
    spread = jnp.mean(centre * centre, axis=-1, keepdims=True)
    return centre * lax.rsqrt(spread + norm_eps) * gain_vector + shift_vector


def gelu_exact(values):
    return jax.nn.gelu(values, approximate=False)


def column_sums(values):
    return jnp.sum(values.astype(f32), axis=0)


def clip_outputs(logit_maxima, threshold, query_weight, query_bias, key_weight, device_rank):
    clip_limit = threshold.astype(f32)[0] * 0.01
    factors = jnp.sqrt(clip_limit / jnp.maximum(logit_maxima, clip_limit))
    column_scale = jnp.repeat(factors, HD)
    query_clipped = (query_weight.astype(f32) * column_scale[None, :]).astype(bf16)
    key_clipped = (key_weight.astype(f32) * column_scale[None, :]).astype(bf16)
    bias_count = query_bias.shape[0]
    bias_heads = (device_rank * bias_count + jnp.arange(bias_count)) // HD
    bias_scale = jnp.sum(jnp.where(bias_heads[:, None] == jnp.arange(H)[None, :], factors[None, :], 0.0), axis=1)
    return query_clipped, (query_bias.astype(f32) * bias_scale).astype(bf16), key_clipped


def fast_shards(
    nz,
    inputs, cotangent, query_weight, query_bias, key_weight, value_weight, value_bias, output_weight, output_bias,
    first_gain, first_shift, inner_weight, inner_bias, outer_weight, outer_bias, second_gain, second_shift,
    lengths, random_blocks, threshold,
):
    local = inputs.shape[1]
    pieces = nz * 8
    rows, rows_u = query_weight.shape[0], outer_weight.shape[0]
    y = lax.axis_index("ctx")
    blocks = local // BLK
    first_block = y * blocks
    random_here = lax.dynamic_slice_in_dim(random_blocks[0], first_block, blocks, 0)
    compact = compact_mask(random_here, lengths[0], first_block)
    small = pack_small(
        [query_bias, value_bias, output_bias, first_gain, first_shift, outer_bias, second_gain, second_shift], inner_bias
    )
    x = inputs[0]
    weights = (query_weight, key_weight, value_weight, output_weight, inner_weight, outer_weight)
    (
        output, r1, r2, gp, gt, n1t, at, q, k, kt, v, xt, lse, tops, wa, wi, wu, vectors
    ) = run_forward(nz, x, weights, small, compact, lengths)
    input_grad, ga, gi, gu, gs, top = run_backward(
        nz, local, rows, rows_u, lengths, compact, vectors, cotangent[0], r1, r2, gp, gt, n1t, at, q, k, kt, v, xt, lse, tops,
        wa, wi, wu,
    )
    logit_maxima = top[:H, 0]
    rank = lax.axis_index("dp") * 2 + y
    query_clipped, bias_clipped, key_clipped = clip_outputs(
        logit_maxima, threshold, query_weight, query_bias, key_weight, rank
    )
    vec = [gs[n, :rows] for n in range(8)]
    qkv = [jnp.concatenate([ga[:, g * D + n * 256 : g * D + (n + 1) * 256] for g in range(3)], axis=1) for n in range(3)]
    return (
        output[None], input_grad[None],
        qkv[0], vec[0], qkv[1], qkv[2], vec[1], ga[:, 3 * D :], vec[2], vec[3], vec[4],
        gi, gs[8, : FF // pieces], gu, vec[5], vec[6], vec[7],
        query_clipped, bias_clipped, key_clipped, logit_maxima,
    )


def general_shards(
    inputs, cotangent, query_weight, query_bias, key_weight, value_weight, value_bias, output_weight, output_bias,
    first_gain, first_shift, inner_weight, inner_bias, outer_weight, outer_bias, second_gain, second_shift,
    lengths, random_blocks, threshold,
):
    both = ("dp", "ctx")
    shards = (
        query_weight, query_bias, key_weight, value_weight, value_bias, output_weight, output_bias, first_gain, first_shift,
        inner_weight, inner_bias, outer_weight, outer_bias, second_gain, second_shift,
    )
    wq, bq, wk, wv, bv, wo, bo, g1, s1, wi, bi, wu, bu, g2, s2 = (lax.all_gather(w, both, axis=0, tiled=True) for w in shards)
    bq, bv, bo, g1, s1, bi, bu, g2, s2 = (v.astype(f32) for v in (bq, bv, bo, g1, s1, bi, bu, g2, s2))
    seqs, local, _ = inputs.shape
    blocks = local // BLK
    y = lax.axis_index("ctx")
    first_block = y * blocks
    scale = HD**-0.5
    outs = []
    sums = None
    top = jnp.full((H,), neg_large, f32)
    for s in range(seqs):
        x, length = inputs[s], lengths[s]
        random_here = lax.dynamic_slice_in_dim(random_blocks[s], first_block, blocks, 0)
        mask = compact_mask(random_here, length, first_block)[:, :, :NB]
        mask = jnp.repeat(jnp.repeat(mask, BLK, axis=1), BLK, axis=2)
        seen = jnp.arange(NB * BLK) < length
        mask = jnp.where(seen[None, None, :], mask, neg_large)
        live = (y * local + jnp.arange(local)) < length
        q = (dot_nn(x, wq) + bq).astype(bf16)
        k = lax.all_gather(dot_nn(x, wk).astype(bf16), "ctx", axis=0, tiled=True)
        v = lax.all_gather((dot_nn(x, wv) + bv).astype(bf16), "ctx", axis=0, tiled=True)
        qh, kh, vh = (a.reshape(-1, H, HD) for a in (q, k, v))
        raw = jnp.einsum("qhd,khd->hqk", qh, kh, preferred_element_type=f32) * scale + mask
        row_top = jnp.max(raw, axis=-1, keepdims=True)
        top = jnp.maximum(top, jnp.max(jnp.where(live[None, :, None], row_top, neg_large), axis=(1, 2)))
        exponent = jnp.exp(raw - row_top)
        prob = exponent / jnp.sum(exponent, axis=-1, keepdims=True)
        low = prob.astype(bf16)
        attended = jnp.einsum("hqk,khd->qhd", low, vh, preferred_element_type=f32).reshape(local, D).astype(bf16)
        first_sum = x.astype(f32) + dot_nn(attended, wo) + bo
        normed = layer_norm(first_sum, g1, s1)
        normed_low = normed.astype(bf16)
        pre_act = dot_nn(normed_low, wi) + bi
        activated = gelu_exact(pre_act).astype(bf16)
        second_sum = normed + dot_nn(activated, wu) + bu
        output = layer_norm(second_sum, g2, s2).astype(bf16)
        cot = jnp.where(live[:, None], cotangent[s].astype(f32), 0.0)
        grad_second, g2_grad, s2_grad = jax.vjp(layer_norm, second_sum, g2, s2)[1](cot)
        dm = grad_second.astype(bf16)
        du = jax.vjp(gelu_exact, pre_act)[1](dot_nt(dm, wu))[0].astype(bf16)
        grad_normed = grad_second + dot_nt(du, wi)
        grad_first, g1_grad, s1_grad = jax.vjp(layer_norm, first_sum, g1, s1)[1](grad_normed)
        dp = grad_first.astype(bf16)
        da = dot_nt(dp, wo).astype(bf16).reshape(local, H, HD)
        dprob = jnp.einsum("qhd,khd->hqk", da, vh, preferred_element_type=f32)
        ds = (prob * (dprob - jnp.sum(prob * dprob, axis=-1, keepdims=True))).astype(bf16)
        dq = (jnp.einsum("hqk,khd->qhd", ds, kh, preferred_element_type=f32) * scale).reshape(local, D).astype(bf16)
        dk = (jnp.einsum("hqk,qhd->khd", ds, qh, preferred_element_type=f32) * scale).reshape(-1, D)
        dv = jnp.einsum("hqk,qhd->khd", low, da, preferred_element_type=f32).reshape(-1, D)
        dk, dv = (lax.psum_scatter(a.astype(bf16), "ctx", scatter_dimension=0, tiled=True).astype(bf16) for a in (dk, dv))
        input_grad = grad_first + dot_nt(dq, wq) + dot_nt(dk, wk) + dot_nt(dv, wv)
        outs.append((output, input_grad))
        here = (
            dot_tn(x, dq), column_sums(dq), dot_tn(x, dk), dot_tn(x, dv), column_sums(dv), dot_tn(attended, dp),
            column_sums(dp), g1_grad, s1_grad, dot_tn(normed_low, du), column_sums(du), dot_tn(activated, dm),
            column_sums(dm), g2_grad, s2_grad,
        )
        sums = here if sums is None else tuple(a + b for a, b in zip(sums, here))
    grads = tuple(lax.psum_scatter(g, both, scatter_dimension=0, tiled=True) for g in sums)
    logit_maxima = lax.pmax(top, both)
    rank = lax.axis_index(both)
    clipped = clip_outputs(logit_maxima, threshold, query_weight, query_bias, key_weight, rank)
    return (jnp.stack([o for o, _ in outs]), jnp.stack([g for _, g in outs]), *grads, *clipped, logit_maxima)


def solution(mesh):
    both = P(("dp", "ctx"))
    rows = P(("dp", "ctx"), None)
    tokens = P("dp", "ctx", None)
    in_specs = (
        tokens, tokens, rows, both, rows, rows, both, rows, both, both, both, rows, both, rows, both, both, both,
        P("dp"), P("dp", None, None, None), P(),
    )
    out_specs = (
        tokens, tokens, rows, both, rows, rows, both, rows, both, both, both, rows, both, rows, both, both, both,
        rows, both, rows, P(),
    )
    dp, ctx = mesh.shape["dp"], mesh.shape["ctx"]
    pieces = dp * ctx
    fits = ctx == 2 and dp % 4 == 0 and D % (8 * pieces) == 0 and FF // pieces <= 128

    def step(*args):
        if fits and args[0].shape[0] == 1:
            return fast_shards(dp // 4, *args)
        return general_shards(*args)

    return jax.shard_map(step, mesh=mesh, in_specs=in_specs, out_specs=out_specs, check_vma=False)
```

```python
import functools

import jax
import jax.numpy as jnp
import numpy as np
from jax import lax
from jax.experimental import pallas as pl
from jax.experimental.pallas import tpu as pltpu
from jax.sharding import PartitionSpec as P

H = 12
HD = 64
BLK = 64
LEN = 1024
NB = 16
D = 768
FF = 3072

norm_eps = 1e-12
neg_large = -1e30
bf16 = jnp.bfloat16
f32 = jnp.float32
ANY = pl.BlockSpec(memory_space=pl.ANY)
INVMEM = pl.BlockSpec(memory_space=pltpu.VMEM)
INSMEM = pl.BlockSpec(memory_space=pltpu.SMEM)
MESH = pl.DeviceIdType.MESH


def dot_nn(a, b):
    return jnp.dot(a, b, preferred_element_type=f32)


def dot_nt(a, b):
    return lax.dot_general(a, b, (((1,), (1,)), ((), ())), preferred_element_type=f32)


def dot_tn(a, b):
    return lax.dot_general(a, b, (((0,), (0,)), ((), ())), preferred_element_type=f32)


def ds128(index, width):
    return pl.ds(pl.multiple_of(index * width, width), width)


class Place:
    def __init__(self, nz):
        self.nz = nz
        dp = lax.axis_index("dp")
        self.y = lax.axis_index("ctx")
        self.c = lax.rem(dp, 2)
        self.x = lax.rem(lax.div(dp, 2), 2)
        self.z = lax.div(dp, 4)

    def at(self, z=None, x=None, c=None, y=None):
        z = self.z if z is None else z
        x = self.x if x is None else x
        c = self.c if c is None else c
        y = self.y if y is None else y
        return ((z * 2 + x) * 2 + c, y)

    def z_off(self, k):
        return lax.rem(self.z + k, self.nz)

    def along(self, axis):
        if axis == "z":
            return [self.at(z=self.z_off(k)) for k in range(1, self.nz)]
        return [self.at(x=1 - self.x) if axis == "x" else self.at(y=1 - self.y)]

    def peers(self):
        return (
            [self.at(z=self.z_off(k)) for k in range(1, self.nz)]
            + [self.at(x=1 - self.x), self.at(y=1 - self.y), self.at(c=1 - self.c)]
        )


def entry_barrier(place):
    barrier = pltpu.get_barrier_semaphore()
    peers = place.peers()
    for peer in peers:
        pl.semaphore_signal(barrier, inc=1, device_id=peer, device_id_type=MESH)
    pl.semaphore_wait(barrier, len(peers))


class Remote:
    def __init__(self, send_sems, recv_sems):
        self.send_sems, self.recv_sems, self.used, self.copies = send_sems, recv_sems, 0, []

    def make(self, src, dst, peer):
        k = self.used
        self.used += 1
        copy = pltpu.make_async_remote_copy(
            src_ref=src, dst_ref=dst, send_sem=self.send_sems.at[k], recv_sem=self.recv_sems.at[k],
            device_id=peer, device_id_type=MESH,
        )
        self.copies.append(copy)
        return copy

    def finish(self):
        for copy in self.copies:
            copy.wait_send()


class Stripe:
    def __init__(self):
        self.stages, self.at = [], 0

    def take(self, n):
        pass

    def step(self):
        n = self.at
        if n > 0:
            for copy in self.stages[n - 1]:
                copy.wait_recv()
            self.take(n - 1)
        if n < len(self.stages):
            for copy in self.stages[n]:
                copy.start()
        self.at = n + 1


class GatherStripe(Stripe):
    def __init__(self, remote, place, buf, cols, order):
        super().__init__()
        have = {"z": place.z, "x": place.x, "y": place.y}
        for axis in order:
            ref = buf.at[have["z"], have["x"], place.c, have["y"], :, cols]
            self.stages.append([remote.make(ref, ref, peer) for peer in place.along(axis)])
            have[axis] = slice(None)
        ref = buf.at[:, :, place.c, :, :, cols]
        self.stages.append([remote.make(ref, ref, place.at(c=1 - place.c))])


class GatherTile(Stripe):
    def __init__(self, remote, place, buf):
        super().__init__()
        z, x, c, y = place.z, place.x, place.c, place.y
        for ref, peers in (
            (buf.at[z, x, c, y], place.along("z")),
            (buf.at[:, x, c, y], place.along("x")),
            (buf.at[:, :, c, y], place.along("y")),
            (buf.at[:, :, c], [place.at(c=1 - c)]),
        ):
            self.stages.append([remote.make(ref, ref, peer) for peer in peers])


class ScatterStripe(Stripe):
    def __init__(self, remote, place, g, cols, order, bufs, out):
        super().__init__()
        self.place, self.g, self.cols, self.order, self.bufs, self.out = place, g, cols, order, bufs, out
        own = {"z": place.z, "x": place.x, "y": place.y}
        have = {"z": slice(None), "x": slice(None), "y": slice(None)}
        ref = g.at[:, :, 1 - place.c, :, :, cols]
        self.stages.append([remote.make(ref, bufs[0], place.at(c=1 - place.c))])
        for n, axis in enumerate(order):
            made = []
            for k, peer in enumerate(place.along(axis)):
                there = dict(have)
                there[axis] = place.z_off(k + 1) if axis == "z" else 1 - own[axis]
                ref = g.at[there["z"], there["x"], place.c, there["y"], :, cols]
                made.append(remote.make(ref, bufs[n + 1].at[k] if axis == "z" else bufs[n + 1], peer))
            self.stages.append(made)
            have[axis] = own[axis]

    def take(self, n):
        place, g, cols, buf = self.place, self.g, self.cols, self.bufs[n]
        axis = self.order[n - 1] if n > 0 else "c"
        still = self.order[n:]
        sizes = {"z": place.nz, "x": 2, "y": 2}
        names = [name for name in "zxy" if name in still]
        count = 1
        for name in names:
            count *= sizes[name]

        def add(k, last):
            here = {"z": place.z, "x": place.x, "y": place.y}
            left = k
            for name in reversed(names):
                here[name] = lax.rem(left, sizes[name])
                left = lax.div(left, sizes[name])
            index = tuple(here[name] for name in names)
            spot = (here["z"], here["x"], place.c, here["y"], slice(None), cols)
            total = g[spot].astype(f32)
            for part in range(place.nz - 1) if axis == "z" else (None,):
                total = total + buf[index if part is None else (part, *index)].astype(f32)
            if last:
                self.out[:, cols] = total
            else:
                g[spot] = total.astype(bf16)

        if not names:
            add(0, True)
        elif count <= 2:
            for k in range(count):
                add(k, False)
        else:

            def twice(k, carry):
                add(2 * k, False)
                add(2 * k + 1, False)
                return carry

            lax.fori_loop(0, count // 2, twice, 0)


def scatter_buffers(nz, rows, width, order):
    sizes = {"z": nz, "x": 2, "y": 2}
    made = [((nz, 2, 2, rows, width), bf16)]
    for n, axis in enumerate(order):
        left = [sizes[name] for name in "zxy" if name in order[n + 1 :]]
        made.append((((nz - 1,) if axis == "z" else ()) + (*left, rows, width), bf16))
    return made


class SmallSums(Stripe):
    def __init__(self, remote, place, t, bufs):
        super().__init__()
        z, x, c, y = place.z, place.x, place.c, place.y
        rc, ry, rx, rz = bufs
        self.place, self.t, self.bufs = place, t, bufs
        self.stages = [
            [remote.make(t.at[:, :, 1 - c], rc, place.at(c=1 - c))],
            [remote.make(t.at[:, :, c, 1 - y], ry, place.at(y=1 - y))],
            [remote.make(t.at[:, 1 - x, c, y], rx, place.at(x=1 - x))],
            [remote.make(t.at[place.z_off(k + 1), x, c, y], rz.at[k], peer) for k, peer in enumerate(place.along("z"))],
        ]

    def take(self, n):
        place, t = self.place, self.t
        rc, ry, rx, rz = self.bufs
        z, x, c, y = place.z, place.x, place.c, place.y
        if n == 0:
            t[:, :, c] = t[:, :, c] + rc[...]
        elif n == 1:
            t[:, :, c, y] = t[:, :, c, y] + ry[...]
        elif n == 2:
            t[:, x, c, y] = t[:, x, c, y] + rx[...]
        else:
            total = t[z, x, c, y]
            for k in range(place.nz - 1):
                total = total + rz[k]
            t[z, x, c, y] = total


def small_buffers(nz):
    return [((nz, 2, 2, 16, 128), f32), ((nz, 2, 16, 128), f32), ((nz, 16, 128), f32), ((nz - 1, 16, 128), f32)]


class TopOfAll(Stripe):
    def __init__(self, remote, place, top, tops):
        super().__init__()
        self.top, self.tops, self.slots, slot = top, tops, [], 0
        for n, peers in enumerate(([place.at(c=1 - place.c)], place.along("y"), place.along("x"), place.along("z"))):
            self.slots.append(list(range(slot, slot + len(peers))))
            self.stages.append([remote.make(top.at[n], tops.at[slot + k], peer) for k, peer in enumerate(peers)])
            slot += len(peers)

    def take(self, n):
        best = self.top[n]
        for slot in self.slots[n]:
            best = jnp.maximum(best, self.tops[slot])
        self.top[n + 1] = best


class Script:
    def __init__(self, plan, stripes, swap):
        self.plan, self.stripes, self.swap, self.spent = plan, stripes, swap, 0

    def point(self):
        for item in self.plan[self.spent]:
            if item < 0:
                self.swap.start()
            else:
                self.stripes[item].step()
        self.spent += 1

    def points(self, index, first, count):
        for k in range(count):
            pl.when(index == first + k)(self.point)

    def close(self):
        assert self.spent == len(self.plan)
        assert all(s.at == len(s.stages) + 1 for s in self.stripes)


VMEM_BYTES = 60 << 20
GATHER_ITEMS = (
    (0, 0, 384, "yzx"), (0, 384, 384, "zxy"), (0, 768, 256, "zyx"), (0, 1024, 256, "yzx"), (0, 1280, 256, "yzx"),
    (0, 1536, 256, "zxy"), (0, 1792, 256, "zxy"), (0, 2048, 256, "yzx"), (0, 2304, 768, "zyx"), (1, 0, 768, "zyx"),
    (1, 768, 384, "zyx"), (1, 1152, 384, "xzy"), (1, 1536, 384, "zyx"), (1, 1920, 384, "xzy"), (1, 2304, 384, "zxy"),
    (1, 2688, 384, "zyx"), (2, 0, 256, "xzy"), (2, 256, 256, "zyx"), (2, 512, 128, "zxy"), (2, 640, 128, "yzx"),
)
GATHER_PLAN = (
    (20, 0, 1, 2, 3, 4, 5, 6, -1), (0, 3, 4, 7, 8, 20, 20, 1, 2, 5, 6, 1, 5, 0, 6, 3, 4, 0, 7, 20, 8, 2, 0, 9, 20, 3, 10),
    (3, 11, 4, 1, 7, 4, 12, 2, 11, 1, 13), (2, 5, 14), (5, 6, 7, 9, 13, 15, 10, 8, 6, 12, 16, 7, 17), (), (9,), (10,),
    (11, 12, 14), (8,), (13, 16), (8, 11, 15, 18), (), (11, 13, 19, 9), (15,), (13, 19, 10, 17), (9,), (10, 12), (),
    (12, 14, 17, 16), (), (15, 18), (14,), (15, 19), (14,), (), (17,), (), (16, 18), (17,), (19,), (16,), (18, 19), (),
    (18,), (), (),
)
SCATTER_ITEMS = (
    (2, 0, 256, "yzx"), (2, 256, 256, "xyz"), (2, 512, 256, "xyz"), (1, 0, 768, "yzx"), (1, 768, 768, "yxz"),
    (1, 1536, 384, "xzy"), (1, 1920, 384, "yxz"), (1, 2304, 384, "xzy"), (1, 2688, 384, "xyz"), (0, 0, 384, "yxz"),
    (0, 384, 384, "xzy"), (0, 768, 384, "xzy"), (0, 1152, 384, "xzy"), (0, 1536, 256, "yxz"), (0, 1792, 256, "yxz"),
    (0, 2048, 256, "xzy"), (0, 2304, 768, "xyz"),
)
SCATTER_PLAN = (
    (), (), (), (), (0,), (1,), (2,), (0, 3, 17), (1, 4), (2, 5, 6), (3, 17, 4, 7, 8), (5, 6), (7, 8), (0,), (), (1,),
    (16,), (3, 17, 16), (2,), (0, 4, 5), (), (6, 7), (1, 3, 17, 8, 9, 10), (5, 9), (2, 7, 10), (0, 5, 8, 16), (9, 1, 17, 7),
    (4, 6, -1), (2, 3, 16), (10,), (9, 11, 12), (8, 11), (4, 6, 12), (16, 11, 13, 14, 15), (18, 13), (12, 14, 15, 18, 10),
    (9,), (13, 15, 11, 14, 13, 12, 18, 10, 11, 14, 15, 12, 18, 13, 15, 14, 18),
)

def layer_norm_parts(rows):
    centre = rows - jnp.mean(rows, axis=-1, keepdims=True)
    spread = jnp.mean(centre * centre, axis=-1, keepdims=True)
    inverse = lax.rsqrt(spread + norm_eps)
    return centre * inverse, inverse


def head_lanes(rows, half):
    lane = lax.broadcasted_iota(jnp.int32, rows.shape, 1)
    return jnp.where((lane >= HD) == (half == 1), rows, jnp.zeros_like(rows))


def key_structure(local, y, length):
    lane = lax.broadcasted_iota(jnp.int32, (2 * local, 128), 1)
    row = lax.broadcasted_iota(jnp.int32, (2 * local, 128), 0)
    position = jnp.where(row < local, row + y * local, row - y * local)
    own = lane == lax.shift_right_logical(position, 6)
    beyond = (lane == NB) & (position >= length)
    return jnp.where(own | beyond | ((lane > NB) & (lane < NB + 4)), 1.0, 0.0).astype(bf16)


def head_rows(rows, half):
    row = lax.broadcasted_iota(jnp.int32, rows.shape, 0)
    return jnp.where((row >= HD) == (half == 1), rows, jnp.zeros_like(rows))


def in_three(values):
    high = values.astype(bf16)
    rest = values - high.astype(f32)
    middle = rest.astype(bf16)
    return high, middle, (rest - middle.astype(f32)).astype(bf16)


def with_rows(base, values):
    row = lax.broadcasted_iota(jnp.int32, base.shape, 0)
    for k, part in enumerate(in_three(-values)):
        base = base + jnp.where(row == NB + 1 + k, part.astype(f32), 0.0)
    return base.astype(bf16)


def spread_vectors(tiles, width, pieces):
    rows = tiles.shape[1]
    total = pieces * width
    lane = lax.broadcasted_iota(jnp.int32, (128, total), 1).astype(f32)
    row = lax.broadcasted_iota(jnp.int32, (128, total), 0).astype(f32)
    owner = jnp.floor((lane + 0.5) * (1.0 / width))
    chooser = jnp.where(lane - owner * width == row, 1.0, 0.0).astype(bf16)
    wide = dot_nn(tiles.reshape(pieces * rows, 128), chooser).reshape(pieces, rows, total)
    lane3 = lax.broadcasted_iota(jnp.int32, (pieces, rows, total), 2).astype(f32)
    piece3 = lax.broadcasted_iota(jnp.int32, (pieces, rows, total), 0).astype(f32)
    mine = jnp.floor((lane3 + 0.5) * (1.0 / width)) == piece3
    return jnp.sum(jnp.where(mine, wide, 0.0), axis=0)


def forward_kernel(
    nz, local, length_ref, masks_ref, x_hbm, wq, wk, wv, wo, wi, wu, small,
    out_hbm, r1_hbm, r2_hbm, gp_hbm, gt_hbm, n1t_hbm, at_hbm, atf_hbm, q_hbm, qt_hbm, k_hbm, kt_hbm, v_hbm, xt_hbm, lse_hbm,
    top_hbm, wa_hbm, wi_hbm, wu_hbm, vec_hbm,
    WA, WI, WU, SM, XF, XT, Q, QT, K, KT, V, VT, AT, ATF, R1, R2, N1L, N1T, U, GP, G, GT, E, VEC, IB, LSE, TOP, TT, OUT,
    send_sems, recv_sems, local_sems, out_sems,
):
    place = Place(nz)
    z, x, c, y = place.z, place.x, place.c, place.y
    remote = Remote(send_sems, recv_sems)
    mine = (z, x, c, y)
    locals_ = [(x_hbm, XF.at[0]), (small, SM.at[mine])]
    for g in range(3):
        for n, w in enumerate((wq, wk, wv)):
            lo = g * D + n * 256
            locals_.append((w.at[:, g * 256 : (g + 1) * 256], WA.at[(*mine, slice(None), slice(lo, lo + 256))]))
    locals_ += [(wo, WA.at[(*mine, slice(None), slice(3 * D, 4 * D))]), (wi, WI.at[mine]), (wu, WU.at[mine])]
    locals_ = [pltpu.make_async_copy(src, dst, local_sems.at[k]) for k, (src, dst) in enumerate(locals_)]
    for copy in locals_:
        copy.start()
    entry_barrier(place)
    for copy in locals_:
        copy.wait()

    outs = []

    def put(src, dst):
        copy = pltpu.make_async_copy(src, dst, out_sems.at[len(outs)])
        copy.start()
        outs.append(copy)

    swap = remote.make(XF.at[0], XF.at[1], place.at(y=1 - y))
    stripes = [
        GatherStripe(remote, place, (WA, WI, WU)[buf], slice(lo, lo + width), order) for buf, lo, width, order in GATHER_ITEMS
    ]
    stripes.append(GatherTile(remote, place, SM))
    script = Script(GATHER_PLAN, stripes, swap)
    script.point()
    length = length_ref[0]
    E[...] = key_structure(local, y, length)
    XT[:, :local] = XF[0].T
    script.point()

    tiles = SM[...].reshape(-1, 16, 128)
    pieces = tiles.shape[0]
    VEC[...] = spread_vectors(tiles, D // pieces, pieces)
    IB[...] = spread_vectors(tiles[:, 8:16, :], FF // pieces, pieces)
    put(VEC, vec_hbm)
    script.point()
    position = y * local + lax.broadcasted_iota(jnp.int32, (1, local), 1)
    live = position < length

    def wide(buf, lo, width):
        return buf[:, :, :, :, :, lo : lo + width].reshape(-1, width)

    for g in range(3):
        cols = slice(g * 256, (g + 1) * 256)
        own = dot_nn(XF[0], wide(WA, g * D, D))
        q = ((own[:, :256] + VEC[0:1, cols]).astype(bf16).astype(f32) * (HD**-0.5)).astype(bf16)
        Q[:, cols] = q
        QT[cols, :] = q.T
        K[:local, cols] = own[:, 256:512].astype(bf16)
        values = (own[:, 512:] + VEC[1:2, cols]).astype(bf16)
        V[:local, cols] = values
        VT[cols, :local] = values.T
        script.point()
    put(Q, q_hbm)
    put(QT, qt_hbm)
    swap.wait_recv()
    for g in range(3):
        cols = slice(g * 256, (g + 1) * 256)
        theirs = dot_nn(XF[1], wide(WA, g * D + 256, 512))
        K[local:, cols] = theirs[:, :256].astype(bf16)
        values = (theirs[:, 256:] + VEC[1:2, cols]).astype(bf16)
        V[local:, cols] = values
        VT[cols, local:] = values.T
        script.point()

        def head_step(h, carry):
            lanes = ds128(lax.div(h, 2), 128)
            half = lax.rem(h, 2)
            own = pl.ds(pl.multiple_of(h * HD, HD), HD)
            left = jnp.concatenate([K[:, lanes], E[...]], axis=1)
            right = jnp.concatenate(
                [head_rows(QT[lanes, :], half), masks_ref[h], jnp.zeros((128 - 32, local), bf16)], axis=0
            )
            for part in range(local // 256):
                cols = slice(part * 256, (part + 1) * 256)
                scores = dot_nn(left, right[:, cols])
                top = jnp.max(scores, axis=0, keepdims=True)
                exponent = jnp.exp(scores - top)
                total = jnp.sum(exponent, axis=0, keepdims=True)
                low = (exponent * (1.0 / total)).astype(bf16)
                mixture = dot_nn(VT[own, :], low)
                ATF[own, cols] = mixture
                AT[own, cols] = mixture.astype(bf16)
                LSE[h, :, cols] = top + jnp.log(total)
                TOP[h, :, cols] = jnp.where(live[:, cols], top, neg_large)
            script.points(h, 4 * g, 4)
            return carry

        lax.fori_loop(4 * g, 4 * g + 4, head_step, 0)
    put(WA, wa_hbm)
    put(K, k_hbm)
    put(V, v_hbm)
    put(LSE, lse_hbm)
    TT[...] = jnp.zeros((16, 128), f32) + neg_large
    TT[0:H, :] = jnp.broadcast_to(jnp.max(TOP[:, 0, :], axis=1, keepdims=True), (H, 128))
    put(TT, top_hbm)
    put(AT, at_hbm)
    put(ATF, atf_hbm)
    R1[...] = dot_nn(AT[...].T, wide(WA, 3 * D, D))
    script.point()

    def first_norm(k, carry):
        rows = ds128(k, 64)
        summed = XF[0, rows, :].astype(f32) + R1[rows, :] + VEC[2:3, :]
        R1[rows, :] = summed
        normal, _ = layer_norm_parts(summed)
        value = normal * VEC[3:4, :] + VEC[4:5, :]
        N1L[rows, :] = value.astype(bf16)
        R2[rows, :] = value + VEC[5:6, :]
        return carry

    lax.fori_loop(0, local // 64, first_norm, 0)
    put(R1, r1_hbm)
    script.point()
    N1T[...] = N1L[...].T
    put(N1T, n1t_hbm)
    XT[:, local:] = XF[1].T
    put(XT, xt_hbm)
    script.point()
    KT[...] = K[...].T
    put(KT, kt_hbm)
    script.point()
    for n in range(FF // D):
        cols = slice(n * D, (n + 1) * D)
        U[...] = dot_nn(N1L[...], wide(WI, n * D, D)) + IB[0:1, cols]
        script.point()

        def activate(k, carry):
            rows = ds128(k, 16)
            u = U[rows, :]
            below = 0.5 * (1.0 + lax.erf(u * np.float32(0.5**0.5)))
            G[rows, cols] = (u * below).astype(bf16)
            GP[n, rows, :] = below + u * jnp.exp(-0.5 * u * u) * np.float32((2.0 * np.pi) ** -0.5)
            return carry

        lax.fori_loop(0, local // 16, activate, 0)
        GT[cols, :] = G[:, cols].T
        script.point()
    put(WI, wi_hbm)
    put(GP, gp_hbm)
    put(GT, gt_hbm)
    for n in range(3):
        cols = slice(n * 256, (n + 1) * 256)
        R2[:, cols] += dot_nn(G[...], WU[:, :, :, :, :, cols].reshape(FF, 256))
        script.point()
    put(WU, wu_hbm)

    def second_norm(k, carry):
        rows = ds128(k, 64)
        normal, _ = layer_norm_parts(R2[rows, :])
        OUT[rows, :] = (normal * VEC[6:7, :] + VEC[7:8, :]).astype(bf16)
        return carry

    lax.fori_loop(0, local // 64, second_norm, 0)
    put(R2, r2_hbm)
    put(OUT, out_hbm)
    script.point()
    script.close()
    remote.finish()
    for copy in outs:
        copy.wait()


def copies_of(items, nz):
    return sum(3 + (nz - 1) for _ in items)


def run_forward(nz, x, weights, small, masks, length):
    local = x.shape[0]
    wq, wk, wv, wo, wi, wu = weights
    grid = (nz, 2, 2, 2)
    rows, rows_u = wq.shape[0], wu.shape[0]
    seq = 2 * local
    blocks = FF // D
    outs = [
        ((local, D), bf16), ((local, D), f32), ((local, D), f32), ((blocks, local, D), f32), ((FF, local), bf16),
        ((D, local), bf16), ((D, local), bf16), ((D, local), f32), ((local, D), bf16), ((D, local), bf16), ((seq, D), bf16),
        ((D, seq), bf16), ((seq, D), bf16), ((D, seq), bf16), ((H, 1, local), f32), ((16, 128), f32),
        ((*grid, rows, 4 * D), bf16), ((*grid, rows, FF), bf16), ((*grid, rows_u, D), bf16), ((16, D), f32),
    ]
    scratch = [
        ((*grid, rows, 4 * D), bf16), ((*grid, rows, FF), bf16), ((*grid, rows_u, D), bf16), ((*grid, 16, 128), bf16),
        ((2, local, D), bf16), ((D, seq), bf16), ((local, D), bf16), ((D, local), bf16), ((seq, D), bf16), ((D, seq), bf16),
        ((seq, D), bf16), ((D, seq), bf16), ((D, local), bf16), ((D, local), f32), ((local, D), f32), ((local, D), f32),
        ((local, D), bf16), ((D, local), bf16), ((local, D), f32), ((blocks, local, D), f32), ((local, FF), bf16),
        ((FF, local), bf16), ((seq, 128), bf16), ((16, D), f32), ((8, FF), f32), ((H, 1, local), f32), ((H, 1, local), f32),
        ((16, 128), f32), ((local, D), bf16),
    ]
    copies = copies_of(GATHER_ITEMS, nz) + 3 + (nz - 1) + 1
    return pl.pallas_call(
        functools.partial(forward_kernel, nz, local),
        out_shape=[jax.ShapeDtypeStruct(*o) for o in outs],
        in_specs=[INSMEM, INVMEM] + [ANY] * 8,
        out_specs=[ANY] * len(outs),
        scratch_shapes=[pltpu.VMEM(*s) for s in scratch]
        + [
            pltpu.SemaphoreType.DMA((copies,)),
            pltpu.SemaphoreType.DMA((copies,)),
            pltpu.SemaphoreType.DMA((14,)),
            pltpu.SemaphoreType.DMA((len(outs),)),
        ],
        compiler_params=pltpu.CompilerParams(collective_id=1, has_side_effects=True, vmem_limit_bytes=VMEM_BYTES),
        name="gather_forward",
    )(length, masks, x, wq, wk, wv, wo, wi, wu, small)


def compact_mask(random_here, length, first_block):
    blocks = random_here.shape[0]
    query = (first_block + jnp.arange(blocks, dtype=jnp.int32))[None, :, None]
    key = jnp.arange(NB, dtype=jnp.int32)[None, None, :]
    last = (length - 1) // BLK
    ok = (jnp.abs(query - key) <= 1) | (key == 0) | (key == last) | (query == 0) | (query == last)
    heads = jnp.transpose(random_here, (1, 0, 2))
    for k in range(heads.shape[2]):
        ok = ok | (heads[:, :, k : k + 1] == key)
    return jnp.where(ok, 0.0, neg_large).astype(f32)


def mask_rows(random_here, length, first_block):
    compact = jnp.transpose(compact_mask(random_here, length, first_block), (0, 2, 1))
    rows = jnp.repeat(compact, BLK, axis=2)
    heads, _, queries = rows.shape
    return jnp.concatenate(
        [rows, jnp.full((heads, 1, queries), neg_large, f32), jnp.zeros((heads, 15, queries), f32)], axis=1
    ).astype(bf16)


def pack_small(vectors, wide):
    rows = [jnp.pad(v, (0, 128 - v.shape[0])) for v in vectors] + [jnp.pad(wide, (0, 128 - wide.shape[0]))]
    rows += [jnp.zeros((128,), bf16)] * (16 - len(rows))
    return jnp.stack(rows)


def gather_vectors(rows, width, pieces):
    n, total = rows.shape
    lane3 = lax.broadcasted_iota(jnp.int32, (pieces, n, total), 2).astype(f32)
    piece3 = lax.broadcasted_iota(jnp.int32, (pieces, n, total), 0).astype(f32)
    mine = jnp.floor((lane3 + 0.5) * (1.0 / width)) == piece3
    spread = jnp.where(mine, rows[None], 0.0).reshape(pieces * n, total)
    lane = lax.broadcasted_iota(jnp.int32, (128, total), 1).astype(f32)
    row = lax.broadcasted_iota(jnp.int32, (128, total), 0).astype(f32)
    owner = jnp.floor((lane + 0.5) * (1.0 / width))
    chooser = jnp.where(lane - owner * width == row, 1.0, 0.0).astype(bf16)
    high, middle, lowest = in_three(spread)
    tiles = dot_nt(high, chooser) + (dot_nt(middle, chooser) + dot_nt(lowest, chooser))
    return tiles.reshape(pieces, n, 128)


def norm_back(normal, inverse, grads, gain):
    scaled = grads * gain
    first = jnp.mean(scaled, axis=-1, keepdims=True)
    second = jnp.mean(scaled * normal, axis=-1, keepdims=True)
    return inverse * (scaled - first - normal * second)


def row_sum(values):
    return jnp.sum(values, axis=0, keepdims=True)


def back_half(pair, local, own_keys, BQ, BD, Q, QT, DA, DAT, K, KT, V, E, PB, DS, DQF, DQT, DK, DV):
    keys = slice(0, local) if own_keys else slice(local, 2 * local)
    lanes = ds128(pair, 128)
    structure = E[keys, :]
    left = jnp.concatenate([K[keys, lanes], structure], axis=1)
    left_values = jnp.concatenate([V[keys, lanes], structure], axis=1)
    empty = jnp.zeros((128 - 32, local), bf16)
    for half in (0, 1):
        h = pair * 2 + half
        own = pl.ds(pl.multiple_of(h * HD, HD), HD)
        spot = slice(half * local, (half + 1) * local)
        right = jnp.concatenate([head_rows(QT[lanes, :], half), BQ[h], empty], axis=0)
        prob = jnp.exp(dot_nn(left, right))
        PB[:, spot] = prob.astype(bf16)
        right_values = jnp.concatenate([head_rows(DAT[lanes, :], half), BD[h], empty], axis=0)
        low = (prob * dot_nn(left_values, right_values)).astype(bf16)
        DS[:, spot] = low
        part = dot_nn(KT[own, keys], low)
        if own_keys:
            DQT[own, :] = ((DQF[own, :] + part) * (HD**-0.5)).astype(bf16)
        else:
            DQF[own, :] = part
    q_pair, a_pair = Q[:, lanes], DA[:, lanes]
    DK[keys, lanes] = dot_nn(DS[...], jnp.concatenate([head_lanes(q_pair, n) for n in (0, 1)], axis=0)).astype(bf16)
    DV[keys, lanes] = dot_nn(PB[...], jnp.concatenate([head_lanes(a_pair, n) for n in (0, 1)], axis=0)).astype(bf16)


def backward_kernel(
    nz, local, length_ref, masks_ref, VEC, cot_hbm, r1_hbm, r2_hbm, gp_hbm, gt_hbm, n1t_hbm, at_hbm, atf_hbm, q_hbm, qt_hbm,
    k_hbm, kt_hbm, v_hbm, xt_hbm, lse_hbm, top_hbm, wa_hbm, wi_hbm, wu_hbm,
    dx_hbm, OA, OI, OU, OS, OT, *rest,
):
    place = Place(nz)
    z, x, c, y = place.z, place.x, place.c, place.y
    GA, GI, GU, WA, T, TOP, TOPS, DP, AT, DR1, E, SUMS, ISUM, SEND, RECV = rest[:15]
    used = 15
    bufs = []
    for _ in SCATTER_ITEMS:
        bufs.append(rest[used : used + 4])
        used += 4
    sbufs = rest[used : used + 4]
    send_sems, recv_sems, load_sems = rest[used + 4 :]
    blocks = FF // D
    pieces = nz * 8
    seq_len = 2 * local
    length = length_ref[0]
    loads = [0]

    def load(src, dst):
        copy = pltpu.make_async_copy(src, dst, load_sems.at[loads[0]])
        loads[0] += 1
        copy.start()
        return copy

    remote = Remote(send_sems, recv_sems)
    stripes = [
        ScatterStripe(remote, place, (GA, GI, GU)[buf], slice(lo, lo + width), order, bufs[n], (OA, OI, OU)[buf])
        for n, (buf, lo, width, order) in enumerate(SCATTER_ITEMS)
    ]
    stripes += [TopOfAll(remote, place, TOP, TOPS), SmallSums(remote, place, T, sbufs)]
    swap = remote.make(SEND, RECV, place.at(y=1 - y))
    script = Script(SCATTER_PLAN, stripes, swap)
    grid = (nz, 2, 2, 2)
    SUMS[...] = jnp.zeros_like(SUMS)
    ISUM[...] = jnp.zeros_like(ISUM)

    def first_stage(COT, R2, R1, DM, GT, DU, GP, N1T, WUS, WIS):
        l_r2, l_cot = load(r2_hbm, R2), load(cot_hbm, COT)
        l_wu = [load(wu_hbm.at[0], WUS.at[0]), load(wu_hbm.at[1], WUS.at[1])]
        l_gp = [load(gp_hbm.at[0], GP.at[0]), load(gp_hbm.at[1], GP.at[1])]
        l_gt = load(gt_hbm, GT)
        l_n1t, l_r1 = load(n1t_hbm, N1T), load(r1_hbm, R1)

        def wi_of(n):
            return wi_hbm.at[:, :, :, :, :, n * D : (n + 1) * D]

        l_wi = [load(wi_of(0), WIS.at[0]), load(wi_of(1), WIS.at[1])]
        l_top, l_at, l_wa = load(top_hbm, TOP.at[0]), load(at_hbm, AT), load(wa_hbm, WA)
        script.point()
        entry_barrier(place)
        E[...] = key_structure(local, y, length)
        l_r2.wait()
        l_cot.wait()
        script.point()

        def second_norm(k, carry):
            rows = ds128(k, 64)
            normal, inverse = layer_norm_parts(R2[rows, :])
            position = y * local + k * 64 + lax.broadcasted_iota(jnp.int32, (64, D), 0)
            grads = jnp.where(position < length, COT[rows, :].astype(f32), 0.0)
            through = norm_back(normal, inverse, grads, VEC[6:7, :])
            R2[rows, :] = through
            low = through.astype(bf16)
            DM[rows, :] = low
            SUMS[5:6, :] += row_sum(low.astype(f32))
            SUMS[6:7, :] += row_sum(grads * normal)
            SUMS[7:8, :] += row_sum(grads)
            return carry

        lax.fori_loop(0, local // 64, second_norm, 0)
        script.point()
        for n in range(blocks):
            l_wu[n].wait()
            l_gp[n].wait()
            grads = dot_nt(DM[...], WUS[n % 2].reshape(D, D)) * GP[n % 2]
            low = grads.astype(bf16)
            DU[n] = low
            ISUM[0:1, n * D : (n + 1) * D] = row_sum(low.astype(f32))
            if n + 2 < blocks:
                l_wu.append(load(wu_hbm.at[n + 2], WUS.at[n % 2]))
                l_gp.append(load(gp_hbm.at[n + 2], GP.at[n % 2]))
        l_gt.wait()
        script.point()
        for n in range(3):
            cols = slice(n * 256, (n + 1) * 256)

            def outer_grad(zz, carry):
                rows = ds128(zz, FF // nz)
                made = dot_nn(GT[rows, :], DM[:, cols]).astype(bf16)
                GU[zz, :, :, :, :, cols] = made.reshape(2, 2, 2, -1, 256)
                return carry

            lax.fori_loop(0, nz, outer_grad, 0)
            script.point()
        l_top.wait()
        l_n1t.wait()
        for n in range(blocks):
            made = dot_nn(N1T[...], DU[n]).astype(bf16)
            GI[:, :, :, :, :, n * D : (n + 1) * D] = made.reshape(*grid, -1, D)
            script.point()
        for n in range(blocks):
            l_wi[n].wait()
            R2[...] += dot_nt(DU[n], WIS[n % 2].reshape(D, D))
            if n + 2 < blocks:
                l_wi.append(load(wi_of(n + 2), WIS.at[n % 2]))
            script.point()
        l_r1.wait()

        def first_norm(k, carry):
            rows = ds128(k, 64)
            normal, inverse = layer_norm_parts(R1[rows, :])
            grads = R2[rows, :]
            through = norm_back(normal, inverse, grads, VEC[3:4, :])
            DR1[rows, :] = through
            low = through.astype(bf16)
            DP[rows, :] = low
            SUMS[2:3, :] += row_sum(low.astype(f32))
            SUMS[3:4, :] += row_sum(grads * normal)
            SUMS[4:5, :] += row_sum(grads)
            return carry

        lax.fori_loop(0, local // 64, first_norm, 0)
        script.point()
        l_at.wait()
        l_wa.wait()

    pl.run_scoped(
        first_stage,
        pltpu.VMEM((local, D), bf16), pltpu.VMEM((local, D), f32), pltpu.VMEM((local, D), f32), pltpu.VMEM((local, D), bf16),
        pltpu.VMEM((FF, local), bf16), pltpu.VMEM((blocks, local, D), bf16), pltpu.VMEM((2, local, D), f32),
        pltpu.VMEM((D, local), bf16), pltpu.VMEM((2, 2, 2, 2, FF // (nz * 8), D), bf16),
        pltpu.VMEM((2, *grid, D // (nz * 8), D), bf16),
    )

    def second_stage(Q, QT, K, KT, V, XT, LSE, BQ, BD, DA, DAT, PB, DS, DQF, DQT, DQ, DK, DV):
        pairs = ((lse_hbm, LSE), (atf_hbm, DQF), (k_hbm, K), (q_hbm, Q), (qt_hbm, QT), (kt_hbm, KT), (v_hbm, V), (xt_hbm, XT))
        waits = [load(s, d) for s, d in pairs]
        made = dot_nn(AT[...], DP[...]).astype(bf16)
        GA[:, :, :, :, :, 3 * D : 4 * D] = made.reshape(*grid, -1, D)
        script.point()
        DAT[...] = dot_nt(WA[:, :, :, :, :, 3 * D : 4 * D].reshape(D, D), DP[...]).astype(bf16)
        DA[...] = DAT[...].T
        waits[0].wait()
        waits[1].wait()

        def prepare(h, carry):
            own = pl.ds(pl.multiple_of(h * HD, HD), HD)
            delta = row_sum(DAT[own, :].astype(f32) * DQF[own, :])
            BD[h] = with_rows(jnp.zeros((32, local), f32), delta)
            BQ[h] = with_rows(masks_ref[h].astype(f32), LSE[h])
            return carry

        lax.fori_loop(0, H, prepare, 0)
        for wait in waits[2:]:
            wait.wait()
        script.point()

        def halves(own_keys, g):
            def pair_step(pair, carry):
                back_half(pair, local, own_keys, BQ, BD, Q, QT, DA, DAT, K, KT, V, E, PB, DS, DQF, DQT, DK, DV)
                script.points(pair, 2 * g, 2)
                return carry

            lax.fori_loop(2 * g, 2 * g + 2, pair_step, 0)

        def group(g):
            lo = g * D
            cols = slice(g * 256, (g + 1) * 256)
            dq = DQT[cols, :].T
            DQ[:, cols] = dq
            SUMS[0:1, cols] = row_sum(dq.astype(f32))
            SUMS[1:2, cols] = row_sum(DV[:, cols].astype(f32))
            for n, made in enumerate(
                (dot_nn(XT[:, :local], dq), dot_nn(XT[...], DK[:, cols]), dot_nn(XT[...], DV[:, cols]))
            ):
                GA[:, :, :, :, :, lo + n * 256 : lo + (n + 1) * 256] = made.astype(bf16).reshape(*grid, -1, 256)
            script.point()

        halves(False, 0)
        halves(True, 0)
        group(0)
        halves(False, 1)
        halves(False, 2)
        groups = [slice(g * 256, (g + 1) * 256) for g in range(3)]
        theirs = jnp.concatenate([a[local:, cols] for cols in groups for a in (DK, DV)], axis=1)
        through = [WA[:, :, :, :, :, g * D + 256 : (g + 1) * D].reshape(D, 512) for g in range(3)]
        SEND[...] = dot_nt(theirs, jnp.concatenate(through, axis=1)).astype(bf16)
        script.point()
        halves(True, 1)
        group(1)
        halves(True, 2)
        group(2)
        T[:, :, :, :, 0:8, :] = gather_vectors(SUMS[0:8, :], D // pieces, pieces).reshape(*grid, 8, 128)
        wide = gather_vectors(ISUM[...], FF // pieces, pieces)
        T[:, :, :, :, 8:16, :] = wide.reshape(*grid, 8, 128)
        script.point()
        for g in range(3):
            cols = slice(g * 256, (g + 1) * 256)
            ours = jnp.concatenate([DQ[:, cols], DK[:local, cols], DV[:local, cols]], axis=1)
            DR1[...] += dot_nt(ours, WA[:, :, :, :, :, g * D : (g + 1) * D].reshape(D, D))
            script.point()
        script.close()
        swap.wait_recv()

        def last(k, carry):
            rows = ds128(k, 64)
            DR1[rows, :] = DR1[rows, :] + RECV[rows, :].astype(f32)
            return carry

        lax.fori_loop(0, local // 64, last, 0)
        out = pltpu.make_async_copy(DR1, dx_hbm, load_sems.at[loads[0]])
        out.start()
        OS[...] = T[z, x, c, y]
        OT[...] = TOP[4]
        out.wait()

    scoped = [
        ((local, D), bf16), ((D, local), bf16), ((seq_len, D), bf16), ((D, seq_len), bf16), ((seq_len, D), bf16),
        ((D, seq_len), bf16), ((H, 1, local), f32), ((H, 32, local), bf16), ((H, 32, local), bf16), ((local, D), bf16),
        ((D, local), bf16), ((local, 2 * local), bf16), ((local, 2 * local), bf16), ((D, local), f32), ((D, local), bf16),
        ((local, D), bf16), ((seq_len, D), bf16), ((seq_len, D), bf16),
    ]
    pl.run_scoped(second_stage, *(pltpu.VMEM(*s) for s in scoped))
    remote.finish()


def run_backward(nz, local, rows, rows_u, length, masks, vec, *arrays):
    grid = (nz, 2, 2, 2)
    seq = 2 * local
    outs = [((local, D), f32), ((rows, 4 * D), f32), ((rows, FF), f32), ((rows_u, D), f32), ((16, 128), f32), ((16, 128), f32)]
    scratch = [
        ((*grid, rows, 4 * D), bf16), ((*grid, rows, FF), bf16), ((*grid, rows_u, D), bf16), ((*grid, rows, 4 * D), bf16),
        ((*grid, 16, 128), f32), ((5, 16, 128), f32), ((3 + nz - 1, 16, 128), f32),
        ((local, D), bf16), ((D, local), bf16), ((local, D), f32), ((seq, 128), bf16),
        ((8, D), f32), ((8, FF), f32), ((local, D), bf16), ((local, D), bf16),
    ]
    for buf, _, width, order in SCATTER_ITEMS:
        scratch += scatter_buffers(nz, rows_u if buf == 2 else rows, width, order)
    scratch += small_buffers(nz)
    copies = copies_of(SCATTER_ITEMS, nz) + 2 * (3 + nz - 1) + 1
    return pl.pallas_call(
        functools.partial(backward_kernel, nz, local),
        out_shape=[jax.ShapeDtypeStruct(*o) for o in outs],
        in_specs=[INSMEM, INVMEM, INVMEM] + [ANY] * len(arrays),
        out_specs=[ANY] + [INVMEM] * 5,
        scratch_shapes=[pltpu.VMEM(*s) for s in scratch]
        + [pltpu.SemaphoreType.DMA((copies,)), pltpu.SemaphoreType.DMA((copies,)), pltpu.SemaphoreType.DMA((32,))],
        compiler_params=pltpu.CompilerParams(collective_id=2, has_side_effects=True, vmem_limit_bytes=VMEM_BYTES),
        name="backward_scatter",
    )(length, masks, vec, *arrays)


def layer_norm(row_values, gain_vector, shift_vector):
    centre = row_values - jnp.mean(row_values, axis=-1, keepdims=True)
    spread = jnp.mean(centre * centre, axis=-1, keepdims=True)
    return centre * lax.rsqrt(spread + norm_eps) * gain_vector + shift_vector


def gelu_exact(values):
    return jax.nn.gelu(values, approximate=False)


def column_sums(values):
    return jnp.sum(values.astype(f32), axis=0)


def clip_outputs(logit_maxima, threshold, query_weight, query_bias, key_weight, device_rank):
    clip_limit = threshold.astype(f32)[0] * 0.01
    factors = jnp.sqrt(clip_limit / jnp.maximum(logit_maxima, clip_limit))
    column_scale = jnp.repeat(factors, HD)
    query_clipped = (query_weight.astype(f32) * column_scale[None, :]).astype(bf16)
    key_clipped = (key_weight.astype(f32) * column_scale[None, :]).astype(bf16)
    bias_count = query_bias.shape[0]
    bias_heads = (device_rank * bias_count + jnp.arange(bias_count)) // HD
    bias_scale = jnp.sum(jnp.where(bias_heads[:, None] == jnp.arange(H)[None, :], factors[None, :], 0.0), axis=1)
    return query_clipped, (query_bias.astype(f32) * bias_scale).astype(bf16), key_clipped


def fast_shards(
    nz,
    inputs, cotangent, query_weight, query_bias, key_weight, value_weight, value_bias, output_weight, output_bias,
    first_gain, first_shift, inner_weight, inner_bias, outer_weight, outer_bias, second_gain, second_shift,
    lengths, random_blocks, threshold,
):
    local = inputs.shape[1]
    pieces = nz * 8
    rows, rows_u = query_weight.shape[0], outer_weight.shape[0]
    y = lax.axis_index("ctx")
    blocks = local // BLK
    first_block = y * blocks
    random_here = lax.dynamic_slice_in_dim(random_blocks[0], first_block, blocks, 0)
    masks = mask_rows(random_here, lengths[0], first_block)
    small = pack_small(
        [query_bias, value_bias, output_bias, first_gain, first_shift, outer_bias, second_gain, second_shift], inner_bias
    )
    x = inputs[0]
    weights = (query_weight, key_weight, value_weight, output_weight, inner_weight, outer_weight)
    output, *saved, vectors = run_forward(nz, x, weights, small, masks, lengths)
    input_grad, ga, gi, gu, gs, top = run_backward(nz, local, rows, rows_u, lengths, masks, vectors, cotangent[0], *saved)
    logit_maxima = top[:H, 0]
    rank = lax.axis_index("dp") * 2 + y
    query_clipped, bias_clipped, key_clipped = clip_outputs(
        logit_maxima, threshold, query_weight, query_bias, key_weight, rank
    )
    vec = [gs[n, :rows] for n in range(8)]
    qkv = [jnp.concatenate([ga[:, g * D + n * 256 : g * D + (n + 1) * 256] for g in range(3)], axis=1) for n in range(3)]
    return (
        output[None], input_grad[None],
        qkv[0], vec[0], qkv[1], qkv[2], vec[1], ga[:, 3 * D :], vec[2], vec[3], vec[4],
        gi, gs[8, : FF // pieces], gu, vec[5], vec[6], vec[7],
        query_clipped, bias_clipped, key_clipped, logit_maxima,
    )


def general_shards(
    inputs, cotangent, query_weight, query_bias, key_weight, value_weight, value_bias, output_weight, output_bias,
    first_gain, first_shift, inner_weight, inner_bias, outer_weight, outer_bias, second_gain, second_shift,
    lengths, random_blocks, threshold,
):
    both = ("dp", "ctx")
    shards = (
        query_weight, query_bias, key_weight, value_weight, value_bias, output_weight, output_bias, first_gain, first_shift,
        inner_weight, inner_bias, outer_weight, outer_bias, second_gain, second_shift,
    )
    wq, bq, wk, wv, bv, wo, bo, g1, s1, wi, bi, wu, bu, g2, s2 = (lax.all_gather(w, both, axis=0, tiled=True) for w in shards)
    bq, bv, bo, g1, s1, bi, bu, g2, s2 = (v.astype(f32) for v in (bq, bv, bo, g1, s1, bi, bu, g2, s2))
    seqs, local, _ = inputs.shape
    blocks = local // BLK
    y = lax.axis_index("ctx")
    first_block = y * blocks
    scale = HD**-0.5
    outs = []
    sums = None
    top = jnp.full((H,), neg_large, f32)
    for s in range(seqs):
        x, length = inputs[s], lengths[s]
        random_here = lax.dynamic_slice_in_dim(random_blocks[s], first_block, blocks, 0)
        mask = compact_mask(random_here, length, first_block)
        mask = jnp.repeat(jnp.repeat(mask, BLK, axis=1), BLK, axis=2)
        seen = jnp.arange(NB * BLK) < length
        mask = jnp.where(seen[None, None, :], mask, neg_large)
        live = (y * local + jnp.arange(local)) < length
        q = (dot_nn(x, wq) + bq).astype(bf16)
        k = lax.all_gather(dot_nn(x, wk).astype(bf16), "ctx", axis=0, tiled=True)
        v = lax.all_gather((dot_nn(x, wv) + bv).astype(bf16), "ctx", axis=0, tiled=True)
        qh, kh, vh = (a.reshape(-1, H, HD) for a in (q, k, v))
        raw = jnp.einsum("qhd,khd->hqk", qh, kh, preferred_element_type=f32) * scale + mask
        row_top = jnp.max(raw, axis=-1, keepdims=True)
        top = jnp.maximum(top, jnp.max(jnp.where(live[None, :, None], row_top, neg_large), axis=(1, 2)))
        exponent = jnp.exp(raw - row_top)
        prob = exponent / jnp.sum(exponent, axis=-1, keepdims=True)
        low = prob.astype(bf16)
        attended = jnp.einsum("hqk,khd->qhd", low, vh, preferred_element_type=f32).reshape(local, D).astype(bf16)
        first_sum = x.astype(f32) + dot_nn(attended, wo) + bo
        normed = layer_norm(first_sum, g1, s1)
        normed_low = normed.astype(bf16)
        pre_act = dot_nn(normed_low, wi) + bi
        activated = gelu_exact(pre_act).astype(bf16)
        second_sum = normed + dot_nn(activated, wu) + bu
        output = layer_norm(second_sum, g2, s2).astype(bf16)
        cot = jnp.where(live[:, None], cotangent[s].astype(f32), 0.0)
        grad_second, g2_grad, s2_grad = jax.vjp(layer_norm, second_sum, g2, s2)[1](cot)
        dm = grad_second.astype(bf16)
        du = jax.vjp(gelu_exact, pre_act)[1](dot_nt(dm, wu))[0].astype(bf16)
        grad_normed = grad_second + dot_nt(du, wi)
        grad_first, g1_grad, s1_grad = jax.vjp(layer_norm, first_sum, g1, s1)[1](grad_normed)
        dp = grad_first.astype(bf16)
        da = dot_nt(dp, wo).astype(bf16).reshape(local, H, HD)
        dprob = jnp.einsum("qhd,khd->hqk", da, vh, preferred_element_type=f32)
        ds = (prob * (dprob - jnp.sum(prob * dprob, axis=-1, keepdims=True))).astype(bf16)
        dq = (jnp.einsum("hqk,khd->qhd", ds, kh, preferred_element_type=f32) * scale).reshape(local, D).astype(bf16)
        dk = (jnp.einsum("hqk,qhd->khd", ds, qh, preferred_element_type=f32) * scale).reshape(-1, D)
        dv = jnp.einsum("hqk,qhd->khd", low, da, preferred_element_type=f32).reshape(-1, D)
        dk, dv = (lax.psum_scatter(a.astype(bf16), "ctx", scatter_dimension=0, tiled=True).astype(bf16) for a in (dk, dv))
        input_grad = grad_first + dot_nt(dq, wq) + dot_nt(dk, wk) + dot_nt(dv, wv)
        outs.append((output, input_grad))
        here = (
            dot_tn(x, dq), column_sums(dq), dot_tn(x, dk), dot_tn(x, dv), column_sums(dv), dot_tn(attended, dp),
            column_sums(dp), g1_grad, s1_grad, dot_tn(normed_low, du), column_sums(du), dot_tn(activated, dm),
            column_sums(dm), g2_grad, s2_grad,
        )
        sums = here if sums is None else tuple(a + b for a, b in zip(sums, here))
    grads = tuple(lax.psum_scatter(g, both, scatter_dimension=0, tiled=True) for g in sums)
    logit_maxima = lax.pmax(top, both)
    rank = lax.axis_index(both)
    clipped = clip_outputs(logit_maxima, threshold, query_weight, query_bias, key_weight, rank)
    return (jnp.stack([o for o, _ in outs]), jnp.stack([g for _, g in outs]), *grads, *clipped, logit_maxima)


def solution(mesh):
    both = P(("dp", "ctx"))
    rows = P(("dp", "ctx"), None)
    tokens = P("dp", "ctx", None)
    in_specs = (
        tokens, tokens, rows, both, rows, rows, both, rows, both, both, both, rows, both, rows, both, both, both,
        P("dp"), P("dp", None, None, None), P(),
    )
    out_specs = (
        tokens, tokens, rows, both, rows, rows, both, rows, both, both, both, rows, both, rows, both, both, both,
        rows, both, rows, P(),
    )
    dp, ctx = mesh.shape["dp"], mesh.shape["ctx"]
    pieces = dp * ctx
    fits = ctx == 2 and dp % 4 == 0 and D % (8 * pieces) == 0 and FF // pieces <= 128

    def step(*args):
        if fits and args[0].shape[0] == 1:
            return fast_shards(dp // 4, *args)
        return general_shards(*args)

    return jax.shard_map(step, mesh=mesh, in_specs=in_specs, out_specs=out_specs, check_vma=False)
```

```python
import functools

import jax
import jax.numpy as jnp
import numpy as np
from jax import lax
from jax.experimental import pallas as pl
from jax.experimental.pallas import tpu as pltpu
from jax.sharding import PartitionSpec as P

H = 12
HD = 64
BLK = 64
LEN = 1024
NB = 16
D = 768
FF = 3072

norm_eps = 1e-12
neg_large = -1e30
bf16 = jnp.bfloat16
f32 = jnp.float32
ANY = pl.BlockSpec(memory_space=pl.ANY)
INVMEM = pl.BlockSpec(memory_space=pltpu.VMEM)
INSMEM = pl.BlockSpec(memory_space=pltpu.SMEM)
MESH = pl.DeviceIdType.MESH


def dot_nn(a, b):
    return jnp.dot(a, b, preferred_element_type=f32)


def dot_nt(a, b):
    return lax.dot_general(a, b, (((1,), (1,)), ((), ())), preferred_element_type=f32)


def dot_tn(a, b):
    return lax.dot_general(a, b, (((0,), (0,)), ((), ())), preferred_element_type=f32)


def ds128(index, width):
    return pl.ds(pl.multiple_of(index * width, width), width)


class Place:
    def __init__(self, nz):
        self.nz = nz
        dp = lax.axis_index("dp")
        self.y = lax.axis_index("ctx")
        self.c = lax.rem(dp, 2)
        self.x = lax.rem(lax.div(dp, 2), 2)
        self.z = lax.div(dp, 4)

    def at(self, z=None, x=None, c=None, y=None):
        z = self.z if z is None else z
        x = self.x if x is None else x
        c = self.c if c is None else c
        y = self.y if y is None else y
        return ((z * 2 + x) * 2 + c, y)

    def z_off(self, k):
        return lax.rem(self.z + k, self.nz)

    def along(self, axis):
        if axis == "z":
            return [self.at(z=self.z_off(k)) for k in range(1, self.nz)]
        return [self.at(x=1 - self.x) if axis == "x" else self.at(y=1 - self.y)]

    def peers(self):
        return (
            [self.at(z=self.z_off(k)) for k in range(1, self.nz)]
            + [self.at(x=1 - self.x), self.at(y=1 - self.y), self.at(c=1 - self.c)]
        )


def entry_barrier(place):
    barrier = pltpu.get_barrier_semaphore()
    peers = place.peers()
    for peer in peers:
        pl.semaphore_signal(barrier, inc=1, device_id=peer, device_id_type=MESH)
    pl.semaphore_wait(barrier, len(peers))


class Remote:
    def __init__(self, send_sems, recv_sems):
        self.send_sems, self.recv_sems, self.used, self.copies = send_sems, recv_sems, 0, []

    def make(self, src, dst, peer):
        k = self.used
        self.used += 1
        copy = pltpu.make_async_remote_copy(
            src_ref=src, dst_ref=dst, send_sem=self.send_sems.at[k], recv_sem=self.recv_sems.at[k],
            device_id=peer, device_id_type=MESH,
        )
        self.copies.append(copy)
        return copy

    def finish(self):
        for copy in self.copies:
            copy.wait_send()


class Stripe:
    def __init__(self):
        self.stages, self.at = [], 0

    def take(self, n):
        pass

    def step(self):
        n = self.at
        if n > 0:
            for copy in self.stages[n - 1]:
                copy.wait_recv()
            self.take(n - 1)
        if n < len(self.stages):
            for copy in self.stages[n]:
                copy.start()
        self.at = n + 1


class GatherStripe(Stripe):
    def __init__(self, remote, place, buf, cols, order):
        super().__init__()
        have = {"z": place.z, "x": place.x, "y": place.y}
        for axis in order:
            ref = buf.at[have["z"], have["x"], place.c, have["y"], :, cols]
            self.stages.append([remote.make(ref, ref, peer) for peer in place.along(axis)])
            have[axis] = slice(None)
        ref = buf.at[:, :, place.c, :, :, cols]
        self.stages.append([remote.make(ref, ref, place.at(c=1 - place.c))])


class GatherTile(Stripe):
    def __init__(self, remote, place, buf):
        super().__init__()
        z, x, c, y = place.z, place.x, place.c, place.y
        for ref, peers in (
            (buf.at[z, x, c, y], place.along("z")),
            (buf.at[:, x, c, y], place.along("x")),
            (buf.at[:, :, c, y], place.along("y")),
            (buf.at[:, :, c], [place.at(c=1 - c)]),
        ):
            self.stages.append([remote.make(ref, ref, peer) for peer in peers])


class ScatterStripe(Stripe):
    def __init__(self, remote, place, g, cols, order, bufs, out):
        super().__init__()
        self.place, self.g, self.cols, self.order, self.bufs, self.out = place, g, cols, order, bufs, out
        own = {"z": place.z, "x": place.x, "y": place.y}
        have = {"z": slice(None), "x": slice(None), "y": slice(None)}
        ref = g.at[:, :, 1 - place.c, :, :, cols]
        self.stages.append([remote.make(ref, bufs[0], place.at(c=1 - place.c))])
        for n, axis in enumerate(order):
            made = []
            for k, peer in enumerate(place.along(axis)):
                there = dict(have)
                there[axis] = place.z_off(k + 1) if axis == "z" else 1 - own[axis]
                ref = g.at[there["z"], there["x"], place.c, there["y"], :, cols]
                made.append(remote.make(ref, bufs[n + 1].at[k] if axis == "z" else bufs[n + 1], peer))
            self.stages.append(made)
            have[axis] = own[axis]

    def take(self, n):
        place, g, cols, buf = self.place, self.g, self.cols, self.bufs[n]
        axis = self.order[n - 1] if n > 0 else "c"
        still = self.order[n:]
        sizes = {"z": place.nz, "x": 2, "y": 2}
        names = [name for name in "zxy" if name in still]
        count = 1
        for name in names:
            count *= sizes[name]

        def add(k, last):
            here = {"z": place.z, "x": place.x, "y": place.y}
            left = k
            for name in reversed(names):
                here[name] = lax.rem(left, sizes[name])
                left = lax.div(left, sizes[name])
            index = tuple(here[name] for name in names)
            spot = (here["z"], here["x"], place.c, here["y"], slice(None), cols)
            if axis != "z" and not last:
                g[spot] = g[spot] + buf[index]
                return
            total = g[spot].astype(f32)
            for part in range(place.nz - 1) if axis == "z" else (None,):
                total = total + buf[index if part is None else (part, *index)].astype(f32)
            if last:
                self.out[:, cols] = total
            else:
                g[spot] = total.astype(bf16)

        if not names:
            add(0, True)
        elif count <= 2:
            for k in range(count):
                add(k, False)
        else:

            def twice(k, carry):
                add(2 * k, False)
                add(2 * k + 1, False)
                return carry

            lax.fori_loop(0, count // 2, twice, 0)


def scatter_buffers(nz, rows, width, order):
    sizes = {"z": nz, "x": 2, "y": 2}
    made = [((nz, 2, 2, rows, width), bf16)]
    for n, axis in enumerate(order):
        left = [sizes[name] for name in "zxy" if name in order[n + 1 :]]
        made.append((((nz - 1,) if axis == "z" else ()) + (*left, rows, width), bf16))
    return made


class SmallSums(Stripe):
    def __init__(self, remote, place, t, bufs):
        super().__init__()
        z, x, c, y = place.z, place.x, place.c, place.y
        rc, ry, rx, rz = bufs
        self.place, self.t, self.bufs = place, t, bufs
        self.stages = [
            [remote.make(t.at[:, :, 1 - c], rc, place.at(c=1 - c))],
            [remote.make(t.at[:, :, c, 1 - y], ry, place.at(y=1 - y))],
            [remote.make(t.at[:, 1 - x, c, y], rx, place.at(x=1 - x))],
            [remote.make(t.at[place.z_off(k + 1), x, c, y], rz.at[k], peer) for k, peer in enumerate(place.along("z"))],
        ]

    def take(self, n):
        place, t = self.place, self.t
        rc, ry, rx, rz = self.bufs
        z, x, c, y = place.z, place.x, place.c, place.y
        if n == 0:
            t[:, :, c] = t[:, :, c] + rc[...]
        elif n == 1:
            t[:, :, c, y] = t[:, :, c, y] + ry[...]
        elif n == 2:
            t[:, x, c, y] = t[:, x, c, y] + rx[...]
        else:
            total = t[z, x, c, y]
            for k in range(place.nz - 1):
                total = total + rz[k]
            t[z, x, c, y] = total


def small_buffers(nz):
    return [((nz, 2, 2, 16, 128), f32), ((nz, 2, 16, 128), f32), ((nz, 16, 128), f32), ((nz - 1, 16, 128), f32)]


class TopOfAll(Stripe):
    def __init__(self, remote, place, top, tops):
        super().__init__()
        self.top, self.tops, self.slots, slot = top, tops, [], 0
        for n, peers in enumerate(([place.at(c=1 - place.c)], place.along("y"), place.along("x"), place.along("z"))):
            self.slots.append(list(range(slot, slot + len(peers))))
            self.stages.append([remote.make(top.at[n], tops.at[slot + k], peer) for k, peer in enumerate(peers)])
            slot += len(peers)

    def take(self, n):
        best = self.top[n]
        for slot in self.slots[n]:
            best = jnp.maximum(best, self.tops[slot])
        self.top[n + 1] = best


class Script:
    def __init__(self, plan, stripes, swap):
        self.plan, self.stripes, self.swap, self.spent = plan, stripes, swap, 0

    def point(self):
        for item in self.plan[self.spent]:
            if item < 0:
                self.swap.start()
            else:
                self.stripes[item].step()
        self.spent += 1

    def points(self, index, first, count):
        for k in range(count):
            pl.when(index == first + k)(self.point)

    def close(self):
        assert self.spent == len(self.plan)
        assert all(s.at == len(s.stages) + 1 for s in self.stripes)


VMEM_BYTES = 60 << 20
GATHER_ITEMS = (
    (0, 0, 384, "yzx"), (0, 384, 384, "yzx"), (0, 768, 384, "zxy"), (0, 1152, 384, "zyx"), (0, 1536, 256, "zxy"),
    (0, 1792, 256, "zxy"), (0, 2048, 256, "yzx"), (0, 2304, 768, "zxy"), (1, 0, 768, "zyx"), (1, 768, 768, "zxy"),
    (1, 1536, 256, "zxy"), (1, 1792, 256, "zxy"), (1, 2048, 256, "yzx"), (1, 2304, 768, "zyx"), (2, 0, 128, "zyx"),
    (2, 128, 128, "yzx"), (2, 256, 256, "xzy"), (2, 512, 128, "xzy"), (2, 640, 128, "yzx"),
)
GATHER_PLAN = (
    (0, 1, 2, 3, 19, 4, 5, 6, -1),
    (0, 1, 6, 2, 3, 19, 4, 5, 2, 19, 4, 0, 5, 7, 8, 1, 0, 3, 6, 0, 9, 1, 2, 19, 7, 1, 10, 2, 11, 3, 19, 12), (4, 8),
    (3, 13, 6), (4, 5, 9, 12, 14, 6, 15, 5, 7, 16), (8,), (10, 15, 11), (9, 16), (), (7,), (), (7, 8, 13, 17), (10, 11, 12),
    (8, 9, 14, 17, 18), (12,), (9, 12, 13, 15), (10,), (10, 11), (11, 16), (14, 18), (13, 17), (), (), (13,), (15, 18), (),
    (), (15, 16), (14,), (), (), (16, 17, 14), (18,), (17,), (18,), (), (),
)
SCATTER_ITEMS = (
    (2, 0, 128, "yzx"), (2, 128, 128, "xzy"), (2, 256, 256, "yxz"), (2, 512, 256, "xzy"), (1, 0, 384, "yxz"),
    (1, 384, 384, "xyz"), (1, 768, 768, "yxz"), (1, 1536, 768, "xyz"), (1, 2304, 768, "yxz"), (0, 0, 384, "yxz"),
    (0, 384, 384, "xzy"), (0, 768, 256, "xzy"), (0, 1024, 256, "xzy"), (0, 1280, 256, "xzy"), (0, 1536, 256, "yxz"),
    (0, 1792, 256, "xzy"), (0, 2048, 256, "xzy"), (0, 2304, 384, "xzy"), (0, 2688, 384, "xyz"),
)
SCATTER_PLAN = (
    (), (), (), (0, 1), (2,), (0, 1, 3), (2, 3, 0, 1), (4, 5, 19), (6,), (), (4, 5, 19), (), (6, 7, 8), (), (0,), (2, 7, 3),
    (1, 8, 17, 18), (0, 4, 5, 19, 17, 18), (2,), (1, 6), (), (3,), (2, 7, 9, 10, 4, 19, 8), (5, 9, 10, 3, 4, 19, 17), (),
    (7, 18, 5), (), (6, 17, 18, 9, -1), (7, 8, 17), (), (10, 11, 12, 13), (6, 9, 11, 12), (18, 13), (8, 11, 14, 15, 16),
    (20,), (10, 12, 14, 15, 16, 20, 9), (13,), (11, 15, 10, 12, 16, 14, 13, 20, 11, 12, 13, 14, 15, 20, 16, 15, 14, 20, 16),
)

def layer_norm_parts(rows):
    centre = rows - jnp.mean(rows, axis=-1, keepdims=True)
    spread = jnp.mean(centre * centre, axis=-1, keepdims=True)
    inverse = lax.rsqrt(spread + norm_eps)
    return centre * inverse, inverse


def head_lanes(rows, half):
    lane = lax.broadcasted_iota(jnp.int32, rows.shape, 1)
    return jnp.where((lane >= HD) == (half == 1), rows, jnp.zeros_like(rows))


def key_structure(local, y, length):
    lane = lax.broadcasted_iota(jnp.int32, (2 * local, 128), 1)
    row = lax.broadcasted_iota(jnp.int32, (2 * local, 128), 0)
    position = jnp.where(row < local, row + y * local, row - y * local)
    own = lane == lax.shift_right_logical(position, 6)
    beyond = (lane == NB) & (position >= length)
    return jnp.where(own | beyond | ((lane > NB) & (lane < NB + 4)), 1.0, 0.0).astype(bf16)


def head_rows(rows, half):
    row = lax.broadcasted_iota(jnp.int32, rows.shape, 0)
    return jnp.where((row >= HD) == (half == 1), rows, jnp.zeros_like(rows))


def in_three(values):
    high = values.astype(bf16)
    rest = values - high.astype(f32)
    middle = rest.astype(bf16)
    return high, middle, (rest - middle.astype(f32)).astype(bf16)


def with_rows(base, values):
    row = lax.broadcasted_iota(jnp.int32, base.shape, 0)
    for k, part in enumerate(in_three(-values)):
        base = base + jnp.where(row == NB + 1 + k, part.astype(f32), 0.0)
    return base.astype(bf16)


def spread_vectors(tiles, width, pieces):
    rows = tiles.shape[1]
    total = pieces * width
    lane = lax.broadcasted_iota(jnp.int32, (128, total), 1).astype(f32)
    row = lax.broadcasted_iota(jnp.int32, (128, total), 0).astype(f32)
    owner = jnp.floor((lane + 0.5) * (1.0 / width))
    chooser = jnp.where(lane - owner * width == row, 1.0, 0.0).astype(bf16)
    wide = dot_nn(tiles.reshape(pieces * rows, 128), chooser).reshape(pieces, rows, total)
    lane3 = lax.broadcasted_iota(jnp.int32, (pieces, rows, total), 2).astype(f32)
    piece3 = lax.broadcasted_iota(jnp.int32, (pieces, rows, total), 0).astype(f32)
    mine = jnp.floor((lane3 + 0.5) * (1.0 / width)) == piece3
    return jnp.sum(jnp.where(mine, wide, 0.0), axis=0)


def forward_kernel(
    nz, local, length_ref, masks_ref, x_hbm, wq, wk, wv, wo, wi, wu, v0, v1, v2, v3, v4, v5, v6, v7, v8,
    out_hbm, r1_hbm, r2_hbm, gp_hbm, gt_hbm, n1t_hbm, at_hbm, atf_hbm, q_hbm, qt_hbm, k_hbm, kt_hbm, v_hbm, xt_hbm, lse_hbm,
    top_hbm, wa_hbm, wi_hbm, wu_hbm, vec_hbm,
    WA, WI, WU, SM, XF, XT, Q, QT, K, KT, V, VT, AT, ATF, R1, R2, N1L, N1T, U, GP, G, GT, E, VEC, IB, LSE, TOP, TT, OUT,
    send_sems, recv_sems, local_sems, out_sems,
):
    place = Place(nz)
    z, x, c, y = place.z, place.x, place.c, place.y
    remote = Remote(send_sems, recv_sems)
    mine = (z, x, c, y)
    locals_ = [(x_hbm, XF.at[0])]
    for g in range(3):
        for n, w in enumerate((wq, wk, wv)):
            lo = g * D + n * 256
            locals_.append((w.at[:, g * 256 : (g + 1) * 256], WA.at[(*mine, slice(None), slice(lo, lo + 256))]))
    locals_ += [(wo, WA.at[(*mine, slice(None), slice(3 * D, 4 * D))]), (wi, WI.at[mine]), (wu, WU.at[mine])]
    locals_ = [pltpu.make_async_copy(src, dst, local_sems.at[k]) for k, (src, dst) in enumerate(locals_)]
    for copy in locals_:
        copy.start()
    TT[...] = jnp.zeros((16, 128), f32)
    for n, v in enumerate((v0, v1, v2, v3, v4, v5, v6, v7, v8)):
        TT[n : n + 1, 0 : v.shape[1]] = v[...].astype(f32)
    SM[mine] = TT[...].astype(bf16)
    entry_barrier(place)
    for copy in locals_:
        copy.wait()

    outs = []

    def put(src, dst):
        copy = pltpu.make_async_copy(src, dst, out_sems.at[len(outs)])
        copy.start()
        outs.append(copy)

    swap = remote.make(XF.at[0], XF.at[1], place.at(y=1 - y))
    stripes = [
        GatherStripe(remote, place, (WA, WI, WU)[buf], slice(lo, lo + width), order) for buf, lo, width, order in GATHER_ITEMS
    ]
    stripes.append(GatherTile(remote, place, SM))
    script = Script(GATHER_PLAN, stripes, swap)
    script.point()
    length = length_ref[0]
    E[...] = key_structure(local, y, length)
    XT[:, :local] = XF[0].T
    script.point()

    tiles = SM[...].reshape(-1, 16, 128)
    pieces = tiles.shape[0]
    VEC[...] = spread_vectors(tiles, D // pieces, pieces)
    IB[...] = spread_vectors(tiles[:, 8:16, :], FF // pieces, pieces)
    put(VEC, vec_hbm)
    script.point()
    position = y * local + lax.broadcasted_iota(jnp.int32, (1, local), 1)
    live = position < length

    def wide(buf, lo, width):
        return buf[:, :, :, :, :, lo : lo + width].reshape(-1, width)

    for g in range(3):
        cols = slice(g * 256, (g + 1) * 256)
        own = dot_nn(XF[0], wide(WA, g * D, D))
        q = ((own[:, :256] + VEC[0:1, cols]).astype(bf16).astype(f32) * (HD**-0.5)).astype(bf16)
        Q[:, cols] = q
        QT[cols, :] = q.T
        K[:local, cols] = own[:, 256:512].astype(bf16)
        values = (own[:, 512:] + VEC[1:2, cols]).astype(bf16)
        V[:local, cols] = values
        VT[cols, :local] = values.T
        script.point()
    put(Q, q_hbm)
    put(QT, qt_hbm)
    swap.wait_recv()
    for g in range(3):
        cols = slice(g * 256, (g + 1) * 256)
        theirs = dot_nn(XF[1], wide(WA, g * D + 256, 512))
        K[local:, cols] = theirs[:, :256].astype(bf16)
        values = (theirs[:, 256:] + VEC[1:2, cols]).astype(bf16)
        V[local:, cols] = values
        VT[cols, local:] = values.T
        script.point()

        def head_step(h, carry):
            lanes = ds128(lax.div(h, 2), 128)
            half = lax.rem(h, 2)
            own = pl.ds(pl.multiple_of(h * HD, HD), HD)
            left = jnp.concatenate([K[:, lanes], E[...]], axis=1)
            right = jnp.concatenate(
                [head_rows(QT[lanes, :], half), masks_ref[h], jnp.zeros((128 - 32, local), bf16)], axis=0
            )
            for part in range(local // 256):
                cols = slice(part * 256, (part + 1) * 256)
                scores = dot_nn(left, right[:, cols])
                top = jnp.max(scores, axis=0, keepdims=True)
                exponent = jnp.exp(scores - top)
                total = jnp.sum(exponent, axis=0, keepdims=True)
                low = (exponent * (1.0 / total)).astype(bf16)
                mixture = dot_nn(VT[own, :], low)
                ATF[own, cols] = mixture
                AT[own, cols] = mixture.astype(bf16)
                LSE[h, :, cols] = top + jnp.log(total)
                TOP[h, :, cols] = jnp.where(live[:, cols], top, neg_large)
            script.points(h, 4 * g, 4)
            return carry

        lax.fori_loop(4 * g, 4 * g + 4, head_step, 0)
    put(WA, wa_hbm)
    put(K, k_hbm)
    put(V, v_hbm)
    put(LSE, lse_hbm)
    TT[...] = jnp.zeros((16, 128), f32) + neg_large
    TT[0:H, :] = jnp.broadcast_to(jnp.max(TOP[:, 0, :], axis=1, keepdims=True), (H, 128))
    put(TT, top_hbm)
    put(AT, at_hbm)
    put(ATF, atf_hbm)
    R1[...] = dot_nn(AT[...].T, wide(WA, 3 * D, D))
    script.point()

    def first_norm(k, carry):
        rows = ds128(k, 64)
        summed = XF[0, rows, :].astype(f32) + R1[rows, :] + VEC[2:3, :]
        R1[rows, :] = summed
        normal, _ = layer_norm_parts(summed)
        value = normal * VEC[3:4, :] + VEC[4:5, :]
        N1L[rows, :] = value.astype(bf16)
        R2[rows, :] = value + VEC[5:6, :]
        return carry

    lax.fori_loop(0, local // 64, first_norm, 0)
    put(R1, r1_hbm)
    script.point()
    N1T[...] = N1L[...].T
    put(N1T, n1t_hbm)
    XT[:, local:] = XF[1].T
    put(XT, xt_hbm)
    script.point()
    KT[...] = K[...].T
    put(KT, kt_hbm)
    script.point()
    for n in range(FF // D):
        cols = slice(n * D, (n + 1) * D)
        U[...] = dot_nn(N1L[...], wide(WI, n * D, D)) + IB[0:1, cols]
        script.point()

        def activate(k, carry):
            rows = ds128(k, 16)
            u = U[rows, :]
            below = 0.5 * (1.0 + lax.erf(u * np.float32(0.5**0.5)))
            G[rows, cols] = (u * below).astype(bf16)
            GP[n, rows, :] = below + u * jnp.exp(-0.5 * u * u) * np.float32((2.0 * np.pi) ** -0.5)
            return carry

        lax.fori_loop(0, local // 16, activate, 0)
        GT[cols, :] = G[:, cols].T
        script.point()
    put(WI, wi_hbm)
    put(GP, gp_hbm)
    put(GT, gt_hbm)
    for n in range(3):
        cols = slice(n * 256, (n + 1) * 256)
        R2[:, cols] += dot_nn(G[...], WU[:, :, :, :, :, cols].reshape(FF, 256))
        script.point()
    put(WU, wu_hbm)

    def second_norm(k, carry):
        rows = ds128(k, 64)
        normal, _ = layer_norm_parts(R2[rows, :])
        OUT[rows, :] = (normal * VEC[6:7, :] + VEC[7:8, :]).astype(bf16)
        return carry

    lax.fori_loop(0, local // 64, second_norm, 0)
    put(R2, r2_hbm)
    put(OUT, out_hbm)
    script.point()
    script.close()
    remote.finish()
    for copy in outs:
        copy.wait()


def copies_of(items, nz):
    return sum(3 + (nz - 1) for _ in items)


def run_forward(nz, x, weights, vectors, masks, length):
    local = x.shape[0]
    wq, wk, wv, wo, wi, wu = weights
    grid = (nz, 2, 2, 2)
    rows, rows_u = wq.shape[0], wu.shape[0]
    seq = 2 * local
    blocks = FF // D
    outs = [
        ((local, D), bf16), ((local, D), f32), ((local, D), f32), ((blocks, local, D), f32), ((FF, local), bf16),
        ((D, local), bf16), ((D, local), bf16), ((D, local), f32), ((local, D), bf16), ((D, local), bf16), ((seq, D), bf16),
        ((D, seq), bf16), ((seq, D), bf16), ((D, seq), bf16), ((H, 1, local), f32), ((16, 128), f32),
        ((*grid, rows, 4 * D), bf16), ((*grid, rows, FF), bf16), ((*grid, rows_u, D), bf16), ((16, D), f32),
    ]
    scratch = [
        ((*grid, rows, 4 * D), bf16), ((*grid, rows, FF), bf16), ((*grid, rows_u, D), bf16), ((*grid, 16, 128), bf16),
        ((2, local, D), bf16), ((D, seq), bf16), ((local, D), bf16), ((D, local), bf16), ((seq, D), bf16), ((D, seq), bf16),
        ((seq, D), bf16), ((D, seq), bf16), ((D, local), bf16), ((D, local), f32), ((local, D), f32), ((local, D), f32),
        ((local, D), bf16), ((D, local), bf16), ((local, D), f32), ((blocks, local, D), f32), ((local, FF), bf16),
        ((FF, local), bf16), ((seq, 128), bf16), ((16, D), f32), ((8, FF), f32), ((H, 1, local), f32), ((H, 1, local), f32),
        ((16, 128), f32), ((local, D), bf16),
    ]
    copies = copies_of(GATHER_ITEMS, nz) + 3 + (nz - 1) + 1
    return pl.pallas_call(
        functools.partial(forward_kernel, nz, local),
        out_shape=[jax.ShapeDtypeStruct(*o) for o in outs],
        in_specs=[INSMEM, INVMEM] + [ANY] * 7 + [INVMEM] * 9,
        out_specs=[ANY] * len(outs),
        scratch_shapes=[pltpu.VMEM(*s) for s in scratch]
        + [
            pltpu.SemaphoreType.DMA((copies,)),
            pltpu.SemaphoreType.DMA((copies,)),
            pltpu.SemaphoreType.DMA((13,)),
            pltpu.SemaphoreType.DMA((len(outs),)),
        ],
        compiler_params=pltpu.CompilerParams(collective_id=1, has_side_effects=True, vmem_limit_bytes=VMEM_BYTES),
        name="gather_forward",
    )(length, masks, x, wq, wk, wv, wo, wi, wu, *(v.reshape(1, -1) for v in vectors))


def compact_mask(random_here, length, first_block):
    blocks = random_here.shape[0]
    query = (first_block + jnp.arange(blocks, dtype=jnp.int32))[None, :, None]
    key = jnp.arange(NB, dtype=jnp.int32)[None, None, :]
    last = (length - 1) // BLK
    ok = (jnp.abs(query - key) <= 1) | (key == 0) | (key == last) | (query == 0) | (query == last)
    heads = jnp.transpose(random_here, (1, 0, 2))
    for k in range(heads.shape[2]):
        ok = ok | (heads[:, :, k : k + 1] == key)
    return jnp.where(ok, 0.0, neg_large).astype(f32)


def mask_rows(random_here, length, first_block):
    compact = jnp.transpose(compact_mask(random_here, length, first_block), (0, 2, 1))
    rows = jnp.repeat(compact, BLK, axis=2)
    heads, _, queries = rows.shape
    return jnp.concatenate(
        [rows, jnp.full((heads, 1, queries), neg_large, f32), jnp.zeros((heads, 15, queries), f32)], axis=1
    ).astype(bf16)


def gather_vectors(rows, width, pieces):
    n, total = rows.shape
    if n == 1:
        lane2 = lax.broadcasted_iota(jnp.int32, (pieces, total), 1).astype(f32)
        piece2 = lax.broadcasted_iota(jnp.int32, (pieces, total), 0).astype(f32)
        mine = jnp.floor((lane2 + 0.5) * (1.0 / width)) == piece2
        spread = jnp.where(mine, rows, 0.0)
    else:
        lane3 = lax.broadcasted_iota(jnp.int32, (pieces, n, total), 2).astype(f32)
        piece3 = lax.broadcasted_iota(jnp.int32, (pieces, n, total), 0).astype(f32)
        mine = jnp.floor((lane3 + 0.5) * (1.0 / width)) == piece3
        spread = jnp.where(mine, rows[None], 0.0).reshape(pieces * n, total)
    lane = lax.broadcasted_iota(jnp.int32, (128, total), 1).astype(f32)
    row = lax.broadcasted_iota(jnp.int32, (128, total), 0).astype(f32)
    owner = jnp.floor((lane + 0.5) * (1.0 / width))
    chooser = jnp.where(lane - owner * width == row, 1.0, 0.0).astype(bf16)
    high, middle, lowest = in_three(spread)
    tiles = dot_nt(high, chooser) + (dot_nt(middle, chooser) + dot_nt(lowest, chooser))
    return tiles.reshape(pieces, n, 128)


def norm_back(normal, inverse, grads, gain):
    scaled = grads * gain
    first = jnp.mean(scaled, axis=-1, keepdims=True)
    second = jnp.mean(scaled * normal, axis=-1, keepdims=True)
    return inverse * (scaled - first - normal * second)


def row_sum(values):
    return jnp.sum(values, axis=0, keepdims=True)


def back_half(pair, local, own_keys, BQ, BD, Q, QT, DA, DAT, K, KT, V, E, PB, DS, DQF, DQT, DK, DV):
    keys = slice(0, local) if own_keys else slice(local, 2 * local)
    lanes = ds128(pair, 128)
    structure = E[keys, :]
    left = jnp.concatenate([K[keys, lanes], structure], axis=1)
    left_values = jnp.concatenate([V[keys, lanes], structure], axis=1)
    empty = jnp.zeros((128 - 32, local), bf16)
    for half in (0, 1):
        h = pair * 2 + half
        own = pl.ds(pl.multiple_of(h * HD, HD), HD)
        spot = slice(half * local, (half + 1) * local)
        right = jnp.concatenate([head_rows(QT[lanes, :], half), BQ[h], empty], axis=0)
        prob = jnp.exp(dot_nn(left, right))
        PB[:, spot] = prob.astype(bf16)
        right_values = jnp.concatenate([head_rows(DAT[lanes, :], half), BD[h], empty], axis=0)
        low = (prob * dot_nn(left_values, right_values)).astype(bf16)
        DS[:, spot] = low
        part = dot_nn(KT[own, keys], low)
        if own_keys:
            DQT[own, :] = ((DQF[own, :] + part) * (HD**-0.5)).astype(bf16)
        else:
            DQF[own, :] = part
    q_pair, a_pair = Q[:, lanes], DA[:, lanes]
    DK[keys, lanes] = dot_nn(DS[...], jnp.concatenate([head_lanes(q_pair, n) for n in (0, 1)], axis=0)).astype(bf16)
    DV[keys, lanes] = dot_nn(PB[...], jnp.concatenate([head_lanes(a_pair, n) for n in (0, 1)], axis=0)).astype(bf16)


def backward_kernel(
    nz, local, length_ref, masks_ref, VEC, cot_hbm, r1_hbm, r2_hbm, gp_hbm, gt_hbm, n1t_hbm, at_hbm, atf_hbm, q_hbm, qt_hbm,
    k_hbm, kt_hbm, v_hbm, xt_hbm, lse_hbm, top_hbm, wa_hbm, wi_hbm, wu_hbm,
    dx_hbm, taken_hbm, OA, OI, OU, OS, OT, *rest,
):
    place = Place(nz)
    z, x, c, y = place.z, place.x, place.c, place.y
    GA, GI, GU, WA, T, TOP, TOPS, DP, AT, DR1, E, SUMS, ISUM, SEND, RECV = rest[:15]
    used = 15
    bufs = []
    for _ in SCATTER_ITEMS:
        bufs.append(rest[used : used + 4])
        used += 4
    sbufs = rest[used : used + 4]
    send_sems, recv_sems, load_sems = rest[used + 4 :]
    blocks = FF // D
    pieces = nz * 8
    seq_len = 2 * local
    length = length_ref[0]
    loads = [0]

    def load(src, dst):
        copy = pltpu.make_async_copy(src, dst, load_sems.at[loads[0]])
        loads[0] += 1
        copy.start()
        return copy

    remote = Remote(send_sems, recv_sems)
    stripes = [
        ScatterStripe(remote, place, (GA, GI, GU)[buf], slice(lo, lo + width), order, bufs[n], (OA, OI, OU)[buf])
        for n, (buf, lo, width, order) in enumerate(SCATTER_ITEMS)
    ]
    stripes += [TopOfAll(remote, place, TOP, TOPS), SmallSums(remote, place, T, sbufs)]
    swap = remote.make(SEND, RECV, place.at(y=1 - y))
    script = Script(SCATTER_PLAN, stripes, swap)
    grid = (nz, 2, 2, 2)
    SUMS[...] = jnp.zeros_like(SUMS)
    ISUM[...] = jnp.zeros_like(ISUM)

    def first_stage(COT, R2, R1, DM, GT, DU, GP, N1T, WUS, WIS):
        l_r2, l_cot = load(r2_hbm, R2), load(cot_hbm, COT)
        l_gt = load(gt_hbm, GT)
        l_wu, l_gp = [], []
        for n in range(2):
            l_wu.append(load(wu_hbm.at[n], WUS.at[n]))
            l_gp.append(load(gp_hbm.at[n], GP.at[n]))

        def wi_of(n):
            return wi_hbm.at[:, :, :, :, :, n * D : (n + 1) * D]

        script.point()
        entry_barrier(place)
        E[...] = key_structure(local, y, length)
        l_r2.wait()
        l_cot.wait()
        script.point()

        def second_norm(k, carry):
            rows = ds128(k, 64)
            normal, inverse = layer_norm_parts(R2[rows, :])
            position = y * local + k * 64 + lax.broadcasted_iota(jnp.int32, (64, D), 0)
            grads = jnp.where(position < length, COT[rows, :].astype(f32), 0.0)
            through = norm_back(normal, inverse, grads, VEC[6:7, :])
            R2[rows, :] = through
            low = through.astype(bf16)
            DM[rows, :] = low
            SUMS[5:6, :] += row_sum(low.astype(f32))
            SUMS[6:7, :] += row_sum(grads * normal)
            SUMS[7:8, :] += row_sum(grads)
            return carry

        lax.fori_loop(0, local // 64, second_norm, 0)
        script.point()
        l_gt.wait()
        for n in range(3):
            cols = slice(n * 256, (n + 1) * 256)

            def outer_grad(zz, carry):
                rows = ds128(zz, FF // nz)
                made = dot_nn(GT[rows, :], DM[:, cols]).astype(bf16)
                GU[zz, :, :, :, :, cols] = made.reshape(2, 2, 2, -1, 256)
                return carry

            lax.fori_loop(0, nz, outer_grad, 0)
            script.point()
        for n in range(blocks):
            l_wu[n].wait()
            l_gp[n].wait()
            grads = dot_nt(DM[...], WUS[n % 2].reshape(D, D)) * GP[n % 2]
            low = grads.astype(bf16)
            DU[n] = low
            ISUM[0:1, n * D : (n + 1) * D] = row_sum(low.astype(f32))
            if n + 2 < blocks:
                l_wu.append(load(wu_hbm.at[n + 2], WUS.at[n % 2]))
                l_gp.append(load(gp_hbm.at[n + 2], GP.at[n % 2]))
        l_top, l_n1t = load(top_hbm, TOP.at[0]), load(n1t_hbm, N1T)
        l_wi = [load(wi_of(0), WIS.at[0]), load(wi_of(1), WIS.at[1])]
        l_r1, l_at, l_wa = load(r1_hbm, R1), load(at_hbm, AT), load(wa_hbm, WA)
        wide = gather_vectors(ISUM[...], FF // pieces, pieces).reshape(*grid, 1, 128)
        T[:, :, :, :, 8:16, :] = jnp.broadcast_to(wide, (*grid, 8, 128))
        script.point()
        l_top.wait()
        l_n1t.wait()
        for n in range(blocks):
            made = dot_nn(N1T[...], DU[n]).astype(bf16)
            GI[:, :, :, :, :, n * D : (n + 1) * D] = made.reshape(*grid, -1, D)
            script.point()
        for n in range(blocks):
            l_wi[n].wait()
            R2[...] += dot_nt(DU[n], WIS[n % 2].reshape(D, D))
            if n + 2 < blocks:
                l_wi.append(load(wi_of(n + 2), WIS.at[n % 2]))
            script.point()
        l_r1.wait()

        def first_norm(k, carry):
            rows = ds128(k, 64)
            normal, inverse = layer_norm_parts(R1[rows, :])
            grads = R2[rows, :]
            through = norm_back(normal, inverse, grads, VEC[3:4, :])
            DR1[rows, :] = through
            low = through.astype(bf16)
            DP[rows, :] = low
            SUMS[2:3, :] += row_sum(low.astype(f32))
            SUMS[3:4, :] += row_sum(grads * normal)
            SUMS[4:5, :] += row_sum(grads)
            return carry

        lax.fori_loop(0, local // 64, first_norm, 0)
        script.point()
        l_at.wait()
        l_wa.wait()

    pl.run_scoped(
        first_stage,
        pltpu.VMEM((local, D), bf16), pltpu.VMEM((local, D), f32), pltpu.VMEM((local, D), f32), pltpu.VMEM((local, D), bf16),
        pltpu.VMEM((FF, local), bf16), pltpu.VMEM((blocks, local, D), bf16), pltpu.VMEM((2, local, D), f32),
        pltpu.VMEM((D, local), bf16), pltpu.VMEM((2, 2, 2, 2, FF // (nz * 8), D), bf16),
        pltpu.VMEM((2, *grid, D // (nz * 8), D), bf16),
    )

    def second_stage(Q, QT, K, KT, V, XT, LSE, BQ, BD, DA, DAT, PB, DS, DQF, DQT, DQ, DK, DV):
        pairs = ((lse_hbm, LSE), (atf_hbm, DQF), (k_hbm, K), (q_hbm, Q), (qt_hbm, QT), (kt_hbm, KT), (v_hbm, V), (xt_hbm, XT))
        waits = [load(s, d) for s, d in pairs]
        made = dot_nn(AT[...], DP[...]).astype(bf16)
        GA[:, :, :, :, :, 3 * D : 4 * D] = made.reshape(*grid, -1, D)
        script.point()
        DAT[...] = dot_nt(WA[:, :, :, :, :, 3 * D : 4 * D].reshape(D, D), DP[...]).astype(bf16)
        DA[...] = DAT[...].T
        waits[0].wait()
        waits[1].wait()

        def prepare(h, carry):
            own = pl.ds(pl.multiple_of(h * HD, HD), HD)
            delta = row_sum(DAT[own, :].astype(f32) * DQF[own, :])
            BD[h] = with_rows(jnp.zeros((32, local), f32), delta)
            BQ[h] = with_rows(masks_ref[h].astype(f32), LSE[h])
            return carry

        lax.fori_loop(0, H, prepare, 0)
        for wait in waits[2:]:
            wait.wait()
        script.point()

        def halves(own_keys, g):
            def pair_step(pair, carry):
                back_half(pair, local, own_keys, BQ, BD, Q, QT, DA, DAT, K, KT, V, E, PB, DS, DQF, DQT, DK, DV)
                script.points(pair, 2 * g, 2)
                return carry

            lax.fori_loop(2 * g, 2 * g + 2, pair_step, 0)

        def group(g):
            lo = g * D
            cols = slice(g * 256, (g + 1) * 256)
            dq = DQT[cols, :].T
            DQ[:, cols] = dq
            SUMS[0:1, cols] = row_sum(dq.astype(f32))
            SUMS[1:2, cols] = row_sum(DV[:, cols].astype(f32))
            for n, made in enumerate(
                (dot_nn(XT[:, :local], dq), dot_nn(XT[...], DK[:, cols]), dot_nn(XT[...], DV[:, cols]))
            ):
                GA[:, :, :, :, :, lo + n * 256 : lo + (n + 1) * 256] = made.astype(bf16).reshape(*grid, -1, 256)
            script.point()

        halves(False, 0)
        halves(True, 0)
        group(0)
        halves(False, 1)
        halves(False, 2)
        groups = [slice(g * 256, (g + 1) * 256) for g in range(3)]
        theirs = jnp.concatenate([a[local:, cols] for cols in groups for a in (DK, DV)], axis=1)
        through = [WA[:, :, :, :, :, g * D + 256 : (g + 1) * D].reshape(D, 512) for g in range(3)]
        SEND[...] = dot_nt(theirs, jnp.concatenate(through, axis=1)).astype(bf16)
        script.point()
        halves(True, 1)
        group(1)
        halves(True, 2)
        group(2)
        T[:, :, :, :, 0:8, :] = gather_vectors(SUMS[0:8, :], D // pieces, pieces).reshape(*grid, 8, 128)
        script.point()
        for g in range(3):
            cols = slice(g * 256, (g + 1) * 256)
            ours = jnp.concatenate([DQ[:, cols], DK[:local, cols], DV[:local, cols]], axis=1)
            DR1[...] += dot_nt(ours, WA[:, :, :, :, :, g * D : (g + 1) * D].reshape(D, D))
            script.point()
        script.close()
        out = pltpu.make_async_copy(DR1, dx_hbm, load_sems.at[loads[0]])
        out.start()
        swap.wait_recv()
        taken = pltpu.make_async_copy(RECV, taken_hbm, load_sems.at[loads[0] + 1])
        taken.start()
        OS[...] = T[z, x, c, y]
        OT[...] = TOP[4]
        out.wait()
        taken.wait()

    scoped = [
        ((local, D), bf16), ((D, local), bf16), ((seq_len, D), bf16), ((D, seq_len), bf16), ((seq_len, D), bf16),
        ((D, seq_len), bf16), ((H, 1, local), f32), ((H, 32, local), bf16), ((H, 32, local), bf16), ((local, D), bf16),
        ((D, local), bf16), ((local, 2 * local), bf16), ((local, 2 * local), bf16), ((D, local), f32), ((D, local), bf16),
        ((local, D), bf16), ((seq_len, D), bf16), ((seq_len, D), bf16),
    ]
    pl.run_scoped(second_stage, *(pltpu.VMEM(*s) for s in scoped))
    remote.finish()


def run_backward(nz, local, rows, rows_u, length, masks, vec, *arrays):
    grid = (nz, 2, 2, 2)
    seq = 2 * local
    outs = [((local, D), f32), ((local, D), bf16), ((rows, 4 * D), f32), ((rows, FF), f32), ((rows_u, D), f32)]
    outs += [((16, 128), f32)] * 2
    scratch = [
        ((*grid, rows, 4 * D), bf16), ((*grid, rows, FF), bf16), ((*grid, rows_u, D), bf16), ((*grid, rows, 4 * D), bf16),
        ((*grid, 16, 128), f32), ((5, 16, 128), f32), ((3 + nz - 1, 16, 128), f32),
        ((local, D), bf16), ((D, local), bf16), ((local, D), f32), ((seq, 128), bf16),
        ((8, D), f32), ((1, FF), f32), ((local, D), bf16), ((local, D), bf16),
    ]
    for buf, _, width, order in SCATTER_ITEMS:
        scratch += scatter_buffers(nz, rows_u if buf == 2 else rows, width, order)
    scratch += small_buffers(nz)
    copies = copies_of(SCATTER_ITEMS, nz) + 2 * (3 + nz - 1) + 1
    return pl.pallas_call(
        functools.partial(backward_kernel, nz, local),
        out_shape=[jax.ShapeDtypeStruct(*o) for o in outs],
        in_specs=[INSMEM, INVMEM, INVMEM] + [ANY] * len(arrays),
        out_specs=[ANY] * 2 + [INVMEM] * 5,
        scratch_shapes=[pltpu.VMEM(*s) for s in scratch]
        + [pltpu.SemaphoreType.DMA((copies,)), pltpu.SemaphoreType.DMA((copies,)), pltpu.SemaphoreType.DMA((32,))],
        compiler_params=pltpu.CompilerParams(collective_id=2, has_side_effects=True, vmem_limit_bytes=VMEM_BYTES),
        name="backward_scatter",
    )(length, masks, vec, *arrays)


def finish_kernel(
    threshold_ref, dx_hbm, taken_hbm, ga_hbm, gi_hbm, gu_hbm, gs_hbm, top_hbm, out_hbm, WQ, WK, BQ,
    o_out, o_dx, o_q, o_k, o_v, o_o, o_i, o_u, o_wq, o_wk, o_bq, o_top, *rest,
):
    o_vecs, (DX, TAKEN, GS, TOP, GA, GI, GU, OUT, sems) = rest[:9], rest[9:]
    pairs = [(dx_hbm, DX), (taken_hbm, TAKEN), (ga_hbm, GA), (gi_hbm, GI), (gu_hbm, GU), (out_hbm, OUT), (gs_hbm, GS), (top_hbm, TOP)]
    loads = [pltpu.make_async_copy(src, dst, sems.at[n]) for n, (src, dst) in enumerate(pairs)]
    for copy in loads:
        copy.start()
    stores = []

    def put(src, dst):
        copy = pltpu.make_async_copy(src, dst, sems.at[len(loads) + len(stores)])
        copy.start()
        stores.append(copy)

    loads[0].wait()
    loads[1].wait()
    DX[...] = DX[...] + TAKEN[...].astype(f32)
    put(DX, o_dx)
    loads[2].wait()
    for g in range(3):
        for n, o in enumerate((o_q, o_k, o_v)):
            lo = g * D + n * 256
            put(GA.at[:, lo : lo + 256], o.at[:, g * 256 : (g + 1) * 256])
    put(GA.at[:, 3 * D : 4 * D], o_o)
    for copy, src, dst in zip(loads[3:6], (GI, GU, OUT), (o_i, o_u, o_out)):
        copy.wait()
        put(src, dst)
    loads[6].wait()
    loads[7].wait()
    for n, o in enumerate(o_vecs):
        o[...] = GS[n : n + 1, 0 : o.shape[1]]
    limit = threshold_ref[0].astype(f32) * 0.01
    top = TOP[...]
    factors = jnp.sqrt(limit / jnp.maximum(top, limit))
    head = lax.broadcasted_iota(jnp.int32, (16, D), 0)
    column = lax.broadcasted_iota(jnp.int32, (16, D), 1)
    wide = jnp.concatenate([factors] * (D // 128), axis=1)
    scale = row_sum(jnp.where(head == lax.shift_right_logical(column, 6), wide, 0.0))
    o_wq[...] = (WQ[...].astype(f32) * scale).astype(bf16)
    o_wk[...] = (WK[...].astype(f32) * scale).astype(bf16)
    count = BQ.shape[1]
    row = lax.broadcasted_iota(jnp.int32, (16, 128), 0)
    lane = lax.broadcasted_iota(jnp.int32, (16, 128), 1)
    entry = (lax.axis_index("dp") * 2 + lax.axis_index("ctx")) * count + lane
    own = row_sum(jnp.where(row == lax.shift_right_logical(entry, 6), factors, 0.0))
    o_bq[...] = (BQ[...].astype(f32) * own[:, 0:count]).astype(bf16)
    o_top[...] = row_sum(jnp.where(row == lane, top, 0.0))
    for copy in stores:
        copy.wait()


def run_finish(threshold, dx, taken, ga, gi, gu, gs, top, output, wq, wk, bq, wide):
    local, rows, rows_u, count = dx.shape[0], ga.shape[0], gu.shape[0], bq.shape[0]
    outs = [((local, D), bf16), ((local, D), f32)] + [((rows, D), f32)] * 4 + [((rows, FF), f32), ((rows_u, D), f32)]
    outs += [((rows, D), bf16)] * 2 + [((1, count), bf16), ((1, 128), f32)] + [((1, count), f32)] * 8 + [((1, wide), f32)]
    return pl.pallas_call(
        finish_kernel,
        out_shape=[jax.ShapeDtypeStruct(*o) for o in outs],
        in_specs=[INSMEM] + [ANY] * 8 + [INVMEM] * 3,
        out_specs=[ANY] * 8 + [INVMEM] * (len(outs) - 8),
        scratch_shapes=[
            pltpu.VMEM((local, D), f32), pltpu.VMEM((local, D), bf16), pltpu.VMEM((16, 128), f32), pltpu.VMEM((16, 128), f32),
            pltpu.VMEM((rows, 4 * D), f32), pltpu.VMEM((rows, FF), f32), pltpu.VMEM((rows_u, D), f32),
            pltpu.VMEM((local, D), bf16), pltpu.SemaphoreType.DMA((22,)),
        ],
        compiler_params=pltpu.CompilerParams(vmem_limit_bytes=VMEM_BYTES),
        name="finish",
    )(threshold, dx, taken, ga, gi, gu, gs, top, output, wq, wk, bq.reshape(1, -1))


def layer_norm(row_values, gain_vector, shift_vector):
    centre = row_values - jnp.mean(row_values, axis=-1, keepdims=True)
    spread = jnp.mean(centre * centre, axis=-1, keepdims=True)
    return centre * lax.rsqrt(spread + norm_eps) * gain_vector + shift_vector


def gelu_exact(values):
    return jax.nn.gelu(values, approximate=False)


def column_sums(values):
    return jnp.sum(values.astype(f32), axis=0)


def clip_outputs(logit_maxima, threshold, query_weight, query_bias, key_weight, device_rank):
    clip_limit = threshold.astype(f32)[0] * 0.01
    factors = jnp.sqrt(clip_limit / jnp.maximum(logit_maxima, clip_limit))
    column_scale = jnp.repeat(factors, HD)
    query_clipped = (query_weight.astype(f32) * column_scale[None, :]).astype(bf16)
    key_clipped = (key_weight.astype(f32) * column_scale[None, :]).astype(bf16)
    bias_count = query_bias.shape[0]
    bias_heads = (device_rank * bias_count + jnp.arange(bias_count)) // HD
    bias_scale = jnp.sum(jnp.where(bias_heads[:, None] == jnp.arange(H)[None, :], factors[None, :], 0.0), axis=1)
    return query_clipped, (query_bias.astype(f32) * bias_scale).astype(bf16), key_clipped


def fast_shards(
    nz,
    inputs, cotangent, query_weight, query_bias, key_weight, value_weight, value_bias, output_weight, output_bias,
    first_gain, first_shift, inner_weight, inner_bias, outer_weight, outer_bias, second_gain, second_shift,
    lengths, random_blocks, threshold,
):
    local = inputs.shape[1]
    pieces = nz * 8
    rows, rows_u = query_weight.shape[0], outer_weight.shape[0]
    y = lax.axis_index("ctx")
    blocks = local // BLK
    first_block = y * blocks
    random_here = lax.dynamic_slice_in_dim(random_blocks[0], first_block, blocks, 0)
    masks = mask_rows(random_here, lengths[0], first_block)
    small = (
        query_bias, value_bias, output_bias, first_gain, first_shift, outer_bias, second_gain, second_shift, inner_bias
    )
    x = inputs[0]
    weights = (query_weight, key_weight, value_weight, output_weight, inner_weight, outer_weight)
    output, *saved, vectors = run_forward(nz, x, weights, small, masks, lengths)
    made = run_backward(nz, local, rows, rows_u, lengths, masks, vectors, cotangent[0], *saved)
    (
        output, input_grad, g_query, g_key, g_value, g_out, g_inner, g_outer, query_clipped, key_clipped, bias_clipped, top, *vec
    ) = run_finish(threshold, *made, output, query_weight, key_weight, query_bias, FF // pieces)
    vec = [v.reshape(-1) for v in vec]
    return (
        output[None], input_grad[None],
        g_query, vec[0], g_key, g_value, vec[1], g_out, vec[2], vec[3], vec[4],
        g_inner, vec[8], g_outer, vec[5], vec[6], vec[7],
        query_clipped, bias_clipped.reshape(-1), key_clipped, top[0, :H],
    )


def general_shards(
    inputs, cotangent, query_weight, query_bias, key_weight, value_weight, value_bias, output_weight, output_bias,
    first_gain, first_shift, inner_weight, inner_bias, outer_weight, outer_bias, second_gain, second_shift,
    lengths, random_blocks, threshold,
):
    both = ("dp", "ctx")
    shards = (
        query_weight, query_bias, key_weight, value_weight, value_bias, output_weight, output_bias, first_gain, first_shift,
        inner_weight, inner_bias, outer_weight, outer_bias, second_gain, second_shift,
    )
    wq, bq, wk, wv, bv, wo, bo, g1, s1, wi, bi, wu, bu, g2, s2 = (lax.all_gather(w, both, axis=0, tiled=True) for w in shards)
    bq, bv, bo, g1, s1, bi, bu, g2, s2 = (v.astype(f32) for v in (bq, bv, bo, g1, s1, bi, bu, g2, s2))
    seqs, local, _ = inputs.shape
    blocks = local // BLK
    y = lax.axis_index("ctx")
    first_block = y * blocks
    scale = HD**-0.5
    outs = []
    sums = None
    top = jnp.full((H,), neg_large, f32)
    for s in range(seqs):
        x, length = inputs[s], lengths[s]
        random_here = lax.dynamic_slice_in_dim(random_blocks[s], first_block, blocks, 0)
        mask = compact_mask(random_here, length, first_block)
        mask = jnp.repeat(jnp.repeat(mask, BLK, axis=1), BLK, axis=2)
        seen = jnp.arange(NB * BLK) < length
        mask = jnp.where(seen[None, None, :], mask, neg_large)
        live = (y * local + jnp.arange(local)) < length
        q = (dot_nn(x, wq) + bq).astype(bf16)
        k = lax.all_gather(dot_nn(x, wk).astype(bf16), "ctx", axis=0, tiled=True)
        v = lax.all_gather((dot_nn(x, wv) + bv).astype(bf16), "ctx", axis=0, tiled=True)
        qh, kh, vh = (a.reshape(-1, H, HD) for a in (q, k, v))
        raw = jnp.einsum("qhd,khd->hqk", qh, kh, preferred_element_type=f32) * scale + mask
        row_top = jnp.max(raw, axis=-1, keepdims=True)
        top = jnp.maximum(top, jnp.max(jnp.where(live[None, :, None], row_top, neg_large), axis=(1, 2)))
        exponent = jnp.exp(raw - row_top)
        prob = exponent / jnp.sum(exponent, axis=-1, keepdims=True)
        low = prob.astype(bf16)
        attended = jnp.einsum("hqk,khd->qhd", low, vh, preferred_element_type=f32).reshape(local, D).astype(bf16)
        first_sum = x.astype(f32) + dot_nn(attended, wo) + bo
        normed = layer_norm(first_sum, g1, s1)
        normed_low = normed.astype(bf16)
        pre_act = dot_nn(normed_low, wi) + bi
        activated = gelu_exact(pre_act).astype(bf16)
        second_sum = normed + dot_nn(activated, wu) + bu
        output = layer_norm(second_sum, g2, s2).astype(bf16)
        cot = jnp.where(live[:, None], cotangent[s].astype(f32), 0.0)
        grad_second, g2_grad, s2_grad = jax.vjp(layer_norm, second_sum, g2, s2)[1](cot)
        dm = grad_second.astype(bf16)
        du = jax.vjp(gelu_exact, pre_act)[1](dot_nt(dm, wu))[0].astype(bf16)
        grad_normed = grad_second + dot_nt(du, wi)
        grad_first, g1_grad, s1_grad = jax.vjp(layer_norm, first_sum, g1, s1)[1](grad_normed)
        dp = grad_first.astype(bf16)
        da = dot_nt(dp, wo).astype(bf16).reshape(local, H, HD)
        dprob = jnp.einsum("qhd,khd->hqk", da, vh, preferred_element_type=f32)
        ds = (prob * (dprob - jnp.sum(prob * dprob, axis=-1, keepdims=True))).astype(bf16)
        dq = (jnp.einsum("hqk,khd->qhd", ds, kh, preferred_element_type=f32) * scale).reshape(local, D).astype(bf16)
        dk = (jnp.einsum("hqk,qhd->khd", ds, qh, preferred_element_type=f32) * scale).reshape(-1, D)
        dv = jnp.einsum("hqk,qhd->khd", low, da, preferred_element_type=f32).reshape(-1, D)
        dk, dv = (lax.psum_scatter(a.astype(bf16), "ctx", scatter_dimension=0, tiled=True).astype(bf16) for a in (dk, dv))
        input_grad = grad_first + dot_nt(dq, wq) + dot_nt(dk, wk) + dot_nt(dv, wv)
        outs.append((output, input_grad))
        here = (
            dot_tn(x, dq), column_sums(dq), dot_tn(x, dk), dot_tn(x, dv), column_sums(dv), dot_tn(attended, dp),
            column_sums(dp), g1_grad, s1_grad, dot_tn(normed_low, du), column_sums(du), dot_tn(activated, dm),
            column_sums(dm), g2_grad, s2_grad,
        )
        sums = here if sums is None else tuple(a + b for a, b in zip(sums, here))
    grads = tuple(lax.psum_scatter(g, both, scatter_dimension=0, tiled=True) for g in sums)
    logit_maxima = lax.pmax(top, both)
    rank = lax.axis_index(both)
    clipped = clip_outputs(logit_maxima, threshold, query_weight, query_bias, key_weight, rank)
    return (jnp.stack([o for o, _ in outs]), jnp.stack([g for _, g in outs]), *grads, *clipped, logit_maxima)


def solution(mesh):
    both = P(("dp", "ctx"))
    rows = P(("dp", "ctx"), None)
    tokens = P("dp", "ctx", None)
    in_specs = (
        tokens, tokens, rows, both, rows, rows, both, rows, both, both, both, rows, both, rows, both, both, both,
        P("dp"), P("dp", None, None, None), P(),
    )
    out_specs = (
        tokens, tokens, rows, both, rows, rows, both, rows, both, both, both, rows, both, rows, both, both, both,
        rows, both, rows, P(),
    )
    dp, ctx = mesh.shape["dp"], mesh.shape["ctx"]
    pieces = dp * ctx
    fits = ctx == 2 and dp % 4 == 0 and D % (8 * pieces) == 0 and FF // pieces <= 128

    def step(*args):
        if fits and args[0].shape[0] == 1:
            return fast_shards(dp // 4, *args)
        return general_shards(*args)

    return jax.shard_map(step, mesh=mesh, in_specs=in_specs, out_specs=out_specs, check_vma=False)
```

```python
import functools

import jax
import jax.numpy as jnp
import numpy as np
from jax import lax
from jax.experimental import pallas as pl
from jax.experimental.pallas import tpu as pltpu
from jax.sharding import PartitionSpec as P

H = 12
HD = 64
BLK = 64
LEN = 1024
NB = 16
D = 768
FF = 3072

norm_eps = 1e-12
neg_large = -1e30
bf16 = jnp.bfloat16
f32 = jnp.float32
ANY = pl.BlockSpec(memory_space=pl.ANY)
INVMEM = pl.BlockSpec(memory_space=pltpu.VMEM)
INSMEM = pl.BlockSpec(memory_space=pltpu.SMEM)
MESH = pl.DeviceIdType.MESH


def dot_nn(a, b):
    return jnp.dot(a, b, preferred_element_type=f32)


def dot_nt(a, b):
    return lax.dot_general(a, b, (((1,), (1,)), ((), ())), preferred_element_type=f32)


def dot_tn(a, b):
    return lax.dot_general(a, b, (((0,), (0,)), ((), ())), preferred_element_type=f32)


def ds128(index, width):
    return pl.ds(pl.multiple_of(index * width, width), width)


class Place:
    def __init__(self, nz):
        self.nz = nz
        dp = lax.axis_index("dp")
        self.y = lax.axis_index("ctx")
        self.c = lax.rem(dp, 2)
        self.x = lax.rem(lax.div(dp, 2), 2)
        self.z = lax.div(dp, 4)

    def at(self, z=None, x=None, c=None, y=None):
        z = self.z if z is None else z
        x = self.x if x is None else x
        c = self.c if c is None else c
        y = self.y if y is None else y
        return ((z * 2 + x) * 2 + c, y)

    def z_off(self, k):
        return lax.rem(self.z + k, self.nz)

    def along(self, axis):
        if axis == "z":
            return [self.at(z=self.z_off(k)) for k in range(1, self.nz)]
        return [self.at(x=1 - self.x) if axis == "x" else self.at(y=1 - self.y)]

    def peers(self):
        return (
            [self.at(z=self.z_off(k)) for k in range(1, self.nz)]
            + [self.at(x=1 - self.x), self.at(y=1 - self.y), self.at(c=1 - self.c)]
        )


def entry_barrier(place):
    barrier = pltpu.get_barrier_semaphore()
    peers = place.peers()
    for peer in peers:
        pl.semaphore_signal(barrier, inc=1, device_id=peer, device_id_type=MESH)
    pl.semaphore_wait(barrier, len(peers))


class Conditional:
    def __init__(self, copy, sends, receives):
        self.copy, self.sends, self.receives = copy, sends, receives

    def start(self):
        pl.when(self.sends)(self.copy.start)

    def wait_recv(self):
        pl.when(self.receives)(self.copy.wait_recv)

    def wait_send(self):
        pl.when(self.sends)(self.copy.wait_send)


class Remote:
    def __init__(self, send_sems, recv_sems):
        self.send_sems, self.recv_sems, self.used, self.copies = send_sems, recv_sems, 0, []

    def make(self, src, dst, peer, sends=None, receives=None):
        k = self.used
        self.used += 1
        copy = pltpu.make_async_remote_copy(
            src_ref=src, dst_ref=dst, send_sem=self.send_sems.at[k], recv_sem=self.recv_sems.at[k],
            device_id=peer, device_id_type=MESH,
        )
        if sends is not None:
            copy = Conditional(copy, sends, receives)
        self.copies.append(copy)
        return copy

    def finish(self):
        for copy in self.copies:
            copy.wait_send()


class Stripe:
    def __init__(self):
        self.stages, self.awaited, self.at = [], {}, 0

    def take(self, n):
        pass

    def step(self):
        n = self.at
        if n > 0:
            for copy in self.awaited.get(n, self.stages[n - 1]):
                copy.wait_recv()
            self.take(n - 1)
        if n < len(self.stages):
            for copy in self.stages[n]:
                copy.start()
        self.at = n + 1


class GatherStripe(Stripe):
    def __init__(self, remote, place, buf, cols, order):
        super().__init__()
        have = {"z": place.z, "x": place.x, "y": place.y}
        for axis in order:
            ref = buf.at[have["z"], have["x"], place.c, have["y"], :, cols]
            if axis == "z" and place.nz == 4:
                self.along_line(remote, place, lambda z: buf.at[z, have["x"], place.c, have["y"], :, cols])
            else:
                self.stages.append([remote.make(ref, ref, peer) for peer in place.along(axis)])
                if axis == "z":
                    self.stages.append([])
                    self.awaited[len(self.stages) - 1] = []
                    self.awaited[len(self.stages)] = self.stages[-2]
            have[axis] = slice(None)
        ref = buf.at[:, :, place.c, :, :, cols]
        self.stages.append([remote.make(ref, ref, place.at(c=1 - place.c))])

    def along_line(self, remote, place, block):
        z, mine = place.z, block(place.z)
        moves = [
            remote.make(mine, mine, place.at(z=lax.rem(z + 2, 4)), z < 2, z >= 2),
            remote.make(mine, mine, place.at(z=lax.rem(z + 2, 4)), z >= 2, z < 2),
            remote.make(mine, mine, place.at(z=lax.rem(z + 1, 4)), z < 3, z > 0),
            remote.make(mine, mine, place.at(z=lax.rem(z + 3, 4)), z > 0, z < 3),
        ]
        onward = [
            remote.make(block(0), block(0), place.at(z=lax.rem(z + 1, 4)), z == 2, z == 3),
            remote.make(block(3), block(3), place.at(z=lax.rem(z + 3, 4)), z == 1, z == 0),
        ]
        self.stages += [moves, onward]
        self.awaited[len(self.stages) - 1] = moves[:2]
        self.awaited[len(self.stages)] = moves[2:] + onward


class GatherTile(Stripe):
    def __init__(self, remote, place, buf):
        super().__init__()
        z, x, c, y = place.z, place.x, place.c, place.y
        for ref, peers in (
            (buf.at[z, x, c, y], place.along("z")),
            (buf.at[:, x, c, y], place.along("x")),
            (buf.at[:, :, c, y], place.along("y")),
            (buf.at[:, :, c], [place.at(c=1 - c)]),
        ):
            self.stages.append([remote.make(ref, ref, peer) for peer in peers])


class ScatterStripe(Stripe):
    def __init__(self, remote, place, g, cols, order, bufs, out):
        super().__init__()
        self.place, self.g, self.cols, self.order, self.bufs, self.out = place, g, cols, order, bufs, out
        own = {"z": place.z, "x": place.x, "y": place.y}
        have = {"z": slice(None), "x": slice(None), "y": slice(None)}
        ref = g.at[:, :, 1 - place.c, :, :, cols]
        self.stages.append([remote.make(ref, bufs[0], place.at(c=1 - place.c))])
        for n, axis in enumerate(order):
            made = []
            for k, peer in enumerate(place.along(axis)):
                there = dict(have)
                there[axis] = place.z_off(k + 1) if axis == "z" else 1 - own[axis]
                ref = g.at[there["z"], there["x"], place.c, there["y"], :, cols]
                made.append(remote.make(ref, bufs[n + 1].at[k] if axis == "z" else bufs[n + 1], peer))
            self.stages.append(made)
            have[axis] = own[axis]

    def take(self, n):
        place, g, cols, buf = self.place, self.g, self.cols, self.bufs[n]
        axis = self.order[n - 1] if n > 0 else "c"
        still = self.order[n:]
        sizes = {"z": place.nz, "x": 2, "y": 2}
        names = [name for name in "zxy" if name in still]
        count = 1
        for name in names:
            count *= sizes[name]

        def add(k, last):
            here = {"z": place.z, "x": place.x, "y": place.y}
            left = k
            for name in reversed(names):
                here[name] = lax.rem(left, sizes[name])
                left = lax.div(left, sizes[name])
            index = tuple(here[name] for name in names)
            spot = (here["z"], here["x"], place.c, here["y"], slice(None), cols)
            if axis != "z" and not last:
                g[spot] = g[spot] + buf[index]
                return
            total = g[spot].astype(f32)
            for part in range(place.nz - 1) if axis == "z" else (None,):
                total = total + buf[index if part is None else (part, *index)].astype(f32)
            if last:
                self.out[:, cols] = total
            else:
                g[spot] = total.astype(bf16)

        if not names:
            add(0, True)
        elif count <= 2:
            for k in range(count):
                add(k, False)
        else:

            def twice(k, carry):
                add(2 * k, False)
                add(2 * k + 1, False)
                return carry

            lax.fori_loop(0, count // 2, twice, 0)


def scatter_buffers(nz, rows, width, order):
    sizes = {"z": nz, "x": 2, "y": 2}
    made = [((nz, 2, 2, rows, width), bf16)]
    for n, axis in enumerate(order):
        left = [sizes[name] for name in "zxy" if name in order[n + 1 :]]
        made.append((((nz - 1,) if axis == "z" else ()) + (*left, rows, width), bf16))
    return made


class SmallSums(Stripe):
    def __init__(self, remote, place, t, bufs):
        super().__init__()
        z, x, c, y = place.z, place.x, place.c, place.y
        rc, ry, rx, rz = bufs
        self.place, self.t, self.bufs = place, t, bufs
        self.stages = [
            [remote.make(t.at[:, :, 1 - c], rc, place.at(c=1 - c))],
            [remote.make(t.at[:, :, c, 1 - y], ry, place.at(y=1 - y))],
            [remote.make(t.at[:, 1 - x, c, y], rx, place.at(x=1 - x))],
            [remote.make(t.at[place.z_off(k + 1), x, c, y], rz.at[k], peer) for k, peer in enumerate(place.along("z"))],
        ]

    def take(self, n):
        place, t = self.place, self.t
        rc, ry, rx, rz = self.bufs
        z, x, c, y = place.z, place.x, place.c, place.y
        if n == 0:
            t[:, :, c] = t[:, :, c] + rc[...]
        elif n == 1:
            t[:, :, c, y] = t[:, :, c, y] + ry[...]
        elif n == 2:
            t[:, x, c, y] = t[:, x, c, y] + rx[...]
        else:
            total = t[z, x, c, y]
            for k in range(place.nz - 1):
                total = total + rz[k]
            t[z, x, c, y] = total


def small_buffers(nz):
    return [((nz, 2, 2, 16, 128), f32), ((nz, 2, 16, 128), f32), ((nz, 16, 128), f32), ((nz - 1, 16, 128), f32)]


class TopOfAll(Stripe):
    def __init__(self, remote, place, top, tops):
        super().__init__()
        self.top, self.tops, self.slots, slot = top, tops, [], 0
        for n, peers in enumerate(([place.at(c=1 - place.c)], place.along("y"), place.along("x"), place.along("z"))):
            self.slots.append(list(range(slot, slot + len(peers))))
            self.stages.append([remote.make(top.at[n], tops.at[slot + k], peer) for k, peer in enumerate(peers)])
            slot += len(peers)

    def take(self, n):
        best = self.top[n]
        for slot in self.slots[n]:
            best = jnp.maximum(best, self.tops[slot])
        self.top[n + 1] = best


class Script:
    def __init__(self, plan, stripes, swap):
        self.plan, self.stripes, self.swap, self.spent = plan, stripes, swap, 0

    def point(self):
        for item in self.plan[self.spent]:
            if item < 0:
                self.swap.start()
            else:
                self.stripes[item].step()
        self.spent += 1

    def points(self, index, first, count):
        for k in range(count):
            pl.when(index == first + k)(self.point)

    def close(self):
        assert self.spent == len(self.plan)
        assert all(s.at == len(s.stages) + 1 for s in self.stripes)


VMEM_BYTES = 60 << 20
GATHER_ITEMS = (
    (0, 0, 384, "yzx"), (0, 384, 384, "yzx"), (0, 768, 384, "yzx"), (0, 1152, 384, "zxy"), (0, 1536, 256, "yzx"),
    (0, 1792, 256, "yzx"), (0, 2048, 256, "yzx"), (0, 2304, 384, "zyx"), (0, 2688, 384, "xzy"), (1, 0, 384, "zxy"),
    (1, 384, 384, "yzx"), (1, 768, 768, "zxy"), (1, 1536, 256, "zyx"), (1, 1792, 256, "yzx"), (1, 2048, 256, "yzx"),
    (1, 2304, 384, "zxy"), (1, 2688, 384, "zyx"), (2, 0, 256, "xzy"), (2, 256, 128, "zyx"), (2, 384, 128, "yzx"),
    (2, 512, 128, "xzy"), (2, 640, 128, "yzx"),
)
GATHER_PLAN = (
    (0, 1, 22, 2, 3, 4, 5, 6, -1),
    (0, 1, 2, 4, 22, 3, 5, 6, 22, 3, 0, 3, 0, 1, 2, 7, 8, 9, 11, 1, 2, 0, 8, 4, 0, 10, 4, 1, 5, 6, 7, 5, 1, 12, 6, 22, 7, 9, 2, 22, 13),
    (11,), (2, 4, 8, 9, 14, 3, 10, 11, 12, 4, 15, 5, 8, 7, 13, 3, 16), (5, 12, 14, 18, 6, 9, 6, 17), (8, 10), (12, 15),
    (8, 11, 10, 13, 15, 19), (9, 13, 14, 16), (7, 14, 18, 17), (9, 16, 18, 21), (7, 12), (11, 12, 19, 20), (10, 16),
    (11, 15, 17), (10, 13, 18, 21), (14,), (13, 14, 15, 17, 20), (19,), (15, 16, 21), (19,), (16, 18, 21, 20), (), (),
    (18, 20), (17,), (), (19,), (), (17,), (19, 20), (21,), (), (21, 20), (), (), (),
)
SCATTER_ITEMS = (
    (2, 0, 128, "xzy"), (2, 128, 128, "yxz"), (2, 256, 256, "yzx"), (2, 512, 128, "xzy"), (2, 640, 128, "yxz"),
    (1, 0, 768, "xyz"), (1, 768, 768, "yxz"), (1, 1536, 768, "xyz"), (1, 2304, 768, "xyz"), (0, 0, 768, "xzy"),
    (0, 768, 384, "xzy"), (0, 1152, 384, "xyz"), (0, 1536, 384, "xzy"), (0, 1920, 384, "xyz"), (0, 2304, 768, "yxz"),
)
SCATTER_PLAN = (
    (), (), (), (0, 1), (2,), (0, 1, 3, 4), (2, 3, 4, 0, 1), (5, 15), (6,), (7,), (8, 5, 15), (3, 6, 0), (), (1, 7), (8, 2),
    (), (), (4, 5, 15), (3,), (1, 14), (0, 6, 7), (14,), (2, 3, 5, 9), (8, 7), (4, 15, 9), (6,), (2, 5, 14), (7, -1),
    (4, 15, 8), (9,), (6, 10, 11), (14, 10), (11,), (8, 12, 13), (10, 16), (12, 13), (11, 16),
    (9, 14, 12, 11, 16, 13, 9, 10, 16, 12, 13, 10, 11, 12, 16, 13),
)

def layer_norm_parts(rows):
    centre = rows - jnp.mean(rows, axis=-1, keepdims=True)
    spread = jnp.mean(centre * centre, axis=-1, keepdims=True)
    inverse = lax.rsqrt(spread + norm_eps)
    return centre * inverse, inverse


def head_lanes(rows, half):
    lane = lax.broadcasted_iota(jnp.int32, rows.shape, 1)
    return jnp.where((lane >= HD) == (half == 1), rows, jnp.zeros_like(rows))


def key_structure(local, y, length):
    lane = lax.broadcasted_iota(jnp.int32, (2 * local, 128), 1)
    row = lax.broadcasted_iota(jnp.int32, (2 * local, 128), 0)
    position = jnp.where(row < local, row + y * local, row - y * local)
    own = lane == lax.shift_right_logical(position, 6)
    beyond = (lane == NB) & (position >= length)
    return jnp.where(own | beyond | ((lane > NB) & (lane < NB + 4)), 1.0, 0.0).astype(bf16)


def head_rows(rows, half):
    row = lax.broadcasted_iota(jnp.int32, rows.shape, 0)
    return jnp.where((row >= HD) == (half == 1), rows, jnp.zeros_like(rows))


def in_three(values):
    high = values.astype(bf16)
    rest = values - high.astype(f32)
    middle = rest.astype(bf16)
    return high, middle, (rest - middle.astype(f32)).astype(bf16)


def with_rows(base, values):
    row = lax.broadcasted_iota(jnp.int32, base.shape, 0)
    for k, part in enumerate(in_three(-values)):
        base = base + jnp.where(row == NB + 1 + k, part.astype(f32), 0.0)
    return base.astype(bf16)


def spread_vectors(tiles, width, pieces):
    rows = tiles.shape[1]
    total = pieces * width
    lane = lax.broadcasted_iota(jnp.int32, (128, total), 1).astype(f32)
    row = lax.broadcasted_iota(jnp.int32, (128, total), 0).astype(f32)
    owner = jnp.floor((lane + 0.5) * (1.0 / width))
    chooser = jnp.where(lane - owner * width == row, 1.0, 0.0).astype(bf16)
    wide = dot_nn(tiles.reshape(pieces * rows, 128), chooser).reshape(pieces, rows, total)
    lane3 = lax.broadcasted_iota(jnp.int32, (pieces, rows, total), 2).astype(f32)
    piece3 = lax.broadcasted_iota(jnp.int32, (pieces, rows, total), 0).astype(f32)
    mine = jnp.floor((lane3 + 0.5) * (1.0 / width)) == piece3
    return jnp.sum(jnp.where(mine, wide, 0.0), axis=0)


def forward_kernel(
    nz, local, length_ref, random_ref, x_hbm, wq, wk, wv, wo, wi, wu, v0, v1, v2, v3, v4, v5, v6, v7, v8,
    out_hbm, r1_hbm, r2_hbm, gp_hbm, gt_hbm, n1t_hbm, at_hbm, atf_hbm, q_hbm, qt_hbm, k_hbm, kt_hbm, v_hbm, xt_hbm, lse_hbm,
    top_hbm, wa_hbm, wi_hbm, wu_hbm, vec_hbm, mask_hbm,
    WA, WI, WU, SM, XF, XT, Q, QT, K, KT, V, VT, AT, ATF, R1, R2, N1L, N1T, U, GP, G, GT, E, VEC, IB, LSE, TOP, TT, OUT, MASK, *rest,
):
    place = Place(nz)
    z, x, c, y = place.z, place.x, place.c, place.y
    small, (send_sems, recv_sems, local_sems, out_sems) = rest[:9], rest[9:]
    remote = Remote(send_sems, recv_sems)
    mine = (z, x, c, y)
    locals_ = list(zip((v0, v1, v2, v3, v4, v5, v6, v7, v8), small))
    locals_.append((x_hbm, XF.at[0]))
    for g in range(3):
        for n, w in enumerate((wq, wk, wv)):
            lo = g * D + n * 256
            locals_.append((w.at[:, g * 256 : (g + 1) * 256], WA.at[(*mine, slice(None), slice(lo, lo + 256))]))
    locals_ += [(wo, WA.at[(*mine, slice(None), slice(3 * D, 4 * D))]), (wi, WI.at[mine]), (wu, WU.at[mine])]
    locals_ = [pltpu.make_async_copy(src, dst, local_sems.at[k]) for k, (src, dst) in enumerate(locals_)]
    for copy in locals_:
        copy.start()
    TT[...] = jnp.zeros((16, 128), f32)
    for n, v in enumerate(small):
        locals_[n].wait()
        TT[n : n + 1, 0 : v.shape[1]] = v[...].astype(f32)
    SM[mine] = TT[...].astype(bf16)
    entry_barrier(place)
    for copy in locals_[9:]:
        copy.wait()

    outs = []

    def put(src, dst):
        copy = pltpu.make_async_copy(src, dst, out_sems.at[len(outs)])
        copy.start()
        outs.append(copy)

    swap = remote.make(XF.at[0], XF.at[1], place.at(y=1 - y))
    stripes = [
        GatherStripe(remote, place, (WA, WI, WU)[buf], slice(lo, lo + width), order) for buf, lo, width, order in GATHER_ITEMS
    ]
    stripes.append(GatherTile(remote, place, SM))
    script = Script(GATHER_PLAN, stripes, swap)
    script.point()
    length = length_ref[0]
    E[...] = key_structure(local, y, length)
    fill_masks(MASK, random_ref, y * (local // BLK), length)
    put(MASK, mask_hbm)
    XT[:, :local] = XF[0].T
    script.point()

    tiles = SM[...].reshape(-1, 16, 128)
    pieces = tiles.shape[0]
    VEC[...] = spread_vectors(tiles, D // pieces, pieces)
    IB[...] = spread_vectors(tiles[:, 8:16, :], FF // pieces, pieces)
    put(VEC, vec_hbm)
    script.point()
    position = y * local + lax.broadcasted_iota(jnp.int32, (1, local), 1)
    live = position < length

    def put_columns(buf, dst, lo, width):
        put(buf.at[:, :, :, :, :, lo : lo + width], dst.at[:, :, :, :, :, lo : lo + width])

    def wide(buf, lo, width):
        return buf[:, :, :, :, :, lo : lo + width].reshape(-1, width)

    for g in range(3):
        cols = slice(g * 256, (g + 1) * 256)
        put_columns(WA, wa_hbm, g * D, D)
        own = dot_nn(XF[0], wide(WA, g * D, D))
        q = ((own[:, :256] + VEC[0:1, cols]).astype(bf16).astype(f32) * (HD**-0.5)).astype(bf16)
        Q[:, cols] = q
        QT[cols, :] = q.T
        K[:local, cols] = own[:, 256:512].astype(bf16)
        values = (own[:, 512:] + VEC[1:2, cols]).astype(bf16)
        V[:local, cols] = values
        VT[cols, :local] = values.T
        script.point()
    put(Q, q_hbm)
    put(QT, qt_hbm)
    swap.wait_recv()
    for g in range(3):
        cols = slice(g * 256, (g + 1) * 256)
        theirs = dot_nn(XF[1], wide(WA, g * D + 256, 512))
        K[local:, cols] = theirs[:, :256].astype(bf16)
        values = (theirs[:, 256:] + VEC[1:2, cols]).astype(bf16)
        V[local:, cols] = values
        VT[cols, local:] = values.T
        script.point()

        def head_step(h, carry):
            lanes = ds128(lax.div(h, 2), 128)
            half = lax.rem(h, 2)
            own = pl.ds(pl.multiple_of(h * HD, HD), HD)
            left = jnp.concatenate([K[:, lanes], E[...]], axis=1)
            right = jnp.concatenate(
                [head_rows(QT[lanes, :], half), MASK[h], jnp.zeros((128 - 32, local), bf16)], axis=0
            )
            for part in range(local // 256):
                cols = slice(part * 256, (part + 1) * 256)
                scores = dot_nn(left, right[:, cols])
                top = jnp.max(scores, axis=0, keepdims=True)
                exponent = jnp.exp(scores - top)
                total = jnp.sum(exponent, axis=0, keepdims=True)
                low = (exponent * (1.0 / total)).astype(bf16)
                mixture = dot_nn(VT[own, :], low)
                ATF[own, cols] = mixture
                AT[own, cols] = mixture.astype(bf16)
                LSE[h, :, cols] = top + jnp.log(total)
                TOP[h, :, cols] = jnp.where(live[:, cols], top, neg_large)
            script.points(h, 4 * g, 4)
            return carry

        lax.fori_loop(4 * g, 4 * g + 4, head_step, 0)
    put(K, k_hbm)
    put(V, v_hbm)
    put(LSE, lse_hbm)
    TT[...] = jnp.zeros((16, 128), f32) + neg_large
    TT[0:H, :] = jnp.broadcast_to(jnp.max(TOP[:, 0, :], axis=1, keepdims=True), (H, 128))
    put(TT, top_hbm)
    put(AT, at_hbm)
    put(ATF, atf_hbm)
    put_columns(WA, wa_hbm, 3 * D, D)
    R1[...] = dot_nn(AT[...].T, wide(WA, 3 * D, D))
    script.point()

    def first_norm(k, carry):
        rows = ds128(k, 64)
        summed = XF[0, rows, :].astype(f32) + R1[rows, :] + VEC[2:3, :]
        R1[rows, :] = summed
        normal, _ = layer_norm_parts(summed)
        value = normal * VEC[3:4, :] + VEC[4:5, :]
        N1L[rows, :] = value.astype(bf16)
        R2[rows, :] = value + VEC[5:6, :]
        return carry

    lax.fori_loop(0, local // 64, first_norm, 0)
    put(R1, r1_hbm)
    script.point()
    N1T[...] = N1L[...].T
    put(N1T, n1t_hbm)
    XT[:, local:] = XF[1].T
    put(XT, xt_hbm)
    script.point()
    KT[...] = K[...].T
    put(KT, kt_hbm)
    script.point()
    for n in range(FF // D):
        cols = slice(n * D, (n + 1) * D)
        put_columns(WI, wi_hbm, n * D, D)
        U[...] = dot_nn(N1L[...], wide(WI, n * D, D)) + IB[0:1, cols]
        script.point()

        def activate(k, carry):
            rows = ds128(k, 16)
            u = U[rows, :]
            below = 0.5 * (1.0 + lax.erf(u * np.float32(0.5**0.5)))
            G[rows, cols] = (u * below).astype(bf16)
            GP[n, rows, :] = below + u * jnp.exp(-0.5 * u * u) * np.float32((2.0 * np.pi) ** -0.5)
            return carry

        lax.fori_loop(0, local // 16, activate, 0)
        put(GP.at[n], gp_hbm.at[n])
        GT[cols, :] = G[:, cols].T
        put(GT.at[cols, :], gt_hbm.at[cols, :])
        script.point()
    for n in range(3):
        cols = slice(n * 256, (n + 1) * 256)
        put_columns(WU, wu_hbm, n * 256, 256)
        R2[:, cols] += dot_nn(G[...], WU[:, :, :, :, :, cols].reshape(FF, 256))
        script.point()

    def second_norm(k, carry):
        rows = ds128(k, 64)
        normal, _ = layer_norm_parts(R2[rows, :])
        OUT[rows, :] = (normal * VEC[6:7, :] + VEC[7:8, :]).astype(bf16)
        return carry

    lax.fori_loop(0, local // 64, second_norm, 0)
    put(R2, r2_hbm)
    put(OUT, out_hbm)
    script.point()
    script.close()
    remote.finish()
    for copy in outs:
        copy.wait()


def copies_of(items, nz):
    return len(items) * (3 + max(6, nz - 1))


def run_forward(nz, x, weights, vectors, random_blocks, length):
    local = x.shape[0]
    wq, wk, wv, wo, wi, wu = weights
    grid = (nz, 2, 2, 2)
    rows, rows_u = wq.shape[0], wu.shape[0]
    seq = 2 * local
    blocks = FF // D
    outs = [
        ((local, D), bf16), ((local, D), f32), ((local, D), f32), ((blocks, local, D), f32), ((FF, local), bf16),
        ((D, local), bf16), ((D, local), bf16), ((D, local), f32), ((local, D), bf16), ((D, local), bf16), ((seq, D), bf16),
        ((D, seq), bf16), ((seq, D), bf16), ((D, seq), bf16), ((H, 1, local), f32), ((16, 128), f32),
        ((*grid, rows, 4 * D), bf16), ((*grid, rows, FF), bf16), ((*grid, rows_u, D), bf16), ((16, D), f32),
        ((H, 32, local), bf16),
    ]
    scratch = [
        ((*grid, rows, 4 * D), bf16), ((*grid, rows, FF), bf16), ((*grid, rows_u, D), bf16), ((*grid, 16, 128), bf16),
        ((2, local, D), bf16), ((D, seq), bf16), ((local, D), bf16), ((D, local), bf16), ((seq, D), bf16), ((D, seq), bf16),
        ((seq, D), bf16), ((D, seq), bf16), ((D, local), bf16), ((D, local), f32), ((local, D), f32), ((local, D), f32),
        ((local, D), bf16), ((D, local), bf16), ((local, D), f32), ((blocks, local, D), f32), ((local, FF), bf16),
        ((FF, local), bf16), ((seq, 128), bf16), ((16, D), f32), ((8, FF), f32), ((H, 1, local), f32), ((H, 1, local), f32),
        ((16, 128), f32), ((local, D), bf16), ((H, 32, local), bf16),
    ]
    scratch += [((1, v.shape[0]), bf16) for v in vectors]
    copies = copies_of(GATHER_ITEMS, nz) + 3 + (nz - 1) + 1
    return pl.pallas_call(
        functools.partial(forward_kernel, nz, local),
        out_shape=[jax.ShapeDtypeStruct(*o) for o in outs],
        in_specs=[INSMEM] * 2 + [ANY] * 16,
        out_specs=[ANY] * len(outs),
        scratch_shapes=[pltpu.VMEM(*s) for s in scratch]
        + [
            pltpu.SemaphoreType.DMA((copies,)),
            pltpu.SemaphoreType.DMA((copies,)),
            pltpu.SemaphoreType.DMA((22,)),
            pltpu.SemaphoreType.DMA((40,)),
        ],
        compiler_params=pltpu.CompilerParams(collective_id=1, has_side_effects=True, vmem_limit_bytes=VMEM_BYTES),
        name="gather_forward",
    )(length, random_blocks, x, wq, wk, wv, wo, wi, wu, *(v.reshape(1, -1) for v in vectors))


def compact_mask(random_here, length, first_block):
    blocks = random_here.shape[0]
    query = (first_block + jnp.arange(blocks, dtype=jnp.int32))[None, :, None]
    key = jnp.arange(NB, dtype=jnp.int32)[None, None, :]
    last = (length - 1) // BLK
    ok = (jnp.abs(query - key) <= 1) | (key == 0) | (key == last) | (query == 0) | (query == last)
    heads = jnp.transpose(random_here, (1, 0, 2))
    for k in range(heads.shape[2]):
        ok = ok | (heads[:, :, k : k + 1] == key)
    return jnp.where(ok, 0.0, neg_large).astype(f32)


def fill_masks(masks, random_ref, first_block, length):
    queries = masks.shape[2]
    row = lax.broadcasted_iota(jnp.int32, (32, queries), 0)
    here = lax.shift_right_logical(lax.broadcasted_iota(jnp.int32, (32, queries), 1), 6)
    one = lax.shift_right_logical(lax.broadcasted_iota(jnp.int32, (1, queries), 1), 6)
    block = here + first_block
    last = lax.shift_right_logical(length - 1, 6)
    fixed = (jnp.abs(block - row) <= 1) | (row == 0) | (row == last) | (block == 0) | (block == last) | (row > NB)
    base = jnp.where(fixed & (row != NB), 0.0, neg_large)

    def head(h, carry):
        mask = base
        for k in range(3):
            chosen = jnp.zeros((1, queries), jnp.int32)
            for b in range(queries // BLK):
                chosen = jnp.where(one == b, random_ref[h, k, first_block + b], chosen)
            mask = jnp.where((row == chosen) & (row < NB), 0.0, mask)
        masks[h] = mask.astype(bf16)
        return carry

    lax.fori_loop(0, H, head, 0)


def gather_vectors(rows, width, pieces):
    n, total = rows.shape
    if n == 1:
        lane2 = lax.broadcasted_iota(jnp.int32, (pieces, total), 1).astype(f32)
        piece2 = lax.broadcasted_iota(jnp.int32, (pieces, total), 0).astype(f32)
        mine = jnp.floor((lane2 + 0.5) * (1.0 / width)) == piece2
        spread = jnp.where(mine, rows, 0.0)
    else:
        lane3 = lax.broadcasted_iota(jnp.int32, (pieces, n, total), 2).astype(f32)
        piece3 = lax.broadcasted_iota(jnp.int32, (pieces, n, total), 0).astype(f32)
        mine = jnp.floor((lane3 + 0.5) * (1.0 / width)) == piece3
        spread = jnp.where(mine, rows[None], 0.0).reshape(pieces * n, total)
    lane = lax.broadcasted_iota(jnp.int32, (128, total), 1).astype(f32)
    row = lax.broadcasted_iota(jnp.int32, (128, total), 0).astype(f32)
    owner = jnp.floor((lane + 0.5) * (1.0 / width))
    chooser = jnp.where(lane - owner * width == row, 1.0, 0.0).astype(bf16)
    high, middle, lowest = in_three(spread)
    tiles = dot_nt(high, chooser) + (dot_nt(middle, chooser) + dot_nt(lowest, chooser))
    return tiles.reshape(pieces, n, 128)


def norm_back(normal, inverse, grads, gain):
    scaled = grads * gain
    first = jnp.mean(scaled, axis=-1, keepdims=True)
    second = jnp.mean(scaled * normal, axis=-1, keepdims=True)
    return inverse * (scaled - first - normal * second)


def row_sum(values):
    return jnp.sum(values, axis=0, keepdims=True)


def back_half(pair, local, own_keys, BQ, BD, Q, QT, DA, DAT, K, KT, V, E, PB, DS, DQF, DQT, DK, DV):
    keys = slice(0, local) if own_keys else slice(local, 2 * local)
    lanes = ds128(pair, 128)
    structure = E[keys, :]
    left = jnp.concatenate([K[keys, lanes], structure], axis=1)
    left_values = jnp.concatenate([V[keys, lanes], structure], axis=1)
    empty = jnp.zeros((128 - 32, local), bf16)
    for half in (0, 1):
        h = pair * 2 + half
        own = pl.ds(pl.multiple_of(h * HD, HD), HD)
        spot = slice(half * local, (half + 1) * local)
        right = jnp.concatenate([head_rows(QT[lanes, :], half), BQ[h], empty], axis=0)
        prob = jnp.exp(dot_nn(left, right))
        PB[:, spot] = prob.astype(bf16)
        right_values = jnp.concatenate([head_rows(DAT[lanes, :], half), BD[h], empty], axis=0)
        low = (prob * dot_nn(left_values, right_values)).astype(bf16)
        DS[:, spot] = low
        part = dot_nn(KT[own, keys], low)
        if own_keys:
            DQT[own, :] = ((DQF[own, :] + part) * (HD**-0.5)).astype(bf16)
        else:
            DQF[own, :] = part
    q_pair, a_pair = Q[:, lanes], DA[:, lanes]
    DK[keys, lanes] = dot_nn(DS[...], jnp.concatenate([head_lanes(q_pair, n) for n in (0, 1)], axis=0)).astype(bf16)
    DV[keys, lanes] = dot_nn(PB[...], jnp.concatenate([head_lanes(a_pair, n) for n in (0, 1)], axis=0)).astype(bf16)


def backward_kernel(
    nz, local, length_ref, cot_hbm, r1_hbm, r2_hbm, gp_hbm, gt_hbm, n1t_hbm, at_hbm, atf_hbm, q_hbm, qt_hbm,
    k_hbm, kt_hbm, v_hbm, xt_hbm, lse_hbm, top_hbm, wa_hbm, wi_hbm, wu_hbm, vec_hbm,
    mask_hbm, dx_hbm, taken_hbm, oa_hbm, oi_hbm, ou_hbm, os_hbm, ot_hbm, *rest,
):
    place = Place(nz)
    z, x, c, y = place.z, place.x, place.c, place.y
    GA, GI, GU, WA, T, TOP, TOPS, DP, AT, DR1, E, SUMS, ISUM, SEND, RECV, VEC, OA, OI, OU = rest[:19]
    used = 19
    bufs = []
    for _ in SCATTER_ITEMS:
        bufs.append(rest[used : used + 4])
        used += 4
    sbufs = rest[used : used + 4]
    send_sems, recv_sems, load_sems = rest[used + 4 :]
    blocks = FF // D
    pieces = nz * 8
    seq_len = 2 * local
    length = length_ref[0]
    loads = [0]

    def load(src, dst):
        copy = pltpu.make_async_copy(src, dst, load_sems.at[loads[0]])
        loads[0] += 1
        copy.start()
        return copy

    remote = Remote(send_sems, recv_sems)
    stripes = [
        ScatterStripe(remote, place, (GA, GI, GU)[buf], slice(lo, lo + width), order, bufs[n], (OA, OI, OU)[buf])
        for n, (buf, lo, width, order) in enumerate(SCATTER_ITEMS)
    ]
    stripes += [TopOfAll(remote, place, TOP, TOPS), SmallSums(remote, place, T, sbufs)]
    swap = remote.make(SEND, RECV, place.at(y=1 - y))
    script = Script(SCATTER_PLAN, stripes, swap)
    grid = (nz, 2, 2, 2)
    SUMS[...] = jnp.zeros_like(SUMS)
    ISUM[...] = jnp.zeros_like(ISUM)

    def first_stage(COT, R2, R1, DM, GT, DU, GP, N1T, WUS, WIS):
        l_r2, l_cot, l_vec = load(r2_hbm, R2), load(cot_hbm, COT), load(vec_hbm, VEC)
        l_gt = load(gt_hbm, GT)
        l_wu, l_gp = [], []
        for n in range(2):
            l_wu.append(load(wu_hbm.at[n], WUS.at[n]))
            l_gp.append(load(gp_hbm.at[n], GP.at[n]))

        def wi_of(n):
            return wi_hbm.at[:, :, :, :, :, n * D : (n + 1) * D]

        script.point()
        entry_barrier(place)
        E[...] = key_structure(local, y, length)
        l_r2.wait()
        l_cot.wait()
        l_vec.wait()
        script.point()

        def second_norm(k, carry):
            rows = ds128(k, 64)
            normal, inverse = layer_norm_parts(R2[rows, :])
            position = y * local + k * 64 + lax.broadcasted_iota(jnp.int32, (64, D), 0)
            grads = jnp.where(position < length, COT[rows, :].astype(f32), 0.0)
            through = norm_back(normal, inverse, grads, VEC[6:7, :])
            R2[rows, :] = through
            low = through.astype(bf16)
            DM[rows, :] = low
            SUMS[5:6, :] += row_sum(low.astype(f32))
            SUMS[6:7, :] += row_sum(grads * normal)
            SUMS[7:8, :] += row_sum(grads)
            return carry

        lax.fori_loop(0, local // 64, second_norm, 0)
        script.point()
        l_gt.wait()
        for n in range(3):
            cols = slice(n * 256, (n + 1) * 256)

            def outer_grad(zz, carry):
                rows = ds128(zz, FF // nz)
                made = dot_nn(GT[rows, :], DM[:, cols]).astype(bf16)
                GU[zz, :, :, :, :, cols] = made.reshape(2, 2, 2, -1, 256)
                return carry

            lax.fori_loop(0, nz, outer_grad, 0)
            script.point()
        for n in range(blocks):
            l_wu[n].wait()
            l_gp[n].wait()
            grads = dot_nt(DM[...], WUS[n % 2].reshape(D, D)) * GP[n % 2]
            low = grads.astype(bf16)
            DU[n] = low
            ISUM[0:1, n * D : (n + 1) * D] = row_sum(low.astype(f32))
            if n + 2 < blocks:
                l_wu.append(load(wu_hbm.at[n + 2], WUS.at[n % 2]))
                l_gp.append(load(gp_hbm.at[n + 2], GP.at[n % 2]))
        l_top, l_n1t = load(top_hbm, TOP.at[0]), load(n1t_hbm, N1T)
        l_wi = [load(wi_of(0), WIS.at[0]), load(wi_of(1), WIS.at[1])]
        l_r1, l_at, l_wa = load(r1_hbm, R1), load(at_hbm, AT), load(wa_hbm, WA)
        wide = gather_vectors(ISUM[...], FF // pieces, pieces).reshape(*grid, 1, 128)
        T[:, :, :, :, 8:16, :] = jnp.broadcast_to(wide, (*grid, 8, 128))
        script.point()
        l_top.wait()
        l_n1t.wait()
        for n in range(blocks):
            made = dot_nn(N1T[...], DU[n]).astype(bf16)
            GI[:, :, :, :, :, n * D : (n + 1) * D] = made.reshape(*grid, -1, D)
            script.point()
        for n in range(blocks):
            l_wi[n].wait()
            R2[...] += dot_nt(DU[n], WIS[n % 2].reshape(D, D))
            if n + 2 < blocks:
                l_wi.append(load(wi_of(n + 2), WIS.at[n % 2]))
            script.point()
        l_r1.wait()

        def first_norm(k, carry):
            rows = ds128(k, 64)
            normal, inverse = layer_norm_parts(R1[rows, :])
            grads = R2[rows, :]
            through = norm_back(normal, inverse, grads, VEC[3:4, :])
            DR1[rows, :] = through
            low = through.astype(bf16)
            DP[rows, :] = low
            SUMS[2:3, :] += row_sum(low.astype(f32))
            SUMS[3:4, :] += row_sum(grads * normal)
            SUMS[4:5, :] += row_sum(grads)
            return carry

        lax.fori_loop(0, local // 64, first_norm, 0)
        script.point()
        l_at.wait()
        l_wa.wait()

    pl.run_scoped(
        first_stage,
        pltpu.VMEM((local, D), bf16), pltpu.VMEM((local, D), f32), pltpu.VMEM((local, D), f32), pltpu.VMEM((local, D), bf16),
        pltpu.VMEM((FF, local), bf16), pltpu.VMEM((blocks, local, D), bf16), pltpu.VMEM((2, local, D), f32),
        pltpu.VMEM((D, local), bf16), pltpu.VMEM((2, 2, 2, 2, FF // (nz * 8), D), bf16),
        pltpu.VMEM((2, *grid, D // (nz * 8), D), bf16),
    )

    def second_stage(Q, QT, K, KT, V, XT, LSE, BQ, BD, DA, DAT, PB, DS, DQF, DQT, DQ, DK, DV):
        pairs = ((lse_hbm, LSE), (atf_hbm, DQF), (mask_hbm, BQ), (k_hbm, K), (q_hbm, Q), (qt_hbm, QT), (kt_hbm, KT), (v_hbm, V), (xt_hbm, XT))
        waits = [load(s, d) for s, d in pairs]
        made = dot_nn(AT[...], DP[...]).astype(bf16)
        GA[:, :, :, :, :, 3 * D : 4 * D] = made.reshape(*grid, -1, D)
        script.point()
        DAT[...] = dot_nt(WA[:, :, :, :, :, 3 * D : 4 * D].reshape(D, D), DP[...]).astype(bf16)
        DA[...] = DAT[...].T
        for wait in waits[:3]:
            wait.wait()

        def prepare(h, carry):
            own = pl.ds(pl.multiple_of(h * HD, HD), HD)
            delta = row_sum(DAT[own, :].astype(f32) * DQF[own, :])
            BD[h] = with_rows(jnp.zeros((32, local), f32), delta)
            BQ[h] = with_rows(BQ[h].astype(f32), LSE[h])
            return carry

        lax.fori_loop(0, H, prepare, 0)
        for wait in waits[3:]:
            wait.wait()
        script.point()

        def halves(own_keys, g):
            def pair_step(pair, carry):
                back_half(pair, local, own_keys, BQ, BD, Q, QT, DA, DAT, K, KT, V, E, PB, DS, DQF, DQT, DK, DV)
                script.points(pair, 2 * g, 2)
                return carry

            lax.fori_loop(2 * g, 2 * g + 2, pair_step, 0)

        def group(g):
            lo = g * D
            cols = slice(g * 256, (g + 1) * 256)
            dq = DQT[cols, :].T
            DQ[:, cols] = dq
            SUMS[0:1, cols] = row_sum(dq.astype(f32))
            SUMS[1:2, cols] = row_sum(DV[:, cols].astype(f32))
            for n, made in enumerate(
                (dot_nn(XT[:, :local], dq), dot_nn(XT[...], DK[:, cols]), dot_nn(XT[...], DV[:, cols]))
            ):
                GA[:, :, :, :, :, lo + n * 256 : lo + (n + 1) * 256] = made.astype(bf16).reshape(*grid, -1, 256)
            script.point()

        halves(False, 0)
        halves(True, 0)
        group(0)
        halves(False, 1)
        halves(False, 2)
        groups = [slice(g * 256, (g + 1) * 256) for g in range(3)]
        theirs = jnp.concatenate([a[local:, cols] for cols in groups for a in (DK, DV)], axis=1)
        through = [WA[:, :, :, :, :, g * D + 256 : (g + 1) * D].reshape(D, 512) for g in range(3)]
        SEND[...] = dot_nt(theirs, jnp.concatenate(through, axis=1)).astype(bf16)
        script.point()
        halves(True, 1)
        group(1)
        halves(True, 2)
        group(2)
        T[:, :, :, :, 0:8, :] = gather_vectors(SUMS[0:8, :], D // pieces, pieces).reshape(*grid, 8, 128)
        script.point()
        for g in range(3):
            cols = slice(g * 256, (g + 1) * 256)
            ours = jnp.concatenate([DQ[:, cols], DK[:local, cols], DV[:local, cols]], axis=1)
            DR1[...] += dot_nt(ours, WA[:, :, :, :, :, g * D : (g + 1) * D].reshape(D, D))
            script.point()
        script.close()
        out = pltpu.make_async_copy(DR1, dx_hbm, load_sems.at[loads[0]])
        out.start()
        swap.wait_recv()
        taken = pltpu.make_async_copy(RECV, taken_hbm, load_sems.at[loads[0] + 1])
        taken.start()
        pairs = ((OA, oa_hbm), (OI, oi_hbm), (OU, ou_hbm), (T.at[z, x, c, y], os_hbm), (TOP.at[4], ot_hbm))
        ends = [pltpu.make_async_copy(s, d, load_sems.at[loads[0] + 2 + n]) for n, (s, d) in enumerate(pairs)]
        for end in ends:
            end.start()
        for end in (out, taken, *ends):
            end.wait()

    scoped = [
        ((local, D), bf16), ((D, local), bf16), ((seq_len, D), bf16), ((D, seq_len), bf16), ((seq_len, D), bf16),
        ((D, seq_len), bf16), ((H, 1, local), f32), ((H, 32, local), bf16), ((H, 32, local), bf16), ((local, D), bf16),
        ((D, local), bf16), ((local, 2 * local), bf16), ((local, 2 * local), bf16), ((D, local), f32), ((D, local), bf16),
        ((local, D), bf16), ((seq_len, D), bf16), ((seq_len, D), bf16),
    ]
    pl.run_scoped(second_stage, *(pltpu.VMEM(*s) for s in scoped))
    remote.finish()


def run_backward(nz, local, rows, rows_u, length, *arrays):
    grid = (nz, 2, 2, 2)
    seq = 2 * local
    outs = [((local, D), f32), ((local, D), bf16), ((rows, 4 * D), f32), ((rows, FF), f32), ((rows_u, D), f32)]
    outs += [((16, 128), f32)] * 2
    scratch = [
        ((*grid, rows, 4 * D), bf16), ((*grid, rows, FF), bf16), ((*grid, rows_u, D), bf16), ((*grid, rows, 4 * D), bf16),
        ((*grid, 16, 128), f32), ((5, 16, 128), f32), ((3 + nz - 1, 16, 128), f32),
        ((local, D), bf16), ((D, local), bf16), ((local, D), f32), ((seq, 128), bf16),
        ((8, D), f32), ((1, FF), f32), ((local, D), bf16), ((local, D), bf16),
        ((16, D), f32), ((rows, 4 * D), f32), ((rows, FF), f32), ((rows_u, D), f32),
    ]
    for buf, _, width, order in SCATTER_ITEMS:
        scratch += scatter_buffers(nz, rows_u if buf == 2 else rows, width, order)
    scratch += small_buffers(nz)
    copies = copies_of(SCATTER_ITEMS, nz) + 2 * (3 + nz - 1) + 1
    return pl.pallas_call(
        functools.partial(backward_kernel, nz, local),
        out_shape=[jax.ShapeDtypeStruct(*o) for o in outs],
        in_specs=[INSMEM] + [ANY] * len(arrays),
        out_specs=[ANY] * len(outs),
        scratch_shapes=[pltpu.VMEM(*s) for s in scratch]
        + [pltpu.SemaphoreType.DMA((copies,)), pltpu.SemaphoreType.DMA((copies,)), pltpu.SemaphoreType.DMA((40,))],
        compiler_params=pltpu.CompilerParams(collective_id=2, has_side_effects=True, vmem_limit_bytes=VMEM_BYTES),
        name="backward_scatter",
    )(length, *arrays)


def finish_kernel(
    threshold_ref, dx_hbm, taken_hbm, ga_hbm, gi_hbm, gu_hbm, gs_hbm, top_hbm, out_hbm, WQ, WK, BQ,
    o_out, o_dx, o_q, o_k, o_v, o_o, o_i, o_u, o_wq, o_wk, o_bq, o_top, *rest,
):
    v_hbm, (DX, TAKEN, GS, TOP, GA, GI, GU, OUT), (s_wq, s_wk, s_bq, s_top), o_vecs, sems = (
        rest[:9], rest[9:17], rest[17:21], rest[21:30], rest[30]
    )
    pairs = [(dx_hbm, DX), (taken_hbm, TAKEN), (ga_hbm, GA), (gi_hbm, GI), (gu_hbm, GU), (out_hbm, OUT), (gs_hbm, GS), (top_hbm, TOP)]
    loads = [pltpu.make_async_copy(src, dst, sems.at[n]) for n, (src, dst) in enumerate(pairs)]
    for copy in loads:
        copy.start()
    stores = []

    def put(src, dst):
        copy = pltpu.make_async_copy(src, dst, sems.at[len(loads) + len(stores)])
        copy.start()
        stores.append(copy)

    loads[0].wait()
    loads[1].wait()
    DX[...] = DX[...] + TAKEN[...].astype(f32)
    put(DX, o_dx)
    loads[2].wait()
    for g in range(3):
        for n, o in enumerate((o_q, o_k, o_v)):
            lo = g * D + n * 256
            put(GA.at[:, lo : lo + 256], o.at[:, g * 256 : (g + 1) * 256])
    put(GA.at[:, 3 * D : 4 * D], o_o)
    for copy, src, dst in zip(loads[3:6], (GI, GU, OUT), (o_i, o_u, o_out)):
        copy.wait()
        put(src, dst)
    loads[6].wait()
    loads[7].wait()
    for n, o in enumerate(o_vecs):
        o[...] = GS[n : n + 1, 0 : o.shape[1]]
    limit = threshold_ref[0].astype(f32) * 0.01
    top = TOP[...]
    factors = jnp.sqrt(limit / jnp.maximum(top, limit))
    head = lax.broadcasted_iota(jnp.int32, (16, D), 0)
    column = lax.broadcasted_iota(jnp.int32, (16, D), 1)
    wide = jnp.concatenate([factors] * (D // 128), axis=1)
    scale = row_sum(jnp.where(head == lax.shift_right_logical(column, 6), wide, 0.0))
    s_wq[...] = (WQ[...].astype(f32) * scale).astype(bf16)
    s_wk[...] = (WK[...].astype(f32) * scale).astype(bf16)
    count = BQ.shape[1]
    row = lax.broadcasted_iota(jnp.int32, (16, 128), 0)
    lane = lax.broadcasted_iota(jnp.int32, (16, 128), 1)
    entry = (lax.axis_index("dp") * 2 + lax.axis_index("ctx")) * count + lane
    own = row_sum(jnp.where(row == lax.shift_right_logical(entry, 6), factors, 0.0))
    s_bq[...] = (BQ[...].astype(f32) * own[:, 0:count]).astype(bf16)
    s_top[...] = row_sum(jnp.where(row == lane, top, 0.0))
    for src, dst in zip((s_wq, s_wk, s_bq, s_top, *o_vecs), (o_wq, o_wk, o_bq, o_top, *v_hbm)):
        put(src, dst)
    for copy in stores:
        copy.wait()


def run_finish(threshold, dx, taken, ga, gi, gu, gs, top, output, wq, wk, bq, wide):
    local, rows, rows_u, count = dx.shape[0], ga.shape[0], gu.shape[0], bq.shape[0]
    outs = [((local, D), bf16), ((local, D), f32)] + [((rows, D), f32)] * 4 + [((rows, FF), f32), ((rows_u, D), f32)]
    outs += [((rows, D), bf16)] * 2 + [((1, count), bf16), ((1, 128), f32)] + [((1, count), f32)] * 8 + [((1, wide), f32)]
    return pl.pallas_call(
        finish_kernel,
        out_shape=[jax.ShapeDtypeStruct(*o) for o in outs],
        in_specs=[INSMEM] + [ANY] * 8 + [INVMEM] * 3,
        out_specs=[ANY] * len(outs),
        scratch_shapes=[
            pltpu.VMEM((local, D), f32), pltpu.VMEM((local, D), bf16), pltpu.VMEM((16, 128), f32), pltpu.VMEM((16, 128), f32),
            pltpu.VMEM((rows, 4 * D), f32), pltpu.VMEM((rows, FF), f32), pltpu.VMEM((rows_u, D), f32),
            pltpu.VMEM((local, D), bf16),
        ]
        + [pltpu.VMEM(*o) for o in outs[8:]]
        + [pltpu.SemaphoreType.DMA((36,))],
        compiler_params=pltpu.CompilerParams(vmem_limit_bytes=VMEM_BYTES),
        name="finish",
    )(threshold, dx, taken, ga, gi, gu, gs, top, output, wq, wk, bq.reshape(1, -1))


def layer_norm(row_values, gain_vector, shift_vector):
    centre = row_values - jnp.mean(row_values, axis=-1, keepdims=True)
    spread = jnp.mean(centre * centre, axis=-1, keepdims=True)
    return centre * lax.rsqrt(spread + norm_eps) * gain_vector + shift_vector


def gelu_exact(values):
    return jax.nn.gelu(values, approximate=False)


def column_sums(values):
    return jnp.sum(values.astype(f32), axis=0)


def clip_outputs(logit_maxima, threshold, query_weight, query_bias, key_weight, device_rank):
    clip_limit = threshold.astype(f32)[0] * 0.01
    factors = jnp.sqrt(clip_limit / jnp.maximum(logit_maxima, clip_limit))
    column_scale = jnp.repeat(factors, HD)
    query_clipped = (query_weight.astype(f32) * column_scale[None, :]).astype(bf16)
    key_clipped = (key_weight.astype(f32) * column_scale[None, :]).astype(bf16)
    bias_count = query_bias.shape[0]
    bias_heads = (device_rank * bias_count + jnp.arange(bias_count)) // HD
    bias_scale = jnp.sum(jnp.where(bias_heads[:, None] == jnp.arange(H)[None, :], factors[None, :], 0.0), axis=1)
    return query_clipped, (query_bias.astype(f32) * bias_scale).astype(bf16), key_clipped


def fast_shards(
    nz,
    inputs, cotangent, query_weight, query_bias, key_weight, value_weight, value_bias, output_weight, output_bias,
    first_gain, first_shift, inner_weight, inner_bias, outer_weight, outer_bias, second_gain, second_shift,
    lengths, random_blocks, threshold,
):
    local = inputs.shape[1]
    pieces = nz * 8
    rows, rows_u = query_weight.shape[0], outer_weight.shape[0]
    small = (
        query_bias, value_bias, output_bias, first_gain, first_shift, outer_bias, second_gain, second_shift, inner_bias
    )
    x = inputs[0]
    weights = (query_weight, key_weight, value_weight, output_weight, inner_weight, outer_weight)
    output, *saved = run_forward(nz, x, weights, small, jnp.transpose(random_blocks[0], (1, 2, 0)), lengths)
    made = run_backward(nz, local, rows, rows_u, lengths, cotangent[0], *saved)
    (
        output, input_grad, g_query, g_key, g_value, g_out, g_inner, g_outer, query_clipped, key_clipped, bias_clipped, top, *vec
    ) = run_finish(threshold, *made, output, query_weight, key_weight, query_bias, FF // pieces)
    vec = [v.reshape(-1) for v in vec]
    return (
        output[None], input_grad[None],
        g_query, vec[0], g_key, g_value, vec[1], g_out, vec[2], vec[3], vec[4],
        g_inner, vec[8], g_outer, vec[5], vec[6], vec[7],
        query_clipped, bias_clipped.reshape(-1), key_clipped, top[0, :H],
    )


def general_shards(
    inputs, cotangent, query_weight, query_bias, key_weight, value_weight, value_bias, output_weight, output_bias,
    first_gain, first_shift, inner_weight, inner_bias, outer_weight, outer_bias, second_gain, second_shift,
    lengths, random_blocks, threshold,
):
    both = ("dp", "ctx")
    shards = (
        query_weight, query_bias, key_weight, value_weight, value_bias, output_weight, output_bias, first_gain, first_shift,
        inner_weight, inner_bias, outer_weight, outer_bias, second_gain, second_shift,
    )
    wq, bq, wk, wv, bv, wo, bo, g1, s1, wi, bi, wu, bu, g2, s2 = (lax.all_gather(w, both, axis=0, tiled=True) for w in shards)
    bq, bv, bo, g1, s1, bi, bu, g2, s2 = (v.astype(f32) for v in (bq, bv, bo, g1, s1, bi, bu, g2, s2))
    seqs, local, _ = inputs.shape
    blocks = local // BLK
    y = lax.axis_index("ctx")
    first_block = y * blocks
    scale = HD**-0.5
    outs = []
    sums = None
    top = jnp.full((H,), neg_large, f32)
    for s in range(seqs):
        x, length = inputs[s], lengths[s]
        random_here = lax.dynamic_slice_in_dim(random_blocks[s], first_block, blocks, 0)
        mask = compact_mask(random_here, length, first_block)
        mask = jnp.repeat(jnp.repeat(mask, BLK, axis=1), BLK, axis=2)
        seen = jnp.arange(NB * BLK) < length
        mask = jnp.where(seen[None, None, :], mask, neg_large)
        live = (y * local + jnp.arange(local)) < length
        q = (dot_nn(x, wq) + bq).astype(bf16)
        k = lax.all_gather(dot_nn(x, wk).astype(bf16), "ctx", axis=0, tiled=True)
        v = lax.all_gather((dot_nn(x, wv) + bv).astype(bf16), "ctx", axis=0, tiled=True)
        qh, kh, vh = (a.reshape(-1, H, HD) for a in (q, k, v))
        raw = jnp.einsum("qhd,khd->hqk", qh, kh, preferred_element_type=f32) * scale + mask
        row_top = jnp.max(raw, axis=-1, keepdims=True)
        top = jnp.maximum(top, jnp.max(jnp.where(live[None, :, None], row_top, neg_large), axis=(1, 2)))
        exponent = jnp.exp(raw - row_top)
        prob = exponent / jnp.sum(exponent, axis=-1, keepdims=True)
        low = prob.astype(bf16)
        attended = jnp.einsum("hqk,khd->qhd", low, vh, preferred_element_type=f32).reshape(local, D).astype(bf16)
        first_sum = x.astype(f32) + dot_nn(attended, wo) + bo
        normed = layer_norm(first_sum, g1, s1)
        normed_low = normed.astype(bf16)
        pre_act = dot_nn(normed_low, wi) + bi
        activated = gelu_exact(pre_act).astype(bf16)
        second_sum = normed + dot_nn(activated, wu) + bu
        output = layer_norm(second_sum, g2, s2).astype(bf16)
        cot = jnp.where(live[:, None], cotangent[s].astype(f32), 0.0)
        grad_second, g2_grad, s2_grad = jax.vjp(layer_norm, second_sum, g2, s2)[1](cot)
        dm = grad_second.astype(bf16)
        du = jax.vjp(gelu_exact, pre_act)[1](dot_nt(dm, wu))[0].astype(bf16)
        grad_normed = grad_second + dot_nt(du, wi)
        grad_first, g1_grad, s1_grad = jax.vjp(layer_norm, first_sum, g1, s1)[1](grad_normed)
        dp = grad_first.astype(bf16)
        da = dot_nt(dp, wo).astype(bf16).reshape(local, H, HD)
        dprob = jnp.einsum("qhd,khd->hqk", da, vh, preferred_element_type=f32)
        ds = (prob * (dprob - jnp.sum(prob * dprob, axis=-1, keepdims=True))).astype(bf16)
        dq = (jnp.einsum("hqk,khd->qhd", ds, kh, preferred_element_type=f32) * scale).reshape(local, D).astype(bf16)
        dk = (jnp.einsum("hqk,qhd->khd", ds, qh, preferred_element_type=f32) * scale).reshape(-1, D)
        dv = jnp.einsum("hqk,qhd->khd", low, da, preferred_element_type=f32).reshape(-1, D)
        dk, dv = (lax.psum_scatter(a.astype(bf16), "ctx", scatter_dimension=0, tiled=True).astype(bf16) for a in (dk, dv))
        input_grad = grad_first + dot_nt(dq, wq) + dot_nt(dk, wk) + dot_nt(dv, wv)
        outs.append((output, input_grad))
        here = (
            dot_tn(x, dq), column_sums(dq), dot_tn(x, dk), dot_tn(x, dv), column_sums(dv), dot_tn(attended, dp),
            column_sums(dp), g1_grad, s1_grad, dot_tn(normed_low, du), column_sums(du), dot_tn(activated, dm),
            column_sums(dm), g2_grad, s2_grad,
        )
        sums = here if sums is None else tuple(a + b for a, b in zip(sums, here))
    grads = tuple(lax.psum_scatter(g, both, scatter_dimension=0, tiled=True) for g in sums)
    logit_maxima = lax.pmax(top, both)
    rank = lax.axis_index(both)
    clipped = clip_outputs(logit_maxima, threshold, query_weight, query_bias, key_weight, rank)
    return (jnp.stack([o for o, _ in outs]), jnp.stack([g for _, g in outs]), *grads, *clipped, logit_maxima)


def solution(mesh):
    both = P(("dp", "ctx"))
    rows = P(("dp", "ctx"), None)
    tokens = P("dp", "ctx", None)
    in_specs = (
        tokens, tokens, rows, both, rows, rows, both, rows, both, both, both, rows, both, rows, both, both, both,
        P("dp"), P("dp", None, None, None), P(),
    )
    out_specs = (
        tokens, tokens, rows, both, rows, rows, both, rows, both, both, both, rows, both, rows, both, both, both,
        rows, both, rows, P(),
    )
    dp, ctx = mesh.shape["dp"], mesh.shape["ctx"]
    pieces = dp * ctx
    fits = ctx == 2 and dp % 4 == 0 and D % (8 * pieces) == 0 and FF // pieces <= 128

    def step(*args):
        if fits and args[0].shape[0] == 1:
            return fast_shards(dp // 4, *args)
        return general_shards(*args)

    return jax.shard_map(step, mesh=mesh, in_specs=in_specs, out_specs=out_specs, check_vma=False)
```

```python
import functools

import jax
import jax.numpy as jnp
import numpy as np
from jax import lax
from jax.experimental import pallas as pl
from jax.experimental.pallas import tpu as pltpu
from jax.sharding import PartitionSpec as P

H = 12
HD = 64
BLK = 64
LEN = 1024
NB = 16
D = 768
FF = 3072

norm_eps = 1e-12
neg_large = -1e30
bf16 = jnp.bfloat16
f32 = jnp.float32
ANY = pl.BlockSpec(memory_space=pl.ANY)
INVMEM = pl.BlockSpec(memory_space=pltpu.VMEM)
INSMEM = pl.BlockSpec(memory_space=pltpu.SMEM)
MESH = pl.DeviceIdType.MESH


def dot_nn(a, b):
    return jnp.dot(a, b, preferred_element_type=f32)


def dot_nt(a, b):
    return lax.dot_general(a, b, (((1,), (1,)), ((), ())), preferred_element_type=f32)


def dot_tn(a, b):
    return lax.dot_general(a, b, (((0,), (0,)), ((), ())), preferred_element_type=f32)


def ds128(index, width):
    return pl.ds(pl.multiple_of(index * width, width), width)


class Place:
    def __init__(self, nz):
        self.nz = nz
        dp = lax.axis_index("dp")
        self.y = lax.axis_index("ctx")
        self.c = lax.rem(dp, 2)
        self.x = lax.rem(lax.div(dp, 2), 2)
        self.z = lax.div(dp, 4)

    def at(self, z=None, x=None, c=None, y=None):
        z = self.z if z is None else z
        x = self.x if x is None else x
        c = self.c if c is None else c
        y = self.y if y is None else y
        return ((z * 2 + x) * 2 + c, y)

    def z_off(self, k):
        return lax.rem(self.z + k, self.nz)

    def along(self, axis):
        if axis == "z":
            return [self.at(z=self.z_off(k)) for k in range(1, self.nz)]
        return [self.at(x=1 - self.x) if axis == "x" else self.at(y=1 - self.y)]

    def peers(self):
        return (
            [self.at(z=self.z_off(k)) for k in range(1, self.nz)]
            + [self.at(x=1 - self.x), self.at(y=1 - self.y), self.at(c=1 - self.c)]
        )


def entry_barrier(place):
    barrier = pltpu.get_barrier_semaphore()
    peers = place.peers()
    for peer in peers:
        pl.semaphore_signal(barrier, inc=1, device_id=peer, device_id_type=MESH)
    pl.semaphore_wait(barrier, len(peers))


class Conditional:
    def __init__(self, copy, sends, receives):
        self.copy, self.sends, self.receives = copy, sends, receives

    def start(self):
        pl.when(self.sends)(self.copy.start)

    def wait_recv(self):
        pl.when(self.receives)(self.copy.wait_recv)

    def wait_send(self):
        pl.when(self.sends)(self.copy.wait_send)


class Remote:
    def __init__(self, send_sems, recv_sems):
        self.send_sems, self.recv_sems, self.used, self.copies = send_sems, recv_sems, 0, []

    def make(self, src, dst, peer, sends=None, receives=None):
        k = self.used
        self.used += 1
        copy = pltpu.make_async_remote_copy(
            src_ref=src, dst_ref=dst, send_sem=self.send_sems.at[k], recv_sem=self.recv_sems.at[k],
            device_id=peer, device_id_type=MESH,
        )
        if sends is not None:
            copy = Conditional(copy, sends, receives)
        self.copies.append(copy)
        return copy

    def finish(self):
        for copy in self.copies:
            copy.wait_send()


class Stripe:
    def __init__(self):
        self.stages, self.awaited, self.at = [], {}, 0

    def take(self, n):
        pass

    def step(self):
        n = self.at
        if n > 0:
            for copy in self.awaited.get(n, self.stages[n - 1]):
                copy.wait_recv()
            self.take(n - 1)
        if n < len(self.stages):
            for copy in self.stages[n]:
                copy.start()
        self.at = n + 1


class GatherStripe(Stripe):
    def __init__(self, remote, place, buf, cols, order):
        super().__init__()
        have = {"z": place.z, "x": place.x, "y": place.y}
        for axis in order:
            ref = buf.at[have["z"], have["x"], place.c, have["y"], :, cols]
            if axis == "z" and place.nz == 4:
                self.along_line(remote, place, lambda z: buf.at[z, have["x"], place.c, have["y"], :, cols])
            else:
                self.stages.append([remote.make(ref, ref, peer) for peer in place.along(axis)])
                if axis == "z":
                    self.stages.append([])
                    self.awaited[len(self.stages) - 1] = []
                    self.awaited[len(self.stages)] = self.stages[-2]
            have[axis] = slice(None)
        ref = buf.at[:, :, place.c, :, :, cols]
        self.stages.append([remote.make(ref, ref, place.at(c=1 - place.c))])

    def along_line(self, remote, place, block):
        z, mine = place.z, block(place.z)
        moves = [
            remote.make(mine, mine, place.at(z=lax.rem(z + 2, 4)), z < 2, z >= 2),
            remote.make(mine, mine, place.at(z=lax.rem(z + 2, 4)), z >= 2, z < 2),
            remote.make(mine, mine, place.at(z=lax.rem(z + 1, 4)), z < 3, z > 0),
            remote.make(mine, mine, place.at(z=lax.rem(z + 3, 4)), z > 0, z < 3),
        ]
        onward = [
            remote.make(block(0), block(0), place.at(z=lax.rem(z + 1, 4)), z == 2, z == 3),
            remote.make(block(3), block(3), place.at(z=lax.rem(z + 3, 4)), z == 1, z == 0),
        ]
        self.stages += [moves, onward]
        self.awaited[len(self.stages) - 1] = moves[:2]
        self.awaited[len(self.stages)] = moves[2:] + onward


class GatherTile(Stripe):
    def __init__(self, remote, place, buf):
        super().__init__()
        z, x, c, y = place.z, place.x, place.c, place.y
        for ref, peers in (
            (buf.at[z, x, c, y], place.along("z")),
            (buf.at[:, x, c, y], place.along("x")),
            (buf.at[:, :, c, y], place.along("y")),
            (buf.at[:, :, c], [place.at(c=1 - c)]),
        ):
            self.stages.append([remote.make(ref, ref, peer) for peer in peers])


class ScatterStripe(Stripe):
    def __init__(self, remote, place, g, cols, order, bufs, out):
        super().__init__()
        self.place, self.g, self.cols, self.order, self.bufs, self.out = place, g, cols, order, bufs, out
        own = {"z": place.z, "x": place.x, "y": place.y}
        have = {"z": slice(None), "x": slice(None), "y": slice(None)}
        ref = g.at[:, :, 1 - place.c, :, :, cols]
        self.stages.append([remote.make(ref, bufs[0], place.at(c=1 - place.c))])
        for n, axis in enumerate(order):
            made = []
            for k, peer in enumerate(place.along(axis)):
                there = dict(have)
                there[axis] = place.z_off(k + 1) if axis == "z" else 1 - own[axis]
                ref = g.at[there["z"], there["x"], place.c, there["y"], :, cols]
                made.append(remote.make(ref, bufs[n + 1].at[k] if axis == "z" else bufs[n + 1], peer))
            self.stages.append(made)
            have[axis] = own[axis]

    def take(self, n):
        place, g, cols, buf = self.place, self.g, self.cols, self.bufs[n]
        axis = self.order[n - 1] if n > 0 else "c"
        still = self.order[n:]
        sizes = {"z": place.nz, "x": 2, "y": 2}
        names = [name for name in "zxy" if name in still]
        count = 1
        for name in names:
            count *= sizes[name]

        def add(k, last):
            here = {"z": place.z, "x": place.x, "y": place.y}
            left = k
            for name in reversed(names):
                here[name] = lax.rem(left, sizes[name])
                left = lax.div(left, sizes[name])
            index = tuple(here[name] for name in names)
            spot = (here["z"], here["x"], place.c, here["y"], slice(None), cols)
            if axis != "z" and not last:
                g[spot] = g[spot] + buf[index]
                return
            total = g[spot].astype(f32)
            for part in range(place.nz - 1) if axis == "z" else (None,):
                total = total + buf[index if part is None else (part, *index)].astype(f32)
            if last:
                self.out[:, cols] = total
            else:
                g[spot] = total.astype(bf16)

        if not names:
            add(0, True)
        elif count <= 2:
            for k in range(count):
                add(k, False)
        else:

            def twice(k, carry):
                add(2 * k, False)
                add(2 * k + 1, False)
                return carry

            lax.fori_loop(0, count // 2, twice, 0)


def scatter_buffers(nz, rows, width, order):
    sizes = {"z": nz, "x": 2, "y": 2}
    made = [((nz, 2, 2, rows, width), bf16)]
    for n, axis in enumerate(order):
        left = [sizes[name] for name in "zxy" if name in order[n + 1 :]]
        made.append((((nz - 1,) if axis == "z" else ()) + (*left, rows, width), bf16))
    return made


class SmallSums(Stripe):
    def __init__(self, remote, place, t, bufs):
        super().__init__()
        z, x, c, y = place.z, place.x, place.c, place.y
        rc, ry, rx, rz = bufs
        self.place, self.t, self.bufs = place, t, bufs
        self.stages = [
            [remote.make(t.at[:, :, 1 - c], rc, place.at(c=1 - c))],
            [remote.make(t.at[:, :, c, 1 - y], ry, place.at(y=1 - y))],
            [remote.make(t.at[:, 1 - x, c, y], rx, place.at(x=1 - x))],
            [remote.make(t.at[place.z_off(k + 1), x, c, y], rz.at[k], peer) for k, peer in enumerate(place.along("z"))],
        ]

    def take(self, n):
        place, t = self.place, self.t
        rc, ry, rx, rz = self.bufs
        z, x, c, y = place.z, place.x, place.c, place.y
        if n == 0:
            t[:, :, c] = t[:, :, c] + rc[...]
        elif n == 1:
            t[:, :, c, y] = t[:, :, c, y] + ry[...]
        elif n == 2:
            t[:, x, c, y] = t[:, x, c, y] + rx[...]
        else:
            total = t[z, x, c, y]
            for k in range(place.nz - 1):
                total = total + rz[k]
            t[z, x, c, y] = total


def small_buffers(nz):
    return [((nz, 2, 2, 16, 128), f32), ((nz, 2, 16, 128), f32), ((nz, 16, 128), f32), ((nz - 1, 16, 128), f32)]


class TopOfAll(Stripe):
    def __init__(self, remote, place, top, tops):
        super().__init__()
        self.top, self.tops, self.slots, slot = top, tops, [], 0
        for n, peers in enumerate(([place.at(c=1 - place.c)], place.along("y"), place.along("x"), place.along("z"))):
            self.slots.append(list(range(slot, slot + len(peers))))
            self.stages.append([remote.make(top.at[n], tops.at[slot + k], peer) for k, peer in enumerate(peers)])
            slot += len(peers)

    def take(self, n):
        best = self.top[n]
        for slot in self.slots[n]:
            best = jnp.maximum(best, self.tops[slot])
        self.top[n + 1] = best


class Script:
    def __init__(self, plan, stripes, swap):
        self.plan, self.stripes, self.swap, self.spent = plan, stripes, swap, 0

    def point(self):
        for item in self.plan[self.spent]:
            if item < 0:
                self.swap.start()
            else:
                self.stripes[item].step()
        self.spent += 1

    def points(self, index, first, count):
        for k in range(count):
            pl.when(index == first + k)(self.point)

    def close(self):
        assert self.spent == len(self.plan)
        assert all(s.at == len(s.stages) + 1 for s in self.stripes)


VMEM_BYTES = 60 << 20
GATHER_ITEMS = (
    (0, 0, 384, "yzx"), (0, 384, 384, "yzx"), (0, 768, 384, "yzx"), (0, 1152, 384, "zxy"), (0, 1536, 256, "yzx"),
    (0, 1792, 256, "yzx"), (0, 2048, 256, "yzx"), (0, 2304, 384, "zyx"), (0, 2688, 384, "xzy"), (1, 0, 384, "zxy"),
    (1, 384, 384, "yzx"), (1, 768, 768, "zxy"), (1, 1536, 256, "zyx"), (1, 1792, 256, "yzx"), (1, 2048, 256, "yzx"),
    (1, 2304, 384, "zxy"), (1, 2688, 384, "zyx"), (2, 0, 256, "xzy"), (2, 256, 128, "zyx"), (2, 384, 128, "yzx"),
    (2, 512, 128, "xzy"), (2, 640, 128, "yzx"),
)
GATHER_PLAN = (
    (0, 1, 22, 2, 3, 4, 5, 6, -1),
    (0, 1, 2, 4, 22, 3, 5, 6, 22, 3, 0, 3, 0, 1, 2, 7, 8, 9, 11, 1, 2, 0, 8, 4, 0, 10, 4, 1, 5, 6, 7, 5, 1, 12, 6, 22, 7, 9, 2, 22, 13),
    (11,), (2, 4, 8, 9, 14, 3, 10, 11, 12, 4, 15, 5, 8, 7, 13, 3, 16), (5, 12, 14, 18, 6, 9, 6, 17), (8, 10), (12, 15),
    (8, 11, 10, 13, 15, 19), (9, 13, 14, 16), (7, 14, 18, 17), (9, 16, 18, 21), (7, 12), (11, 12, 19, 20), (10, 16),
    (11, 15, 17), (10, 13, 18, 21), (14,), (13, 14, 15, 17, 20), (19,), (15, 16, 21), (19,), (16, 18, 21, 20), (), (),
    (18, 20), (17,), (), (19,), (), (17,), (19, 20), (21,), (), (21, 20), (), (), (),
)
SCATTER_ITEMS = (
    (2, 0, 128, "xzy"), (2, 128, 128, "yxz"), (2, 256, 256, "yzx"), (2, 512, 128, "xzy"), (2, 640, 128, "yxz"),
    (1, 0, 768, "xyz"), (1, 768, 768, "yxz"), (1, 1536, 768, "xyz"), (1, 2304, 768, "xyz"), (0, 0, 768, "xzy"),
    (0, 768, 384, "xzy"), (0, 1152, 384, "xyz"), (0, 1536, 384, "xzy"), (0, 1920, 384, "xyz"), (0, 2304, 768, "yxz"),
)
SCATTER_PLAN = (
    (), (), (), (0, 1), (2,), (0, 1, 3, 4), (2, 3, 4, 0, 1), (5, 15), (6,), (7,), (8, 5, 15), (3, 6, 0), (), (1, 7), (8, 2),
    (), (), (4, 5, 15), (3,), (1, 14), (0, 6, 7), (14,), (2, 3, 5, 9), (8, 7), (4, 15, 9), (6,), (2, 5, 14), (7, -1),
    (4, 15, 8), (9,), (6, 10, 11), (14, 10), (11,), (8, 12, 13), (10, 16), (12, 13), (11, 16),
    (9, 14, 12, 11, 16, 13, 9, 10, 16, 12, 13, 10, 11, 12, 16, 13),
)

def layer_norm_parts(rows):
    centre = rows - jnp.mean(rows, axis=-1, keepdims=True)
    spread = jnp.mean(centre * centre, axis=-1, keepdims=True)
    inverse = lax.rsqrt(spread + norm_eps)
    return centre * inverse, inverse


def head_lanes(rows, half):
    lane = lax.broadcasted_iota(jnp.int32, rows.shape, 1)
    return jnp.where((lane >= HD) == (half == 1), rows, jnp.zeros_like(rows))


def key_structure(local, y, length):
    lane = lax.broadcasted_iota(jnp.int32, (2 * local, 128), 1)
    row = lax.broadcasted_iota(jnp.int32, (2 * local, 128), 0)
    position = jnp.where(row < local, row + y * local, row - y * local)
    own = lane == lax.shift_right_logical(position, 6)
    beyond = (lane == NB) & (position >= length)
    return jnp.where(own | beyond | ((lane > NB) & (lane < NB + 4)), 1.0, 0.0).astype(bf16)


def head_rows(rows, half):
    row = lax.broadcasted_iota(jnp.int32, rows.shape, 0)
    return jnp.where((row >= HD) == (half == 1), rows, jnp.zeros_like(rows))


def in_three(values):
    high = values.astype(bf16)
    rest = values - high.astype(f32)
    middle = rest.astype(bf16)
    return high, middle, (rest - middle.astype(f32)).astype(bf16)


def with_rows(base, values):
    row = lax.broadcasted_iota(jnp.int32, base.shape, 0)
    for k, part in enumerate(in_three(-values)):
        base = base + jnp.where(row == NB + 1 + k, part.astype(f32), 0.0)
    return base.astype(bf16)


def spread_vectors(tiles, width, pieces):
    rows = tiles.shape[1]
    total = pieces * width
    lane = lax.broadcasted_iota(jnp.int32, (128, total), 1).astype(f32)
    row = lax.broadcasted_iota(jnp.int32, (128, total), 0).astype(f32)
    owner = jnp.floor((lane + 0.5) * (1.0 / width))
    chooser = jnp.where(lane - owner * width == row, 1.0, 0.0).astype(bf16)
    wide = dot_nn(tiles.reshape(pieces * rows, 128), chooser).reshape(pieces, rows, total)
    lane3 = lax.broadcasted_iota(jnp.int32, (pieces, rows, total), 2).astype(f32)
    piece3 = lax.broadcasted_iota(jnp.int32, (pieces, rows, total), 0).astype(f32)
    mine = jnp.floor((lane3 + 0.5) * (1.0 / width)) == piece3
    return jnp.sum(jnp.where(mine, wide, 0.0), axis=0)


def forward_kernel(
    nz, local, length_ref, random_hbm, x_hbm, wq, wk, wv, wo, wi, wu, v0, v1, v2, v3, v4, v5, v6, v7, v8,
    out_hbm, r1_hbm, r2_hbm, gp_hbm, gt_hbm, n1t_hbm, at_hbm, atf_hbm, q_hbm, qt_hbm, k_hbm, kt_hbm, v_hbm, xt_hbm, lse_hbm,
    top_hbm, wa_hbm, wi_hbm, wu_hbm, vec_hbm, mask_hbm,
    WA, WI, WU, SM, XF, XT, Q, QT, K, KT, V, VT, AT, ATF, R1, R2, N1L, N1T, U, GP, G, GT, E, VEC, IB, LSE, TOP, TT, OUT, MASK, *rest,
):
    place = Place(nz)
    z, x, c, y = place.z, place.x, place.c, place.y
    small, (random_ref, send_sems, recv_sems, local_sems, out_sems) = rest[:9], rest[9:]
    remote = Remote(send_sems, recv_sems)
    mine = (z, x, c, y)
    locals_ = list(zip((v0, v1, v2, v3, v4, v5, v6, v7, v8), small))
    locals_ += [(x_hbm, XF.at[0]), (random_hbm, random_ref)]
    for g in range(3):
        for n, w in enumerate((wq, wk, wv)):
            lo = g * D + n * 256
            locals_.append((w.at[:, g * 256 : (g + 1) * 256], WA.at[(*mine, slice(None), slice(lo, lo + 256))]))
    locals_ += [(wo, WA.at[(*mine, slice(None), slice(3 * D, 4 * D))]), (wi, WI.at[mine]), (wu, WU.at[mine])]
    locals_ = [pltpu.make_async_copy(src, dst, local_sems.at[k]) for k, (src, dst) in enumerate(locals_)]
    for copy in locals_:
        copy.start()
    TT[...] = jnp.zeros((16, 128), f32)
    for n, v in enumerate(small):
        locals_[n].wait()
        TT[n : n + 1, 0 : v.shape[1]] = v[...].astype(f32)
    SM[mine] = TT[...].astype(bf16)
    entry_barrier(place)
    for copy in locals_[9:]:
        copy.wait()

    outs = []

    def put(src, dst):
        copy = pltpu.make_async_copy(src, dst, out_sems.at[len(outs)])
        copy.start()
        outs.append(copy)

    swap = remote.make(XF.at[0], XF.at[1], place.at(y=1 - y))
    stripes = [
        GatherStripe(remote, place, (WA, WI, WU)[buf], slice(lo, lo + width), order) for buf, lo, width, order in GATHER_ITEMS
    ]
    stripes.append(GatherTile(remote, place, SM))
    script = Script(GATHER_PLAN, stripes, swap)
    script.point()
    length = length_ref[0]
    E[...] = key_structure(local, y, length)
    fill_masks(MASK, random_ref, y * (local // BLK), length)
    put(MASK, mask_hbm)
    XT[:, :local] = XF[0].T
    script.point()

    tiles = SM[...].reshape(-1, 16, 128)
    pieces = tiles.shape[0]
    VEC[...] = spread_vectors(tiles, D // pieces, pieces)
    IB[...] = spread_vectors(tiles[:, 8:16, :], FF // pieces, pieces)
    put(VEC, vec_hbm)
    script.point()
    position = y * local + lax.broadcasted_iota(jnp.int32, (1, local), 1)
    live = position < length

    def put_columns(buf, dst, lo, width):
        put(buf.at[:, :, :, :, :, lo : lo + width], dst.at[:, :, :, :, :, lo : lo + width])

    def wide(buf, lo, width):
        return buf[:, :, :, :, :, lo : lo + width].reshape(-1, width)

    for g in range(3):
        cols = slice(g * 256, (g + 1) * 256)
        put_columns(WA, wa_hbm, g * D, D)
        own = dot_nn(XF[0], wide(WA, g * D, D))
        q = ((own[:, :256] + VEC[0:1, cols]).astype(bf16).astype(f32) * (HD**-0.5)).astype(bf16)
        Q[:, cols] = q
        QT[cols, :] = q.T
        K[:local, cols] = own[:, 256:512].astype(bf16)
        values = (own[:, 512:] + VEC[1:2, cols]).astype(bf16)
        V[:local, cols] = values
        VT[cols, :local] = values.T
        script.point()
    put(Q, q_hbm)
    put(QT, qt_hbm)
    swap.wait_recv()
    for g in range(3):
        cols = slice(g * 256, (g + 1) * 256)
        theirs = dot_nn(XF[1], wide(WA, g * D + 256, 512))
        K[local:, cols] = theirs[:, :256].astype(bf16)
        values = (theirs[:, 256:] + VEC[1:2, cols]).astype(bf16)
        V[local:, cols] = values
        VT[cols, local:] = values.T
        script.point()

        def head_step(h, carry):
            lanes = ds128(lax.div(h, 2), 128)
            half = lax.rem(h, 2)
            own = pl.ds(pl.multiple_of(h * HD, HD), HD)
            left = jnp.concatenate([K[:, lanes], E[...]], axis=1)
            right = jnp.concatenate(
                [head_rows(QT[lanes, :], half), MASK[h], jnp.zeros((128 - 32, local), bf16)], axis=0
            )
            for part in range(local // 256):
                cols = slice(part * 256, (part + 1) * 256)
                scores = dot_nn(left, right[:, cols])
                top = jnp.max(scores, axis=0, keepdims=True)
                exponent = jnp.exp(scores - top)
                total = jnp.sum(exponent, axis=0, keepdims=True)
                low = (exponent * (1.0 / total)).astype(bf16)
                mixture = dot_nn(VT[own, :], low)
                ATF[own, cols] = mixture
                AT[own, cols] = mixture.astype(bf16)
                LSE[h, :, cols] = top + jnp.log(total)
                TOP[h, :, cols] = jnp.where(live[:, cols], top, neg_large)
            script.points(h, 4 * g, 4)
            return carry

        lax.fori_loop(4 * g, 4 * g + 4, head_step, 0)
    put(K, k_hbm)
    put(V, v_hbm)
    put(LSE, lse_hbm)
    TT[...] = jnp.zeros((16, 128), f32) + neg_large
    TT[0:H, :] = jnp.broadcast_to(jnp.max(TOP[:, 0, :], axis=1, keepdims=True), (H, 128))
    put(TT, top_hbm)
    put(AT, at_hbm)
    put(ATF, atf_hbm)
    put_columns(WA, wa_hbm, 3 * D, D)
    R1[...] = dot_nn(AT[...].T, wide(WA, 3 * D, D))
    script.point()

    def first_norm(k, carry):
        rows = ds128(k, 64)
        summed = XF[0, rows, :].astype(f32) + R1[rows, :] + VEC[2:3, :]
        R1[rows, :] = summed
        normal, _ = layer_norm_parts(summed)
        value = normal * VEC[3:4, :] + VEC[4:5, :]
        N1L[rows, :] = value.astype(bf16)
        R2[rows, :] = value + VEC[5:6, :]
        return carry

    lax.fori_loop(0, local // 64, first_norm, 0)
    put(R1, r1_hbm)
    script.point()
    N1T[...] = N1L[...].T
    put(N1T, n1t_hbm)
    XT[:, local:] = XF[1].T
    put(XT, xt_hbm)
    script.point()
    KT[...] = K[...].T
    put(KT, kt_hbm)
    script.point()
    for n in range(FF // D):
        cols = slice(n * D, (n + 1) * D)
        put_columns(WI, wi_hbm, n * D, D)
        U[...] = dot_nn(N1L[...], wide(WI, n * D, D)) + IB[0:1, cols]
        script.point()

        def activate(k, carry):
            rows = ds128(k, 16)
            u = U[rows, :]
            below = 0.5 * (1.0 + lax.erf(u * np.float32(0.5**0.5)))
            G[rows, cols] = (u * below).astype(bf16)
            GP[n, rows, :] = below + u * jnp.exp(-0.5 * u * u) * np.float32((2.0 * np.pi) ** -0.5)
            return carry

        lax.fori_loop(0, local // 16, activate, 0)
        put(GP.at[n], gp_hbm.at[n])
        GT[cols, :] = G[:, cols].T
        put(GT.at[cols, :], gt_hbm.at[cols, :])
        script.point()
    for n in range(3):
        cols = slice(n * 256, (n + 1) * 256)
        put_columns(WU, wu_hbm, n * 256, 256)
        R2[:, cols] += dot_nn(G[...], WU[:, :, :, :, :, cols].reshape(FF, 256))
        script.point()

    def second_norm(k, carry):
        rows = ds128(k, 64)
        normal, _ = layer_norm_parts(R2[rows, :])
        OUT[rows, :] = (normal * VEC[6:7, :] + VEC[7:8, :]).astype(bf16)
        return carry

    lax.fori_loop(0, local // 64, second_norm, 0)
    put(R2, r2_hbm)
    put(OUT, out_hbm)
    script.point()
    script.close()
    remote.finish()
    for copy in outs:
        copy.wait()


def copies_of(items, nz):
    return len(items) * (3 + max(6, nz - 1))


def run_forward(nz, x, weights, vectors, random_blocks, length):
    local = x.shape[0]
    wq, wk, wv, wo, wi, wu = weights
    grid = (nz, 2, 2, 2)
    rows, rows_u = wq.shape[0], wu.shape[0]
    seq = 2 * local
    blocks = FF // D
    outs = [
        ((local, D), bf16), ((local, D), f32), ((local, D), f32), ((blocks, local, D), f32), ((FF, local), bf16),
        ((D, local), bf16), ((D, local), bf16), ((D, local), f32), ((local, D), bf16), ((D, local), bf16), ((seq, D), bf16),
        ((D, seq), bf16), ((seq, D), bf16), ((D, seq), bf16), ((H, 1, local), f32), ((16, 128), f32),
        ((*grid, rows, 4 * D), bf16), ((*grid, rows, FF), bf16), ((*grid, rows_u, D), bf16), ((16, D), f32),
        ((H, 32, local), bf16),
    ]
    scratch = [
        ((*grid, rows, 4 * D), bf16), ((*grid, rows, FF), bf16), ((*grid, rows_u, D), bf16), ((*grid, 16, 128), bf16),
        ((2, local, D), bf16), ((D, seq), bf16), ((local, D), bf16), ((D, local), bf16), ((seq, D), bf16), ((D, seq), bf16),
        ((seq, D), bf16), ((D, seq), bf16), ((D, local), bf16), ((D, local), f32), ((local, D), f32), ((local, D), f32),
        ((local, D), bf16), ((D, local), bf16), ((local, D), f32), ((blocks, local, D), f32), ((local, FF), bf16),
        ((FF, local), bf16), ((seq, 128), bf16), ((16, D), f32), ((8, FF), f32), ((H, 1, local), f32), ((H, 1, local), f32),
        ((16, 128), f32), ((local, D), bf16), ((H, 32, local), bf16),
    ]
    scratch += [((1, v.shape[0]), bf16) for v in vectors]
    copies = copies_of(GATHER_ITEMS, nz) + 3 + (nz - 1) + 1
    return pl.pallas_call(
        functools.partial(forward_kernel, nz, local),
        out_shape=[jax.ShapeDtypeStruct(*o) for o in outs],
        in_specs=[INSMEM] + [ANY] * 17,
        out_specs=[ANY] * len(outs),
        scratch_shapes=[pltpu.VMEM(*s) for s in scratch]
        + [
            pltpu.SMEM(random_blocks.shape, jnp.int32),
            pltpu.SemaphoreType.DMA((copies,)),
            pltpu.SemaphoreType.DMA((copies,)),
            pltpu.SemaphoreType.DMA((23,)),
            pltpu.SemaphoreType.DMA((40,)),
        ],
        compiler_params=pltpu.CompilerParams(collective_id=1, has_side_effects=True, vmem_limit_bytes=VMEM_BYTES),
        name="gather_forward",
    )(length, random_blocks, x, wq, wk, wv, wo, wi, wu, *(v.reshape(1, -1) for v in vectors))


def compact_mask(random_here, length, first_block):
    blocks = random_here.shape[0]
    query = (first_block + jnp.arange(blocks, dtype=jnp.int32))[None, :, None]
    key = jnp.arange(NB, dtype=jnp.int32)[None, None, :]
    last = (length - 1) // BLK
    ok = (jnp.abs(query - key) <= 1) | (key == 0) | (key == last) | (query == 0) | (query == last)
    heads = jnp.transpose(random_here, (1, 0, 2))
    for k in range(heads.shape[2]):
        ok = ok | (heads[:, :, k : k + 1] == key)
    return jnp.where(ok, 0.0, neg_large).astype(f32)


def fill_masks(masks, random_ref, first_block, length):
    queries = masks.shape[2]
    row = lax.broadcasted_iota(jnp.int32, (32, queries), 0)
    here = lax.shift_right_logical(lax.broadcasted_iota(jnp.int32, (32, queries), 1), 6)
    one = lax.shift_right_logical(lax.broadcasted_iota(jnp.int32, (1, queries), 1), 6)
    block = here + first_block
    last = lax.shift_right_logical(length - 1, 6)
    fixed = (jnp.abs(block - row) <= 1) | (row == 0) | (row == last) | (block == 0) | (block == last) | (row > NB)
    base = jnp.where(fixed & (row != NB), 0.0, neg_large)

    def head(h, carry):
        mask = base
        for k in range(3):
            chosen = jnp.zeros((1, queries), jnp.int32)
            for b in range(queries // BLK):
                chosen = jnp.where(one == b, random_ref[h, k, 0, first_block + b], chosen)
            mask = jnp.where((row == chosen) & (row < NB), 0.0, mask)
        masks[h] = mask.astype(bf16)
        return carry

    lax.fori_loop(0, H, head, 0)


def gather_vectors(rows, width, pieces):
    n, total = rows.shape
    if n == 1:
        lane2 = lax.broadcasted_iota(jnp.int32, (pieces, total), 1).astype(f32)
        piece2 = lax.broadcasted_iota(jnp.int32, (pieces, total), 0).astype(f32)
        mine = jnp.floor((lane2 + 0.5) * (1.0 / width)) == piece2
        spread = jnp.where(mine, rows, 0.0)
    else:
        lane3 = lax.broadcasted_iota(jnp.int32, (pieces, n, total), 2).astype(f32)
        piece3 = lax.broadcasted_iota(jnp.int32, (pieces, n, total), 0).astype(f32)
        mine = jnp.floor((lane3 + 0.5) * (1.0 / width)) == piece3
        spread = jnp.where(mine, rows[None], 0.0).reshape(pieces * n, total)
    lane = lax.broadcasted_iota(jnp.int32, (128, total), 1).astype(f32)
    row = lax.broadcasted_iota(jnp.int32, (128, total), 0).astype(f32)
    owner = jnp.floor((lane + 0.5) * (1.0 / width))
    chooser = jnp.where(lane - owner * width == row, 1.0, 0.0).astype(bf16)
    high, middle, lowest = in_three(spread)
    tiles = dot_nt(high, chooser) + (dot_nt(middle, chooser) + dot_nt(lowest, chooser))
    return tiles.reshape(pieces, n, 128)


def norm_back(normal, inverse, grads, gain):
    scaled = grads * gain
    first = jnp.mean(scaled, axis=-1, keepdims=True)
    second = jnp.mean(scaled * normal, axis=-1, keepdims=True)
    return inverse * (scaled - first - normal * second)


def row_sum(values):
    return jnp.sum(values, axis=0, keepdims=True)


def back_half(pair, local, own_keys, BQ, BD, Q, QT, DA, DAT, K, KT, V, E, PB, DS, DQF, DQT, DK, DV):
    keys = slice(0, local) if own_keys else slice(local, 2 * local)
    lanes = ds128(pair, 128)
    structure = E[keys, :]
    left = jnp.concatenate([K[keys, lanes], structure], axis=1)
    left_values = jnp.concatenate([V[keys, lanes], structure], axis=1)
    empty = jnp.zeros((128 - 32, local), bf16)
    for half in (0, 1):
        h = pair * 2 + half
        own = pl.ds(pl.multiple_of(h * HD, HD), HD)
        spot = slice(half * local, (half + 1) * local)
        right = jnp.concatenate([head_rows(QT[lanes, :], half), BQ[h], empty], axis=0)
        prob = jnp.exp(dot_nn(left, right))
        PB[:, spot] = prob.astype(bf16)
        right_values = jnp.concatenate([head_rows(DAT[lanes, :], half), BD[h], empty], axis=0)
        low = (prob * dot_nn(left_values, right_values)).astype(bf16)
        DS[:, spot] = low
        part = dot_nn(KT[own, keys], low)
        if own_keys:
            DQT[own, :] = ((DQF[own, :] + part) * (HD**-0.5)).astype(bf16)
        else:
            DQF[own, :] = part
    q_pair, a_pair = Q[:, lanes], DA[:, lanes]
    DK[keys, lanes] = dot_nn(DS[...], jnp.concatenate([head_lanes(q_pair, n) for n in (0, 1)], axis=0)).astype(bf16)
    DV[keys, lanes] = dot_nn(PB[...], jnp.concatenate([head_lanes(a_pair, n) for n in (0, 1)], axis=0)).astype(bf16)


def backward_kernel(
    nz, local, length_ref, cot_hbm, r1_hbm, r2_hbm, gp_hbm, gt_hbm, n1t_hbm, at_hbm, atf_hbm, q_hbm, qt_hbm,
    k_hbm, kt_hbm, v_hbm, xt_hbm, lse_hbm, top_hbm, wa_hbm, wi_hbm, wu_hbm, vec_hbm,
    mask_hbm, dx_hbm, taken_hbm, oa_hbm, oi_hbm, ou_hbm, os_hbm, ot_hbm, *rest,
):
    place = Place(nz)
    z, x, c, y = place.z, place.x, place.c, place.y
    GA, GI, GU, WA, T, TOP, TOPS, DP, AT, DR1, E, SUMS, ISUM, SEND, RECV, VEC, OA, OI, OU = rest[:19]
    used = 19
    bufs = []
    for _ in SCATTER_ITEMS:
        bufs.append(rest[used : used + 4])
        used += 4
    sbufs = rest[used : used + 4]
    send_sems, recv_sems, load_sems = rest[used + 4 :]
    blocks = FF // D
    pieces = nz * 8
    seq_len = 2 * local
    length = length_ref[0]
    loads = [0]

    def load(src, dst):
        copy = pltpu.make_async_copy(src, dst, load_sems.at[loads[0]])
        loads[0] += 1
        copy.start()
        return copy

    remote = Remote(send_sems, recv_sems)
    stripes = [
        ScatterStripe(remote, place, (GA, GI, GU)[buf], slice(lo, lo + width), order, bufs[n], (OA, OI, OU)[buf])
        for n, (buf, lo, width, order) in enumerate(SCATTER_ITEMS)
    ]
    stripes += [TopOfAll(remote, place, TOP, TOPS), SmallSums(remote, place, T, sbufs)]
    swap = remote.make(SEND, RECV, place.at(y=1 - y))
    script = Script(SCATTER_PLAN, stripes, swap)
    grid = (nz, 2, 2, 2)
    SUMS[...] = jnp.zeros_like(SUMS)
    ISUM[...] = jnp.zeros_like(ISUM)

    def first_stage(COT, R2, R1, DM, GT, DU, GP, N1T, WUS, WIS):
        l_r2, l_cot, l_vec = load(r2_hbm, R2), load(cot_hbm, COT), load(vec_hbm, VEC)
        l_gt = load(gt_hbm, GT)
        l_wu, l_gp = [], []
        for n in range(2):
            l_wu.append(load(wu_hbm.at[n], WUS.at[n]))
            l_gp.append(load(gp_hbm.at[n], GP.at[n]))

        def wi_of(n):
            return wi_hbm.at[:, :, :, :, :, n * D : (n + 1) * D]

        script.point()
        entry_barrier(place)
        E[...] = key_structure(local, y, length)
        l_r2.wait()
        l_cot.wait()
        l_vec.wait()
        script.point()

        def second_norm(k, carry):
            rows = ds128(k, 64)
            normal, inverse = layer_norm_parts(R2[rows, :])
            position = y * local + k * 64 + lax.broadcasted_iota(jnp.int32, (64, D), 0)
            grads = jnp.where(position < length, COT[rows, :].astype(f32), 0.0)
            through = norm_back(normal, inverse, grads, VEC[6:7, :])
            R2[rows, :] = through
            low = through.astype(bf16)
            DM[rows, :] = low
            SUMS[5:6, :] += row_sum(low.astype(f32))
            SUMS[6:7, :] += row_sum(grads * normal)
            SUMS[7:8, :] += row_sum(grads)
            return carry

        lax.fori_loop(0, local // 64, second_norm, 0)
        script.point()
        l_gt.wait()
        for n in range(3):
            cols = slice(n * 256, (n + 1) * 256)

            def outer_grad(zz, carry):
                rows = ds128(zz, FF // nz)
                made = dot_nn(GT[rows, :], DM[:, cols]).astype(bf16)
                GU[zz, :, :, :, :, cols] = made.reshape(2, 2, 2, -1, 256)
                return carry

            lax.fori_loop(0, nz, outer_grad, 0)
            script.point()
        for n in range(blocks):
            l_wu[n].wait()
            l_gp[n].wait()
            grads = dot_nt(DM[...], WUS[n % 2].reshape(D, D)) * GP[n % 2]
            low = grads.astype(bf16)
            DU[n] = low
            ISUM[0:1, n * D : (n + 1) * D] = row_sum(low.astype(f32))
            if n + 2 < blocks:
                l_wu.append(load(wu_hbm.at[n + 2], WUS.at[n % 2]))
                l_gp.append(load(gp_hbm.at[n + 2], GP.at[n % 2]))
        l_top, l_n1t = load(top_hbm, TOP.at[0]), load(n1t_hbm, N1T)
        l_wi = [load(wi_of(0), WIS.at[0]), load(wi_of(1), WIS.at[1])]
        l_r1, l_at, l_wa = load(r1_hbm, R1), load(at_hbm, AT), load(wa_hbm, WA)
        wide = gather_vectors(ISUM[...], FF // pieces, pieces).reshape(*grid, 1, 128)
        T[:, :, :, :, 8:16, :] = jnp.broadcast_to(wide, (*grid, 8, 128))
        script.point()
        l_top.wait()
        l_n1t.wait()
        for n in range(blocks):
            made = dot_nn(N1T[...], DU[n]).astype(bf16)
            GI[:, :, :, :, :, n * D : (n + 1) * D] = made.reshape(*grid, -1, D)
            script.point()
        for n in range(blocks):
            l_wi[n].wait()
            R2[...] += dot_nt(DU[n], WIS[n % 2].reshape(D, D))
            if n + 2 < blocks:
                l_wi.append(load(wi_of(n + 2), WIS.at[n % 2]))
            script.point()
        l_r1.wait()

        def first_norm(k, carry):
            rows = ds128(k, 64)
            normal, inverse = layer_norm_parts(R1[rows, :])
            grads = R2[rows, :]
            through = norm_back(normal, inverse, grads, VEC[3:4, :])
            DR1[rows, :] = through
            low = through.astype(bf16)
            DP[rows, :] = low
            SUMS[2:3, :] += row_sum(low.astype(f32))
            SUMS[3:4, :] += row_sum(grads * normal)
            SUMS[4:5, :] += row_sum(grads)
            return carry

        lax.fori_loop(0, local // 64, first_norm, 0)
        script.point()
        l_at.wait()
        l_wa.wait()

    pl.run_scoped(
        first_stage,
        pltpu.VMEM((local, D), bf16), pltpu.VMEM((local, D), f32), pltpu.VMEM((local, D), f32), pltpu.VMEM((local, D), bf16),
        pltpu.VMEM((FF, local), bf16), pltpu.VMEM((blocks, local, D), bf16), pltpu.VMEM((2, local, D), f32),
        pltpu.VMEM((D, local), bf16), pltpu.VMEM((2, 2, 2, 2, FF // (nz * 8), D), bf16),
        pltpu.VMEM((2, *grid, D // (nz * 8), D), bf16),
    )

    def second_stage(Q, QT, K, KT, V, XT, LSE, BQ, BD, DA, DAT, PB, DS, DQF, DQT, DQ, DK, DV):
        pairs = ((lse_hbm, LSE), (atf_hbm, DQF), (mask_hbm, BQ), (k_hbm, K), (q_hbm, Q), (qt_hbm, QT), (kt_hbm, KT), (v_hbm, V), (xt_hbm, XT))
        waits = [load(s, d) for s, d in pairs]
        made = dot_nn(AT[...], DP[...]).astype(bf16)
        GA[:, :, :, :, :, 3 * D : 4 * D] = made.reshape(*grid, -1, D)
        script.point()
        DAT[...] = dot_nt(WA[:, :, :, :, :, 3 * D : 4 * D].reshape(D, D), DP[...]).astype(bf16)
        DA[...] = DAT[...].T
        for wait in waits[:3]:
            wait.wait()

        def prepare(h, carry):
            own = pl.ds(pl.multiple_of(h * HD, HD), HD)
            delta = row_sum(DAT[own, :].astype(f32) * DQF[own, :])
            BD[h] = with_rows(jnp.zeros((32, local), f32), delta)
            BQ[h] = with_rows(BQ[h].astype(f32), LSE[h])
            return carry

        lax.fori_loop(0, H, prepare, 0)
        for wait in waits[3:]:
            wait.wait()
        script.point()

        def halves(own_keys, g):
            def pair_step(pair, carry):
                back_half(pair, local, own_keys, BQ, BD, Q, QT, DA, DAT, K, KT, V, E, PB, DS, DQF, DQT, DK, DV)
                script.points(pair, 2 * g, 2)
                return carry

            lax.fori_loop(2 * g, 2 * g + 2, pair_step, 0)

        def group(g):
            lo = g * D
            cols = slice(g * 256, (g + 1) * 256)
            dq = DQT[cols, :].T
            DQ[:, cols] = dq
            SUMS[0:1, cols] = row_sum(dq.astype(f32))
            SUMS[1:2, cols] = row_sum(DV[:, cols].astype(f32))
            for n, made in enumerate(
                (dot_nn(XT[:, :local], dq), dot_nn(XT[...], DK[:, cols]), dot_nn(XT[...], DV[:, cols]))
            ):
                GA[:, :, :, :, :, lo + n * 256 : lo + (n + 1) * 256] = made.astype(bf16).reshape(*grid, -1, 256)
            script.point()

        halves(False, 0)
        halves(True, 0)
        group(0)
        halves(False, 1)
        halves(False, 2)
        groups = [slice(g * 256, (g + 1) * 256) for g in range(3)]
        theirs = jnp.concatenate([a[local:, cols] for cols in groups for a in (DK, DV)], axis=1)
        through = [WA[:, :, :, :, :, g * D + 256 : (g + 1) * D].reshape(D, 512) for g in range(3)]
        SEND[...] = dot_nt(theirs, jnp.concatenate(through, axis=1)).astype(bf16)
        script.point()
        halves(True, 1)
        group(1)
        halves(True, 2)
        group(2)
        T[:, :, :, :, 0:8, :] = gather_vectors(SUMS[0:8, :], D // pieces, pieces).reshape(*grid, 8, 128)
        script.point()
        for g in range(3):
            cols = slice(g * 256, (g + 1) * 256)
            ours = jnp.concatenate([DQ[:, cols], DK[:local, cols], DV[:local, cols]], axis=1)
            DR1[...] += dot_nt(ours, WA[:, :, :, :, :, g * D : (g + 1) * D].reshape(D, D))
            script.point()
        script.close()
        out = pltpu.make_async_copy(DR1, dx_hbm, load_sems.at[loads[0]])
        out.start()
        swap.wait_recv()
        taken = pltpu.make_async_copy(RECV, taken_hbm, load_sems.at[loads[0] + 1])
        taken.start()
        pairs = ((OA, oa_hbm), (OI, oi_hbm), (OU, ou_hbm), (T.at[z, x, c, y], os_hbm), (TOP.at[4], ot_hbm))
        ends = [pltpu.make_async_copy(s, d, load_sems.at[loads[0] + 2 + n]) for n, (s, d) in enumerate(pairs)]
        for end in ends:
            end.start()
        for end in (out, taken, *ends):
            end.wait()

    scoped = [
        ((local, D), bf16), ((D, local), bf16), ((seq_len, D), bf16), ((D, seq_len), bf16), ((seq_len, D), bf16),
        ((D, seq_len), bf16), ((H, 1, local), f32), ((H, 32, local), bf16), ((H, 32, local), bf16), ((local, D), bf16),
        ((D, local), bf16), ((local, 2 * local), bf16), ((local, 2 * local), bf16), ((D, local), f32), ((D, local), bf16),
        ((local, D), bf16), ((seq_len, D), bf16), ((seq_len, D), bf16),
    ]
    pl.run_scoped(second_stage, *(pltpu.VMEM(*s) for s in scoped))
    remote.finish()


def run_backward(nz, local, rows, rows_u, length, *arrays):
    grid = (nz, 2, 2, 2)
    seq = 2 * local
    outs = [((local, D), f32), ((local, D), bf16), ((rows, 4 * D), f32), ((rows, FF), f32), ((rows_u, D), f32)]
    outs += [((16, 128), f32)] * 2
    scratch = [
        ((*grid, rows, 4 * D), bf16), ((*grid, rows, FF), bf16), ((*grid, rows_u, D), bf16), ((*grid, rows, 4 * D), bf16),
        ((*grid, 16, 128), f32), ((5, 16, 128), f32), ((3 + nz - 1, 16, 128), f32),
        ((local, D), bf16), ((D, local), bf16), ((local, D), f32), ((seq, 128), bf16),
        ((8, D), f32), ((1, FF), f32), ((local, D), bf16), ((local, D), bf16),
        ((16, D), f32), ((rows, 4 * D), f32), ((rows, FF), f32), ((rows_u, D), f32),
    ]
    for buf, _, width, order in SCATTER_ITEMS:
        scratch += scatter_buffers(nz, rows_u if buf == 2 else rows, width, order)
    scratch += small_buffers(nz)
    copies = copies_of(SCATTER_ITEMS, nz) + 2 * (3 + nz - 1) + 1
    return pl.pallas_call(
        functools.partial(backward_kernel, nz, local),
        out_shape=[jax.ShapeDtypeStruct(*o) for o in outs],
        in_specs=[INSMEM] + [ANY] * len(arrays),
        out_specs=[ANY] * len(outs),
        scratch_shapes=[pltpu.VMEM(*s) for s in scratch]
        + [pltpu.SemaphoreType.DMA((copies,)), pltpu.SemaphoreType.DMA((copies,)), pltpu.SemaphoreType.DMA((40,))],
        compiler_params=pltpu.CompilerParams(collective_id=2, has_side_effects=True, vmem_limit_bytes=VMEM_BYTES),
        name="backward_scatter",
    )(length, *arrays)


def finish_kernel(
    threshold_ref, dx_hbm, taken_hbm, ga_hbm, gi_hbm, gu_hbm, gs_hbm, top_hbm, out_hbm, WQ, WK, BQ,
    o_out, o_dx, o_q, o_k, o_v, o_o, o_i, o_u, o_wq, o_wk, o_bq, o_top, *rest,
):
    v_hbm, (DX, TAKEN, GS, TOP, GA, GI, GU, OUT), (s_wq, s_wk, s_bq, s_top), o_vecs, sems = (
        rest[:9], rest[9:17], rest[17:21], rest[21:30], rest[30]
    )
    pairs = [(dx_hbm, DX), (taken_hbm, TAKEN), (ga_hbm, GA), (gi_hbm, GI), (gu_hbm, GU), (out_hbm, OUT), (gs_hbm, GS), (top_hbm, TOP)]
    loads = [pltpu.make_async_copy(src, dst, sems.at[n]) for n, (src, dst) in enumerate(pairs)]
    for copy in loads:
        copy.start()
    stores = []

    def put(src, dst):
        copy = pltpu.make_async_copy(src, dst, sems.at[len(loads) + len(stores)])
        copy.start()
        stores.append(copy)

    loads[0].wait()
    loads[1].wait()
    DX[...] = DX[...] + TAKEN[...].astype(f32)
    put(DX, o_dx)
    loads[2].wait()
    for g in range(3):
        for n, o in enumerate((o_q, o_k, o_v)):
            lo = g * D + n * 256
            put(GA.at[:, lo : lo + 256], o.at[:, g * 256 : (g + 1) * 256])
    put(GA.at[:, 3 * D : 4 * D], o_o)
    for copy, src, dst in zip(loads[3:6], (GI, GU, OUT), (o_i, o_u, o_out)):
        copy.wait()
        put(src, dst)
    loads[6].wait()
    loads[7].wait()
    for n, o in enumerate(o_vecs):
        o[...] = GS[n : n + 1, 0 : o.shape[1]]
    limit = threshold_ref[0].astype(f32) * 0.01
    top = TOP[...]
    factors = jnp.sqrt(limit / jnp.maximum(top, limit))
    head = lax.broadcasted_iota(jnp.int32, (16, D), 0)
    column = lax.broadcasted_iota(jnp.int32, (16, D), 1)
    wide = jnp.concatenate([factors] * (D // 128), axis=1)
    scale = row_sum(jnp.where(head == lax.shift_right_logical(column, 6), wide, 0.0))
    s_wq[...] = (WQ[...].astype(f32) * scale).astype(bf16)
    s_wk[...] = (WK[...].astype(f32) * scale).astype(bf16)
    count = BQ.shape[1]
    row = lax.broadcasted_iota(jnp.int32, (16, 128), 0)
    lane = lax.broadcasted_iota(jnp.int32, (16, 128), 1)
    entry = (lax.axis_index("dp") * 2 + lax.axis_index("ctx")) * count + lane
    own = row_sum(jnp.where(row == lax.shift_right_logical(entry, 6), factors, 0.0))
    s_bq[...] = (BQ[...].astype(f32) * own[:, 0:count]).astype(bf16)
    s_top[...] = row_sum(jnp.where(row == lane, top, 0.0))[:, 0:H]
    for src, dst in zip((s_wq, s_wk, s_bq, s_top, *o_vecs), (o_wq, o_wk, o_bq, o_top, *v_hbm)):
        put(src, dst)
    for copy in stores:
        copy.wait()


def run_finish(threshold, dx, taken, ga, gi, gu, gs, top, output, wq, wk, bq, wide):
    local, rows, rows_u, count = dx.shape[0], ga.shape[0], gu.shape[0], bq.shape[0]
    outs = [((local, D), bf16), ((local, D), f32)] + [((rows, D), f32)] * 4 + [((rows, FF), f32), ((rows_u, D), f32)]
    outs += [((rows, D), bf16)] * 2 + [((1, count), bf16), ((1, H), f32)] + [((1, count), f32)] * 8 + [((1, wide), f32)]
    return pl.pallas_call(
        finish_kernel,
        out_shape=[jax.ShapeDtypeStruct(*o) for o in outs],
        in_specs=[INSMEM] + [ANY] * 8 + [INVMEM] * 3,
        out_specs=[ANY] * len(outs),
        scratch_shapes=[
            pltpu.VMEM((local, D), f32), pltpu.VMEM((local, D), bf16), pltpu.VMEM((16, 128), f32), pltpu.VMEM((16, 128), f32),
            pltpu.VMEM((rows, 4 * D), f32), pltpu.VMEM((rows, FF), f32), pltpu.VMEM((rows_u, D), f32),
            pltpu.VMEM((local, D), bf16),
        ]
        + [pltpu.VMEM(*o) for o in outs[8:]]
        + [pltpu.SemaphoreType.DMA((36,))],
        compiler_params=pltpu.CompilerParams(vmem_limit_bytes=VMEM_BYTES),
        name="finish",
    )(threshold, dx, taken, ga, gi, gu, gs, top, output, wq, wk, bq.reshape(1, -1))


def layer_norm(row_values, gain_vector, shift_vector):
    centre = row_values - jnp.mean(row_values, axis=-1, keepdims=True)
    spread = jnp.mean(centre * centre, axis=-1, keepdims=True)
    return centre * lax.rsqrt(spread + norm_eps) * gain_vector + shift_vector


def gelu_exact(values):
    return jax.nn.gelu(values, approximate=False)


def column_sums(values):
    return jnp.sum(values.astype(f32), axis=0)


def clip_outputs(logit_maxima, threshold, query_weight, query_bias, key_weight, device_rank):
    clip_limit = threshold.astype(f32)[0] * 0.01
    factors = jnp.sqrt(clip_limit / jnp.maximum(logit_maxima, clip_limit))
    column_scale = jnp.repeat(factors, HD)
    query_clipped = (query_weight.astype(f32) * column_scale[None, :]).astype(bf16)
    key_clipped = (key_weight.astype(f32) * column_scale[None, :]).astype(bf16)
    bias_count = query_bias.shape[0]
    bias_heads = (device_rank * bias_count + jnp.arange(bias_count)) // HD
    bias_scale = jnp.sum(jnp.where(bias_heads[:, None] == jnp.arange(H)[None, :], factors[None, :], 0.0), axis=1)
    return query_clipped, (query_bias.astype(f32) * bias_scale).astype(bf16), key_clipped


def fast_shards(
    nz,
    inputs, cotangent, query_weight, query_bias, key_weight, value_weight, value_bias, output_weight, output_bias,
    first_gain, first_shift, inner_weight, inner_bias, outer_weight, outer_bias, second_gain, second_shift,
    lengths, random_blocks, threshold,
):
    local = inputs.shape[1]
    pieces = nz * 8
    rows, rows_u = query_weight.shape[0], outer_weight.shape[0]
    small = (
        query_bias, value_bias, output_bias, first_gain, first_shift, outer_bias, second_gain, second_shift, inner_bias
    )
    x = inputs[0]
    weights = (query_weight, key_weight, value_weight, output_weight, inner_weight, outer_weight)
    output, *saved = run_forward(nz, x, weights, small, jnp.transpose(random_blocks, (2, 3, 0, 1)), lengths)
    made = run_backward(nz, local, rows, rows_u, lengths, cotangent[0], *saved)
    (
        output, input_grad, g_query, g_key, g_value, g_out, g_inner, g_outer, query_clipped, key_clipped, bias_clipped, top, *vec
    ) = run_finish(threshold, *made, output, query_weight, key_weight, query_bias, FF // pieces)
    vec = [v.reshape(-1) for v in vec]
    return (
        output[None], input_grad[None],
        g_query, vec[0], g_key, g_value, vec[1], g_out, vec[2], vec[3], vec[4],
        g_inner, vec[8], g_outer, vec[5], vec[6], vec[7],
        query_clipped, bias_clipped.reshape(-1), key_clipped, top.reshape(-1),
    )


def general_shards(
    inputs, cotangent, query_weight, query_bias, key_weight, value_weight, value_bias, output_weight, output_bias,
    first_gain, first_shift, inner_weight, inner_bias, outer_weight, outer_bias, second_gain, second_shift,
    lengths, random_blocks, threshold,
):
    both = ("dp", "ctx")
    shards = (
        query_weight, query_bias, key_weight, value_weight, value_bias, output_weight, output_bias, first_gain, first_shift,
        inner_weight, inner_bias, outer_weight, outer_bias, second_gain, second_shift,
    )
    wq, bq, wk, wv, bv, wo, bo, g1, s1, wi, bi, wu, bu, g2, s2 = (lax.all_gather(w, both, axis=0, tiled=True) for w in shards)
    bq, bv, bo, g1, s1, bi, bu, g2, s2 = (v.astype(f32) for v in (bq, bv, bo, g1, s1, bi, bu, g2, s2))
    seqs, local, _ = inputs.shape
    blocks = local // BLK
    y = lax.axis_index("ctx")
    first_block = y * blocks
    scale = HD**-0.5
    outs = []
    sums = None
    top = jnp.full((H,), neg_large, f32)
    for s in range(seqs):
        x, length = inputs[s], lengths[s]
        random_here = lax.dynamic_slice_in_dim(random_blocks[s], first_block, blocks, 0)
        mask = compact_mask(random_here, length, first_block)
        mask = jnp.repeat(jnp.repeat(mask, BLK, axis=1), BLK, axis=2)
        seen = jnp.arange(NB * BLK) < length
        mask = jnp.where(seen[None, None, :], mask, neg_large)
        live = (y * local + jnp.arange(local)) < length
        q = (dot_nn(x, wq) + bq).astype(bf16)
        k = lax.all_gather(dot_nn(x, wk).astype(bf16), "ctx", axis=0, tiled=True)
        v = lax.all_gather((dot_nn(x, wv) + bv).astype(bf16), "ctx", axis=0, tiled=True)
        qh, kh, vh = (a.reshape(-1, H, HD) for a in (q, k, v))
        raw = jnp.einsum("qhd,khd->hqk", qh, kh, preferred_element_type=f32) * scale + mask
        row_top = jnp.max(raw, axis=-1, keepdims=True)
        top = jnp.maximum(top, jnp.max(jnp.where(live[None, :, None], row_top, neg_large), axis=(1, 2)))
        exponent = jnp.exp(raw - row_top)
        prob = exponent / jnp.sum(exponent, axis=-1, keepdims=True)
        low = prob.astype(bf16)
        attended = jnp.einsum("hqk,khd->qhd", low, vh, preferred_element_type=f32).reshape(local, D).astype(bf16)
        first_sum = x.astype(f32) + dot_nn(attended, wo) + bo
        normed = layer_norm(first_sum, g1, s1)
        normed_low = normed.astype(bf16)
        pre_act = dot_nn(normed_low, wi) + bi
        activated = gelu_exact(pre_act).astype(bf16)
        second_sum = normed + dot_nn(activated, wu) + bu
        output = layer_norm(second_sum, g2, s2).astype(bf16)
        cot = jnp.where(live[:, None], cotangent[s].astype(f32), 0.0)
        grad_second, g2_grad, s2_grad = jax.vjp(layer_norm, second_sum, g2, s2)[1](cot)
        dm = grad_second.astype(bf16)
        du = jax.vjp(gelu_exact, pre_act)[1](dot_nt(dm, wu))[0].astype(bf16)
        grad_normed = grad_second + dot_nt(du, wi)
        grad_first, g1_grad, s1_grad = jax.vjp(layer_norm, first_sum, g1, s1)[1](grad_normed)
        dp = grad_first.astype(bf16)
        da = dot_nt(dp, wo).astype(bf16).reshape(local, H, HD)
        dprob = jnp.einsum("qhd,khd->hqk", da, vh, preferred_element_type=f32)
        ds = (prob * (dprob - jnp.sum(prob * dprob, axis=-1, keepdims=True))).astype(bf16)
        dq = (jnp.einsum("hqk,khd->qhd", ds, kh, preferred_element_type=f32) * scale).reshape(local, D).astype(bf16)
        dk = (jnp.einsum("hqk,qhd->khd", ds, qh, preferred_element_type=f32) * scale).reshape(-1, D)
        dv = jnp.einsum("hqk,qhd->khd", low, da, preferred_element_type=f32).reshape(-1, D)
        dk, dv = (lax.psum_scatter(a.astype(bf16), "ctx", scatter_dimension=0, tiled=True).astype(bf16) for a in (dk, dv))
        input_grad = grad_first + dot_nt(dq, wq) + dot_nt(dk, wk) + dot_nt(dv, wv)
        outs.append((output, input_grad))
        here = (
            dot_tn(x, dq), column_sums(dq), dot_tn(x, dk), dot_tn(x, dv), column_sums(dv), dot_tn(attended, dp),
            column_sums(dp), g1_grad, s1_grad, dot_tn(normed_low, du), column_sums(du), dot_tn(activated, dm),
            column_sums(dm), g2_grad, s2_grad,
        )
        sums = here if sums is None else tuple(a + b for a, b in zip(sums, here))
    grads = tuple(lax.psum_scatter(g, both, scatter_dimension=0, tiled=True) for g in sums)
    logit_maxima = lax.pmax(top, both)
    rank = lax.axis_index(both)
    clipped = clip_outputs(logit_maxima, threshold, query_weight, query_bias, key_weight, rank)
    return (jnp.stack([o for o, _ in outs]), jnp.stack([g for _, g in outs]), *grads, *clipped, logit_maxima)


def solution(mesh):
    both = P(("dp", "ctx"))
    rows = P(("dp", "ctx"), None)
    tokens = P("dp", "ctx", None)
    in_specs = (
        tokens, tokens, rows, both, rows, rows, both, rows, both, both, both, rows, both, rows, both, both, both,
        P("dp"), P("dp", None, None, None), P(),
    )
    out_specs = (
        tokens, tokens, rows, both, rows, rows, both, rows, both, both, both, rows, both, rows, both, both, both,
        rows, both, rows, P(),
    )
    dp, ctx = mesh.shape["dp"], mesh.shape["ctx"]
    pieces = dp * ctx
    fits = ctx == 2 and dp % 4 == 0 and D % (8 * pieces) == 0 and FF // pieces <= 128

    def step(*args):
        if fits and args[0].shape[0] == 1:
            return fast_shards(dp // 4, *args)
        return general_shards(*args)

    return jax.shard_map(step, mesh=mesh, in_specs=in_specs, out_specs=out_specs, check_vma=False)
```

```python
import functools

import jax
import jax.numpy as jnp
import numpy as np
from jax import lax
from jax.experimental import pallas as pl
from jax.experimental.pallas import tpu as pltpu
from jax.sharding import PartitionSpec as P

H = 12
HD = 64
BLK = 64
LEN = 1024
NB = 16
D = 768
FF = 3072

norm_eps = 1e-12
neg_large = -1e30
bf16 = jnp.bfloat16
f32 = jnp.float32
ANY = pl.BlockSpec(memory_space=pl.ANY)
INVMEM = pl.BlockSpec(memory_space=pltpu.VMEM)
INSMEM = pl.BlockSpec(memory_space=pltpu.SMEM)
MESH = pl.DeviceIdType.MESH


def dot_nn(a, b):
    return jnp.dot(a, b, preferred_element_type=f32)


def dot_nt(a, b):
    return lax.dot_general(a, b, (((1,), (1,)), ((), ())), preferred_element_type=f32)


def dot_tn(a, b):
    return lax.dot_general(a, b, (((0,), (0,)), ((), ())), preferred_element_type=f32)


def ds128(index, width):
    return pl.ds(pl.multiple_of(index * width, width), width)


class Place:
    def __init__(self, nz):
        self.nz = nz
        dp = lax.axis_index("dp")
        self.y = lax.axis_index("ctx")
        self.c = lax.rem(dp, 2)
        self.x = lax.rem(lax.div(dp, 2), 2)
        self.z = lax.div(dp, 4)

    def at(self, z=None, x=None, c=None, y=None):
        z = self.z if z is None else z
        x = self.x if x is None else x
        c = self.c if c is None else c
        y = self.y if y is None else y
        return ((z * 2 + x) * 2 + c, y)

    def z_off(self, k):
        return lax.rem(self.z + k, self.nz)

    def along(self, axis):
        if axis == "z":
            return [self.at(z=self.z_off(k)) for k in range(1, self.nz)]
        return [self.at(x=1 - self.x) if axis == "x" else self.at(y=1 - self.y)]

    def peers(self):
        return (
            [self.at(z=self.z_off(k)) for k in range(1, self.nz)]
            + [self.at(x=1 - self.x), self.at(y=1 - self.y), self.at(c=1 - self.c)]
        )


def entry_barrier(place):
    barrier = pltpu.get_barrier_semaphore()
    peers = place.peers()
    for peer in peers:
        pl.semaphore_signal(barrier, inc=1, device_id=peer, device_id_type=MESH)
    pl.semaphore_wait(barrier, len(peers))


class Conditional:
    def __init__(self, copy, sends, receives):
        self.copy, self.sends, self.receives = copy, sends, receives

    def start(self):
        pl.when(self.sends)(self.copy.start)

    def wait_recv(self):
        pl.when(self.receives)(self.copy.wait_recv)

    def wait_send(self):
        pl.when(self.sends)(self.copy.wait_send)


class Remote:
    def __init__(self, send_sems, recv_sems):
        self.send_sems, self.recv_sems, self.used, self.copies = send_sems, recv_sems, 0, []

    def make(self, src, dst, peer, sends=None, receives=None):
        k = self.used
        self.used += 1
        copy = pltpu.make_async_remote_copy(
            src_ref=src, dst_ref=dst, send_sem=self.send_sems.at[k], recv_sem=self.recv_sems.at[k],
            device_id=peer, device_id_type=MESH,
        )
        if sends is not None:
            copy = Conditional(copy, sends, receives)
        self.copies.append(copy)
        return copy

    def finish(self):
        for copy in self.copies:
            copy.wait_send()


class Stripe:
    def __init__(self):
        self.stages, self.awaited, self.at = [], {}, 0

    def take(self, n):
        pass

    def step(self):
        n = self.at
        if n > 0:
            for copy in self.awaited.get(n, self.stages[n - 1]):
                copy.wait_recv()
            self.take(n - 1)
        if n < len(self.stages):
            for copy in self.stages[n]:
                copy.start()
        self.at = n + 1


class GatherStripe(Stripe):
    def __init__(self, remote, place, buf, cols, order):
        super().__init__()
        have = {"z": place.z, "x": place.x, "y": place.y}
        for axis in order:
            ref = buf.at[have["z"], have["x"], place.c, have["y"], :, cols]
            if axis == "z" and place.nz == 4:
                self.along_line(remote, place, lambda z: buf.at[z, have["x"], place.c, have["y"], :, cols])
            else:
                self.stages.append([remote.make(ref, ref, peer) for peer in place.along(axis)])
                if axis == "z":
                    self.stages.append([])
                    self.awaited[len(self.stages) - 1] = []
                    self.awaited[len(self.stages)] = self.stages[-2]
            have[axis] = slice(None)
        ref = buf.at[:, :, place.c, :, :, cols]
        self.stages.append([remote.make(ref, ref, place.at(c=1 - place.c))])

    def along_line(self, remote, place, block):
        z, mine = place.z, block(place.z)
        moves = [
            remote.make(mine, mine, place.at(z=lax.rem(z + 2, 4)), z < 2, z >= 2),
            remote.make(mine, mine, place.at(z=lax.rem(z + 2, 4)), z >= 2, z < 2),
            remote.make(mine, mine, place.at(z=lax.rem(z + 1, 4)), z < 3, z > 0),
            remote.make(mine, mine, place.at(z=lax.rem(z + 3, 4)), z > 0, z < 3),
        ]
        onward = [
            remote.make(block(0), block(0), place.at(z=lax.rem(z + 1, 4)), z == 2, z == 3),
            remote.make(block(3), block(3), place.at(z=lax.rem(z + 3, 4)), z == 1, z == 0),
        ]
        self.stages += [moves, onward]
        self.awaited[len(self.stages) - 1] = moves[:2]
        self.awaited[len(self.stages)] = moves[2:] + onward


class GatherTile(Stripe):
    def __init__(self, remote, place, buf):
        super().__init__()
        z, x, c, y = place.z, place.x, place.c, place.y
        for ref, peers in (
            (buf.at[z, x, c, y], place.along("z")),
            (buf.at[:, x, c, y], place.along("x")),
            (buf.at[:, :, c, y], place.along("y")),
            (buf.at[:, :, c], [place.at(c=1 - c)]),
        ):
            self.stages.append([remote.make(ref, ref, peer) for peer in peers])


class ScatterStripe(Stripe):
    def __init__(self, remote, place, g, cols, order, bufs, out):
        super().__init__()
        self.place, self.g, self.cols, self.order, self.bufs, self.out = place, g, cols, order, bufs, out
        own = {"z": place.z, "x": place.x, "y": place.y}
        have = {"z": slice(None), "x": slice(None), "y": slice(None)}
        ref = g.at[:, :, 1 - place.c, :, :, cols]
        self.stages.append([remote.make(ref, bufs[0], place.at(c=1 - place.c))])
        for n, axis in enumerate(order):
            made = []
            for k, peer in enumerate(place.along(axis)):
                there = dict(have)
                there[axis] = place.z_off(k + 1) if axis == "z" else 1 - own[axis]
                ref = g.at[there["z"], there["x"], place.c, there["y"], :, cols]
                made.append(remote.make(ref, bufs[n + 1].at[k] if axis == "z" else bufs[n + 1], peer))
            self.stages.append(made)
            have[axis] = own[axis]

    def take(self, n):
        place, g, cols, buf = self.place, self.g, self.cols, self.bufs[n]
        axis = self.order[n - 1] if n > 0 else "c"
        still = self.order[n:]
        sizes = {"z": place.nz, "x": 2, "y": 2}
        names = [name for name in "zxy" if name in still]
        count = 1
        for name in names:
            count *= sizes[name]

        def add(k, last):
            here = {"z": place.z, "x": place.x, "y": place.y}
            left = k
            for name in reversed(names):
                here[name] = lax.rem(left, sizes[name])
                left = lax.div(left, sizes[name])
            index = tuple(here[name] for name in names)
            spot = (here["z"], here["x"], place.c, here["y"], slice(None), cols)
            if axis != "z" and not last:
                g[spot] = g[spot] + buf[index]
                return
            total = g[spot].astype(f32)
            for part in range(place.nz - 1) if axis == "z" else (None,):
                total = total + buf[index if part is None else (part, *index)].astype(f32)
            if last:
                self.out[:, cols] = total
            else:
                g[spot] = total.astype(bf16)

        if not names:
            add(0, True)
        elif count <= 2:
            for k in range(count):
                add(k, False)
        else:

            def four(k, carry):
                for n in range(4):
                    add(4 * k + n, False)
                return carry

            lax.fori_loop(0, count // 4, four, 0)


def scatter_buffers(nz, rows, width, order):
    sizes = {"z": nz, "x": 2, "y": 2}
    made = [((nz, 2, 2, rows, width), bf16)]
    for n, axis in enumerate(order):
        left = [sizes[name] for name in "zxy" if name in order[n + 1 :]]
        made.append((((nz - 1,) if axis == "z" else ()) + (*left, rows, width), bf16))
    return made


class SmallSums(Stripe):
    def __init__(self, remote, place, t, bufs):
        super().__init__()
        z, x, c, y = place.z, place.x, place.c, place.y
        rc, ry, rx, rz = bufs
        self.place, self.t, self.bufs = place, t, bufs
        self.stages = [
            [remote.make(t.at[:, :, 1 - c], rc, place.at(c=1 - c))],
            [remote.make(t.at[:, :, c, 1 - y], ry, place.at(y=1 - y))],
            [remote.make(t.at[:, 1 - x, c, y], rx, place.at(x=1 - x))],
            [remote.make(t.at[place.z_off(k + 1), x, c, y], rz.at[k], peer) for k, peer in enumerate(place.along("z"))],
        ]

    def take(self, n):
        place, t = self.place, self.t
        rc, ry, rx, rz = self.bufs
        z, x, c, y = place.z, place.x, place.c, place.y
        if n == 0:
            t[:, :, c] = t[:, :, c] + rc[...]
        elif n == 1:
            t[:, :, c, y] = t[:, :, c, y] + ry[...]
        elif n == 2:
            t[:, x, c, y] = t[:, x, c, y] + rx[...]
        else:
            total = t[z, x, c, y]
            for k in range(place.nz - 1):
                total = total + rz[k]
            t[z, x, c, y] = total


def small_buffers(nz):
    return [((nz, 2, 2, 16, 128), f32), ((nz, 2, 16, 128), f32), ((nz, 16, 128), f32), ((nz - 1, 16, 128), f32)]


class TopOfAll(Stripe):
    def __init__(self, remote, place, top, tops):
        super().__init__()
        self.top, self.tops, self.slots, slot = top, tops, [], 0
        for n, peers in enumerate(([place.at(c=1 - place.c)], place.along("y"), place.along("x"), place.along("z"))):
            self.slots.append(list(range(slot, slot + len(peers))))
            self.stages.append([remote.make(top.at[n], tops.at[slot + k], peer) for k, peer in enumerate(peers)])
            slot += len(peers)

    def take(self, n):
        best = self.top[n]
        for slot in self.slots[n]:
            best = jnp.maximum(best, self.tops[slot])
        self.top[n + 1] = best


class Script:
    def __init__(self, plan, stripes, swap):
        self.plan, self.stripes, self.swap, self.spent = plan, stripes, swap, 0

    def point(self):
        for item in self.plan[self.spent]:
            if item < 0:
                self.swap.start()
            else:
                self.stripes[item].step()
        self.spent += 1

    def points(self, index, first, count):
        for k in range(count):
            pl.when(index == first + k)(self.point)

    def close(self):
        assert self.spent == len(self.plan)
        assert all(s.at == len(s.stages) + 1 for s in self.stripes)


VMEM_BYTES = 60 << 20
GATHER_ITEMS = (
    (0, 0, 384, "yzx"), (0, 384, 384, "yzx"), (0, 768, 384, "yzx"), (0, 1152, 384, "zxy"), (0, 1536, 256, "yzx"),
    (0, 1792, 256, "yzx"), (0, 2048, 256, "yzx"), (0, 2304, 384, "zyx"), (0, 2688, 384, "xzy"), (1, 0, 384, "zxy"),
    (1, 384, 384, "yzx"), (1, 768, 768, "zxy"), (1, 1536, 256, "zyx"), (1, 1792, 256, "yzx"), (1, 2048, 256, "yzx"),
    (1, 2304, 384, "zxy"), (1, 2688, 384, "zyx"), (2, 0, 256, "xzy"), (2, 256, 128, "zyx"), (2, 384, 128, "yzx"),
    (2, 512, 128, "xzy"), (2, 640, 128, "yzx"),
)
GATHER_PLAN = (
    (0, 1, 22, 2, 3, 4, 5, 6, -1),
    (0, 1, 2, 4, 22, 3, 5, 6, 22, 3, 0, 3, 0, 1, 2, 7, 8, 9, 11, 1, 2, 0, 8, 4, 0, 10, 4, 1, 5, 6, 7, 5, 1, 12, 6, 22, 7, 9, 2, 22, 13),
    (11,), (2, 4, 8, 9, 14, 3, 10, 11, 12, 4, 15, 5, 8, 7, 13, 3, 16), (5, 12, 14, 18, 6, 9, 6, 17), (8, 10), (12, 15),
    (8, 11, 10, 13, 15, 19), (9, 13, 14, 16), (7, 14, 18, 17), (9, 16, 18, 21), (7, 12), (11, 12, 19, 20), (10, 16),
    (11, 15, 17), (10, 13, 18, 21), (14,), (13, 14, 15, 17, 20), (19,), (15, 16, 21), (19,), (16, 18, 21, 20), (), (),
    (18, 20), (17,), (), (19,), (), (17,), (19, 20), (21,), (), (21, 20), (), (), (),
)
SCATTER_ITEMS = (
    (2, 0, 128, "xzy"), (2, 128, 128, "yxz"), (2, 256, 256, "yzx"), (2, 512, 128, "xzy"), (2, 640, 128, "yxz"),
    (1, 0, 768, "xyz"), (1, 768, 768, "yxz"), (1, 1536, 768, "xyz"), (1, 2304, 768, "xyz"), (0, 0, 768, "xzy"),
    (0, 768, 384, "xzy"), (0, 1152, 384, "xyz"), (0, 1536, 384, "xzy"), (0, 1920, 384, "xyz"), (0, 2304, 768, "yxz"),
)
SCATTER_PLAN = (
    (), (), (), (0, 1), (2,), (0, 1, 3, 4), (2, 3, 4, 0, 1), (5, 15), (6,), (7,), (8, 5, 15), (3, 6, 0), (), (1, 7), (8, 2),
    (), (), (4, 5, 15), (3,), (1, 14), (0, 6, 7), (14,), (2, 3, 5, 9), (8, 7), (4, 15, 9), (6,), (2, 5, 14), (7, -1),
    (4, 15, 8), (9,), (6, 10, 11), (14, 10), (11,), (8, 12, 13), (10, 16), (12, 13), (11, 16),
    (9, 14, 12, 11, 16, 13, 9, 10, 16, 12, 13, 10, 11, 12, 16, 13),
)

def layer_norm_parts(rows):
    centre = rows - jnp.mean(rows, axis=-1, keepdims=True)
    spread = jnp.mean(centre * centre, axis=-1, keepdims=True)
    inverse = lax.rsqrt(spread + norm_eps)
    return centre * inverse, inverse


def head_lanes(rows, half):
    lane = lax.broadcasted_iota(jnp.int32, rows.shape, 1)
    return jnp.where((lane >= HD) == (half == 1), rows, jnp.zeros_like(rows))


def key_structure(local, y, length):
    lane = lax.broadcasted_iota(jnp.int32, (2 * local, 128), 1)
    row = lax.broadcasted_iota(jnp.int32, (2 * local, 128), 0)
    position = jnp.where(row < local, row + y * local, row - y * local)
    own = lane == lax.shift_right_logical(position, 6)
    beyond = (lane == NB) & (position >= length)
    return jnp.where(own | beyond | ((lane > NB) & (lane < NB + 4)), 1.0, 0.0).astype(bf16)


def head_rows(rows, half):
    row = lax.broadcasted_iota(jnp.int32, rows.shape, 0)
    return jnp.where((row >= HD) == (half == 1), rows, jnp.zeros_like(rows))


def in_three(values):
    high = values.astype(bf16)
    rest = values - high.astype(f32)
    middle = rest.astype(bf16)
    return high, middle, (rest - middle.astype(f32)).astype(bf16)


def with_rows(base, values):
    row = lax.broadcasted_iota(jnp.int32, base.shape, 0)
    for k, part in enumerate(in_three(-values)):
        base = base + jnp.where(row == NB + 1 + k, part.astype(f32), 0.0)
    return base.astype(bf16)


def spread_vectors(tiles, width, pieces):
    rows = tiles.shape[1]
    total = pieces * width
    lane = lax.broadcasted_iota(jnp.int32, (128, total), 1).astype(f32)
    row = lax.broadcasted_iota(jnp.int32, (128, total), 0).astype(f32)
    owner = jnp.floor((lane + 0.5) * (1.0 / width))
    chooser = jnp.where(lane - owner * width == row, 1.0, 0.0).astype(bf16)
    wide = dot_nn(tiles.reshape(pieces * rows, 128), chooser).reshape(pieces, rows, total)
    lane3 = lax.broadcasted_iota(jnp.int32, (pieces, rows, total), 2).astype(f32)
    piece3 = lax.broadcasted_iota(jnp.int32, (pieces, rows, total), 0).astype(f32)
    mine = jnp.floor((lane3 + 0.5) * (1.0 / width)) == piece3
    return jnp.sum(jnp.where(mine, wide, 0.0), axis=0)


def forward_kernel(
    nz, local, length_ref, random_hbm, x_hbm, wq, wk, wv, wo, wi, wu, v0, v1, v2, v3, v4, v5, v6, v7, v8,
    out_hbm, r1_hbm, r2_hbm, gp_hbm, gt_hbm, n1t_hbm, at_hbm, atf_hbm, q_hbm, qt_hbm, k_hbm, kt_hbm, v_hbm, xt_hbm, lse_hbm,
    top_hbm, wa_hbm, wi_hbm, wu_hbm, vec_hbm, mask_hbm,
    WA, WI, WU, SM, XF, XT, Q, QT, K, KT, V, VT, AT, ATF, R1, R2, N1L, N1T, U, GP, G, GT, E, VEC, IB, LSE, TOP, TT, OUT, MASK, *rest,
):
    place = Place(nz)
    z, x, c, y = place.z, place.x, place.c, place.y
    small, (random_ref, send_sems, recv_sems, local_sems, out_sems) = rest[:9], rest[9:]
    remote = Remote(send_sems, recv_sems)
    mine = (z, x, c, y)
    locals_ = list(zip((v0, v1, v2, v3, v4, v5, v6, v7, v8), small))
    locals_ += [(x_hbm, XF.at[0]), (random_hbm, random_ref)]
    for g in range(3):
        for n, w in enumerate((wq, wk, wv)):
            lo = g * D + n * 256
            locals_.append((w.at[:, g * 256 : (g + 1) * 256], WA.at[(*mine, slice(None), slice(lo, lo + 256))]))
    locals_ += [(wo, WA.at[(*mine, slice(None), slice(3 * D, 4 * D))]), (wi, WI.at[mine]), (wu, WU.at[mine])]
    locals_ = [pltpu.make_async_copy(src, dst, local_sems.at[k]) for k, (src, dst) in enumerate(locals_)]
    for copy in locals_:
        copy.start()
    TT[...] = jnp.zeros((16, 128), f32)
    for n, v in enumerate(small):
        locals_[n].wait()
        TT[n : n + 1, 0 : v.shape[1]] = v[...].astype(f32)
    SM[mine] = TT[...].astype(bf16)
    entry_barrier(place)
    for copy in locals_[9:]:
        copy.wait()

    outs = []

    def put(src, dst):
        copy = pltpu.make_async_copy(src, dst, out_sems.at[len(outs)])
        copy.start()
        outs.append(copy)

    swap = remote.make(XF.at[0], XF.at[1], place.at(y=1 - y))
    stripes = [
        GatherStripe(remote, place, (WA, WI, WU)[buf], slice(lo, lo + width), order) for buf, lo, width, order in GATHER_ITEMS
    ]
    stripes.append(GatherTile(remote, place, SM))
    script = Script(GATHER_PLAN, stripes, swap)
    script.point()
    length = length_ref[0]
    E[...] = key_structure(local, y, length)
    fill_masks(MASK, random_ref, y * (local // BLK), length)
    put(MASK, mask_hbm)
    XT[:, :local] = XF[0].T
    script.point()

    tiles = SM[...].reshape(-1, 16, 128)
    pieces = tiles.shape[0]
    VEC[...] = spread_vectors(tiles, D // pieces, pieces)
    IB[...] = spread_vectors(tiles[:, 8:16, :], FF // pieces, pieces)
    put(VEC, vec_hbm)
    script.point()
    position = y * local + lax.broadcasted_iota(jnp.int32, (1, local), 1)
    live = position < length

    def put_columns(buf, dst, lo, width):
        put(buf.at[:, :, :, :, :, lo : lo + width], dst.at[:, :, :, :, :, lo : lo + width])

    def wide(buf, lo, width):
        return buf[:, :, :, :, :, lo : lo + width].reshape(-1, width)

    for g in range(3):
        cols = slice(g * 256, (g + 1) * 256)
        put_columns(WA, wa_hbm, g * D, D)
        own = dot_nn(XF[0], wide(WA, g * D, D))
        q = ((own[:, :256] + VEC[0:1, cols]).astype(bf16).astype(f32) * (HD**-0.5)).astype(bf16)
        Q[:, cols] = q
        QT[cols, :] = q.T
        K[:local, cols] = own[:, 256:512].astype(bf16)
        values = (own[:, 512:] + VEC[1:2, cols]).astype(bf16)
        V[:local, cols] = values
        VT[cols, :local] = values.T
        script.point()
    put(Q, q_hbm)
    put(QT, qt_hbm)
    swap.wait_recv()
    for g in range(3):
        cols = slice(g * 256, (g + 1) * 256)
        theirs = dot_nn(XF[1], wide(WA, g * D + 256, 512))
        K[local:, cols] = theirs[:, :256].astype(bf16)
        values = (theirs[:, 256:] + VEC[1:2, cols]).astype(bf16)
        V[local:, cols] = values
        VT[cols, local:] = values.T
        script.point()

        def head_step(h, carry):
            lanes = ds128(lax.div(h, 2), 128)
            half = lax.rem(h, 2)
            own = pl.ds(pl.multiple_of(h * HD, HD), HD)
            left = jnp.concatenate([K[:, lanes], E[...]], axis=1)
            right = jnp.concatenate(
                [head_rows(QT[lanes, :], half), MASK[h], jnp.zeros((128 - 32, local), bf16)], axis=0
            )
            for part in range(local // 256):
                cols = slice(part * 256, (part + 1) * 256)
                scores = dot_nn(left, right[:, cols])
                top = jnp.max(scores, axis=0, keepdims=True)
                exponent = jnp.exp(scores - top)
                total = jnp.sum(exponent, axis=0, keepdims=True)
                low = (exponent * (1.0 / total)).astype(bf16)
                mixture = dot_nn(VT[own, :], low)
                ATF[own, cols] = mixture
                AT[own, cols] = mixture.astype(bf16)
                LSE[h, :, cols] = top + jnp.log(total)
                TOP[h, :, cols] = jnp.where(live[:, cols], top, neg_large)
            script.points(h, 4 * g, 4)
            return carry

        lax.fori_loop(4 * g, 4 * g + 4, head_step, 0)
    put(K, k_hbm)
    put(V, v_hbm)
    put(LSE, lse_hbm)
    TT[...] = jnp.zeros((16, 128), f32) + neg_large
    TT[0:H, :] = jnp.broadcast_to(jnp.max(TOP[:, 0, :], axis=1, keepdims=True), (H, 128))
    put(TT, top_hbm)
    put(AT, at_hbm)
    put(ATF, atf_hbm)
    put_columns(WA, wa_hbm, 3 * D, D)
    R1[...] = dot_nn(AT[...].T, wide(WA, 3 * D, D))
    script.point()

    def first_norm(k, carry):
        rows = ds128(k, 64)
        summed = XF[0, rows, :].astype(f32) + R1[rows, :] + VEC[2:3, :]
        R1[rows, :] = summed
        normal, _ = layer_norm_parts(summed)
        value = normal * VEC[3:4, :] + VEC[4:5, :]
        N1L[rows, :] = value.astype(bf16)
        R2[rows, :] = value + VEC[5:6, :]
        return carry

    lax.fori_loop(0, local // 64, first_norm, 0)
    put(R1, r1_hbm)
    script.point()
    N1T[...] = N1L[...].T
    put(N1T, n1t_hbm)
    XT[:, local:] = XF[1].T
    put(XT, xt_hbm)
    script.point()
    KT[...] = K[...].T
    put(KT, kt_hbm)
    script.point()
    for n in range(FF // D):
        cols = slice(n * D, (n + 1) * D)
        put_columns(WI, wi_hbm, n * D, D)
        U[...] = dot_nn(N1L[...], wide(WI, n * D, D)) + IB[0:1, cols]
        script.point()

        def activate(k, carry):
            rows = ds128(k, 16)
            u = U[rows, :]
            below = 0.5 * (1.0 + lax.erf(u * np.float32(0.5**0.5)))
            G[rows, cols] = (u * below).astype(bf16)
            GP[n, rows, :] = below + u * jnp.exp(-0.5 * u * u) * np.float32((2.0 * np.pi) ** -0.5)
            return carry

        lax.fori_loop(0, local // 16, activate, 0)
        put(GP.at[n], gp_hbm.at[n])
        GT[cols, :] = G[:, cols].T
        put(GT.at[cols, :], gt_hbm.at[cols, :])
        script.point()
    for n in range(3):
        cols = slice(n * 256, (n + 1) * 256)
        put_columns(WU, wu_hbm, n * 256, 256)
        R2[:, cols] += dot_nn(G[...], WU[:, :, :, :, :, cols].reshape(FF, 256))
        script.point()

    def second_norm(k, carry):
        rows = ds128(k, 64)
        normal, _ = layer_norm_parts(R2[rows, :])
        OUT[rows, :] = (normal * VEC[6:7, :] + VEC[7:8, :]).astype(bf16)
        return carry

    lax.fori_loop(0, local // 64, second_norm, 0)
    put(R2, r2_hbm)
    put(OUT, out_hbm)
    script.point()
    script.close()
    remote.finish()
    for copy in outs:
        copy.wait()


def copies_of(items, nz):
    return len(items) * (3 + max(6, nz - 1))


def run_forward(nz, x, weights, vectors, random_blocks, length):
    local = x.shape[0]
    wq, wk, wv, wo, wi, wu = weights
    grid = (nz, 2, 2, 2)
    rows, rows_u = wq.shape[0], wu.shape[0]
    seq = 2 * local
    blocks = FF // D
    outs = [
        ((local, D), bf16), ((local, D), f32), ((local, D), f32), ((blocks, local, D), f32), ((FF, local), bf16),
        ((D, local), bf16), ((D, local), bf16), ((D, local), f32), ((local, D), bf16), ((D, local), bf16), ((seq, D), bf16),
        ((D, seq), bf16), ((seq, D), bf16), ((D, seq), bf16), ((H, 1, local), f32), ((16, 128), f32),
        ((*grid, rows, 4 * D), bf16), ((*grid, rows, FF), bf16), ((*grid, rows_u, D), bf16), ((16, D), f32),
        ((H, 32, local), bf16),
    ]
    scratch = [
        ((*grid, rows, 4 * D), bf16), ((*grid, rows, FF), bf16), ((*grid, rows_u, D), bf16), ((*grid, 16, 128), bf16),
        ((2, local, D), bf16), ((D, seq), bf16), ((local, D), bf16), ((D, local), bf16), ((seq, D), bf16), ((D, seq), bf16),
        ((seq, D), bf16), ((D, seq), bf16), ((D, local), bf16), ((D, local), f32), ((local, D), f32), ((local, D), f32),
        ((local, D), bf16), ((D, local), bf16), ((local, D), f32), ((blocks, local, D), f32), ((local, FF), bf16),
        ((FF, local), bf16), ((seq, 128), bf16), ((16, D), f32), ((8, FF), f32), ((H, 1, local), f32), ((H, 1, local), f32),
        ((16, 128), f32), ((local, D), bf16), ((H, 32, local), bf16),
    ]
    scratch += [((1, v.shape[0]), bf16) for v in vectors]
    copies = copies_of(GATHER_ITEMS, nz) + 3 + (nz - 1) + 1
    return pl.pallas_call(
        functools.partial(forward_kernel, nz, local),
        out_shape=[jax.ShapeDtypeStruct(*o) for o in outs],
        in_specs=[INSMEM] + [ANY] * 17,
        out_specs=[ANY] * len(outs),
        scratch_shapes=[pltpu.VMEM(*s) for s in scratch]
        + [
            pltpu.SMEM(random_blocks.shape, jnp.int32),
            pltpu.SemaphoreType.DMA((copies,)),
            pltpu.SemaphoreType.DMA((copies,)),
            pltpu.SemaphoreType.DMA((23,)),
            pltpu.SemaphoreType.DMA((40,)),
        ],
        compiler_params=pltpu.CompilerParams(collective_id=1, has_side_effects=True, vmem_limit_bytes=VMEM_BYTES),
        name="gather_forward",
    )(length, random_blocks, x, wq, wk, wv, wo, wi, wu, *(v.reshape(1, -1) for v in vectors))


def compact_mask(random_here, length, first_block):
    blocks = random_here.shape[0]
    query = (first_block + jnp.arange(blocks, dtype=jnp.int32))[None, :, None]
    key = jnp.arange(NB, dtype=jnp.int32)[None, None, :]
    last = (length - 1) // BLK
    ok = (jnp.abs(query - key) <= 1) | (key == 0) | (key == last) | (query == 0) | (query == last)
    heads = jnp.transpose(random_here, (1, 0, 2))
    for k in range(heads.shape[2]):
        ok = ok | (heads[:, :, k : k + 1] == key)
    return jnp.where(ok, 0.0, neg_large).astype(f32)


def fill_masks(masks, random_ref, first_block, length):
    queries = masks.shape[2]
    row = lax.broadcasted_iota(jnp.int32, (32, queries), 0)
    here = lax.shift_right_logical(lax.broadcasted_iota(jnp.int32, (32, queries), 1), 6)
    one = lax.shift_right_logical(lax.broadcasted_iota(jnp.int32, (1, queries), 1), 6)
    block = here + first_block
    last = lax.shift_right_logical(length - 1, 6)
    fixed = (jnp.abs(block - row) <= 1) | (row == 0) | (row == last) | (block == 0) | (block == last) | (row > NB)
    base = jnp.where(fixed & (row != NB), 0.0, neg_large)

    def head(h, carry):
        mask = base
        for k in range(3):
            chosen = jnp.zeros((1, queries), jnp.int32)
            for b in range(queries // BLK):
                chosen = jnp.where(one == b, random_ref[h, k, 0, first_block + b], chosen)
            mask = jnp.where((row == chosen) & (row < NB), 0.0, mask)
        masks[h] = mask.astype(bf16)
        return carry

    lax.fori_loop(0, H, head, 0)


def gather_vectors(rows, width, pieces):
    n, total = rows.shape
    if n == 1:
        lane2 = lax.broadcasted_iota(jnp.int32, (pieces, total), 1).astype(f32)
        piece2 = lax.broadcasted_iota(jnp.int32, (pieces, total), 0).astype(f32)
        mine = jnp.floor((lane2 + 0.5) * (1.0 / width)) == piece2
        spread = jnp.where(mine, rows, 0.0)
    else:
        lane3 = lax.broadcasted_iota(jnp.int32, (pieces, n, total), 2).astype(f32)
        piece3 = lax.broadcasted_iota(jnp.int32, (pieces, n, total), 0).astype(f32)
        mine = jnp.floor((lane3 + 0.5) * (1.0 / width)) == piece3
        spread = jnp.where(mine, rows[None], 0.0).reshape(pieces * n, total)
    lane = lax.broadcasted_iota(jnp.int32, (128, total), 1).astype(f32)
    row = lax.broadcasted_iota(jnp.int32, (128, total), 0).astype(f32)
    owner = jnp.floor((lane + 0.5) * (1.0 / width))
    chooser = jnp.where(lane - owner * width == row, 1.0, 0.0).astype(bf16)
    high, middle, lowest = in_three(spread)
    tiles = dot_nt(high, chooser) + (dot_nt(middle, chooser) + dot_nt(lowest, chooser))
    return tiles.reshape(pieces, n, 128)


def norm_back(normal, inverse, grads, gain):
    scaled = grads * gain
    first = jnp.mean(scaled, axis=-1, keepdims=True)
    second = jnp.mean(scaled * normal, axis=-1, keepdims=True)
    return inverse * (scaled - first - normal * second)


def row_sum(values):
    return jnp.sum(values, axis=0, keepdims=True)


def back_half(pair, local, own_keys, BQ, BD, Q, QT, DA, DAT, K, KT, V, E, PB, DS, DQF, DQT, DK, DV):
    keys = slice(0, local) if own_keys else slice(local, 2 * local)
    lanes = ds128(pair, 128)
    structure = E[keys, :]
    left = jnp.concatenate([K[keys, lanes], structure], axis=1)
    left_values = jnp.concatenate([V[keys, lanes], structure], axis=1)
    empty = jnp.zeros((128 - 32, local), bf16)
    for half in (0, 1):
        h = pair * 2 + half
        own = pl.ds(pl.multiple_of(h * HD, HD), HD)
        spot = slice(half * local, (half + 1) * local)
        right = jnp.concatenate([head_rows(QT[lanes, :], half), BQ[h], empty], axis=0)
        prob = jnp.exp(dot_nn(left, right))
        PB[:, spot] = prob.astype(bf16)
        right_values = jnp.concatenate([head_rows(DAT[lanes, :], half), BD[h], empty], axis=0)
        low = (prob * dot_nn(left_values, right_values)).astype(bf16)
        DS[:, spot] = low
        part = dot_nn(KT[own, keys], low)
        if own_keys:
            DQT[own, :] = ((DQF[own, :] + part) * (HD**-0.5)).astype(bf16)
        else:
            DQF[own, :] = part
    q_pair, a_pair = Q[:, lanes], DA[:, lanes]
    DK[keys, lanes] = dot_nn(DS[...], jnp.concatenate([head_lanes(q_pair, n) for n in (0, 1)], axis=0)).astype(bf16)
    DV[keys, lanes] = dot_nn(PB[...], jnp.concatenate([head_lanes(a_pair, n) for n in (0, 1)], axis=0)).astype(bf16)


def backward_kernel(
    nz, local, length_ref, cot_hbm, r1_hbm, r2_hbm, gp_hbm, gt_hbm, n1t_hbm, at_hbm, atf_hbm, q_hbm, qt_hbm,
    k_hbm, kt_hbm, v_hbm, xt_hbm, lse_hbm, top_hbm, wa_hbm, wi_hbm, wu_hbm, vec_hbm,
    mask_hbm, dx_hbm, taken_hbm, oa_hbm, oi_hbm, ou_hbm, os_hbm, ot_hbm, *rest,
):
    place = Place(nz)
    z, x, c, y = place.z, place.x, place.c, place.y
    GA, GI, GU, WA, T, TOP, TOPS, DP, AT, DR1, E, SUMS, ISUM, SEND, RECV, VEC, OA, OI, OU = rest[:19]
    used = 19
    bufs = []
    for _ in SCATTER_ITEMS:
        bufs.append(rest[used : used + 4])
        used += 4
    sbufs = rest[used : used + 4]
    send_sems, recv_sems, load_sems = rest[used + 4 :]
    blocks = FF // D
    pieces = nz * 8
    seq_len = 2 * local
    length = length_ref[0]
    loads = [0]

    def load(src, dst):
        copy = pltpu.make_async_copy(src, dst, load_sems.at[loads[0]])
        loads[0] += 1
        copy.start()
        return copy

    remote = Remote(send_sems, recv_sems)
    stripes = [
        ScatterStripe(remote, place, (GA, GI, GU)[buf], slice(lo, lo + width), order, bufs[n], (OA, OI, OU)[buf])
        for n, (buf, lo, width, order) in enumerate(SCATTER_ITEMS)
    ]
    stripes += [TopOfAll(remote, place, TOP, TOPS), SmallSums(remote, place, T, sbufs)]
    swap = remote.make(SEND, RECV, place.at(y=1 - y))
    script = Script(SCATTER_PLAN, stripes, swap)
    grid = (nz, 2, 2, 2)
    SUMS[...] = jnp.zeros_like(SUMS)
    ISUM[...] = jnp.zeros_like(ISUM)

    def first_stage(COT, R2, R1, DM, GT, DU, GP, N1T, WUS, WIS):
        l_r2, l_cot, l_vec = load(r2_hbm, R2), load(cot_hbm, COT), load(vec_hbm, VEC)
        l_gt = load(gt_hbm, GT)
        l_wu, l_gp = [], []
        for n in range(2):
            l_wu.append(load(wu_hbm.at[n], WUS.at[n]))
            l_gp.append(load(gp_hbm.at[n], GP.at[n]))

        def wi_of(n):
            return wi_hbm.at[:, :, :, :, :, n * D : (n + 1) * D]

        script.point()
        entry_barrier(place)
        E[...] = key_structure(local, y, length)
        l_r2.wait()
        l_cot.wait()
        l_vec.wait()
        script.point()

        def second_norm(k, carry):
            rows = ds128(k, 64)
            normal, inverse = layer_norm_parts(R2[rows, :])
            position = y * local + k * 64 + lax.broadcasted_iota(jnp.int32, (64, D), 0)
            grads = jnp.where(position < length, COT[rows, :].astype(f32), 0.0)
            through = norm_back(normal, inverse, grads, VEC[6:7, :])
            R2[rows, :] = through
            low = through.astype(bf16)
            DM[rows, :] = low
            SUMS[5:6, :] += row_sum(low.astype(f32))
            SUMS[6:7, :] += row_sum(grads * normal)
            SUMS[7:8, :] += row_sum(grads)
            return carry

        lax.fori_loop(0, local // 64, second_norm, 0)
        script.point()
        l_gt.wait()
        for n in range(3):
            cols = slice(n * 256, (n + 1) * 256)

            def outer_grad(zz, carry):
                rows = ds128(zz, FF // nz)
                made = dot_nn(GT[rows, :], DM[:, cols]).astype(bf16)
                GU[zz, :, :, :, :, cols] = made.reshape(2, 2, 2, -1, 256)
                return carry

            lax.fori_loop(0, nz, outer_grad, 0)
            script.point()
        for n in range(blocks):
            l_wu[n].wait()
            l_gp[n].wait()
            grads = dot_nt(DM[...], WUS[n % 2].reshape(D, D)) * GP[n % 2]
            low = grads.astype(bf16)
            DU[n] = low
            ISUM[0:1, n * D : (n + 1) * D] = row_sum(low.astype(f32))
            if n + 2 < blocks:
                l_wu.append(load(wu_hbm.at[n + 2], WUS.at[n % 2]))
                l_gp.append(load(gp_hbm.at[n + 2], GP.at[n % 2]))
        l_top, l_n1t = load(top_hbm, TOP.at[0]), load(n1t_hbm, N1T)
        l_wi = [load(wi_of(0), WIS.at[0]), load(wi_of(1), WIS.at[1])]
        l_r1, l_at, l_wa = load(r1_hbm, R1), load(at_hbm, AT), load(wa_hbm, WA)
        wide = gather_vectors(ISUM[...], FF // pieces, pieces).reshape(*grid, 1, 128)
        T[:, :, :, :, 8:16, :] = jnp.broadcast_to(wide, (*grid, 8, 128))
        script.point()
        l_top.wait()
        l_n1t.wait()
        for n in range(blocks):
            made = dot_nn(N1T[...], DU[n]).astype(bf16)
            GI[:, :, :, :, :, n * D : (n + 1) * D] = made.reshape(*grid, -1, D)
            script.point()
        for n in range(blocks):
            l_wi[n].wait()
            R2[...] += dot_nt(DU[n], WIS[n % 2].reshape(D, D))
            if n + 2 < blocks:
                l_wi.append(load(wi_of(n + 2), WIS.at[n % 2]))
            script.point()
        l_r1.wait()

        def first_norm(k, carry):
            rows = ds128(k, 64)
            normal, inverse = layer_norm_parts(R1[rows, :])
            grads = R2[rows, :]
            through = norm_back(normal, inverse, grads, VEC[3:4, :])
            DR1[rows, :] = through
            low = through.astype(bf16)
            DP[rows, :] = low
            SUMS[2:3, :] += row_sum(low.astype(f32))
            SUMS[3:4, :] += row_sum(grads * normal)
            SUMS[4:5, :] += row_sum(grads)
            return carry

        lax.fori_loop(0, local // 64, first_norm, 0)
        script.point()
        l_at.wait()
        l_wa.wait()

    pl.run_scoped(
        first_stage,
        pltpu.VMEM((local, D), bf16), pltpu.VMEM((local, D), f32), pltpu.VMEM((local, D), f32), pltpu.VMEM((local, D), bf16),
        pltpu.VMEM((FF, local), bf16), pltpu.VMEM((blocks, local, D), bf16), pltpu.VMEM((2, local, D), f32),
        pltpu.VMEM((D, local), bf16), pltpu.VMEM((2, 2, 2, 2, FF // (nz * 8), D), bf16),
        pltpu.VMEM((2, *grid, D // (nz * 8), D), bf16),
    )

    def second_stage(Q, QT, K, KT, V, XT, LSE, BQ, BD, DA, DAT, PB, DS, DQF, DQT, DQ, DK, DV):
        pairs = ((lse_hbm, LSE), (atf_hbm, DQF), (mask_hbm, BQ), (k_hbm, K), (q_hbm, Q), (qt_hbm, QT), (kt_hbm, KT), (v_hbm, V), (xt_hbm, XT))
        waits = [load(s, d) for s, d in pairs]
        made = dot_nn(AT[...], DP[...]).astype(bf16)
        GA[:, :, :, :, :, 3 * D : 4 * D] = made.reshape(*grid, -1, D)
        script.point()
        DAT[...] = dot_nt(WA[:, :, :, :, :, 3 * D : 4 * D].reshape(D, D), DP[...]).astype(bf16)
        DA[...] = DAT[...].T
        for wait in waits[:3]:
            wait.wait()

        def prepare(h, carry):
            own = pl.ds(pl.multiple_of(h * HD, HD), HD)
            delta = row_sum(DAT[own, :].astype(f32) * DQF[own, :])
            BD[h] = with_rows(jnp.zeros((32, local), f32), delta)
            BQ[h] = with_rows(BQ[h].astype(f32), LSE[h])
            return carry

        lax.fori_loop(0, H, prepare, 0)
        for wait in waits[3:]:
            wait.wait()
        script.point()

        def halves(own_keys, g):
            def pair_step(pair, carry):
                back_half(pair, local, own_keys, BQ, BD, Q, QT, DA, DAT, K, KT, V, E, PB, DS, DQF, DQT, DK, DV)
                script.points(pair, 2 * g, 2)
                return carry

            lax.fori_loop(2 * g, 2 * g + 2, pair_step, 0)

        def group(g):
            lo = g * D
            cols = slice(g * 256, (g + 1) * 256)
            dq = DQT[cols, :].T
            DQ[:, cols] = dq
            SUMS[0:1, cols] = row_sum(dq.astype(f32))
            SUMS[1:2, cols] = row_sum(DV[:, cols].astype(f32))
            for n, made in enumerate(
                (dot_nn(XT[:, :local], dq), dot_nn(XT[...], DK[:, cols]), dot_nn(XT[...], DV[:, cols]))
            ):
                GA[:, :, :, :, :, lo + n * 256 : lo + (n + 1) * 256] = made.astype(bf16).reshape(*grid, -1, 256)
            script.point()

        halves(False, 0)
        halves(True, 0)
        group(0)
        halves(False, 1)
        halves(False, 2)
        groups = [slice(g * 256, (g + 1) * 256) for g in range(3)]
        theirs = jnp.concatenate([a[local:, cols] for cols in groups for a in (DK, DV)], axis=1)
        through = [WA[:, :, :, :, :, g * D + 256 : (g + 1) * D].reshape(D, 512) for g in range(3)]
        SEND[...] = dot_nt(theirs, jnp.concatenate(through, axis=1)).astype(bf16)
        script.point()
        halves(True, 1)
        group(1)
        halves(True, 2)
        group(2)
        T[:, :, :, :, 0:8, :] = gather_vectors(SUMS[0:8, :], D // pieces, pieces).reshape(*grid, 8, 128)
        script.point()
        for g in range(3):
            cols = slice(g * 256, (g + 1) * 256)
            ours = jnp.concatenate([DQ[:, cols], DK[:local, cols], DV[:local, cols]], axis=1)
            DR1[...] += dot_nt(ours, WA[:, :, :, :, :, g * D : (g + 1) * D].reshape(D, D))
            script.point()
        script.close()
        out = pltpu.make_async_copy(DR1, dx_hbm, load_sems.at[loads[0]])
        out.start()
        swap.wait_recv()
        taken = pltpu.make_async_copy(RECV, taken_hbm, load_sems.at[loads[0] + 1])
        taken.start()
        pairs = ((OA, oa_hbm), (OI, oi_hbm), (OU, ou_hbm), (T.at[z, x, c, y], os_hbm), (TOP.at[4], ot_hbm))
        ends = [pltpu.make_async_copy(s, d, load_sems.at[loads[0] + 2 + n]) for n, (s, d) in enumerate(pairs)]
        for end in ends:
            end.start()
        for end in (out, taken, *ends):
            end.wait()

    scoped = [
        ((local, D), bf16), ((D, local), bf16), ((seq_len, D), bf16), ((D, seq_len), bf16), ((seq_len, D), bf16),
        ((D, seq_len), bf16), ((H, 1, local), f32), ((H, 32, local), bf16), ((H, 32, local), bf16), ((local, D), bf16),
        ((D, local), bf16), ((local, 2 * local), bf16), ((local, 2 * local), bf16), ((D, local), f32), ((D, local), bf16),
        ((local, D), bf16), ((seq_len, D), bf16), ((seq_len, D), bf16),
    ]
    pl.run_scoped(second_stage, *(pltpu.VMEM(*s) for s in scoped))
    remote.finish()


def run_backward(nz, local, rows, rows_u, length, *arrays):
    grid = (nz, 2, 2, 2)
    seq = 2 * local
    outs = [((local, D), f32), ((local, D), bf16), ((rows, 4 * D), f32), ((rows, FF), f32), ((rows_u, D), f32)]
    outs += [((16, 128), f32)] * 2
    scratch = [
        ((*grid, rows, 4 * D), bf16), ((*grid, rows, FF), bf16), ((*grid, rows_u, D), bf16), ((*grid, rows, 4 * D), bf16),
        ((*grid, 16, 128), f32), ((5, 16, 128), f32), ((3 + nz - 1, 16, 128), f32),
        ((local, D), bf16), ((D, local), bf16), ((local, D), f32), ((seq, 128), bf16),
        ((8, D), f32), ((1, FF), f32), ((local, D), bf16), ((local, D), bf16),
        ((16, D), f32), ((rows, 4 * D), f32), ((rows, FF), f32), ((rows_u, D), f32),
    ]
    for buf, _, width, order in SCATTER_ITEMS:
        scratch += scatter_buffers(nz, rows_u if buf == 2 else rows, width, order)
    scratch += small_buffers(nz)
    copies = copies_of(SCATTER_ITEMS, nz) + 2 * (3 + nz - 1) + 1
    return pl.pallas_call(
        functools.partial(backward_kernel, nz, local),
        out_shape=[jax.ShapeDtypeStruct(*o) for o in outs],
        in_specs=[INSMEM] + [ANY] * len(arrays),
        out_specs=[ANY] * len(outs),
        scratch_shapes=[pltpu.VMEM(*s) for s in scratch]
        + [pltpu.SemaphoreType.DMA((copies,)), pltpu.SemaphoreType.DMA((copies,)), pltpu.SemaphoreType.DMA((40,))],
        compiler_params=pltpu.CompilerParams(collective_id=2, has_side_effects=True, vmem_limit_bytes=VMEM_BYTES),
        name="backward_scatter",
    )(length, *arrays)


def finish_kernel(
    threshold_ref, dx_hbm, taken_hbm, ga_hbm, gi_hbm, gu_hbm, gs_hbm, top_hbm, out_hbm, WQ, WK, BQ,
    o_out, o_dx, o_q, o_k, o_v, o_o, o_i, o_u, o_wq, o_wk, o_bq, o_top, *rest,
):
    v_hbm, (DX, TAKEN, GS, TOP, GA, GI, GU, OUT), (s_wq, s_wk, s_bq, s_top), o_vecs, sems = (
        rest[:9], rest[9:17], rest[17:21], rest[21:30], rest[30]
    )
    pairs = [(dx_hbm, DX), (taken_hbm, TAKEN), (ga_hbm, GA), (gi_hbm, GI), (gu_hbm, GU), (out_hbm, OUT), (gs_hbm, GS), (top_hbm, TOP)]
    loads = [pltpu.make_async_copy(src, dst, sems.at[n]) for n, (src, dst) in enumerate(pairs)]
    for copy in loads:
        copy.start()
    stores = []

    def put(src, dst):
        copy = pltpu.make_async_copy(src, dst, sems.at[len(loads) + len(stores)])
        copy.start()
        stores.append(copy)

    loads[0].wait()
    loads[1].wait()
    DX[...] = DX[...] + TAKEN[...].astype(f32)
    put(DX, o_dx)
    loads[2].wait()
    for g in range(3):
        for n, o in enumerate((o_q, o_k, o_v)):
            lo = g * D + n * 256
            put(GA.at[:, lo : lo + 256], o.at[:, g * 256 : (g + 1) * 256])
    put(GA.at[:, 3 * D : 4 * D], o_o)
    for copy, src, dst in zip(loads[3:6], (GI, GU, OUT), (o_i, o_u, o_out)):
        copy.wait()
        put(src, dst)
    loads[6].wait()
    loads[7].wait()
    for n, o in enumerate(o_vecs):
        o[...] = GS[n : n + 1, 0 : o.shape[1]]
    limit = threshold_ref[0].astype(f32) * 0.01
    top = TOP[...]
    factors = jnp.sqrt(limit / jnp.maximum(top, limit))
    head = lax.broadcasted_iota(jnp.int32, (16, D), 0)
    column = lax.broadcasted_iota(jnp.int32, (16, D), 1)
    wide = jnp.concatenate([factors] * (D // 128), axis=1)
    scale = row_sum(jnp.where(head == lax.shift_right_logical(column, 6), wide, 0.0))
    s_wq[...] = (WQ[...].astype(f32) * scale).astype(bf16)
    s_wk[...] = (WK[...].astype(f32) * scale).astype(bf16)
    count = BQ.shape[1]
    row = lax.broadcasted_iota(jnp.int32, (16, 128), 0)
    lane = lax.broadcasted_iota(jnp.int32, (16, 128), 1)
    entry = (lax.axis_index("dp") * 2 + lax.axis_index("ctx")) * count + lane
    own = row_sum(jnp.where(row == lax.shift_right_logical(entry, 6), factors, 0.0))
    s_bq[...] = (BQ[...].astype(f32) * own[:, 0:count]).astype(bf16)
    s_top[...] = row_sum(jnp.where(row == lane, top, 0.0))[:, 0:H]
    for src, dst in zip((s_wq, s_wk, s_bq, s_top, *o_vecs), (o_wq, o_wk, o_bq, o_top, *v_hbm)):
        put(src, dst)
    for copy in stores:
        copy.wait()


def run_finish(threshold, dx, taken, ga, gi, gu, gs, top, output, wq, wk, bq, wide):
    local, rows, rows_u, count = dx.shape[0], ga.shape[0], gu.shape[0], bq.shape[0]
    outs = [((local, D), bf16), ((local, D), f32)] + [((rows, D), f32)] * 4 + [((rows, FF), f32), ((rows_u, D), f32)]
    outs += [((rows, D), bf16)] * 2 + [((1, count), bf16), ((1, H), f32)] + [((1, count), f32)] * 8 + [((1, wide), f32)]
    return pl.pallas_call(
        finish_kernel,
        out_shape=[jax.ShapeDtypeStruct(*o) for o in outs],
        in_specs=[INSMEM] + [ANY] * 8 + [INVMEM] * 3,
        out_specs=[ANY] * len(outs),
        scratch_shapes=[
            pltpu.VMEM((local, D), f32), pltpu.VMEM((local, D), bf16), pltpu.VMEM((16, 128), f32), pltpu.VMEM((16, 128), f32),
            pltpu.VMEM((rows, 4 * D), f32), pltpu.VMEM((rows, FF), f32), pltpu.VMEM((rows_u, D), f32),
            pltpu.VMEM((local, D), bf16),
        ]
        + [pltpu.VMEM(*o) for o in outs[8:]]
        + [pltpu.SemaphoreType.DMA((36,))],
        compiler_params=pltpu.CompilerParams(vmem_limit_bytes=VMEM_BYTES),
        name="finish",
    )(threshold, dx, taken, ga, gi, gu, gs, top, output, wq, wk, bq.reshape(1, -1))


def layer_norm(row_values, gain_vector, shift_vector):
    centre = row_values - jnp.mean(row_values, axis=-1, keepdims=True)
    spread = jnp.mean(centre * centre, axis=-1, keepdims=True)
    return centre * lax.rsqrt(spread + norm_eps) * gain_vector + shift_vector


def gelu_exact(values):
    return jax.nn.gelu(values, approximate=False)


def column_sums(values):
    return jnp.sum(values.astype(f32), axis=0)


def clip_outputs(logit_maxima, threshold, query_weight, query_bias, key_weight, device_rank):
    clip_limit = threshold.astype(f32)[0] * 0.01
    factors = jnp.sqrt(clip_limit / jnp.maximum(logit_maxima, clip_limit))
    column_scale = jnp.repeat(factors, HD)
    query_clipped = (query_weight.astype(f32) * column_scale[None, :]).astype(bf16)
    key_clipped = (key_weight.astype(f32) * column_scale[None, :]).astype(bf16)
    bias_count = query_bias.shape[0]
    bias_heads = (device_rank * bias_count + jnp.arange(bias_count)) // HD
    bias_scale = jnp.sum(jnp.where(bias_heads[:, None] == jnp.arange(H)[None, :], factors[None, :], 0.0), axis=1)
    return query_clipped, (query_bias.astype(f32) * bias_scale).astype(bf16), key_clipped


def fast_shards(
    nz,
    inputs, cotangent, query_weight, query_bias, key_weight, value_weight, value_bias, output_weight, output_bias,
    first_gain, first_shift, inner_weight, inner_bias, outer_weight, outer_bias, second_gain, second_shift,
    lengths, random_blocks, threshold,
):
    local = inputs.shape[1]
    pieces = nz * 8
    rows, rows_u = query_weight.shape[0], outer_weight.shape[0]
    small = (
        query_bias, value_bias, output_bias, first_gain, first_shift, outer_bias, second_gain, second_shift, inner_bias
    )
    x = inputs[0]
    weights = (query_weight, key_weight, value_weight, output_weight, inner_weight, outer_weight)
    output, *saved = run_forward(nz, x, weights, small, jnp.transpose(random_blocks, (2, 3, 0, 1)), lengths)
    made = run_backward(nz, local, rows, rows_u, lengths, cotangent[0], *saved)
    (
        output, input_grad, g_query, g_key, g_value, g_out, g_inner, g_outer, query_clipped, key_clipped, bias_clipped, top, *vec
    ) = run_finish(threshold, *made, output, query_weight, key_weight, query_bias, FF // pieces)
    vec = [v.reshape(-1) for v in vec]
    return (
        output[None], input_grad[None],
        g_query, vec[0], g_key, g_value, vec[1], g_out, vec[2], vec[3], vec[4],
        g_inner, vec[8], g_outer, vec[5], vec[6], vec[7],
        query_clipped, bias_clipped.reshape(-1), key_clipped, top.reshape(-1),
    )


def general_shards(
    inputs, cotangent, query_weight, query_bias, key_weight, value_weight, value_bias, output_weight, output_bias,
    first_gain, first_shift, inner_weight, inner_bias, outer_weight, outer_bias, second_gain, second_shift,
    lengths, random_blocks, threshold,
):
    both = ("dp", "ctx")
    shards = (
        query_weight, query_bias, key_weight, value_weight, value_bias, output_weight, output_bias, first_gain, first_shift,
        inner_weight, inner_bias, outer_weight, outer_bias, second_gain, second_shift,
    )
    wq, bq, wk, wv, bv, wo, bo, g1, s1, wi, bi, wu, bu, g2, s2 = (lax.all_gather(w, both, axis=0, tiled=True) for w in shards)
    bq, bv, bo, g1, s1, bi, bu, g2, s2 = (v.astype(f32) for v in (bq, bv, bo, g1, s1, bi, bu, g2, s2))
    seqs, local, _ = inputs.shape
    blocks = local // BLK
    y = lax.axis_index("ctx")
    first_block = y * blocks
    scale = HD**-0.5
    outs = []
    sums = None
    top = jnp.full((H,), neg_large, f32)
    for s in range(seqs):
        x, length = inputs[s], lengths[s]
        random_here = lax.dynamic_slice_in_dim(random_blocks[s], first_block, blocks, 0)
        mask = compact_mask(random_here, length, first_block)
        mask = jnp.repeat(jnp.repeat(mask, BLK, axis=1), BLK, axis=2)
        seen = jnp.arange(NB * BLK) < length
        mask = jnp.where(seen[None, None, :], mask, neg_large)
        live = (y * local + jnp.arange(local)) < length
        q = (dot_nn(x, wq) + bq).astype(bf16)
        k = lax.all_gather(dot_nn(x, wk).astype(bf16), "ctx", axis=0, tiled=True)
        v = lax.all_gather((dot_nn(x, wv) + bv).astype(bf16), "ctx", axis=0, tiled=True)
        qh, kh, vh = (a.reshape(-1, H, HD) for a in (q, k, v))
        raw = jnp.einsum("qhd,khd->hqk", qh, kh, preferred_element_type=f32) * scale + mask
        row_top = jnp.max(raw, axis=-1, keepdims=True)
        top = jnp.maximum(top, jnp.max(jnp.where(live[None, :, None], row_top, neg_large), axis=(1, 2)))
        exponent = jnp.exp(raw - row_top)
        prob = exponent / jnp.sum(exponent, axis=-1, keepdims=True)
        low = prob.astype(bf16)
        attended = jnp.einsum("hqk,khd->qhd", low, vh, preferred_element_type=f32).reshape(local, D).astype(bf16)
        first_sum = x.astype(f32) + dot_nn(attended, wo) + bo
        normed = layer_norm(first_sum, g1, s1)
        normed_low = normed.astype(bf16)
        pre_act = dot_nn(normed_low, wi) + bi
        activated = gelu_exact(pre_act).astype(bf16)
        second_sum = normed + dot_nn(activated, wu) + bu
        output = layer_norm(second_sum, g2, s2).astype(bf16)
        cot = jnp.where(live[:, None], cotangent[s].astype(f32), 0.0)
        grad_second, g2_grad, s2_grad = jax.vjp(layer_norm, second_sum, g2, s2)[1](cot)
        dm = grad_second.astype(bf16)
        du = jax.vjp(gelu_exact, pre_act)[1](dot_nt(dm, wu))[0].astype(bf16)
        grad_normed = grad_second + dot_nt(du, wi)
        grad_first, g1_grad, s1_grad = jax.vjp(layer_norm, first_sum, g1, s1)[1](grad_normed)
        dp = grad_first.astype(bf16)
        da = dot_nt(dp, wo).astype(bf16).reshape(local, H, HD)
        dprob = jnp.einsum("qhd,khd->hqk", da, vh, preferred_element_type=f32)
        ds = (prob * (dprob - jnp.sum(prob * dprob, axis=-1, keepdims=True))).astype(bf16)
        dq = (jnp.einsum("hqk,khd->qhd", ds, kh, preferred_element_type=f32) * scale).reshape(local, D).astype(bf16)
        dk = (jnp.einsum("hqk,qhd->khd", ds, qh, preferred_element_type=f32) * scale).reshape(-1, D)
        dv = jnp.einsum("hqk,qhd->khd", low, da, preferred_element_type=f32).reshape(-1, D)
        dk, dv = (lax.psum_scatter(a.astype(bf16), "ctx", scatter_dimension=0, tiled=True).astype(bf16) for a in (dk, dv))
        input_grad = grad_first + dot_nt(dq, wq) + dot_nt(dk, wk) + dot_nt(dv, wv)
        outs.append((output, input_grad))
        here = (
            dot_tn(x, dq), column_sums(dq), dot_tn(x, dk), dot_tn(x, dv), column_sums(dv), dot_tn(attended, dp),
            column_sums(dp), g1_grad, s1_grad, dot_tn(normed_low, du), column_sums(du), dot_tn(activated, dm),
            column_sums(dm), g2_grad, s2_grad,
        )
        sums = here if sums is None else tuple(a + b for a, b in zip(sums, here))
    grads = tuple(lax.psum_scatter(g, both, scatter_dimension=0, tiled=True) for g in sums)
    logit_maxima = lax.pmax(top, both)
    rank = lax.axis_index(both)
    clipped = clip_outputs(logit_maxima, threshold, query_weight, query_bias, key_weight, rank)
    return (jnp.stack([o for o, _ in outs]), jnp.stack([g for _, g in outs]), *grads, *clipped, logit_maxima)


def solution(mesh):
    both = P(("dp", "ctx"))
    rows = P(("dp", "ctx"), None)
    tokens = P("dp", "ctx", None)
    in_specs = (
        tokens, tokens, rows, both, rows, rows, both, rows, both, both, both, rows, both, rows, both, both, both,
        P("dp"), P("dp", None, None, None), P(),
    )
    out_specs = (
        tokens, tokens, rows, both, rows, rows, both, rows, both, both, both, rows, both, rows, both, both, both,
        rows, both, rows, P(),
    )
    dp, ctx = mesh.shape["dp"], mesh.shape["ctx"]
    pieces = dp * ctx
    fits = ctx == 2 and dp % 4 == 0 and D % (8 * pieces) == 0 and FF // pieces <= 128

    def step(*args):
        if fits and args[0].shape[0] == 1:
            return fast_shards(dp // 4, *args)
        return general_shards(*args)

    return jax.shard_map(step, mesh=mesh, in_specs=in_specs, out_specs=out_specs, check_vma=False)
```
